32 devices in a mesh: wide: 8 (over y, x, core), tp: 4 (over z).
Axes of the slice: x: 2, y: 2, z: 4, core: 2. Of those that a mesh axis runs over, the one named last changes fastest.
Arguments:
- tokens: float32 [8192, 768], P('wide'), may hold values from -6 to 6
- segment_ids: int32 [8, 1024], P('wide'), may hold values from 0 to 3, never falling along the last dimension, each value on 1 to 800 neighbouring positions
- routes: int32 [8192, 1], P('wide'), may hold values from 0 to 7
- out_grad: float32 [8192, 768], P('wide'), may hold values from -6 to 6
- mixer_gain: float32 [768], replicated, may hold values from 0.5 to 1.5
- in_proj_x: bfloat16 [768, 1536], P('wide', 'tp'), may hold values from -0.21875 to 0.21875
- in_proj_z: bfloat16 [768, 1536], P('wide', 'tp'), may hold values from -0.21875 to 0.21875
- conv_weight: float32 [4, 1536], P(None, 'tp'), may hold values from -3 to 3
- conv_bias: float32 [1536], P('tp'), may hold values from -4 to 4
- state_proj: bfloat16 [1536, 80], P('tp'), may hold values from -0.3125 to 0.3125
- step_proj: bfloat16 [48, 1536], P(None, 'tp'), may hold values from -0.875 to 0.875
- step_bias: float32 [1536], P('tp'), may hold values from -6.5 to -2.2
- log_rates: float32 [16, 1536], P(None, 'tp'), may hold values from -0.7 to 2.8
- skip_gain: float32 [1536], P('tp'), may hold values from 0.5 to 1.5
- out_proj: bfloat16 [768, 1536], P('wide', 'tp'), may hold values from -0.3125 to 0.3125
- expert_gain: float32 [768], replicated, may hold values from 0.5 to 1.5
- router_weight: bfloat16 [768, 8], replicated, may hold values from -0.21875 to 0.21875
- expert_up: bfloat16 [8, 768, 3072], P('wide', None, 'tp'), may hold values from -0.21875 to 0.21875
- up_bias: float32 [8, 3072], P('wide', 'tp'), may hold values from -1.5 to 1.5
- expert_down: bfloat16 [8, 3072, 768], P('wide', 'tp'), may hold values from -0.21875 to 0.21875
- down_bias: float32 [8, 768], P('wide'), may hold values from -1.5 to 1.5
Outputs:
- result: float32 [8192, 768], P('wide')
- tokens_grad: float32 [8192, 768], P('wide')
- grad_mixer_gain: float32 [768], replicated
- grad_in_proj_x: float32 [768, 1536], P('wide', 'tp')
- grad_in_proj_z: float32 [768, 1536], P('wide', 'tp')
- grad_conv_weight: float32 [4, 1536], P(None, 'tp')
- grad_conv_bias: float32 [1536], P('tp')
- grad_state_proj: float32 [1536, 80], P('tp')
- grad_step_proj: float32 [48, 1536], P(None, 'tp')
- grad_step_bias: float32 [1536], P('tp')
- grad_log_rates: float32 [16, 1536], P(None, 'tp')
- grad_skip_gain: float32 [1536], P('tp')
- grad_out_proj: float32 [768, 1536], P('wide', 'tp')
- grad_expert_gain: float32 [768], replicated
- grad_router_weight: float32 [768, 8], replicated
- grad_expert_up: float32 [8, 768, 3072], P('wide', None, 'tp')
- grad_up_bias: float32 [8, 3072], P('wide', 'tp')
- grad_expert_down: float32 [8, 3072, 768], P('wide', 'tp')
- grad_down_bias: float32 [8, 768], P('wide')
The draws below stay inside these ranges and needn't reach their ends.
Inputs may be any that keep to these rules, and one draw needn't show every extreme that they name: `segment_ids`: document numbers never fall along a row; each document spans 1 to 800 positions, one exactly 800. `routes`: every expert is named by some token.
All inputs are finite; a program needn't handle non-finite values.
Results may differ from the reference program's by a relative error of at most 0.02.
Values may be sent and summed in bfloat16 or wider, within the bound.
A program may use at most 128 MiB of HBM per device.

```python
import math
import jax
import jax.numpy as jnp
import numpy as np
from jax import lax

D = 768
DI = 1536
NSTATE = 16
DT_RANK = 48
KCONV = 4
FF = 3072
SEQ_LEN = 1024
DOCS = 4
DOC_MOST = 800
SEQS = 8
TOKENS = 8192
EXPERTS = 8
CAP = 160


def block_scale(own_key, shape, pieces, least, high):
    loudness = 1.0
    for dim, blocks in pieces:
        heights = jax.random.uniform(jax.random.fold_in(jax.random.fold_in(own_key, 6), dim), (blocks,), jnp.float32, least / len(pieces), high / len(pieces))
        loudness = loudness * jnp.repeat(jnp.exp(heights), shape[dim] // blocks).reshape((-1,) + (1,) * (len(shape) - 1 - dim))
    return loudness


def different_ones(stream_key, rows, number_of, top, lift):
    sequence = jax.random.permutation(jax.random.fold_in(stream_key, 1), number_of)
    favour = sequence
    for power in range(3):
        favour = favour * favour // number_of
    favour = favour * lift // number_of
    chance = jax.random.randint(jax.random.fold_in(stream_key, 2), (rows, number_of), 0, 4096) + favour
    holders = jax.random.permutation(jax.random.fold_in(stream_key, 3), rows)[jnp.arange(number_of) % rows]
    chance = jnp.where(jnp.arange(rows)[:, None] == holders[None, :], 1 << 14, chance)
    score = chance * number_of + jnp.arange(number_of)
    return lax.top_k(score.astype(jnp.int32), top)[1].astype(jnp.int32)


def split_up(amount, total, bound, skew):
    portions = [(1 << 20) // math.isqrt(rank ** skew) + 1 for rank in range(2, amount + 1)]
    rest, counts = total - bound - (amount - 1), [1] * (amount - 1)
    while rest > 0:
        free = [i for i in range(amount - 1) if counts[i] < bound]
        whole, budget = sum([portions[i] for i in free]), rest
        for i in free:
            extra = min(bound - counts[i], max(1, budget * portions[i] // whole), rest)
            counts[i] = counts[i] + extra
            rest = rest - extra
    return np.array([bound] + counts)


def uneven_parts(rng, count, total, reach, slope):
    if count == 2:
        one = jax.random.randint(rng, (), max(1, total - reach), min(reach, total - 1) + 1)
        return jnp.stack([one, total - one])
    tallies = jnp.asarray(split_up(count, total, reach, slope), jnp.int32)
    couples = (count - 1) // 2
    giver, sink = tallies[1:1 + 2 * couples:2], tallies[2:2 + 2 * couples:2]
    slack = jnp.minimum(giver - 1, reach - sink)
    passed = jax.random.randint(jax.random.fold_in(rng, 1), (couples,), 0, 1 << 20) % (slack + 1)
    tallies = tallies.at[1:1 + 2 * couples:2].set(giver - passed).at[2:2 + 2 * couples:2].set(sink + passed)
    return tallies[jax.random.permutation(jax.random.fold_in(rng, 2), count)]


def scatter_about(rng, dims, spread, limit, split=(), kind=jnp.bfloat16):
    factor_of = block_scale(rng, dims, split, -0.22, 0.18) if split else 1.0
    values = jax.random.normal(rng, dims, jnp.float32) * spread * factor_of
    return jnp.minimum(jnp.maximum(values, -limit), limit).astype(kind)


def setup_inputs(seed: int = 0) -> dict:
    keys = jax.random.split(jax.random.key(seed), 22)
    tokens = scatter_about(keys[0], (TOKENS, D), 1.0, 6.0, ((0, 8),), jnp.float32)
    segment_ids = jax.vmap(lambda own: jnp.searchsorted(jnp.cumsum(uneven_parts(own, DOCS, SEQ_LEN, DOC_MOST, 1)), jnp.arange(SEQ_LEN), side="right"))(jax.random.split(keys[1], SEQS)).reshape((SEQS, SEQ_LEN)).astype(jnp.int32)
    routes = different_ones(keys[2], TOKENS, EXPERTS, 1, 1024)
    out_grad = scatter_about(keys[3], (TOKENS, D), 1.0, 6.0, ((0, 8),), jnp.float32)
    mixer_gain = jnp.clip(1.0 + 0.1 * jax.random.normal(keys[4], (D,), jnp.float32), 0.5, 1.5)
    in_proj_x = scatter_about(keys[5], (D, DI), D ** -0.5, 0.21875, ((0, 8), (1, 4)))
    in_proj_z = scatter_about(keys[6], (D, DI), D ** -0.5, 0.21875, ((0, 8), (1, 4)))
    conv_weight = scatter_about(keys[7], (KCONV, DI), KCONV ** -0.5, 3.0, ((1, 4),), jnp.float32)
    conv_bias = scatter_about(keys[8], (DI,), 0.3, 4.0, ((0, 4),), jnp.float32)
    state_proj = scatter_about(keys[9], (DI, DT_RANK + 2 * NSTATE), (DI // 4) ** -0.5, 0.3125, ((0, 4),))
    step_proj = scatter_about(keys[10], (DT_RANK, DI), DT_RANK ** -0.5, 0.875, ((1, 4),))
    step_bias = jnp.clip(-6.5 + 4.3 * jax.random.uniform(keys[11], (DI,), jnp.float32) ** block_scale(keys[11], (DI,), ((0, 4),), -0.2, 0.2), -6.5, -2.2)
    log_rates = jnp.clip(-0.7 + 3.5 * jax.random.uniform(keys[12], (NSTATE, DI), jnp.float32) ** block_scale(keys[12], (NSTATE, DI), ((1, 4),), -0.2, 0.2), -0.7, 2.8)
    skip_gain = jnp.clip(0.5 + 1.0 * jax.random.uniform(keys[13], (DI,), jnp.float32) ** block_scale(keys[13], (DI,), ((0, 4),), -0.2, 0.2), 0.5, 1.5)
    out_proj = scatter_about(keys[14], (D, DI), (DI // 4) ** -0.5, 0.3125, ((0, 8), (1, 4)))
    expert_gain = jnp.clip(1.0 + 0.1 * jax.random.normal(keys[15], (D,), jnp.float32), 0.5, 1.5)
    router_weight = scatter_about(keys[16], (D, EXPERTS), D ** -0.5, 0.21875)
    expert_up = scatter_about(keys[17], (EXPERTS, D, FF), D ** -0.5, 0.21875, ((0, 8), (2, 4)))
    up_bias = scatter_about(keys[18], (EXPERTS, FF), 0.1, 1.5, ((0, 8), (1, 4)), jnp.float32)
    expert_down = scatter_about(keys[19], (EXPERTS, FF, D), (FF // 4) ** -0.5, 0.21875, ((0, 8), (1, 4)))
    down_bias = scatter_about(keys[20], (EXPERTS, D), 0.1, 1.5, ((0, 8),), jnp.float32)
    return {"tokens": tokens, "segment_ids": segment_ids, "routes": routes, "out_grad": out_grad, "mixer_gain": mixer_gain, "in_proj_x": in_proj_x, "in_proj_z": in_proj_z, "conv_weight": conv_weight, "conv_bias": conv_bias, "state_proj": state_proj, "step_proj": step_proj, "step_bias": step_bias, "log_rates": log_rates, "skip_gain": skip_gain, "out_proj": out_proj, "expert_gain": expert_gain, "router_weight": router_weight, "expert_up": expert_up, "up_bias": up_bias, "expert_down": expert_down, "down_bias": down_bias}


EPS = 1e-05
HIGH = lax.Precision.HIGHEST

@jax.custom_vjp
def low(v):
    return lax.optimization_barrier(v.astype(jnp.bfloat16)).astype(jnp.float32)

@jax.custom_vjp
def low_back(v):
    return v

def low_keep(v):
    return (low(v), None)

def low_pass(kept, grad):
    return (grad,)

def back_keep(v):
    return (v, None)

def back_low(kept, grad):
    return (low(grad),)
low.defvjp(low_keep, low_pass)
low_back.defvjp(back_keep, back_low)

def precise(left, right):
    return jnp.dot(left, right, precision=HIGH)

def shifted_down(values, steps):
    if steps == 0:
        return values
    filler = jnp.zeros((steps,) + values.shape[1:], values.dtype)
    return jnp.concatenate([filler, values[:-steps]], axis=0)

def same_document(doc_ids, steps):
    if steps == 0:
        return jnp.ones(doc_ids.shape, jnp.float32)
    filler = jnp.full((steps,), -1, jnp.int32)
    earlier = jnp.concatenate([filler, doc_ids[:-steps]])
    return (earlier == doc_ids).astype(jnp.float32)

def forward(tokens, doc_ids, route_ids, mixer_gain, in_proj_x, in_proj_z, conv_weight, conv_bias, state_proj, step_proj, step_bias, log_rates, skip_gain, out_proj, expert_gain, router_weight, expert_up, up_bias, expert_down, down_bias):
    first_scale = lax.rsqrt(lax.optimization_barrier(jnp.mean(tokens * tokens, axis=1, keepdims=True)) + EPS)
    normed = low(tokens * first_scale * mixer_gain)
    x_branch = low_back(precise(normed, in_proj_x))
    z_branch = low_back(precise(normed, in_proj_z))
    conv_sum = conv_bias + jnp.zeros_like(x_branch)
    for offset in range(KCONV):
        conv_sum = conv_sum + conv_weight[KCONV - 1 - offset] * same_document(doc_ids, offset)[:, None] * shifted_down(x_branch, offset)
    inner = low(jax.nn.silu(conv_sum))
    projected = low_back(precise(inner, state_proj))
    step_in = low(projected[:, :DT_RANK])
    in_coeff = projected[:, DT_RANK:DT_RANK + NSTATE]
    out_coeff = projected[:, DT_RANK + NSTATE:]
    step_size = jax.nn.softplus(low_back(precise(step_in, step_proj) + step_bias))
    rates = -jnp.exp(log_rates)
    carry_mask = same_document(doc_ids, 1)

    def advance_state(state, item):
        step_row, inner_row, in_row, out_row, mask_row = item
        state = jnp.exp(step_row[None, :] * rates) * mask_row * state + (step_row * inner_row)[None, :] * in_row[:, None]
        return (state, lax.optimization_barrier(jnp.sum(state * out_row[:, None], axis=0)))
    start = jnp.zeros((NSTATE, DI), jnp.float32)
    _, scan_out = lax.scan(jax.checkpoint(advance_state), start, (step_size, inner, in_coeff, out_coeff, carry_mask))
    scan_out = scan_out + skip_gain * inner
    gated = low(scan_out * jax.nn.silu(z_branch))
    hidden = tokens + low_back(precise(gated, out_proj.T))
    second_scale = lax.rsqrt(lax.optimization_barrier(jnp.mean(hidden * hidden, axis=1, keepdims=True)) + EPS)
    expert_in = low(hidden * second_scale * expert_gain)
    chosen_int = (route_ids[:, None] == jnp.arange(EXPERTS, dtype=jnp.int32)[None, :]).astype(jnp.int32)
    logits = precise(expert_in, router_weight)
    gate = jax.nn.sigmoid(lax.optimization_barrier(jnp.sum(logits * chosen_int.astype(jnp.float32), axis=1)))
    position = lax.optimization_barrier(jnp.sum((jnp.cumsum(chosen_int, axis=0) - 1) * chosen_int, axis=1))
    slots = jnp.where(position < CAP, route_ids * CAP + position, -1)
    placing = (slots[:, None] == jnp.arange(EXPERTS * CAP, dtype=jnp.int32)[None, :]).astype(jnp.float32)
    rows_in = low_back(precise(placing.T, expert_in)).reshape(EXPERTS, CAP, D)
    pre_act = low_back(jnp.einsum('ecd,edf->ecf', rows_in, expert_up, precision=HIGH) + up_bias[:, None, :])
    hidden_act = low(jax.nn.gelu(pre_act))
    expert_out = jnp.einsum('ecf,efd->ecd', hidden_act, expert_down, precision=HIGH) + down_bias[:, None, :]
    expert_out = low_back(low(expert_out))
    returned = precise(placing, expert_out.reshape(EXPERTS * CAP, D))
    return hidden + gate[:, None] * returned

def reference(tokens, segment_ids, routes, out_grad, mixer_gain, in_proj_x, in_proj_z, conv_weight, conv_bias, state_proj, step_proj, step_bias, log_rates, skip_gain, out_proj, expert_gain, router_weight, expert_up, up_bias, expert_down, down_bias):
    params = tuple((p.astype(jnp.float32) for p in (mixer_gain, in_proj_x, in_proj_z, conv_weight, conv_bias, state_proj, step_proj, step_bias, log_rates, skip_gain, out_proj, expert_gain, router_weight, expert_up, up_bias, expert_down, down_bias)))

    def one_sequence(totals, item):
        rows, doc_ids, route_ids, cotangent = item

        def run(rows_in, *weights):
            return forward(rows_in, doc_ids, route_ids, *weights)
        outcome, pull = jax.vjp(run, rows, *params)
        grads = pull(cotangent)
        totals = tuple((total + grad for total, grad in zip(totals, grads[1:])))
        return (totals, (outcome, grads[0]))
    zeros = tuple((jnp.zeros_like(p) for p in params))
    items = (tokens.reshape(SEQS, SEQ_LEN, D), segment_ids, routes.reshape(SEQS, SEQ_LEN), out_grad.reshape(SEQS, SEQ_LEN, D))
    totals, (outcomes, row_grads) = lax.scan(one_sequence, zeros, items)
    return (outcomes.reshape(TOKENS, D), row_grads.reshape(TOKENS, D), totals[0], totals[1], totals[2], totals[3], totals[4], totals[5], totals[6], totals[7], totals[8], totals[9], totals[10], totals[11], totals[12], totals[13], totals[14], totals[15], totals[16])
```

```python
import functools

import jax
import jax.numpy as jnp
from jax import lax
from jax.experimental import pallas as pl
from jax.experimental.pallas import tpu as pltpu
from jax.sharding import PartitionSpec as P

EPS = 1e-05
HIGH = lax.Precision.HIGHEST


def in_blocks(shard, dim, size):
    before, after = (shard.shape[:dim], shard.shape[dim + 1 :])
    return jnp.moveaxis(shard.reshape(*before, size, -1, *after), dim, 0)


def summed_on_arrival(shard, axis, dim):
    size = lax.axis_size(axis)
    parts = lax.all_to_all(in_blocks(shard, dim, size), axis, 0, 0, tiled=True)
    return jnp.sum(parts.astype(jnp.float32), axis=0)


def multiply(left, right):
    return jnp.dot(left, right, preferred_element_type=jnp.float32)


def contract_rows(left, right):
    return lax.dot_general(
        left, right, (((0,), (0,)), ((), ())), preferred_element_type=jnp.float32
    )


def contract_cols(left, right):
    return lax.dot_general(
        left, right, (((1,), (1,)), ((), ())), preferred_element_type=jnp.float32
    )


def shifted_down(values, steps):
    if steps == 0:
        return values
    filler = jnp.zeros((steps,) + values.shape[1:], values.dtype)
    return jnp.concatenate([filler, values[:-steps]], axis=0)


def shifted_up(values, steps):
    if steps == 0:
        return values
    filler = jnp.zeros((steps,) + values.shape[1:], values.dtype)
    return jnp.concatenate([values[steps:], filler], axis=0)


def same_document(doc_ids, steps):
    if steps == 0:
        return jnp.ones(doc_ids.shape, jnp.float32)
    filler = jnp.full((steps,), -1, jnp.int32)
    earlier = jnp.concatenate([filler, doc_ids[:-steps]])
    return (earlier == doc_ids).astype(jnp.float32)


def silu_slope(values):
    logistic = jax.nn.sigmoid(values)
    return logistic * (1.0 + values * (1.0 - logistic))


def rms_back(grad_unit, unit, scale):
    return scale * (grad_unit - unit * jnp.mean(grad_unit * unit, axis=1, keepdims=True))


LOG2E = 1.4426950408889634
LANES = 128
F32, BF16 = jnp.float32, jnp.bfloat16


def fold_rows(parts, masks):
    m4, m2, m1 = masks

    def join(a, b, m, shift):
        return jnp.where(m, a, b) + pltpu.roll(jnp.where(m, b, a), shift, 0)

    c = [join(parts[i], parts[i + 4], m4[i], 4) for i in range(4)]
    d = [join(c[i], c[i + 2], m2[i], 6) for i in range(2)]
    return join(d[0], d[1], m1, 7)


def fold_masks(width):
    sub = lax.broadcasted_iota(jnp.int32, (8, width), 0)
    m4 = [((sub - i) & 7) < 4 for i in range(4)]
    m2 = [((sub - i) & 2) == 0 for i in range(2)]
    m1 = (sub & 1) == 0
    return m4, m2, m1


def softplus(v):
    return jnp.maximum(v, 0.0) + jnp.log1p(jnp.exp(-jnp.abs(v)))


def row(ref, c, t, ns):
    one = ref[c, pl.ds(t, 8, stride=0), :]
    return jnp.concatenate([one] * (ns // 8), axis=0)


def spread(ref, value):
    for c in range(ref.shape[0]):
        ref[c] = value[:, c * LANES:(c + 1) * LANES]


def own_column(ns, rank):
    lane = lax.broadcasted_iota(jnp.int32, (ns, LANES), 1)
    n = lax.broadcasted_iota(jnp.int32, (ns, LANES), 0)
    return (lane == rank + n) | (lane == rank + ns + n)


def coefficient_rows(ns, rank, proj_ref, rows_s, wide_s):
    tb = proj_ref.shape[0]
    own = own_column(ns, rank)
    lane = lax.broadcasted_iota(jnp.int32, (LANES, 2 * LANES), 1)
    k = lax.broadcasted_iota(jnp.int32, (LANES, 2 * LANES), 0)
    pick = ((lane < LANES) & (k >= rank) & (k < rank + ns)) | ((lane >= LANES) & (k >= rank + ns) & (k < rank + 2 * ns))
    pick = jnp.where(pick, 1.0, 0.0).astype(BF16)

    def body(g, _):
        for j in range(16):
            t = g * 16 + j
            one = proj_ref[pl.ds(t, 8, stride=0), :]
            both = jnp.where(own, jnp.concatenate([one] * (ns // 8), axis=0), 0.0)
            rows_s[pl.ds(pl.multiple_of(j * ns, ns), ns), :] = both.astype(BF16)
        wide_s[pl.ds(pl.multiple_of(g * 16 * ns, 16 * ns), 16 * ns), :] = jnp.dot(rows_s[...], pick, preferred_element_type=F32)
        return 0

    lax.fori_loop(0, tb // 16, body, 0)


def scan_fwd_kernel(ns, rank, proj_ref, inner_ref, keep_ref, sproj_ref, sbias_ref, lr_ref, skip_ref,
                    scan_ref, step_ref, states_ref, starts_ref, state_s, stepd_s, drive_s, r2_s, rows_s, wide_s):
    tb, ch = inner_ref.shape
    groups = ch // LANES
    i = pl.program_id(0)

    @pl.when(i == 0)
    def _():
        state_s[...] = jnp.zeros_like(state_s)
        spread(r2_s, jnp.exp(lr_ref[...]) * (-LOG2E))

    step_in = proj_ref[...].astype(BF16)
    pre = jnp.dot(step_in, sproj_ref[...], preferred_element_type=F32) + sbias_ref[...]
    step = softplus(pre)
    step_ref[...] = step
    spread(stepd_s, jnp.where(keep_ref[...] > 0.0, step, 1e30))
    inner = inner_ref[...].astype(F32)
    spread(drive_s, step * inner)
    coefficient_rows(ns, rank, proj_ref, rows_s, wide_s)
    starts_ref[0] = state_s[...]
    masks = fold_masks(LANES)

    def body(g, state):
        state = list(state)
        parts = [[] for _ in range(groups)]
        for j in range(8):
            t = g * 8 + j
            here = pl.ds(pl.multiple_of(t * ns, ns), ns)
            in_b = wide_s[here, :LANES]
            out_b = wide_s[here, LANES:]
            for c in range(groups):
                cols = pl.ds(c * LANES, LANES)
                dec = jnp.exp2(row(stepd_s, c, t, ns) * r2_s[c])
                s = dec * state[c] + row(drive_s, c, t, ns) * in_b
                state[c] = s
                states_ref[here, cols] = s.astype(BF16)
                z = out_b * s
                parts[c].append(sum(z[8 * k:8 * k + 8] for k in range(ns // 8)))
        for c in range(groups):
            scan_ref[pl.ds(pl.multiple_of(g * 8, 8), 8), pl.ds(c * LANES, LANES)] = fold_rows(parts[c], masks)
        return tuple(state)

    start = tuple(state_s[:, c * LANES:(c + 1) * LANES] for c in range(groups))
    state = lax.fori_loop(0, tb // 8, body, start)
    for c in range(groups):
        state_s[:, c * LANES:(c + 1) * LANES] = state[c]
    scan_ref[...] += skip_ref[...] * inner


def scan_fwd(proj, inner, keep, sproj, sbias, log_rates, skip, rank):
    seq, ch = inner.shape
    ns = log_rates.shape[0]
    tb = LANES
    nb = seq // tb
    full = lambda a: pl.BlockSpec(a.shape, lambda i: (0,) * a.ndim)
    rows = pl.BlockSpec((tb, ch), lambda i: (i, 0))
    return pl.pallas_call(
        functools.partial(scan_fwd_kernel, ns, rank),
        grid=(nb,),
        in_specs=[pl.BlockSpec((tb, LANES), lambda i: (i, 0)), rows, pl.BlockSpec((tb, 1), lambda i: (i, 0)),
                  full(sproj), full(sbias), full(log_rates), full(skip)],
        out_specs=[rows, rows, pl.BlockSpec((tb * ns, ch), lambda i: (i, 0)), pl.BlockSpec((1, ns, ch), lambda i: (i, 0, 0))],
        out_shape=[jax.ShapeDtypeStruct((seq, ch), F32), jax.ShapeDtypeStruct((seq, ch), F32),
                   jax.ShapeDtypeStruct((seq * ns, ch), BF16), jax.ShapeDtypeStruct((nb, ns, ch), F32)],
        scratch_shapes=[pltpu.VMEM((ns, ch), F32)] + [pltpu.VMEM((ch // LANES, tb, LANES), F32)] * 2 + [pltpu.VMEM((ch // LANES, ns, LANES), F32),
                        pltpu.VMEM((16 * ns, LANES), BF16), pltpu.VMEM((tb * ns, 2 * LANES), F32)],
        compiler_params=pltpu.CompilerParams(vmem_limit_bytes=48 << 20),
        name="scan_fwd",
    )(proj, inner, keep, sproj, sbias, log_rates, skip)


def scan_bwd_kernel(ns, rank, proj_ref, inner_ref, keep_ref, step_ref, states_ref, starts_ref, dscan_ref, sproj_ref, lr_ref, skip_ref,
                    dpre_ref, dinner_ref, dproj_ref, gstep_ref, gsbias_ref, grates_ref, gskip_ref,
                    carry_s, stepd_s, drive_s, dscan_s, step_s, r2_s, coeff_s, exps_s, acc_s, rows_s, wide_s, sums_s):
    tb, ch = inner_ref.shape
    groups = ch // LANES
    i = pl.program_id(0)

    @pl.when(i == 0)
    def _():
        carry_s[...] = jnp.zeros_like(carry_s)
        acc_s[...] = jnp.zeros_like(acc_s)
        spread(r2_s, jnp.exp(lr_ref[...]) * (-LOG2E))
        gstep_ref[...] = jnp.zeros_like(gstep_ref)
        gsbias_ref[...] = jnp.zeros_like(gsbias_ref)
        gskip_ref[...] = jnp.zeros_like(gskip_ref)

    step = step_ref[...]
    inner = inner_ref[...].astype(F32)
    dscan = dscan_ref[...]
    spread(stepd_s, jnp.where(keep_ref[...] > 0.0, step, 1e30))
    spread(drive_s, step * inner)
    spread(dscan_s, dscan)
    spread(step_s, step)
    coefficient_rows(ns, rank, proj_ref, rows_s, wide_s)
    masks = fold_masks(LANES)
    steps = tb // 8

    def body(k, carry):
        later, acc = [list(v) for v in carry]
        g = steps - 1 - k
        cparts = [[None] * 8 for _ in range(groups)]
        eparts = [[None] * 8 for _ in range(groups)]
        last = pl.ds(pl.multiple_of((g * 8 + 7) * ns, ns), ns)
        now = [states_ref[last, pl.ds(c * LANES, LANES)].astype(F32) for c in range(groups)]
        for j in range(7, -1, -1):
            t = g * 8 + j
            here = pl.ds(pl.multiple_of(t * ns, ns), ns)
            prior = pl.ds(pl.multiple_of((t - 1 if j else jnp.maximum(t - 1, 0)) * ns, ns), ns)
            in_b = wide_s[here, :LANES]
            out_b = wide_s[here, LANES:]
            din = dout = None
            for c in range(groups):
                cols = pl.ds(c * LANES, LANES)
                before = states_ref[prior, cols].astype(F32)
                if j == 0:
                    before = jnp.where(jnp.full((ns, LANES), t, jnp.int32) == 0, starts_ref[0, :, cols], before)
                r2 = r2_s[c]
                dec = jnp.exp2(row(stepd_s, c, t, ns) * r2)
                ds = row(dscan_s, c, t, ns)
                d = later[c] + out_b * ds
                later[c] = dec * d
                dexp = later[c] * before
                e = dexp * r2
                cf = d * in_b
                cparts[c][j] = sum(cf[8 * q:8 * q + 8] for q in range(ns // 8))
                eparts[c][j] = sum(e[8 * q:8 * q + 8] for q in range(ns // 8))
                acc[c] = acc[c] + dexp * row(step_s, c, t, ns)
                a = d * row(drive_s, c, t, ns)
                b = now[c] * ds
                din = a if din is None else din + a
                dout = b if dout is None else dout + b
                now[c] = before
            sums_s[here, :LANES] = din.astype(BF16)
            sums_s[here, LANES:] = dout.astype(BF16)
        rows = pl.ds(pl.multiple_of(g * 8, 8), 8)
        for c in range(groups):
            cols = pl.ds(c * LANES, LANES)
            coeff_s[rows, cols] = fold_rows(cparts[c], masks)
            exps_s[rows, cols] = fold_rows(eparts[c], masks)
        return tuple(later), tuple(acc)

    pick = lambda ref: tuple(ref[:, c * LANES:(c + 1) * LANES] for c in range(groups))
    later, acc = lax.fori_loop(0, steps, body, (pick(carry_s), pick(acc_s)))
    for c in range(groups):
        carry_s[:, c * LANES:(c + 1) * LANES] = later[c]
        acc_s[:, c * LANES:(c + 1) * LANES] = acc[c]

    k = lax.broadcasted_iota(jnp.int32, (2 * LANES, LANES), 0)
    lane = lax.broadcasted_iota(jnp.int32, (2 * LANES, LANES), 1)
    into = ((k < LANES) & (lane >= rank) & (lane < rank + ns)) | ((k >= LANES) & (lane >= rank + ns) & (lane < rank + 2 * ns))
    into = jnp.where(into, 1.0, 0.0).astype(BF16)
    own = own_column(ns, rank)

    def gather(g, _):
        got = jnp.dot(sums_s[pl.ds(pl.multiple_of(g * 16 * ns, 16 * ns), 16 * ns), :], into, preferred_element_type=F32)
        for h in range(2):
            parts = []
            for j in range(8):
                one = jnp.where(own, got[(h * 8 + j) * ns:(h * 8 + j + 1) * ns], 0.0)
                parts.append(sum(one[8 * q:8 * q + 8] for q in range(ns // 8)))
            dproj_ref[pl.ds(pl.multiple_of(g * 16 + h * 8, 8), 8), :] = fold_rows(parts, masks)
        return 0

    lax.fori_loop(0, tb // 16, gather, 0)
    coeff = coeff_s[...]
    d_step = coeff * inner + exps_s[...] * (1.0 / LOG2E)
    d_pre = (d_step * (1.0 - jnp.exp(-step))).astype(BF16)
    dpre_ref[...] = d_pre
    dinner_ref[...] = dscan * skip_ref[...] + step * coeff
    step_in = proj_ref[...].astype(BF16)
    gstep_ref[...] += lax.dot_general(step_in, d_pre, (((0,), (0,)), ((), ())), preferred_element_type=F32)
    gsbias_ref[...] += jnp.sum(d_pre.astype(F32), axis=0, keepdims=True)
    gskip_ref[...] += jnp.sum(dscan * inner, axis=0, keepdims=True)
    dproj_ref[...] += lax.dot_general(d_pre, sproj_ref[...], (((1,), (1,)), ((), ())), preferred_element_type=F32)

    @pl.when(i == pl.num_programs(0) - 1)
    def _():
        grates_ref[...] = -jnp.exp(lr_ref[...]) * acc_s[...]


def scan_bwd(proj, inner, keep, step, states, starts, dscan, sproj, log_rates, skip, rank):
    seq, ch = inner.shape
    ns = log_rates.shape[0]
    tb = LANES
    nb = seq // tb
    full = lambda a: pl.BlockSpec(a.shape, lambda i: (0,) * a.ndim)
    rows = pl.BlockSpec((tb, ch), lambda i: (nb - 1 - i, 0))
    prow = pl.BlockSpec((tb, LANES), lambda i: (nb - 1 - i, 0))
    whole = lambda *s: pl.BlockSpec(s, lambda i: (0,) * len(s))
    shape = jax.ShapeDtypeStruct
    return pl.pallas_call(
        functools.partial(scan_bwd_kernel, ns, rank),
        grid=(nb,),
        in_specs=[prow, rows, pl.BlockSpec((tb, 1), lambda i: (nb - 1 - i, 0)), rows,
                  pl.BlockSpec((tb * ns, ch), lambda i: (nb - 1 - i, 0)), pl.BlockSpec((1, ns, ch), lambda i: (nb - 1 - i, 0, 0)),
                  rows, full(sproj), full(log_rates), full(skip)],
        out_specs=[rows, rows, prow, whole(LANES, ch), whole(1, ch), whole(ns, ch), whole(1, ch)],
        out_shape=[shape((seq, ch), BF16), shape((seq, ch), F32), shape((seq, LANES), F32), shape((LANES, ch), F32), shape((1, ch), F32),
                   shape((ns, ch), F32), shape((1, ch), F32)],
        scratch_shapes=[pltpu.VMEM((ns, ch), F32)] + [pltpu.VMEM((ch // LANES, tb, LANES), F32)] * 4 + [pltpu.VMEM((ch // LANES, ns, LANES), F32),
                        pltpu.VMEM((tb, ch), F32), pltpu.VMEM((tb, ch), F32), pltpu.VMEM((ns, ch), F32),
                        pltpu.VMEM((16 * ns, LANES), BF16), pltpu.VMEM((tb * ns, 2 * LANES), F32), pltpu.VMEM((tb * ns, 2 * LANES), BF16)],
        compiler_params=pltpu.CompilerParams(vmem_limit_bytes=48 << 20),
        name="scan_bwd",
    )(proj, inner, keep, step, states, starts, dscan, sproj, log_rates, skip)


def per_device(
    tokens,
    segment_ids,
    routes,
    out_grad,
    mixer_gain,
    in_proj_x,
    in_proj_z,
    conv_weight,
    conv_bias,
    state_proj,
    step_proj,
    step_bias,
    log_rates,
    skip_gain,
    out_proj,
    expert_gain,
    router_weight,
    expert_up,
    up_bias,
    expert_down,
    down_bias,
):
    seq_len, model_width = tokens.shape
    conv_taps = conv_weight.shape[0]
    step_rank = step_proj.shape[0]
    experts = router_weight.shape[1]
    capacity = 5 * seq_len // (4 * experts)
    doc_ids = segment_ids[0]
    conv_masks = [same_document(doc_ids, offset)[:, None] for offset in range(conv_taps)]
    first_scale = lax.rsqrt(jnp.mean(tokens * tokens, axis=1, keepdims=True) + EPS)
    first_unit = tokens * first_scale
    normed = (first_unit * mixer_gain).astype(jnp.bfloat16)
    gathered_x, gathered_z, gathered_out = (
        lax.all_gather(in_proj_x, "wide", axis=0, tiled=True),
        lax.all_gather(in_proj_z, "wide", axis=0, tiled=True),
        lax.all_gather(out_proj, "wide", axis=0, tiled=True),
    )
    x_branch = multiply(normed, gathered_x)
    z_branch = multiply(normed, gathered_z)
    conv_sum = conv_bias + jnp.zeros_like(x_branch)
    for offset in range(conv_taps):
        conv_sum = conv_sum + conv_weight[conv_taps - 1 - offset] * conv_masks[
            offset
        ] * shifted_down(x_branch, offset)
    inner_act = jax.nn.silu(conv_sum).astype(jnp.bfloat16)
    wide_proj = jnp.pad(state_proj, ((0, 0), (0, LANES - state_proj.shape[1])))
    projected = lax.psum(multiply(inner_act, wide_proj), "tp")
    tall_proj = jnp.pad(step_proj, ((0, LANES - step_rank), (0, 0)))
    carry_mask = same_document(doc_ids, 1)[:, None]
    scan_out, step_size, states, starts = scan_fwd(
        projected, inner_act, carry_mask, tall_proj, step_bias[None], log_rates, skip_gain[None], step_rank
    )
    z_gate = jax.nn.silu(z_branch)
    gated = (scan_out * z_gate).astype(jnp.bfloat16)
    mixed = lax.psum(contract_cols(gated, gathered_out).astype(jnp.bfloat16), "tp").astype(
        jnp.float32
    )
    hidden = tokens + mixed
    second_scale = lax.rsqrt(jnp.mean(hidden * hidden, axis=1, keepdims=True) + EPS)
    second_unit = hidden * second_scale
    expert_in = (second_unit * expert_gain).astype(jnp.bfloat16)
    route_ids = routes[:, 0]
    chosen_int = (routes == jnp.arange(experts, dtype=jnp.int32)[None, :]).astype(jnp.int32)
    chosen = chosen_int.astype(jnp.float32)
    logits = multiply(expert_in, router_weight)
    gate = jax.nn.sigmoid(jnp.sum(logits * chosen, axis=1))
    rank_of = jnp.arange(seq_len, dtype=jnp.int32)
    earlier = (rank_of[:, None] > rank_of[None, :]).astype(jnp.bfloat16)
    position = jnp.sum(multiply(earlier, chosen.astype(jnp.bfloat16)) * chosen, axis=1).astype(jnp.int32)
    kept = position < capacity
    slots = jnp.where(kept, route_ids * capacity + position, experts * capacity)
    scaled_grad = (gate[:, None] * out_grad).astype(jnp.bfloat16)
    sent_width = expert_in.shape[1]
    send_in = (
        jnp.zeros((experts * capacity + 1, sent_width), jnp.bfloat16).at[slots].set(expert_in)[:-1]
    )
    send_grad = (
        jnp.zeros((experts * capacity + 1, sent_width), jnp.bfloat16)
        .at[slots]
        .set(scaled_grad)[:-1]
    )
    recv_in, recv_grad = (
        lax.all_to_all(
            send_in.reshape(experts, capacity, sent_width),
            "wide",
            split_axis=0,
            concat_axis=0,
            tiled=True,
        ),
        lax.all_to_all(
            send_grad.reshape(experts, capacity, sent_width),
            "wide",
            split_axis=0,
            concat_axis=0,
            tiled=True,
        ),
    )
    rows_in = recv_in.reshape(-1, model_width)
    rows_grad = recv_grad.reshape(-1, model_width)
    pre_act = multiply(rows_in, expert_up[0]) + up_bias[0]
    hidden_act = jax.nn.gelu(pre_act).astype(jnp.bfloat16)
    partial_out = multiply(hidden_act, expert_down[0])
    up_grad = contract_cols(rows_grad, expert_down[0])
    d_pre = jax.vjp(jax.nn.gelu, pre_act)[1](up_grad)[0].astype(jnp.bfloat16)
    partial_back = contract_cols(d_pre, expert_up[0])
    grad_down = contract_rows(hidden_act, rows_grad)
    grad_dbias = jnp.sum(rows_grad.astype(jnp.float32), axis=0)
    grad_up = contract_rows(rows_in, d_pre)
    grad_ubias = jnp.sum(d_pre.astype(jnp.float32), axis=0)
    out_sum, back_sum = (
        lax.psum(partial_out.astype(jnp.bfloat16), "tp").astype(jnp.float32),
        lax.psum(partial_back.astype(jnp.bfloat16), "tp").astype(jnp.float32),
    )
    bias_part = down_bias[0]
    outgoing = (out_sum + bias_part).astype(jnp.bfloat16).reshape(experts, capacity, -1)
    back_rows = back_sum.astype(jnp.bfloat16).reshape(experts, capacity, -1)
    incoming, arriving = (
        lax.all_to_all(outgoing, "wide", split_axis=0, concat_axis=0, tiled=True),
        lax.all_to_all(back_rows, "wide", split_axis=0, concat_axis=0, tiled=True),
    )
    safe_slots = jnp.minimum(slots, experts * capacity - 1)
    returned = jnp.where(
        kept[:, None], incoming.reshape(-1, model_width)[safe_slots].astype(jnp.float32), 0.0
    )
    result = hidden + gate[:, None] * returned
    d_gate = jnp.sum(out_grad * returned, axis=1)
    d_logit = (d_gate * gate * (1.0 - gate))[:, None] * chosen
    grad_router = jnp.dot(expert_in.astype(jnp.float32).T, d_logit, precision=HIGH)
    d_norm_two = jnp.dot(d_logit, router_weight.astype(jnp.float32).T, precision=HIGH)
    d_norm_two = d_norm_two + jnp.where(
        kept[:, None], arriving.reshape(-1, model_width)[safe_slots].astype(jnp.float32), 0.0
    )
    grad_second_gain = jnp.sum(d_norm_two * second_unit, axis=0)
    d_hidden = out_grad + rms_back(d_norm_two * expert_gain, second_unit, second_scale)
    d_mixed = d_hidden.astype(jnp.bfloat16)
    d_gated = multiply(d_mixed, gathered_out)
    grad_out = contract_rows(d_mixed, gated)
    d_scan = d_gated * z_gate
    d_z = (d_gated * scan_out * silu_slope(z_branch)).astype(jnp.bfloat16)
    d_step_pre, d_inner, d_proj, grad_step, grad_sbias, grad_rates, grad_skip = scan_bwd(
        projected, inner_act, carry_mask, step_size, states, starts, d_scan, tall_proj, log_rates, skip_gain[None], step_rank
    )
    grad_step, grad_sbias, grad_skip = grad_step[:step_rank], grad_sbias[0], grad_skip[0]
    d_projected = lax.psum(d_proj.astype(jnp.bfloat16), "tp")
    grad_state = contract_rows(inner_act, d_projected)[:, : state_proj.shape[1]]
    d_inner = d_inner + contract_cols(d_projected, wide_proj)
    d_conv = d_inner * silu_slope(conv_sum)
    grad_cbias = jnp.sum(d_conv, axis=0)
    conv_rows = []
    d_input = jnp.zeros_like(d_conv)
    for offset in range(conv_taps):
        conv_rows.append(
            jnp.sum(d_conv * conv_masks[offset] * shifted_down(x_branch, offset), axis=0)
        )
        d_input = d_input + conv_weight[conv_taps - 1 - offset] * shifted_up(
            conv_masks[offset] * d_conv, offset
        )
    grad_conv = jnp.stack(conv_rows[::-1])
    d_x_branch = d_input.astype(jnp.bfloat16)
    grad_in_x = contract_rows(normed, d_x_branch)
    grad_in_z = contract_rows(normed, d_z)
    d_normed = lax.psum(
        (contract_cols(d_x_branch, gathered_x) + contract_cols(d_z, gathered_z)).astype(
            jnp.bfloat16
        ),
        "tp",
    ).astype(jnp.float32)
    grad_first_gain = jnp.sum(d_normed * first_unit, axis=0)
    tokens_grad = d_hidden + rms_back(d_normed * mixer_gain, first_unit, first_scale)
    grad_in_x, grad_in_z, grad_out = (
        summed_on_arrival(grad_in_x.astype(jnp.bfloat16), "wide", 0),
        summed_on_arrival(grad_in_z.astype(jnp.bfloat16), "wide", 0),
        summed_on_arrival(grad_out.astype(jnp.bfloat16), "wide", 0),
    )
    (
        grad_first_gain,
        grad_conv,
        grad_cbias,
        grad_state,
        grad_step,
        grad_sbias,
        grad_rates,
        grad_skip,
        grad_second_gain,
        grad_router,
    ) = lax.psum(
        (
            grad_first_gain,
            grad_conv,
            grad_cbias,
            grad_state,
            grad_step,
            grad_sbias,
            grad_rates,
            grad_skip,
            grad_second_gain,
            grad_router,
        ),
        "wide",
    )
    return (
        result,
        tokens_grad,
        grad_first_gain,
        grad_in_x,
        grad_in_z,
        grad_conv,
        grad_cbias,
        grad_state,
        grad_step,
        grad_sbias,
        grad_rates,
        grad_skip,
        grad_out,
        grad_second_gain,
        grad_router,
        grad_up[None],
        grad_ubias[None],
        grad_down[None],
        grad_dbias[None],
    )


def solution(mesh):
    in_specs = (
        P("wide", None),
        P("wide", None),
        P("wide", None),
        P("wide", None),
        P(),
        P("wide", "tp"),
        P("wide", "tp"),
        P(None, "tp"),
        P("tp"),
        P("tp", None),
        P(None, "tp"),
        P("tp"),
        P(None, "tp"),
        P("tp"),
        P("wide", "tp"),
        P(),
        P(),
        P("wide", None, "tp"),
        P("wide", "tp"),
        P("wide", "tp", None),
        P("wide", None),
    )
    out_specs = (
        P("wide", None),
        P("wide", None),
        P(),
        P("wide", "tp"),
        P("wide", "tp"),
        P(None, "tp"),
        P("tp"),
        P("tp", None),
        P(None, "tp"),
        P("tp"),
        P(None, "tp"),
        P("tp"),
        P("wide", "tp"),
        P(),
        P(),
        P("wide", None, "tp"),
        P("wide", "tp"),
        P("wide", "tp", None),
        P("wide", None),
    )
    return jax.shard_map(
        per_device, mesh=mesh, in_specs=in_specs, out_specs=out_specs, check_vma=False
    )
```

```python
import functools

import jax
import jax.numpy as jnp
from jax import lax
from jax.experimental import pallas as pl
from jax.experimental.pallas import tpu as pltpu
from jax.sharding import PartitionSpec as P

EPS = 1e-05
HIGH = lax.Precision.HIGHEST


def in_blocks(shard, dim, size):
    before, after = (shard.shape[:dim], shard.shape[dim + 1 :])
    return jnp.moveaxis(shard.reshape(*before, size, -1, *after), dim, 0)


def summed_on_arrival(shard, axis, dim):
    size = lax.axis_size(axis)
    parts = lax.all_to_all(in_blocks(shard, dim, size), axis, 0, 0, tiled=True)
    return jnp.sum(parts.astype(jnp.float32), axis=0)


def multiply(left, right):
    return jnp.dot(left, right, preferred_element_type=jnp.float32)


def contract_rows(left, right):
    return lax.dot_general(
        left, right, (((0,), (0,)), ((), ())), preferred_element_type=jnp.float32
    )


def contract_cols(left, right):
    return lax.dot_general(
        left, right, (((1,), (1,)), ((), ())), preferred_element_type=jnp.float32
    )


def shifted_down(values, steps):
    if steps == 0:
        return values
    filler = jnp.zeros((steps,) + values.shape[1:], values.dtype)
    return jnp.concatenate([filler, values[:-steps]], axis=0)


def shifted_up(values, steps):
    if steps == 0:
        return values
    filler = jnp.zeros((steps,) + values.shape[1:], values.dtype)
    return jnp.concatenate([values[steps:], filler], axis=0)


def same_document(doc_ids, steps):
    if steps == 0:
        return jnp.ones(doc_ids.shape, jnp.float32)
    filler = jnp.full((steps,), -1, jnp.int32)
    earlier = jnp.concatenate([filler, doc_ids[:-steps]])
    return (earlier == doc_ids).astype(jnp.float32)


def silu_slope(values):
    logistic = jax.nn.sigmoid(values)
    return logistic * (1.0 + values * (1.0 - logistic))


def rms_back(grad_unit, unit, scale):
    return scale * (grad_unit - unit * jnp.mean(grad_unit * unit, axis=1, keepdims=True))


LOG2E = 1.4426950408889634
LANES = 128
F32, BF16 = jnp.float32, jnp.bfloat16
MESH = pl.DeviceIdType.MESH


def fold_rows(parts, masks):
    m4, m2, m1 = masks

    def join(a, b, m, shift):
        return jnp.where(m, a, b) + pltpu.roll(jnp.where(m, b, a), shift, 0)

    c = [join(parts[i], parts[i + 4], m4[i], 4) for i in range(4)]
    d = [join(c[i], c[i + 2], m2[i], 6) for i in range(2)]
    return join(d[0], d[1], m1, 7)


def fold_masks(width):
    sub = lax.broadcasted_iota(jnp.int32, (8, width), 0)
    m4 = [((sub - i) & 7) < 4 for i in range(4)]
    m2 = [((sub - i) & 2) == 0 for i in range(2)]
    m1 = (sub & 1) == 0
    return m4, m2, m1


def softplus(v):
    return jnp.maximum(v, 0.0) + jnp.log1p(jnp.exp(-jnp.abs(v)))


def row(ref, c, t, ns):
    one = ref[c, pl.ds(t, 8, stride=0), :]
    return jnp.concatenate([one] * (ns // 8), axis=0)


def spread(ref, value):
    for c in range(ref.shape[0]):
        ref[c] = value[:, c * LANES:(c + 1) * LANES]


def own_column(ns, rank):
    lane = lax.broadcasted_iota(jnp.int32, (ns, LANES), 1)
    n = lax.broadcasted_iota(jnp.int32, (ns, LANES), 0)
    return (lane == rank + n) | (lane == rank + ns + n)


def coefficient_rows(ns, rank, proj_ref, rows_s, wide_s):
    tb = proj_ref.shape[0]
    own = own_column(ns, rank)
    lane = lax.broadcasted_iota(jnp.int32, (LANES, 2 * LANES), 1)
    k = lax.broadcasted_iota(jnp.int32, (LANES, 2 * LANES), 0)
    pick = ((lane < LANES) & (k >= rank) & (k < rank + ns)) | ((lane >= LANES) & (k >= rank + ns) & (k < rank + 2 * ns))
    pick = jnp.where(pick, 1.0, 0.0).astype(BF16)

    def body(g, _):
        for j in range(16):
            t = g * 16 + j
            one = proj_ref[pl.ds(t, 8, stride=0), :]
            both = jnp.where(own, jnp.concatenate([one] * (ns // 8), axis=0), 0.0)
            rows_s[pl.ds(pl.multiple_of(j * ns, ns), ns), :] = both.astype(BF16)
        wide_s[pl.ds(pl.multiple_of(g * 16 * ns, 16 * ns), 16 * ns), :] = jnp.dot(rows_s[...], pick, preferred_element_type=F32)
        return 0

    lax.fori_loop(0, tb // 16, body, 0)


def scan_fwd_kernel(ns, rank, proj_ref, inner_ref, keep_ref, sproj_ref, sbias_ref, lr_ref, skip_ref,
                    scan_ref, step_ref, states_ref, starts_ref, state_s, stepd_s, drive_s, r2_s, rows_s, wide_s):
    tb, ch = inner_ref.shape
    groups = ch // LANES
    i = pl.program_id(0)

    @pl.when(i == 0)
    def _():
        state_s[...] = jnp.zeros_like(state_s)
        spread(r2_s, jnp.exp(lr_ref[...]) * (-LOG2E))

    step_in = proj_ref[...].astype(BF16)
    pre = jnp.dot(step_in, sproj_ref[...], preferred_element_type=F32) + sbias_ref[...]
    step = softplus(pre)
    step_ref[...] = step
    spread(stepd_s, jnp.where(keep_ref[...] > 0.0, step, 1e30))
    inner = inner_ref[...].astype(F32)
    spread(drive_s, step * inner)
    coefficient_rows(ns, rank, proj_ref, rows_s, wide_s)
    starts_ref[0] = state_s[...]
    masks = fold_masks(LANES)

    def body(g, state):
        state = list(state)
        parts = [[] for _ in range(groups)]
        for j in range(8):
            t = g * 8 + j
            here = pl.ds(pl.multiple_of(t * ns, ns), ns)
            in_b = wide_s[here, :LANES]
            out_b = wide_s[here, LANES:]
            for c in range(groups):
                cols = pl.ds(c * LANES, LANES)
                dec = jnp.exp2(row(stepd_s, c, t, ns) * r2_s[c])
                s = dec * state[c] + row(drive_s, c, t, ns) * in_b
                state[c] = s
                states_ref[here, cols] = s.astype(BF16)
                z = out_b * s
                parts[c].append(sum(z[8 * k:8 * k + 8] for k in range(ns // 8)))
        for c in range(groups):
            scan_ref[pl.ds(pl.multiple_of(g * 8, 8), 8), pl.ds(c * LANES, LANES)] = fold_rows(parts[c], masks)
        return tuple(state)

    start = tuple(state_s[:, c * LANES:(c + 1) * LANES] for c in range(groups))
    state = lax.fori_loop(0, tb // 8, body, start)
    for c in range(groups):
        state_s[:, c * LANES:(c + 1) * LANES] = state[c]
    scan_ref[...] += skip_ref[...] * inner


def scan_fwd(proj, inner, keep, sproj, sbias, log_rates, skip, rank):
    seq, ch = inner.shape
    ns = log_rates.shape[0]
    tb = LANES
    nb = seq // tb
    full = lambda a: pl.BlockSpec(a.shape, lambda i: (0,) * a.ndim)
    rows = pl.BlockSpec((tb, ch), lambda i: (i, 0))
    return pl.pallas_call(
        functools.partial(scan_fwd_kernel, ns, rank),
        grid=(nb,),
        in_specs=[pl.BlockSpec((tb, LANES), lambda i: (i, 0)), rows, pl.BlockSpec((tb, 1), lambda i: (i, 0)),
                  full(sproj), full(sbias), full(log_rates), full(skip)],
        out_specs=[rows, rows, pl.BlockSpec((tb * ns, ch), lambda i: (i, 0)), pl.BlockSpec((1, ns, ch), lambda i: (i, 0, 0))],
        out_shape=[jax.ShapeDtypeStruct((seq, ch), F32), jax.ShapeDtypeStruct((seq, ch), F32),
                   jax.ShapeDtypeStruct((seq * ns, ch), BF16), jax.ShapeDtypeStruct((nb, ns, ch), F32)],
        scratch_shapes=[pltpu.VMEM((ns, ch), F32)] + [pltpu.VMEM((ch // LANES, tb, LANES), F32)] * 2 + [pltpu.VMEM((ch // LANES, ns, LANES), F32),
                        pltpu.VMEM((16 * ns, LANES), BF16), pltpu.VMEM((tb * ns, 2 * LANES), F32)],
        compiler_params=pltpu.CompilerParams(vmem_limit_bytes=48 << 20),
        name="scan_fwd",
    )(proj, inner, keep, sproj, sbias, log_rates, skip)


def scan_bwd_kernel(ns, rank, proj_ref, inner_ref, keep_ref, step_ref, states_ref, starts_ref, dscan_ref, sproj_ref, lr_ref, skip_ref,
                    dpre_ref, dinner_ref, dproj_ref, gstep_ref, gsbias_ref, grates_ref, gskip_ref,
                    carry_s, stepd_s, drive_s, dscan_s, step_s, r2_s, coeff_s, exps_s, acc_s, rows_s, wide_s, sums_s):
    tb, ch = inner_ref.shape
    groups = ch // LANES
    i = pl.program_id(0)

    @pl.when(i == 0)
    def _():
        carry_s[...] = jnp.zeros_like(carry_s)
        acc_s[...] = jnp.zeros_like(acc_s)
        spread(r2_s, jnp.exp(lr_ref[...]) * (-LOG2E))
        gstep_ref[...] = jnp.zeros_like(gstep_ref)
        gsbias_ref[...] = jnp.zeros_like(gsbias_ref)
        gskip_ref[...] = jnp.zeros_like(gskip_ref)

    step = step_ref[...]
    inner = inner_ref[...].astype(F32)
    dscan = dscan_ref[...]
    spread(stepd_s, jnp.where(keep_ref[...] > 0.0, step, 1e30))
    spread(drive_s, step * inner)
    spread(dscan_s, dscan)
    spread(step_s, step)
    coefficient_rows(ns, rank, proj_ref, rows_s, wide_s)
    masks = fold_masks(LANES)
    steps = tb // 8

    def body(k, carry):
        later, acc = [list(v) for v in carry]
        g = steps - 1 - k
        cparts = [[None] * 8 for _ in range(groups)]
        eparts = [[None] * 8 for _ in range(groups)]
        last = pl.ds(pl.multiple_of((g * 8 + 7) * ns, ns), ns)
        now = [states_ref[last, pl.ds(c * LANES, LANES)].astype(F32) for c in range(groups)]
        for j in range(7, -1, -1):
            t = g * 8 + j
            here = pl.ds(pl.multiple_of(t * ns, ns), ns)
            prior = pl.ds(pl.multiple_of((t - 1 if j else jnp.maximum(t - 1, 0)) * ns, ns), ns)
            in_b = wide_s[here, :LANES]
            out_b = wide_s[here, LANES:]
            din = dout = None
            for c in range(groups):
                cols = pl.ds(c * LANES, LANES)
                before = states_ref[prior, cols].astype(F32)
                if j == 0:
                    before = jnp.where(jnp.full((ns, LANES), t, jnp.int32) == 0, starts_ref[0, :, cols], before)
                r2 = r2_s[c]
                dec = jnp.exp2(row(stepd_s, c, t, ns) * r2)
                ds = row(dscan_s, c, t, ns)
                d = later[c] + out_b * ds
                later[c] = dec * d
                dexp = later[c] * before
                e = dexp * r2
                cf = d * in_b
                cparts[c][j] = sum(cf[8 * q:8 * q + 8] for q in range(ns // 8))
                eparts[c][j] = sum(e[8 * q:8 * q + 8] for q in range(ns // 8))
                acc[c] = acc[c] + dexp * row(step_s, c, t, ns)
                a = d * row(drive_s, c, t, ns)
                b = now[c] * ds
                din = a if din is None else din + a
                dout = b if dout is None else dout + b
                now[c] = before
            sums_s[here, :LANES] = din.astype(BF16)
            sums_s[here, LANES:] = dout.astype(BF16)
        rows = pl.ds(pl.multiple_of(g * 8, 8), 8)
        for c in range(groups):
            cols = pl.ds(c * LANES, LANES)
            coeff_s[rows, cols] = fold_rows(cparts[c], masks)
            exps_s[rows, cols] = fold_rows(eparts[c], masks)
        return tuple(later), tuple(acc)

    pick = lambda ref: tuple(ref[:, c * LANES:(c + 1) * LANES] for c in range(groups))
    later, acc = lax.fori_loop(0, steps, body, (pick(carry_s), pick(acc_s)))
    for c in range(groups):
        carry_s[:, c * LANES:(c + 1) * LANES] = later[c]
        acc_s[:, c * LANES:(c + 1) * LANES] = acc[c]

    k = lax.broadcasted_iota(jnp.int32, (2 * LANES, LANES), 0)
    lane = lax.broadcasted_iota(jnp.int32, (2 * LANES, LANES), 1)
    into = ((k < LANES) & (lane >= rank) & (lane < rank + ns)) | ((k >= LANES) & (lane >= rank + ns) & (lane < rank + 2 * ns))
    into = jnp.where(into, 1.0, 0.0).astype(BF16)
    own = own_column(ns, rank)

    def gather(g, _):
        got = jnp.dot(sums_s[pl.ds(pl.multiple_of(g * 16 * ns, 16 * ns), 16 * ns), :], into, preferred_element_type=F32)
        for h in range(2):
            parts = []
            for j in range(8):
                one = jnp.where(own, got[(h * 8 + j) * ns:(h * 8 + j + 1) * ns], 0.0)
                parts.append(sum(one[8 * q:8 * q + 8] for q in range(ns // 8)))
            dproj_ref[pl.ds(pl.multiple_of(g * 16 + h * 8, 8), 8), :] = fold_rows(parts, masks)
        return 0

    lax.fori_loop(0, tb // 16, gather, 0)
    coeff = coeff_s[...]
    d_step = coeff * inner + exps_s[...] * (1.0 / LOG2E)
    d_pre = (d_step * (1.0 - jnp.exp(-step))).astype(BF16)
    dpre_ref[...] = d_pre
    dinner_ref[...] = dscan * skip_ref[...] + step * coeff
    step_in = proj_ref[...].astype(BF16)
    gstep_ref[...] += lax.dot_general(step_in, d_pre, (((0,), (0,)), ((), ())), preferred_element_type=F32)
    gsbias_ref[...] += jnp.sum(d_pre.astype(F32), axis=0, keepdims=True)
    gskip_ref[...] += jnp.sum(dscan * inner, axis=0, keepdims=True)
    dproj_ref[...] += lax.dot_general(d_pre, sproj_ref[...], (((1,), (1,)), ((), ())), preferred_element_type=F32)

    @pl.when(i == pl.num_programs(0) - 1)
    def _():
        grates_ref[...] = -jnp.exp(lr_ref[...]) * acc_s[...]


def scan_bwd(proj, inner, keep, step, states, starts, dscan, sproj, log_rates, skip, rank):
    seq, ch = inner.shape
    ns = log_rates.shape[0]
    tb = LANES
    nb = seq // tb
    full = lambda a: pl.BlockSpec(a.shape, lambda i: (0,) * a.ndim)
    rows = pl.BlockSpec((tb, ch), lambda i: (nb - 1 - i, 0))
    prow = pl.BlockSpec((tb, LANES), lambda i: (nb - 1 - i, 0))
    whole = lambda *s: pl.BlockSpec(s, lambda i: (0,) * len(s))
    shape = jax.ShapeDtypeStruct
    return pl.pallas_call(
        functools.partial(scan_bwd_kernel, ns, rank),
        grid=(nb,),
        in_specs=[prow, rows, pl.BlockSpec((tb, 1), lambda i: (nb - 1 - i, 0)), rows,
                  pl.BlockSpec((tb * ns, ch), lambda i: (nb - 1 - i, 0)), pl.BlockSpec((1, ns, ch), lambda i: (nb - 1 - i, 0, 0)),
                  rows, full(sproj), full(log_rates), full(skip)],
        out_specs=[rows, rows, prow, whole(LANES, ch), whole(1, ch), whole(ns, ch), whole(1, ch)],
        out_shape=[shape((seq, ch), BF16), shape((seq, ch), F32), shape((seq, LANES), F32), shape((LANES, ch), F32), shape((1, ch), F32),
                   shape((ns, ch), F32), shape((1, ch), F32)],
        scratch_shapes=[pltpu.VMEM((ns, ch), F32)] + [pltpu.VMEM((ch // LANES, tb, LANES), F32)] * 4 + [pltpu.VMEM((ch // LANES, ns, LANES), F32),
                        pltpu.VMEM((tb, ch), F32), pltpu.VMEM((tb, ch), F32), pltpu.VMEM((ns, ch), F32),
                        pltpu.VMEM((16 * ns, LANES), BF16), pltpu.VMEM((tb * ns, 2 * LANES), F32), pltpu.VMEM((tb * ns, 2 * LANES), BF16)],
        compiler_params=pltpu.CompilerParams(vmem_limit_bytes=48 << 20),
        name="scan_bwd",
    )(proj, inner, keep, step, states, starts, dscan, sproj, log_rates, skip)


def line_roles():
    me = lax.axis_index("tp")
    end = (me == 0) | (me == 3)
    mate = jnp.where(me < 2, 1 - me, 5 - me)
    return end, jnp.logical_not(end), mate, 3 - me


def greet(end, mid, mate, other, wide):
    barrier = pltpu.get_barrier_semaphore()
    me = lax.axis_index("wide")
    pl.semaphore_signal(barrier, inc=1, device_id={"tp": mate}, device_id_type=MESH)

    @pl.when(mid)
    def _():
        pl.semaphore_signal(barrier, inc=1, device_id={"tp": other}, device_id_type=MESH)

    for k in range(1, wide):
        pl.semaphore_signal(barrier, inc=1, device_id={"wide": lax.rem(me + k, wide)}, device_id_type=MESH)

    @pl.when(end)
    def _():
        pl.semaphore_wait(barrier, wide)

    @pl.when(mid)
    def _():
        pl.semaphore_wait(barrier, wide + 1)


class LineSum:
    def __init__(self, roles, rows, own, near, half, far, total, sends, arrivals):
        self.end, self.mid, self.mate, self.other = roles
        self.rows, self.own, self.near, self.half, self.far, self.total = rows, own, near, half, far, total
        self.sends, self.arrivals = sends, arrivals

    def part(self, ref, k):
        return ref.at[pl.ds(pl.multiple_of(k * self.rows, self.rows), self.rows)]

    def copy(self, source, target, hop, k, to):
        return pltpu.make_async_remote_copy(
            self.part(source, k), self.part(target, k), self.sends.at[hop, k], self.arrivals.at[hop, k],
            device_id={"tp": to}, device_id_type=MESH)

    def up(self, k):
        return self.copy(self.own, self.near, 0, k, self.mate)

    def across(self, k):
        return self.copy(self.half, self.far, 1, k, self.other)

    def down(self, k):
        return self.copy(self.total, self.total, 2, k, self.mate)

    def add(self, a, b, c, k):
        self.part(c, k)[...] = (self.part(a, k)[...].astype(F32) + self.part(b, k)[...].astype(F32)).astype(BF16)

    def first(self, k):
        self.up(k).wait_recv()
        self.add(self.own, self.near, self.half, k)
        self.across(k).start()

    def second(self, k):
        self.across(k).wait_recv()
        self.add(self.half, self.far, self.total, k)
        self.down(k).start()

    def sent(self, count):
        for k in range(count):
            @pl.when(self.end)
            def _():
                self.up(k).wait_send()

            @pl.when(self.mid)
            def _():
                self.across(k).wait_send()
                self.down(k).wait_send()


def line_scratch(rows, cols, blocks):
    return [pltpu.VMEM((rows, cols), BF16)] * 5 + [pltpu.SemaphoreType.DMA((3, blocks))] * 2


def tail_kernel(wide, taps, dproj_ref, dinner_ref, inner_ref, x_ref, csum_ref, masks_ref, wproj_ref, cw_ref, normed_ref, dz_ref,
                dmixed_ref, gated_ref, wx_ref, wz_ref, tokens_ref, scale_ref, gain_ref, dhidden_ref,
                gstep_ref, gsbias_ref, grates_ref, gskip_ref, gsecond_ref, grouter_ref,
                tgrad_ref, gx_ref, gz_ref, go_ref, small_ref,
                dp_own, dp_near, dp_half, dp_far, dp_total, dp_sends, dp_arrivals,
                dn_own, dn_near, dn_half, dn_far, dn_total, dn_sends, dn_arrivals,
                prod_s, inbox_s, prod_sends, prod_arrivals, pack_s, pack_in, pack_sends, pack_arrivals,
                dconv_s, dx_s, first_s):
    seq, ch = dinner_ref.shape
    width = tokens_ref.shape[1]
    tb = LANES
    nb = seq // tb
    me = lax.axis_index("wide")
    roles = line_roles()
    end, mid, mate, other = roles
    greet(*roles, wide)
    dp = LineSum(roles, seq, dp_own, dp_near, dp_half, dp_far, dp_total, dp_sends, dp_arrivals)
    dn = LineSum(roles, tb, dn_own, dn_near, dn_half, dn_far, dn_total, dn_sends, dn_arrivals)

    dp_own[...] = dproj_ref[...].astype(BF16)

    @pl.when(end)
    def _():
        dp.up(0).start()

    block = width // wide

    def deliver(which, k):
        to = lax.rem(me + k, wide)
        return pltpu.make_async_remote_copy(
            prod_s.at[which, pl.ds(pl.multiple_of(to * block, block), block)], inbox_s.at[which, k],
            prod_sends.at[which, k], prod_arrivals.at[which, k], device_id={"wide": to}, device_id_type=MESH)

    def product(which, left, right):
        def tile(j, _):
            cols = pl.ds(pl.multiple_of(j * LANES, LANES), LANES)
            got = lax.dot_general(left[:, cols], right[...], (((0,), (0,)), ((), ())), preferred_element_type=F32)
            prod_s[which, cols, :] = got.astype(BF16)
            return 0

        lax.fori_loop(0, width // LANES, tile, 0)
        for k in range(1, wide):
            deliver(which, k).start()

    product(0, dmixed_ref, gated_ref)

    @pl.when(mid)
    def _():
        dp.first(0)

    product(1, normed_ref, dz_ref)

    @pl.when(mid)
    def _():
        dp.second(0)

    @pl.when(end)
    def _():
        dp.down(0).wait_recv()

    pack_s[...] = jnp.zeros_like(pack_s)
    dconv_s[pl.ds(seq, 8), :] = jnp.zeros((8, ch), F32)
    first_s[...] = jnp.zeros_like(first_s)

    def rows_of(b):
        return pl.ds(pl.multiple_of(b * tb, tb), tb)

    def block_step(k, _):
        b = nb - 1 - k
        rows = rows_of(b)
        base = pl.multiple_of(b * tb, tb)
        d_inner = dinner_ref[rows, :] + lax.dot_general(
            dp_total[rows, :], wproj_ref[...], (((1,), (1,)), ((), ())), preferred_element_type=F32)
        csum = csum_ref[rows, :]
        logistic = 1.0 / (1.0 + jnp.exp(-csum))
        d_conv = d_inner * (logistic * (1.0 + csum * (1.0 - logistic)))
        dconv_s[rows, :] = d_conv
        prior = x_ref[pl.ds(pl.multiple_of(jnp.maximum(base - 8, 0), 8), 8), :]
        history = jnp.concatenate([prior, x_ref[rows, :]], axis=0)
        ahead = jnp.concatenate([d_conv, dconv_s[pl.ds(pl.multiple_of(base + tb, 8), 8), :]], axis=0)
        same = masks_ref[pl.ds(base, tb + 8), :]
        d_x = cw_ref[taps - 1:taps, :] * d_conv
        pack_s[0:1, :] += jnp.sum(d_conv, axis=0, keepdims=True)
        pack_s[8 - 1:8, :] += jnp.sum(d_conv * history[8:, :], axis=0, keepdims=True)
        for s in range(1, taps):
            linked = same[:, s:s + 1] * ahead
            d_x = d_x + cw_ref[taps - 1 - s:taps - s, :] * linked[s:s + tb, :]
            pack_s[7 - s:8 - s, :] += jnp.sum(linked[:tb, :] * history[8 - s:8 - s + tb, :], axis=0, keepdims=True)
        d_x = d_x.astype(BF16)
        dx_s[rows, :] = d_x
        both = lax.dot_general(d_x, wx_ref[...], (((1,), (1,)), ((), ())), preferred_element_type=F32)
        both = both + lax.dot_general(dz_ref[rows, :], wz_ref[...], (((1,), (1,)), ((), ())), preferred_element_type=F32)
        dn_own[rows, :] = both.astype(BF16)

        @pl.when(end)
        def _():
            dn.up(b).start()

        @pl.when(mid & (k > 0))
        def _():
            dn.first(b + 1)

        @pl.when(mid & (k > 1))
        def _():
            dn.second(b + 2)
        return 0

    lax.fori_loop(0, nb, block_step, 0)

    @pl.when(mid)
    def _():
        dn.second(1)
        dn.first(0)

    product(2, normed_ref, dx_s)
    state = lax.dot_general(dp_total[...], inner_ref[...], (((0,), (0,)), ((), ())), preferred_element_type=F32)

    @pl.when(mid)
    def _():
        dn.second(0)

    def finish(k, _):
        b = nb - 1 - k
        rows = rows_of(b)

        @pl.when(end)
        def _():
            dn.down(b).wait_recv()

        d_normed = dn_total[rows, :].astype(F32)
        scale = scale_ref[rows, :]
        unit = tokens_ref[rows, :] * scale
        through = d_normed * gain_ref[...]
        first_s[...] += jnp.sum(d_normed * unit, axis=0, keepdims=True)
        mean = jnp.mean(through * unit, axis=1, keepdims=True)
        tgrad_ref[rows, :] = dhidden_ref[rows, :] + scale * (through - unit * mean)
        return 0

    lax.fori_loop(0, nb, finish, 0)

    rank, states, experts = 48, grates_ref.shape[0], grouter_ref.shape[0]
    rank = gstep_ref.shape[0]
    pack_s[1:2, :] = gsbias_ref[...]
    pack_s[2:3, :] = gskip_ref[...]
    at = 8
    for ref in (grates_ref, gstep_ref):
        pack_s[at:at + ref.shape[0], :] = ref[...]
        at += ref.shape[0]
    held = rank + 2 * states
    pack_s[at:at + held, :] = state[:held, :]
    at += held
    halves = width // ch
    for h in range(halves):
        cols = slice(h * ch, (h + 1) * ch)
        pack_s[at + h:at + h + 1, :] = first_s[:, cols]
        pack_s[at + halves + h:at + halves + h + 1, :] = gsecond_ref[:, cols]
        pack_s[at + 8 + h * experts:at + 8 + (h + 1) * experts, :] = grouter_ref[:, cols]

    share = pack_s.shape[0] // wide

    def chunk(ref, i):
        return ref.at[pl.ds(pl.multiple_of(i * share, share), share)]

    def scatter(k):
        to = lax.rem(me + k, wide)
        return pltpu.make_async_remote_copy(chunk(pack_s, to), pack_in.at[k], pack_sends.at[0, k], pack_arrivals.at[0, k],
                                            device_id={"wide": to}, device_id_type=MESH)

    def spread_out(k):
        to = lax.rem(me + k, wide)
        return pltpu.make_async_remote_copy(chunk(small_ref, me), chunk(small_ref, me), pack_sends.at[1, k], pack_arrivals.at[1, k],
                                            device_id={"wide": to}, device_id_type=MESH)

    for k in range(1, wide):
        scatter(k).start()

    for which, ref in enumerate((go_ref, gz_ref, gx_ref)):
        total = prod_s[which, pl.ds(pl.multiple_of(me * block, block), block), :].astype(F32)
        for k in range(1, wide):
            deliver(which, k).wait_recv()
            total = total + inbox_s[which, k].astype(F32)
        ref[...] = total

    total = chunk(pack_s, me)[...]
    for k in range(1, wide):
        scatter(k).wait_recv()
        total = total + pack_in[k]
    chunk(small_ref, me)[...] = total
    for k in range(1, wide):
        spread_out(k).start()
    dp.sent(1)
    dn.sent(nb)
    for k in range(1, wide):
        for which in range(3):
            deliver(which, k).wait_send()
        scatter(k).wait_send()
    for k in range(1, wide):
        spread_out(k).wait_recv()
    for k in range(1, wide):
        spread_out(k).wait_send()


def pack_rows(rank, states, experts, width, ch, wide):
    rows = 8 + states + rank + (rank + 2 * states) + 8 + (width // ch) * experts
    return -(-rows // (8 * wide)) * (8 * wide)


def tail(wide, taps, *operands):
    (dproj, dinner, inner, x, csum, masks, wproj, cw, normed, dz, dmixed, gated, wx, wz, tokens, scale, gain, dhidden,
     gstep, gsbias, grates, gskip, gsecond, grouter) = operands
    seq, ch = dinner.shape
    width = tokens.shape[1]
    nb = seq // LANES
    packed = pack_rows(gstep.shape[0], grates.shape[0], grouter.shape[0], width, ch, wide)
    vm = pl.BlockSpec(memory_space=pltpu.VMEM)
    shape = jax.ShapeDtypeStruct
    dma = pltpu.SemaphoreType.DMA
    return pl.pallas_call(
        functools.partial(tail_kernel, wide, taps),
        in_specs=[vm] * len(operands),
        out_specs=[vm] * 5,
        out_shape=[shape((seq, width), F32)] + [shape((width // wide, ch), F32)] * 3 + [shape((packed, ch), F32)],
        scratch_shapes=[
            *line_scratch(seq, LANES, 1), *line_scratch(seq, width, nb),
            pltpu.VMEM((3, width, ch), BF16), pltpu.VMEM((3, wide, width // wide, ch), BF16), dma((3, wide)), dma((3, wide)),
            pltpu.VMEM((packed, ch), F32), pltpu.VMEM((wide, packed // wide, ch), F32), dma((2, wide)), dma((2, wide)),
            pltpu.VMEM((seq + 8, ch), F32), pltpu.VMEM((seq, ch), BF16), pltpu.VMEM((1, width), F32)],
        compiler_params=pltpu.CompilerParams(collective_id=1, has_side_effects=True, vmem_limit_bytes=56 << 20),
        name="mixer_tail",
    )(*operands)


def unpack_kernel(rank, states, small_ref, first_ref, cw_ref, cb_ref, state_ref, step_ref, sb_ref, rates_ref, skip_ref, second_ref, router_ref):
    ch = small_ref.shape[1]
    width, experts = router_ref.shape
    cb_ref[...] = small_ref[0:1, :]
    sb_ref[...] = small_ref[1:2, :]
    skip_ref[...] = small_ref[2:3, :]
    cw_ref[...] = small_ref[4:8, :]
    at = 8
    rates_ref[...] = small_ref[at:at + states, :]
    at += states
    step_ref[...] = small_ref[at:at + rank, :]
    at += rank
    held = rank + 2 * states
    state_ref[...] = small_ref[at:at + held, :].T
    at += held
    for h in range(width // ch):
        cols = slice(h * ch, (h + 1) * ch)
        first_ref[:, cols] = small_ref[at + h:at + h + 1, :]
        second_ref[:, cols] = small_ref[at + width // ch + h:at + width // ch + h + 1, :]
        router_ref[cols, :] = small_ref[at + 8 + h * experts:at + 8 + (h + 1) * experts, :].T


def unpack(small, rank, states, experts, width):
    ch = small.shape[1]
    shape = lambda *s: jax.ShapeDtypeStruct(s, F32)
    return pl.pallas_call(
        functools.partial(unpack_kernel, rank, states),
        out_shape=[shape(1, width), shape(4, ch), shape(1, ch), shape(ch, rank + 2 * states), shape(rank, ch), shape(1, ch), shape(states, ch),
                   shape(1, ch), shape(1, width), shape(width, experts)],
        name="unpack",
    )(small)


def plain_device(
    tokens,
    segment_ids,
    routes,
    out_grad,
    mixer_gain,
    in_proj_x,
    in_proj_z,
    conv_weight,
    conv_bias,
    state_proj,
    step_proj,
    step_bias,
    log_rates,
    skip_gain,
    out_proj,
    expert_gain,
    router_weight,
    expert_up,
    up_bias,
    expert_down,
    down_bias,
):
    seq_len, model_width = tokens.shape
    conv_taps = conv_weight.shape[0]
    step_rank = step_proj.shape[0]
    experts = router_weight.shape[1]
    capacity = 5 * seq_len // (4 * experts)
    doc_ids = segment_ids[0]
    conv_masks = [same_document(doc_ids, offset)[:, None] for offset in range(conv_taps)]
    first_scale = lax.rsqrt(jnp.mean(tokens * tokens, axis=1, keepdims=True) + EPS)
    first_unit = tokens * first_scale
    normed = (first_unit * mixer_gain).astype(jnp.bfloat16)
    gathered_x, gathered_z, gathered_out = (
        lax.all_gather(in_proj_x, "wide", axis=0, tiled=True),
        lax.all_gather(in_proj_z, "wide", axis=0, tiled=True),
        lax.all_gather(out_proj, "wide", axis=0, tiled=True),
    )
    x_branch = multiply(normed, gathered_x)
    z_branch = multiply(normed, gathered_z)
    conv_sum = conv_bias + jnp.zeros_like(x_branch)
    for offset in range(conv_taps):
        conv_sum = conv_sum + conv_weight[conv_taps - 1 - offset] * conv_masks[
            offset
        ] * shifted_down(x_branch, offset)
    inner_act = jax.nn.silu(conv_sum).astype(jnp.bfloat16)
    wide_proj = jnp.pad(state_proj, ((0, 0), (0, LANES - state_proj.shape[1])))
    projected = lax.psum(multiply(inner_act, wide_proj), "tp")
    tall_proj = jnp.pad(step_proj, ((0, LANES - step_rank), (0, 0)))
    carry_mask = same_document(doc_ids, 1)[:, None]
    scan_out, step_size, states, starts = scan_fwd(
        projected, inner_act, carry_mask, tall_proj, step_bias[None], log_rates, skip_gain[None], step_rank
    )
    z_gate = jax.nn.silu(z_branch)
    gated = (scan_out * z_gate).astype(jnp.bfloat16)
    mixed = lax.psum(contract_cols(gated, gathered_out).astype(jnp.bfloat16), "tp").astype(
        jnp.float32
    )
    hidden = tokens + mixed
    second_scale = lax.rsqrt(jnp.mean(hidden * hidden, axis=1, keepdims=True) + EPS)
    second_unit = hidden * second_scale
    expert_in = (second_unit * expert_gain).astype(jnp.bfloat16)
    route_ids = routes[:, 0]
    chosen_int = (routes == jnp.arange(experts, dtype=jnp.int32)[None, :]).astype(jnp.int32)
    chosen = chosen_int.astype(jnp.float32)
    logits = multiply(expert_in, router_weight)
    gate = jax.nn.sigmoid(jnp.sum(logits * chosen, axis=1))
    rank_of = jnp.arange(seq_len, dtype=jnp.int32)
    earlier = (rank_of[:, None] > rank_of[None, :]).astype(jnp.bfloat16)
    position = jnp.sum(multiply(earlier, chosen.astype(jnp.bfloat16)) * chosen, axis=1).astype(jnp.int32)
    kept = position < capacity
    slots = jnp.where(kept, route_ids * capacity + position, experts * capacity)
    scaled_grad = (gate[:, None] * out_grad).astype(jnp.bfloat16)
    sent_width = expert_in.shape[1]
    send_in = (
        jnp.zeros((experts * capacity + 1, sent_width), jnp.bfloat16).at[slots].set(expert_in)[:-1]
    )
    send_grad = (
        jnp.zeros((experts * capacity + 1, sent_width), jnp.bfloat16)
        .at[slots]
        .set(scaled_grad)[:-1]
    )
    recv_in, recv_grad = (
        lax.all_to_all(
            send_in.reshape(experts, capacity, sent_width),
            "wide",
            split_axis=0,
            concat_axis=0,
            tiled=True,
        ),
        lax.all_to_all(
            send_grad.reshape(experts, capacity, sent_width),
            "wide",
            split_axis=0,
            concat_axis=0,
            tiled=True,
        ),
    )
    rows_in = recv_in.reshape(-1, model_width)
    rows_grad = recv_grad.reshape(-1, model_width)
    pre_act = multiply(rows_in, expert_up[0]) + up_bias[0]
    hidden_act = jax.nn.gelu(pre_act).astype(jnp.bfloat16)
    partial_out = multiply(hidden_act, expert_down[0])
    up_grad = contract_cols(rows_grad, expert_down[0])
    d_pre = jax.vjp(jax.nn.gelu, pre_act)[1](up_grad)[0].astype(jnp.bfloat16)
    partial_back = contract_cols(d_pre, expert_up[0])
    grad_down = contract_rows(hidden_act, rows_grad)
    grad_dbias = jnp.sum(rows_grad.astype(jnp.float32), axis=0)
    grad_up = contract_rows(rows_in, d_pre)
    grad_ubias = jnp.sum(d_pre.astype(jnp.float32), axis=0)
    out_sum, back_sum = (
        lax.psum(partial_out.astype(jnp.bfloat16), "tp").astype(jnp.float32),
        lax.psum(partial_back.astype(jnp.bfloat16), "tp").astype(jnp.float32),
    )
    bias_part = down_bias[0]
    outgoing = (out_sum + bias_part).astype(jnp.bfloat16).reshape(experts, capacity, -1)
    back_rows = back_sum.astype(jnp.bfloat16).reshape(experts, capacity, -1)
    incoming, arriving = (
        lax.all_to_all(outgoing, "wide", split_axis=0, concat_axis=0, tiled=True),
        lax.all_to_all(back_rows, "wide", split_axis=0, concat_axis=0, tiled=True),
    )
    safe_slots = jnp.minimum(slots, experts * capacity - 1)
    returned = jnp.where(
        kept[:, None], incoming.reshape(-1, model_width)[safe_slots].astype(jnp.float32), 0.0
    )
    result = hidden + gate[:, None] * returned
    d_gate = jnp.sum(out_grad * returned, axis=1)
    d_logit = (d_gate * gate * (1.0 - gate))[:, None] * chosen
    grad_router = jnp.dot(expert_in.astype(jnp.float32).T, d_logit, precision=HIGH)
    d_norm_two = jnp.dot(d_logit, router_weight.astype(jnp.float32).T, precision=HIGH)
    d_norm_two = d_norm_two + jnp.where(
        kept[:, None], arriving.reshape(-1, model_width)[safe_slots].astype(jnp.float32), 0.0
    )
    grad_second_gain = jnp.sum(d_norm_two * second_unit, axis=0)
    d_hidden = out_grad + rms_back(d_norm_two * expert_gain, second_unit, second_scale)
    d_mixed = d_hidden.astype(jnp.bfloat16)
    d_gated = multiply(d_mixed, gathered_out)
    grad_out = contract_rows(d_mixed, gated)
    d_scan = d_gated * z_gate
    d_z = (d_gated * scan_out * silu_slope(z_branch)).astype(jnp.bfloat16)
    d_step_pre, d_inner, d_proj, grad_step, grad_sbias, grad_rates, grad_skip = scan_bwd(
        projected, inner_act, carry_mask, step_size, states, starts, d_scan, tall_proj, log_rates, skip_gain[None], step_rank
    )
    grad_step, grad_sbias, grad_skip = grad_step[:step_rank], grad_sbias[0], grad_skip[0]
    d_projected = lax.psum(d_proj.astype(jnp.bfloat16), "tp")
    grad_state = contract_rows(inner_act, d_projected)[:, : state_proj.shape[1]]
    d_inner = d_inner + contract_cols(d_projected, wide_proj)
    d_conv = d_inner * silu_slope(conv_sum)
    grad_cbias = jnp.sum(d_conv, axis=0)
    conv_rows = []
    d_input = jnp.zeros_like(d_conv)
    for offset in range(conv_taps):
        conv_rows.append(
            jnp.sum(d_conv * conv_masks[offset] * shifted_down(x_branch, offset), axis=0)
        )
        d_input = d_input + conv_weight[conv_taps - 1 - offset] * shifted_up(
            conv_masks[offset] * d_conv, offset
        )
    grad_conv = jnp.stack(conv_rows[::-1])
    d_x_branch = d_input.astype(jnp.bfloat16)
    grad_in_x = contract_rows(normed, d_x_branch)
    grad_in_z = contract_rows(normed, d_z)
    d_normed = lax.psum(
        (contract_cols(d_x_branch, gathered_x) + contract_cols(d_z, gathered_z)).astype(
            jnp.bfloat16
        ),
        "tp",
    ).astype(jnp.float32)
    grad_first_gain = jnp.sum(d_normed * first_unit, axis=0)
    tokens_grad = d_hidden + rms_back(d_normed * mixer_gain, first_unit, first_scale)
    grad_in_x, grad_in_z, grad_out = (
        summed_on_arrival(grad_in_x.astype(jnp.bfloat16), "wide", 0),
        summed_on_arrival(grad_in_z.astype(jnp.bfloat16), "wide", 0),
        summed_on_arrival(grad_out.astype(jnp.bfloat16), "wide", 0),
    )
    (
        grad_first_gain,
        grad_conv,
        grad_cbias,
        grad_state,
        grad_step,
        grad_sbias,
        grad_rates,
        grad_skip,
        grad_second_gain,
        grad_router,
    ) = lax.psum(
        (
            grad_first_gain,
            grad_conv,
            grad_cbias,
            grad_state,
            grad_step,
            grad_sbias,
            grad_rates,
            grad_skip,
            grad_second_gain,
            grad_router,
        ),
        "wide",
    )
    return (
        result,
        tokens_grad,
        grad_first_gain,
        grad_in_x,
        grad_in_z,
        grad_conv,
        grad_cbias,
        grad_state,
        grad_step,
        grad_sbias,
        grad_rates,
        grad_skip,
        grad_out,
        grad_second_gain,
        grad_router,
        grad_up[None],
        grad_ubias[None],
        grad_down[None],
        grad_dbias[None],
    )


def fast_device(
    tokens,
    segment_ids,
    routes,
    out_grad,
    mixer_gain,
    in_proj_x,
    in_proj_z,
    conv_weight,
    conv_bias,
    state_proj,
    step_proj,
    step_bias,
    log_rates,
    skip_gain,
    out_proj,
    expert_gain,
    router_weight,
    expert_up,
    up_bias,
    expert_down,
    down_bias,
):
    seq_len, model_width = tokens.shape
    conv_taps = conv_weight.shape[0]
    step_rank = step_proj.shape[0]
    experts = router_weight.shape[1]
    capacity = 5 * seq_len // (4 * experts)
    doc_ids = segment_ids[0]
    conv_masks = [same_document(doc_ids, offset)[:, None] for offset in range(conv_taps)]
    first_scale = lax.rsqrt(jnp.mean(tokens * tokens, axis=1, keepdims=True) + EPS)
    first_unit = tokens * first_scale
    normed = (first_unit * mixer_gain).astype(jnp.bfloat16)
    gathered_x, gathered_z, gathered_out = (
        lax.all_gather(in_proj_x, "wide", axis=0, tiled=True),
        lax.all_gather(in_proj_z, "wide", axis=0, tiled=True),
        lax.all_gather(out_proj, "wide", axis=0, tiled=True),
    )
    x_branch = multiply(normed, gathered_x)
    z_branch = multiply(normed, gathered_z)
    conv_sum = conv_bias + jnp.zeros_like(x_branch)
    for offset in range(conv_taps):
        conv_sum = conv_sum + conv_weight[conv_taps - 1 - offset] * conv_masks[
            offset
        ] * shifted_down(x_branch, offset)
    inner_act = jax.nn.silu(conv_sum).astype(jnp.bfloat16)
    wide_proj = jnp.pad(state_proj, ((0, 0), (0, LANES - state_proj.shape[1])))
    projected = lax.psum(multiply(inner_act, wide_proj), "tp")
    tall_proj = jnp.pad(step_proj, ((0, LANES - step_rank), (0, 0)))
    carry_mask = same_document(doc_ids, 1)[:, None]
    scan_out, step_size, states, starts = scan_fwd(
        projected, inner_act, carry_mask, tall_proj, step_bias[None], log_rates, skip_gain[None], step_rank
    )
    z_gate = jax.nn.silu(z_branch)
    gated = (scan_out * z_gate).astype(jnp.bfloat16)
    mixed = lax.psum(contract_cols(gated, gathered_out).astype(jnp.bfloat16), "tp").astype(
        jnp.float32
    )
    hidden = tokens + mixed
    second_scale = lax.rsqrt(jnp.mean(hidden * hidden, axis=1, keepdims=True) + EPS)
    second_unit = hidden * second_scale
    expert_in = (second_unit * expert_gain).astype(jnp.bfloat16)
    route_ids = routes[:, 0]
    chosen_int = (routes == jnp.arange(experts, dtype=jnp.int32)[None, :]).astype(jnp.int32)
    chosen = chosen_int.astype(jnp.float32)
    logits = multiply(expert_in, router_weight)
    gate = jax.nn.sigmoid(jnp.sum(logits * chosen, axis=1))
    rank_of = jnp.arange(seq_len, dtype=jnp.int32)
    earlier = (rank_of[:, None] > rank_of[None, :]).astype(jnp.bfloat16)
    position = jnp.sum(multiply(earlier, chosen.astype(jnp.bfloat16)) * chosen, axis=1).astype(jnp.int32)
    kept = position < capacity
    slots = jnp.where(kept, route_ids * capacity + position, experts * capacity)
    scaled_grad = (gate[:, None] * out_grad).astype(jnp.bfloat16)
    sent_width = expert_in.shape[1]
    send_in = (
        jnp.zeros((experts * capacity + 1, sent_width), jnp.bfloat16).at[slots].set(expert_in)[:-1]
    )
    send_grad = (
        jnp.zeros((experts * capacity + 1, sent_width), jnp.bfloat16)
        .at[slots]
        .set(scaled_grad)[:-1]
    )
    recv_in, recv_grad = (
        lax.all_to_all(
            send_in.reshape(experts, capacity, sent_width),
            "wide",
            split_axis=0,
            concat_axis=0,
            tiled=True,
        ),
        lax.all_to_all(
            send_grad.reshape(experts, capacity, sent_width),
            "wide",
            split_axis=0,
            concat_axis=0,
            tiled=True,
        ),
    )
    rows_in = recv_in.reshape(-1, model_width)
    rows_grad = recv_grad.reshape(-1, model_width)
    pre_act = multiply(rows_in, expert_up[0]) + up_bias[0]
    hidden_act = jax.nn.gelu(pre_act).astype(jnp.bfloat16)
    partial_out = multiply(hidden_act, expert_down[0])
    up_grad = contract_cols(rows_grad, expert_down[0])
    d_pre = jax.vjp(jax.nn.gelu, pre_act)[1](up_grad)[0].astype(jnp.bfloat16)
    partial_back = contract_cols(d_pre, expert_up[0])
    grad_down = contract_rows(hidden_act, rows_grad)
    grad_dbias = jnp.sum(rows_grad.astype(jnp.float32), axis=0)
    grad_up = contract_rows(rows_in, d_pre)
    grad_ubias = jnp.sum(d_pre.astype(jnp.float32), axis=0)
    out_sum, back_sum = (
        lax.psum(partial_out.astype(jnp.bfloat16), "tp").astype(jnp.float32),
        lax.psum(partial_back.astype(jnp.bfloat16), "tp").astype(jnp.float32),
    )
    bias_part = down_bias[0]
    outgoing = (out_sum + bias_part).astype(jnp.bfloat16).reshape(experts, capacity, -1)
    back_rows = back_sum.astype(jnp.bfloat16).reshape(experts, capacity, -1)
    incoming, arriving = (
        lax.all_to_all(outgoing, "wide", split_axis=0, concat_axis=0, tiled=True),
        lax.all_to_all(back_rows, "wide", split_axis=0, concat_axis=0, tiled=True),
    )
    safe_slots = jnp.minimum(slots, experts * capacity - 1)
    returned = jnp.where(
        kept[:, None], incoming.reshape(-1, model_width)[safe_slots].astype(jnp.float32), 0.0
    )
    result = hidden + gate[:, None] * returned
    d_gate = jnp.sum(out_grad * returned, axis=1)
    d_logit = (d_gate * gate * (1.0 - gate))[:, None] * chosen
    grad_router = jnp.dot(d_logit.T, expert_in.astype(jnp.float32), precision=HIGH)
    d_norm_two = jnp.dot(d_logit, router_weight.astype(jnp.float32).T, precision=HIGH)
    d_norm_two = d_norm_two + jnp.where(
        kept[:, None], arriving.reshape(-1, model_width)[safe_slots].astype(jnp.float32), 0.0
    )
    grad_second_gain = jnp.sum(d_norm_two * second_unit, axis=0, keepdims=True)
    d_hidden = out_grad + rms_back(d_norm_two * expert_gain, second_unit, second_scale)
    d_mixed = d_hidden.astype(jnp.bfloat16)
    d_gated = multiply(d_mixed, gathered_out)
    d_scan = d_gated * z_gate
    d_z = (d_gated * scan_out * silu_slope(z_branch)).astype(jnp.bfloat16)
    d_step_pre, d_inner, d_proj, grad_step, grad_sbias, grad_rates, grad_skip = scan_bwd(
        projected, inner_act, carry_mask, step_size, states, starts, d_scan, tall_proj, log_rates, skip_gain[None], step_rank
    )
    grad_step = grad_step[:step_rank]
    masks = jnp.pad(jnp.concatenate(conv_masks, axis=1), ((0, 8), (0, 8 - conv_taps)))
    wide = lax.axis_size("wide")
    tokens_grad, grad_in_x, grad_in_z, grad_out, small = tail(
        wide, conv_taps, d_proj, d_inner, inner_act, x_branch, conv_sum, masks, wide_proj, conv_weight, normed, d_z,
        d_mixed, gated, gathered_x, gathered_z, tokens, first_scale, mixer_gain[None], d_hidden,
        grad_step, grad_sbias, grad_rates, grad_skip, grad_second_gain, grad_router,
    )
    (
        grad_first_gain, grad_conv, grad_cbias, grad_state, grad_step, grad_sbias, grad_rates, grad_skip, grad_second_gain, grad_router,
    ) = unpack(small, step_rank, log_rates.shape[0], experts, model_width)
    return (
        result,
        tokens_grad,
        grad_first_gain[0],
        grad_in_x,
        grad_in_z,
        grad_conv,
        grad_cbias[0],
        grad_state,
        grad_step,
        grad_sbias[0],
        grad_rates,
        grad_skip[0],
        grad_out,
        grad_second_gain[0],
        grad_router,
        grad_up[None],
        grad_ubias[None],
        grad_down[None],
        grad_dbias[None],
    )


def solution(mesh):
    in_specs = (
        P("wide", None),
        P("wide", None),
        P("wide", None),
        P("wide", None),
        P(),
        P("wide", "tp"),
        P("wide", "tp"),
        P(None, "tp"),
        P("tp"),
        P("tp", None),
        P(None, "tp"),
        P("tp"),
        P(None, "tp"),
        P("tp"),
        P("wide", "tp"),
        P(),
        P(),
        P("wide", None, "tp"),
        P("wide", "tp"),
        P("wide", "tp", None),
        P("wide", None),
    )
    out_specs = (
        P("wide", None),
        P("wide", None),
        P(),
        P("wide", "tp"),
        P("wide", "tp"),
        P(None, "tp"),
        P("tp"),
        P("tp", None),
        P(None, "tp"),
        P("tp"),
        P(None, "tp"),
        P("tp"),
        P("wide", "tp"),
        P(),
        P(),
        P("wide", None, "tp"),
        P("wide", "tp"),
        P("wide", "tp", None),
        P("wide", None),
    )
    wide, line = mesh.shape["wide"], mesh.shape["tp"]
    per_device = fast_device if line == 4 and wide == 8 else plain_device
    return jax.shard_map(
        per_device, mesh=mesh, in_specs=in_specs, out_specs=out_specs, check_vma=False
    )
```

```python
import functools

import jax
import jax.numpy as jnp
from jax import lax
from jax.experimental import pallas as pl
from jax.experimental.pallas import tpu as pltpu
from jax.sharding import PartitionSpec as P

EPS = 1e-05
HIGH = lax.Precision.HIGHEST


def in_blocks(shard, dim, size):
    before, after = (shard.shape[:dim], shard.shape[dim + 1 :])
    return jnp.moveaxis(shard.reshape(*before, size, -1, *after), dim, 0)


def summed_on_arrival(shard, axis, dim):
    size = lax.axis_size(axis)
    parts = lax.all_to_all(in_blocks(shard, dim, size), axis, 0, 0, tiled=True)
    return jnp.sum(parts.astype(jnp.float32), axis=0)


def multiply(left, right):
    return jnp.dot(left, right, preferred_element_type=jnp.float32)


def contract_rows(left, right):
    return lax.dot_general(
        left, right, (((0,), (0,)), ((), ())), preferred_element_type=jnp.float32
    )


def contract_cols(left, right):
    return lax.dot_general(
        left, right, (((1,), (1,)), ((), ())), preferred_element_type=jnp.float32
    )


def shifted_down(values, steps):
    if steps == 0:
        return values
    filler = jnp.zeros((steps,) + values.shape[1:], values.dtype)
    return jnp.concatenate([filler, values[:-steps]], axis=0)


def shifted_up(values, steps):
    if steps == 0:
        return values
    filler = jnp.zeros((steps,) + values.shape[1:], values.dtype)
    return jnp.concatenate([values[steps:], filler], axis=0)


def same_document(doc_ids, steps):
    if steps == 0:
        return jnp.ones(doc_ids.shape, jnp.float32)
    filler = jnp.full((steps,), -1, jnp.int32)
    earlier = jnp.concatenate([filler, doc_ids[:-steps]])
    return (earlier == doc_ids).astype(jnp.float32)


def silu_slope(values):
    logistic = jax.nn.sigmoid(values)
    return logistic * (1.0 + values * (1.0 - logistic))


def rms_back(grad_unit, unit, scale):
    return scale * (grad_unit - unit * jnp.mean(grad_unit * unit, axis=1, keepdims=True))


LOG2E = 1.4426950408889634
LANES = 128
F32, BF16 = jnp.float32, jnp.bfloat16
MESH = pl.DeviceIdType.MESH


def fold_rows(parts, masks):
    m4, m2, m1 = masks

    def join(a, b, m, shift):
        return jnp.where(m, a, b) + pltpu.roll(jnp.where(m, b, a), shift, 0)

    c = [join(parts[i], parts[i + 4], m4[i], 4) for i in range(4)]
    d = [join(c[i], c[i + 2], m2[i], 6) for i in range(2)]
    return join(d[0], d[1], m1, 7)


def fold_masks(width):
    sub = lax.broadcasted_iota(jnp.int32, (8, width), 0)
    m4 = [((sub - i) & 7) < 4 for i in range(4)]
    m2 = [((sub - i) & 2) == 0 for i in range(2)]
    m1 = (sub & 1) == 0
    return m4, m2, m1


def softplus(v):
    return jnp.maximum(v, 0.0) + jnp.log1p(jnp.exp(-jnp.abs(v)))


def row(ref, c, t, ns):
    one = ref[c, pl.ds(t, 8, stride=0), :]
    return jnp.concatenate([one] * (ns // 8), axis=0)


def spread(ref, value):
    for c in range(ref.shape[0]):
        ref[c] = value[:, c * LANES:(c + 1) * LANES]


def own_column(ns, rank):
    lane = lax.broadcasted_iota(jnp.int32, (ns, LANES), 1)
    n = lax.broadcasted_iota(jnp.int32, (ns, LANES), 0)
    return (lane == rank + n) | (lane == rank + ns + n)


def coefficient_rows(ns, rank, proj_ref, rows_s, wide_s):
    tb = proj_ref.shape[0]
    own = own_column(ns, rank)
    lane = lax.broadcasted_iota(jnp.int32, (LANES, 2 * LANES), 1)
    k = lax.broadcasted_iota(jnp.int32, (LANES, 2 * LANES), 0)
    pick = ((lane < LANES) & (k >= rank) & (k < rank + ns)) | ((lane >= LANES) & (k >= rank + ns) & (k < rank + 2 * ns))
    pick = jnp.where(pick, 1.0, 0.0).astype(BF16)

    def body(g, _):
        for j in range(16):
            t = g * 16 + j
            one = proj_ref[pl.ds(t, 8, stride=0), :]
            both = jnp.where(own, jnp.concatenate([one] * (ns // 8), axis=0), 0.0)
            rows_s[pl.ds(pl.multiple_of(j * ns, ns), ns), :] = both.astype(BF16)
        wide_s[pl.ds(pl.multiple_of(g * 16 * ns, 16 * ns), 16 * ns), :] = jnp.dot(rows_s[...], pick, preferred_element_type=F32)
        return 0

    lax.fori_loop(0, tb // 16, body, 0)


def scan_fwd_kernel(ns, rank, proj_ref, inner_ref, keep_ref, sproj_ref, sbias_ref, lr_ref, skip_ref,
                    scan_ref, step_ref, states_ref, starts_ref, state_s, stepd_s, drive_s, r2_s, rows_s, wide_s):
    tb, ch = inner_ref.shape
    groups = ch // LANES
    i = pl.program_id(0)

    @pl.when(i == 0)
    def _():
        state_s[...] = jnp.zeros_like(state_s)
        spread(r2_s, jnp.exp(lr_ref[...]) * (-LOG2E))

    step_in = proj_ref[...].astype(BF16)
    pre = jnp.dot(step_in, sproj_ref[...], preferred_element_type=F32) + sbias_ref[...]
    step = softplus(pre)
    step_ref[...] = step
    spread(stepd_s, jnp.where(keep_ref[...] > 0.0, step, 1e30))
    inner = inner_ref[...].astype(F32)
    spread(drive_s, step * inner)
    coefficient_rows(ns, rank, proj_ref, rows_s, wide_s)
    starts_ref[0] = state_s[...]
    masks = fold_masks(LANES)

    def body(g, state):
        state = list(state)
        parts = [[] for _ in range(groups)]
        for j in range(8):
            t = g * 8 + j
            here = pl.ds(pl.multiple_of(t * ns, ns), ns)
            in_b = wide_s[here, :LANES]
            out_b = wide_s[here, LANES:]
            for c in range(groups):
                cols = pl.ds(c * LANES, LANES)
                dec = jnp.exp2(row(stepd_s, c, t, ns) * r2_s[c])
                s = dec * state[c] + row(drive_s, c, t, ns) * in_b
                state[c] = s
                states_ref[here, cols] = s.astype(BF16)
                z = out_b * s
                parts[c].append(sum(z[8 * k:8 * k + 8] for k in range(ns // 8)))
        for c in range(groups):
            scan_ref[pl.ds(pl.multiple_of(g * 8, 8), 8), pl.ds(c * LANES, LANES)] = fold_rows(parts[c], masks)
        return tuple(state)

    start = tuple(state_s[:, c * LANES:(c + 1) * LANES] for c in range(groups))
    state = lax.fori_loop(0, tb // 8, body, start)
    for c in range(groups):
        state_s[:, c * LANES:(c + 1) * LANES] = state[c]
    scan_ref[...] += skip_ref[...] * inner


def scan_fwd(proj, inner, keep, sproj, sbias, log_rates, skip, rank):
    seq, ch = inner.shape
    ns = log_rates.shape[0]
    tb = LANES
    nb = seq // tb
    full = lambda a: pl.BlockSpec(a.shape, lambda i: (0,) * a.ndim)
    rows = pl.BlockSpec((tb, ch), lambda i: (i, 0))
    return pl.pallas_call(
        functools.partial(scan_fwd_kernel, ns, rank),
        grid=(nb,),
        in_specs=[pl.BlockSpec((tb, LANES), lambda i: (i, 0)), rows, pl.BlockSpec((tb, 1), lambda i: (i, 0)),
                  full(sproj), full(sbias), full(log_rates), full(skip)],
        out_specs=[rows, rows, pl.BlockSpec((tb * ns, ch), lambda i: (i, 0)), pl.BlockSpec((1, ns, ch), lambda i: (i, 0, 0))],
        out_shape=[jax.ShapeDtypeStruct((seq, ch), F32), jax.ShapeDtypeStruct((seq, ch), F32),
                   jax.ShapeDtypeStruct((seq * ns, ch), BF16), jax.ShapeDtypeStruct((nb, ns, ch), F32)],
        scratch_shapes=[pltpu.VMEM((ns, ch), F32)] + [pltpu.VMEM((ch // LANES, tb, LANES), F32)] * 2 + [pltpu.VMEM((ch // LANES, ns, LANES), F32),
                        pltpu.VMEM((16 * ns, LANES), BF16), pltpu.VMEM((tb * ns, 2 * LANES), F32)],
        compiler_params=pltpu.CompilerParams(vmem_limit_bytes=48 << 20),
        name="scan_fwd",
    )(proj, inner, keep, sproj, sbias, log_rates, skip)


def scan_bwd_kernel(ns, rank, proj_ref, inner_ref, keep_ref, step_ref, states_ref, starts_ref, dscan_ref, sproj_ref, lr_ref, skip_ref,
                    dpre_ref, dinner_ref, dproj_ref, gstep_ref, gsbias_ref, grates_ref, gskip_ref,
                    carry_s, stepd_s, drive_s, dscan_s, step_s, r2_s, coeff_s, exps_s, acc_s, rows_s, wide_s, sums_s):
    tb, ch = inner_ref.shape
    groups = ch // LANES
    i = pl.program_id(0)

    @pl.when(i == 0)
    def _():
        carry_s[...] = jnp.zeros_like(carry_s)
        acc_s[...] = jnp.zeros_like(acc_s)
        spread(r2_s, jnp.exp(lr_ref[...]) * (-LOG2E))
        gstep_ref[...] = jnp.zeros_like(gstep_ref)
        gsbias_ref[...] = jnp.zeros_like(gsbias_ref)
        gskip_ref[...] = jnp.zeros_like(gskip_ref)

    step = step_ref[...]
    inner = inner_ref[...].astype(F32)
    dscan = dscan_ref[...]
    spread(stepd_s, jnp.where(keep_ref[...] > 0.0, step, 1e30))
    spread(drive_s, step * inner)
    spread(dscan_s, dscan)
    spread(step_s, step)
    coefficient_rows(ns, rank, proj_ref, rows_s, wide_s)
    masks = fold_masks(LANES)
    steps = tb // 8

    def body(k, carry):
        later, acc = [list(v) for v in carry]
        g = steps - 1 - k
        cparts = [[None] * 8 for _ in range(groups)]
        eparts = [[None] * 8 for _ in range(groups)]
        last = pl.ds(pl.multiple_of((g * 8 + 7) * ns, ns), ns)
        now = [states_ref[last, pl.ds(c * LANES, LANES)].astype(F32) for c in range(groups)]
        for j in range(7, -1, -1):
            t = g * 8 + j
            here = pl.ds(pl.multiple_of(t * ns, ns), ns)
            prior = pl.ds(pl.multiple_of((t - 1 if j else jnp.maximum(t - 1, 0)) * ns, ns), ns)
            in_b = wide_s[here, :LANES]
            out_b = wide_s[here, LANES:]
            din = dout = None
            for c in range(groups):
                cols = pl.ds(c * LANES, LANES)
                before = states_ref[prior, cols].astype(F32)
                if j == 0:
                    before = jnp.where(jnp.full((ns, LANES), t, jnp.int32) == 0, starts_ref[0, :, cols], before)
                r2 = r2_s[c]
                dec = jnp.exp2(row(stepd_s, c, t, ns) * r2)
                ds = row(dscan_s, c, t, ns)
                d = later[c] + out_b * ds
                later[c] = dec * d
                dexp = later[c] * before
                e = dexp * r2
                cf = d * in_b
                cparts[c][j] = sum(cf[8 * q:8 * q + 8] for q in range(ns // 8))
                eparts[c][j] = sum(e[8 * q:8 * q + 8] for q in range(ns // 8))
                acc[c] = acc[c] + dexp * row(step_s, c, t, ns)
                a = d * row(drive_s, c, t, ns)
                b = now[c] * ds
                din = a if din is None else din + a
                dout = b if dout is None else dout + b
                now[c] = before
            sums_s[here, :LANES] = din.astype(BF16)
            sums_s[here, LANES:] = dout.astype(BF16)
        rows = pl.ds(pl.multiple_of(g * 8, 8), 8)
        for c in range(groups):
            cols = pl.ds(c * LANES, LANES)
            coeff_s[rows, cols] = fold_rows(cparts[c], masks)
            exps_s[rows, cols] = fold_rows(eparts[c], masks)
        return tuple(later), tuple(acc)

    pick = lambda ref: tuple(ref[:, c * LANES:(c + 1) * LANES] for c in range(groups))
    later, acc = lax.fori_loop(0, steps, body, (pick(carry_s), pick(acc_s)))
    for c in range(groups):
        carry_s[:, c * LANES:(c + 1) * LANES] = later[c]
        acc_s[:, c * LANES:(c + 1) * LANES] = acc[c]

    k = lax.broadcasted_iota(jnp.int32, (2 * LANES, LANES), 0)
    lane = lax.broadcasted_iota(jnp.int32, (2 * LANES, LANES), 1)
    into = ((k < LANES) & (lane >= rank) & (lane < rank + ns)) | ((k >= LANES) & (lane >= rank + ns) & (lane < rank + 2 * ns))
    into = jnp.where(into, 1.0, 0.0).astype(BF16)
    own = own_column(ns, rank)

    def gather(g, _):
        got = jnp.dot(sums_s[pl.ds(pl.multiple_of(g * 16 * ns, 16 * ns), 16 * ns), :], into, preferred_element_type=F32)
        for h in range(2):
            parts = []
            for j in range(8):
                one = jnp.where(own, got[(h * 8 + j) * ns:(h * 8 + j + 1) * ns], 0.0)
                parts.append(sum(one[8 * q:8 * q + 8] for q in range(ns // 8)))
            dproj_ref[pl.ds(pl.multiple_of(g * 16 + h * 8, 8), 8), :] = fold_rows(parts, masks)
        return 0

    lax.fori_loop(0, tb // 16, gather, 0)
    coeff = coeff_s[...]
    d_step = coeff * inner + exps_s[...] * (1.0 / LOG2E)
    d_pre = (d_step * (1.0 - jnp.exp(-step))).astype(BF16)
    dpre_ref[...] = d_pre
    dinner_ref[...] = dscan * skip_ref[...] + step * coeff
    step_in = proj_ref[...].astype(BF16)
    gstep_ref[...] += lax.dot_general(step_in, d_pre, (((0,), (0,)), ((), ())), preferred_element_type=F32)
    gsbias_ref[...] += jnp.sum(d_pre.astype(F32), axis=0, keepdims=True)
    gskip_ref[...] += jnp.sum(dscan * inner, axis=0, keepdims=True)
    dproj_ref[...] += lax.dot_general(d_pre, sproj_ref[...], (((1,), (1,)), ((), ())), preferred_element_type=F32)

    @pl.when(i == pl.num_programs(0) - 1)
    def _():
        grates_ref[...] = -jnp.exp(lr_ref[...]) * acc_s[...]


def scan_bwd(proj, inner, keep, step, states, starts, dscan, sproj, log_rates, skip, rank):
    seq, ch = inner.shape
    ns = log_rates.shape[0]
    tb = LANES
    nb = seq // tb
    full = lambda a: pl.BlockSpec(a.shape, lambda i: (0,) * a.ndim)
    rows = pl.BlockSpec((tb, ch), lambda i: (nb - 1 - i, 0))
    prow = pl.BlockSpec((tb, LANES), lambda i: (nb - 1 - i, 0))
    whole = lambda *s: pl.BlockSpec(s, lambda i: (0,) * len(s))
    shape = jax.ShapeDtypeStruct
    return pl.pallas_call(
        functools.partial(scan_bwd_kernel, ns, rank),
        grid=(nb,),
        in_specs=[prow, rows, pl.BlockSpec((tb, 1), lambda i: (nb - 1 - i, 0)), rows,
                  pl.BlockSpec((tb * ns, ch), lambda i: (nb - 1 - i, 0)), pl.BlockSpec((1, ns, ch), lambda i: (nb - 1 - i, 0, 0)),
                  rows, full(sproj), full(log_rates), full(skip)],
        out_specs=[rows, rows, prow, whole(LANES, ch), whole(1, ch), whole(ns, ch), whole(1, ch)],
        out_shape=[shape((seq, ch), BF16), shape((seq, ch), F32), shape((seq, LANES), F32), shape((LANES, ch), F32), shape((1, ch), F32),
                   shape((ns, ch), F32), shape((1, ch), F32)],
        scratch_shapes=[pltpu.VMEM((ns, ch), F32)] + [pltpu.VMEM((ch // LANES, tb, LANES), F32)] * 4 + [pltpu.VMEM((ch // LANES, ns, LANES), F32),
                        pltpu.VMEM((tb, ch), F32), pltpu.VMEM((tb, ch), F32), pltpu.VMEM((ns, ch), F32),
                        pltpu.VMEM((16 * ns, LANES), BF16), pltpu.VMEM((tb * ns, 2 * LANES), F32), pltpu.VMEM((tb * ns, 2 * LANES), BF16)],
        compiler_params=pltpu.CompilerParams(vmem_limit_bytes=48 << 20),
        name="scan_bwd",
    )(proj, inner, keep, step, states, starts, dscan, sproj, log_rates, skip)


def line_roles():
    me = lax.axis_index("tp")
    end = (me == 0) | (me == 3)
    mate = jnp.where(me < 2, 1 - me, 5 - me)
    return end, jnp.logical_not(end), mate, 3 - me


def greet(end, mid, mate, other, wide):
    barrier = pltpu.get_barrier_semaphore()
    me = lax.axis_index("wide")
    pl.semaphore_signal(barrier, inc=1, device_id={"tp": mate}, device_id_type=MESH)

    @pl.when(mid)
    def _():
        pl.semaphore_signal(barrier, inc=1, device_id={"tp": other}, device_id_type=MESH)

    for k in range(1, wide):
        pl.semaphore_signal(barrier, inc=1, device_id={"wide": lax.rem(me + k, wide)}, device_id_type=MESH)

    @pl.when(end)
    def _():
        pl.semaphore_wait(barrier, wide)

    @pl.when(mid)
    def _():
        pl.semaphore_wait(barrier, wide + 1)


class LineSum:
    def __init__(self, roles, rows, own, near, half, far, total, sends, arrivals):
        self.end, self.mid, self.mate, self.other = roles
        self.rows, self.own, self.near, self.half, self.far, self.total = rows, own, near, half, far, total
        self.sends, self.arrivals = sends, arrivals

    def part(self, ref, k):
        return ref.at[pl.ds(pl.multiple_of(k * self.rows, self.rows), self.rows)]

    def copy(self, source, target, hop, k, to):
        return pltpu.make_async_remote_copy(
            self.part(source, k), self.part(target, k), self.sends.at[hop, k], self.arrivals.at[hop, k],
            device_id={"tp": to}, device_id_type=MESH)

    def up(self, k):
        return self.copy(self.own, self.near, 0, k, self.mate)

    def across(self, k):
        return self.copy(self.half, self.far, 1, k, self.other)

    def down(self, k):
        return self.copy(self.total, self.total, 2, k, self.mate)

    def add(self, a, b, c, k):
        self.part(c, k)[...] = (self.part(a, k)[...].astype(F32) + self.part(b, k)[...].astype(F32)).astype(BF16)

    def first(self, k):
        self.up(k).wait_recv()
        self.add(self.own, self.near, self.half, k)
        self.across(k).start()

    def second(self, k):
        self.across(k).wait_recv()
        self.add(self.half, self.far, self.total, k)
        self.down(k).start()

    def sent(self, count):
        for k in range(count):
            @pl.when(self.end)
            def _():
                self.up(k).wait_send()

            @pl.when(self.mid)
            def _():
                self.across(k).wait_send()
                self.down(k).wait_send()


def line_scratch(rows, cols, blocks):
    return [pltpu.VMEM((rows, cols), BF16)] * 5 + [pltpu.SemaphoreType.DMA((3, blocks))] * 2


def tail_kernel(wide, taps, dproj_ref, dinner_ref, inner_ref, x_ref, csum_ref, masks_ref, wproj_ref, cw_ref, normed_ref, dz_ref,
                dmixed_ref, gated_ref, wx_ref, wz_ref, tokens_ref, scale_ref, gain_ref, dhidden_ref,
                gstep_ref, gsbias_ref, grates_ref, gskip_ref, gsecond_ref, grouter_ref,
                tgrad_ref, gx_ref, gz_ref, go_ref, small_ref,
                dp_own, dp_near, dp_half, dp_far, dp_total, dp_sends, dp_arrivals,
                dn_own, dn_near, dn_half, dn_far, dn_total, dn_sends, dn_arrivals,
                prod_s, inbox_s, prod_sends, prod_arrivals, pack_s, pack_in, pack_sends, pack_arrivals,
                dconv_s, dx_s, first_s):
    seq, ch = dinner_ref.shape
    width = tokens_ref.shape[1]
    tb = LANES
    nb = seq // tb
    me = lax.axis_index("wide")
    roles = line_roles()
    end, mid, mate, other = roles
    greet(*roles, wide)
    dp = LineSum(roles, seq, dp_own, dp_near, dp_half, dp_far, dp_total, dp_sends, dp_arrivals)
    dn = LineSum(roles, tb, dn_own, dn_near, dn_half, dn_far, dn_total, dn_sends, dn_arrivals)

    dp_own[...] = dproj_ref[...].astype(BF16)

    @pl.when(end)
    def _():
        dp.up(0).start()

    block = width // wide

    def deliver(which, k):
        to = lax.rem(me + k, wide)
        return pltpu.make_async_remote_copy(
            prod_s.at[which, pl.ds(pl.multiple_of(to * block, block), block)], inbox_s.at[which, k],
            prod_sends.at[which, k], prod_arrivals.at[which, k], device_id={"wide": to}, device_id_type=MESH)

    def product(which, left, right):
        def tile(j, _):
            cols = pl.ds(pl.multiple_of(j * LANES, LANES), LANES)
            got = lax.dot_general(left[:, cols], right[...], (((0,), (0,)), ((), ())), preferred_element_type=F32)
            prod_s[which, cols, :] = got.astype(BF16)
            return 0

        lax.fori_loop(0, width // LANES, tile, 0)
        for k in range(1, wide):
            deliver(which, k).start()

    product(0, dmixed_ref, gated_ref)

    @pl.when(mid)
    def _():
        dp.first(0)

    product(1, normed_ref, dz_ref)

    @pl.when(mid)
    def _():
        dp.second(0)

    @pl.when(end)
    def _():
        dp.down(0).wait_recv()

    pack_s[...] = jnp.zeros_like(pack_s)
    dconv_s[pl.ds(seq, 8), :] = jnp.zeros((8, ch), F32)
    first_s[...] = jnp.zeros_like(first_s)

    def rows_of(b):
        return pl.ds(pl.multiple_of(b * tb, tb), tb)

    def block_step(k, _):
        b = nb - 1 - k
        rows = rows_of(b)
        base = pl.multiple_of(b * tb, tb)
        d_inner = dinner_ref[rows, :] + lax.dot_general(
            dp_total[rows, :], wproj_ref[...], (((1,), (1,)), ((), ())), preferred_element_type=F32)
        csum = csum_ref[rows, :]
        logistic = 1.0 / (1.0 + jnp.exp(-csum))
        d_conv = d_inner * (logistic * (1.0 + csum * (1.0 - logistic)))
        dconv_s[rows, :] = d_conv
        prior = x_ref[pl.ds(pl.multiple_of(jnp.maximum(base - 8, 0), 8), 8), :]
        history = jnp.concatenate([prior, x_ref[rows, :]], axis=0)
        ahead = jnp.concatenate([d_conv, dconv_s[pl.ds(pl.multiple_of(base + tb, 8), 8), :]], axis=0)
        same = masks_ref[pl.ds(base, tb + 8), :]
        d_x = cw_ref[taps - 1:taps, :] * d_conv
        pack_s[0:1, :] += jnp.sum(d_conv, axis=0, keepdims=True)
        pack_s[8 - 1:8, :] += jnp.sum(d_conv * history[8:, :], axis=0, keepdims=True)
        for s in range(1, taps):
            linked = same[:, s:s + 1] * ahead
            d_x = d_x + cw_ref[taps - 1 - s:taps - s, :] * linked[s:s + tb, :]
            pack_s[7 - s:8 - s, :] += jnp.sum(linked[:tb, :] * history[8 - s:8 - s + tb, :], axis=0, keepdims=True)
        d_x = d_x.astype(BF16)
        dx_s[rows, :] = d_x
        both = lax.dot_general(d_x, wx_ref[...], (((1,), (1,)), ((), ())), preferred_element_type=F32)
        both = both + lax.dot_general(dz_ref[rows, :], wz_ref[...], (((1,), (1,)), ((), ())), preferred_element_type=F32)
        dn_own[rows, :] = both.astype(BF16)

        @pl.when(end)
        def _():
            dn.up(b).start()

        @pl.when(mid & (k > 0))
        def _():
            dn.first(b + 1)

        @pl.when(mid & (k > 1))
        def _():
            dn.second(b + 2)
        return 0

    lax.fori_loop(0, nb, block_step, 0)

    @pl.when(mid)
    def _():
        dn.second(1)
        dn.first(0)

    product(2, normed_ref, dx_s)
    state = lax.dot_general(dp_total[...], inner_ref[...], (((0,), (0,)), ((), ())), preferred_element_type=F32)

    @pl.when(mid)
    def _():
        dn.second(0)

    def finish(k, _):
        b = nb - 1 - k
        rows = rows_of(b)

        @pl.when(end)
        def _():
            dn.down(b).wait_recv()

        d_normed = dn_total[rows, :].astype(F32)
        scale = scale_ref[rows, :]
        unit = tokens_ref[rows, :] * scale
        through = d_normed * gain_ref[...]
        first_s[...] += jnp.sum(d_normed * unit, axis=0, keepdims=True)
        mean = jnp.mean(through * unit, axis=1, keepdims=True)
        tgrad_ref[rows, :] = dhidden_ref[rows, :] + scale * (through - unit * mean)
        return 0

    lax.fori_loop(0, nb, finish, 0)

    rank, states, experts = 48, grates_ref.shape[0], grouter_ref.shape[0]
    rank = gstep_ref.shape[0]
    pack_s[1:2, :] = gsbias_ref[...]
    pack_s[2:3, :] = gskip_ref[...]
    at = 8
    for ref in (grates_ref, gstep_ref):
        pack_s[at:at + ref.shape[0], :] = ref[...]
        at += ref.shape[0]
    held = rank + 2 * states
    pack_s[at:at + held, :] = state[:held, :]
    at += held
    halves = width // ch
    for h in range(halves):
        cols = slice(h * ch, (h + 1) * ch)
        pack_s[at + h:at + h + 1, :] = first_s[:, cols]
        pack_s[at + halves + h:at + halves + h + 1, :] = gsecond_ref[:, cols]
        pack_s[at + 8 + h * experts:at + 8 + (h + 1) * experts, :] = grouter_ref[:, cols]

    share = pack_s.shape[0] // wide

    def chunk(ref, i):
        return ref.at[pl.ds(pl.multiple_of(i * share, share), share)]

    def scatter(k):
        to = lax.rem(me + k, wide)
        return pltpu.make_async_remote_copy(chunk(pack_s, to), pack_in.at[k], pack_sends.at[0, k], pack_arrivals.at[0, k],
                                            device_id={"wide": to}, device_id_type=MESH)

    def spread_out(k):
        to = lax.rem(me + k, wide)
        return pltpu.make_async_remote_copy(chunk(small_ref, me), chunk(small_ref, me), pack_sends.at[1, k], pack_arrivals.at[1, k],
                                            device_id={"wide": to}, device_id_type=MESH)

    for k in range(1, wide):
        scatter(k).start()

    for which, ref in enumerate((go_ref, gz_ref, gx_ref)):
        total = prod_s[which, pl.ds(pl.multiple_of(me * block, block), block), :].astype(F32)
        for k in range(1, wide):
            deliver(which, k).wait_recv()
            total = total + inbox_s[which, k].astype(F32)
        ref[...] = total

    total = chunk(pack_s, me)[...]
    for k in range(1, wide):
        scatter(k).wait_recv()
        total = total + pack_in[k]
    chunk(small_ref, me)[...] = total
    for k in range(1, wide):
        spread_out(k).start()
    dp.sent(1)
    dn.sent(nb)
    for k in range(1, wide):
        for which in range(3):
            deliver(which, k).wait_send()
        scatter(k).wait_send()
    for k in range(1, wide):
        spread_out(k).wait_recv()
    for k in range(1, wide):
        spread_out(k).wait_send()


def pack_rows(rank, states, experts, width, ch, wide):
    rows = 8 + states + rank + (rank + 2 * states) + 8 + (width // ch) * experts
    return -(-rows // (8 * wide)) * (8 * wide)


def tail(wide, taps, *operands):
    (dproj, dinner, inner, x, csum, masks, wproj, cw, normed, dz, dmixed, gated, wx, wz, tokens, scale, gain, dhidden,
     gstep, gsbias, grates, gskip, gsecond, grouter) = operands
    seq, ch = dinner.shape
    width = tokens.shape[1]
    nb = seq // LANES
    packed = pack_rows(gstep.shape[0], grates.shape[0], grouter.shape[0], width, ch, wide)
    vm = pl.BlockSpec(memory_space=pltpu.VMEM)
    shape = jax.ShapeDtypeStruct
    dma = pltpu.SemaphoreType.DMA
    return pl.pallas_call(
        functools.partial(tail_kernel, wide, taps),
        in_specs=[vm] * len(operands),
        out_specs=[vm] * 5,
        out_shape=[shape((seq, width), F32)] + [shape((width // wide, ch), F32)] * 3 + [shape((packed, ch), F32)],
        scratch_shapes=[
            *line_scratch(seq, LANES, 1), *line_scratch(seq, width, nb),
            pltpu.VMEM((3, width, ch), BF16), pltpu.VMEM((3, wide, width // wide, ch), BF16), dma((3, wide)), dma((3, wide)),
            pltpu.VMEM((packed, ch), F32), pltpu.VMEM((wide, packed // wide, ch), F32), dma((2, wide)), dma((2, wide)),
            pltpu.VMEM((seq + 8, ch), F32), pltpu.VMEM((seq, ch), BF16), pltpu.VMEM((1, width), F32)],
        compiler_params=pltpu.CompilerParams(collective_id=1, has_side_effects=True, vmem_limit_bytes=56 << 20),
        name="mixer_tail",
    )(*operands)


def unpack_kernel(rank, states, small_ref, first_ref, cw_ref, cb_ref, state_ref, step_ref, sb_ref, rates_ref, skip_ref, second_ref, router_ref):
    ch = small_ref.shape[1]
    width, experts = router_ref.shape
    cb_ref[...] = small_ref[0:1, :]
    sb_ref[...] = small_ref[1:2, :]
    skip_ref[...] = small_ref[2:3, :]
    cw_ref[...] = small_ref[4:8, :]
    at = 8
    rates_ref[...] = small_ref[at:at + states, :]
    at += states
    step_ref[...] = small_ref[at:at + rank, :]
    at += rank
    held = rank + 2 * states
    state_ref[...] = small_ref[at:at + held, :].T
    at += held
    for h in range(width // ch):
        cols = slice(h * ch, (h + 1) * ch)
        first_ref[:, cols] = small_ref[at + h:at + h + 1, :]
        second_ref[:, cols] = small_ref[at + width // ch + h:at + width // ch + h + 1, :]
        router_ref[cols, :] = small_ref[at + 8 + h * experts:at + 8 + (h + 1) * experts, :].T


def unpack(small, rank, states, experts, width):
    ch = small.shape[1]
    shape = lambda *s: jax.ShapeDtypeStruct(s, F32)
    return pl.pallas_call(
        functools.partial(unpack_kernel, rank, states),
        out_shape=[shape(1, width), shape(4, ch), shape(1, ch), shape(ch, rank + 2 * states), shape(rank, ch), shape(1, ch), shape(states, ch),
                   shape(1, ch), shape(1, width), shape(width, experts)],
        name="unpack",
    )(small)


def gelu_pair(v):
    root = 0.7978845608028654
    square = v * v
    t = jnp.tanh(root * v * (1.0 + 0.044715 * square))
    half = 0.5 * (1.0 + t)
    slope = half + (0.5 * root) * v * (1.0 - t * t) * (1.0 + (3.0 * 0.044715) * square)
    return v * half, slope


def experts_kernel(wide, tokens_ref, mixed_ref, ograd_ref, srow_ref, scol_ref, routes_ref, gain_ref, router_ref, up_ref, ub_ref, down_ref, db_ref,
                   gup_ref, gub_ref, gdown_ref, gdb_ref, back_ref, out_ref,
                   pay_s, send_s, inbox_s, act_s, dpre_s, b_own, b_near, b_far, o_own, o_near, o_far, ret_b, ret_o,
                   pay_sends, pay_arrivals, b_sends, b_arrivals, o_sends, o_arrivals, ret_sends, ret_arrivals):
    seq, width = tokens_ref.shape
    hid = up_ref.shape[1]
    cap = inbox_s.shape[0] // wide
    tb = LANES
    me = lax.axis_index("wide")
    roles = line_roles()
    end, mid, mate, other = roles
    greet(*roles, wide)
    back = LineSum(roles, cap, b_own, b_near, b_own, b_far, b_far, b_sends, b_arrivals)
    out = LineSum(roles, cap, o_own, o_near, o_own, o_far, o_far, o_sends, o_arrivals)

    def rows_of(b, size):
        return pl.ds(pl.multiple_of(b * size, size), size)

    lane = lax.broadcasted_iota(jnp.int32, (tb, LANES), 1)

    def prepare(b, _):
        rows = rows_of(b, tb)
        hidden = tokens_ref[rows, :] + mixed_ref[rows, :].astype(F32)
        scale = lax.rsqrt(jnp.mean(hidden * hidden, axis=1, keepdims=True) + EPS)
        expert_in = (hidden * scale * gain_ref[...]).astype(BF16)
        logits = jnp.dot(expert_in, router_ref[...], preferred_element_type=F32)
        logit = jnp.sum(jnp.where(lane == routes_ref[rows, :], logits, 0.0), axis=1, keepdims=True)
        gate = 1.0 / (1.0 + jnp.exp(-logit))
        pay_s[rows, :width] = expert_in
        pay_s[rows, width:] = (gate * ograd_ref[rows, :]).astype(BF16)
        return 0

    lax.fori_loop(0, seq // tb, prepare, 0)

    def payload(expert):
        ids = lax.broadcasted_iota(jnp.int32, (cap, seq), 0) + expert * cap
        chosen = jnp.where(ids == srow_ref[...], 1.0, 0.0).astype(BF16)
        return jnp.dot(chosen, pay_s[...], preferred_element_type=F32).astype(BF16)

    def dispatch(k):
        return pltpu.make_async_remote_copy(
            send_s.at[rows_of(k, cap)], inbox_s.at[rows_of(k, cap)], pay_sends.at[k], pay_arrivals.at[k],
            device_id={"wide": lax.rem(me + k, wide)}, device_id_type=MESH)

    def send(k, _):
        send_s[rows_of(k, cap), :] = payload(lax.rem(me + k, wide))
        dispatch(k).start()
        return 0

    lax.fori_loop(1, wide, send, 0)
    inbox_s[0:cap, :] = payload(me)

    def give_back(c, which, total, ret):
        return pltpu.make_async_remote_copy(
            total.at[rows_of(c, cap)], ret.at[rows_of(me, cap)], ret_sends.at[which, c], ret_arrivals.at[which, c],
            device_id={"wide": lax.rem(me + wide - c, wide)}, device_id_type=MESH)

    def return_chunk(c, which):
        total, ret = ((b_far, ret_b), (o_far, ret_o))[which]

        @pl.when(c == 0)
        def _():
            ret[rows_of(me, cap), :] = total[0:cap, :]

        @pl.when(c != 0)
        def _():
            give_back(c, which, total, ret).start()

    def back_second(c):
        back.second(c)
        return_chunk(c, 0)

    def out_second(c):
        out.across(c).wait_recv()
        part = rows_of(c, cap)
        o_far[part, :] = (o_own[part, :].astype(F32) + o_far[part, :].astype(F32) + db_ref[...]).astype(BF16)
        out.down(c).start()
        return_chunk(c, 1)

    gub_ref[...] = jnp.zeros_like(gub_ref)
    gdb_ref[...] = jnp.zeros_like(gdb_ref)
    turned = (((1,), (1,)), ((), ()))

    def compute(k, _):
        @pl.when(k > 0)
        def _():
            dispatch(k).wait_recv()

        part = rows_of(k, cap)
        rows_in = inbox_s[part, :width]
        rows_grad = inbox_s[part, width:]
        pre = jnp.dot(rows_in, up_ref[...], preferred_element_type=F32) + ub_ref[...]
        act, slope = gelu_pair(pre)
        act = act.astype(BF16)
        act_s[part, :] = act
        d_pre = (lax.dot_general(rows_grad, down_ref[...], turned, preferred_element_type=F32) * slope).astype(BF16)
        dpre_s[part, :] = d_pre
        b_own[part, :] = lax.dot_general(d_pre, up_ref[...], turned, preferred_element_type=F32).astype(BF16)

        @pl.when(end)
        def _():
            back.up(k).start()

        o_own[part, :] = jnp.dot(act, down_ref[...], preferred_element_type=F32).astype(BF16)
        gub_ref[...] += jnp.sum(d_pre.astype(F32), axis=0, keepdims=True)
        gdb_ref[...] += jnp.sum(rows_grad.astype(F32), axis=0, keepdims=True)

        @pl.when(mid & (k > 0))
        def _():
            back.first(k - 1)

        @pl.when(mid & (k > 1))
        def _():
            back_second(k - 2)
        return 0

    lax.fori_loop(0, wide, compute, 0)

    @pl.when(mid)
    def _():
        back.first(wide - 1)
        back_second(wide - 2)
        back_second(wide - 1)

    @pl.when(end)
    def _():
        for k in range(wide):
            out.up(k).start()

    tiles = hid // LANES
    across_rows = (((0,), (0,)), ((), ()))

    def tile(j, _):
        @pl.when(j < tiles)
        def _():
            cols = rows_of(j, LANES)
            gdown_ref[cols, :] = lax.dot_general(act_s[:, cols], inbox_s[:, width:], across_rows, preferred_element_type=F32)

        @pl.when(j >= tiles)
        def _():
            cols = rows_of(j - tiles, LANES)
            gup_ref[cols, :] = lax.dot_general(inbox_s[:, cols], dpre_s[...], across_rows, preferred_element_type=F32)

        @pl.when(end & (j < wide))
        def _():
            back.down(j).wait_recv()
            return_chunk(j, 0)

        @pl.when(mid & (j < wide))
        def _():
            out.first(j)

        @pl.when(mid & (j > 0) & (j <= wide))
        def _():
            out_second(j - 1)
        return 0

    lax.fori_loop(0, 2 * tiles, tile, 0)

    def combine(which, ref):
        ret = (ret_b, ret_o)[which]
        for c in range(1, wide):
            give_back(c, which, (b_far, o_far)[which], ret).wait_recv()

        def block(b, _):
            rows = rows_of(b, tb)
            ids = lax.broadcasted_iota(jnp.int32, (tb, wide * cap), 1)
            chosen = jnp.where(ids == scol_ref[rows, :], 1.0, 0.0).astype(BF16)
            ref[rows, :] = jnp.dot(chosen, ret[...], preferred_element_type=F32).astype(BF16)
            return 0

        lax.fori_loop(0, seq // tb, block, 0)

    combine(0, back_ref)

    @pl.when(end)
    def _():
        for k in range(wide):
            out.down(k).wait_recv()
            return_chunk(jnp.int32(k), 1)

    combine(1, out_ref)
    back.sent(wide)
    out.sent(wide)
    for k in range(1, wide):
        dispatch(k).wait_send()
        give_back(k, 0, b_far, ret_b).wait_send()
        give_back(k, 1, o_far, ret_o).wait_send()


def experts_block(wide, cap, *operands):
    tokens, mixed, ograd, srow, scol, routes, gain, router, up, ub, down, db = operands
    seq, width = tokens.shape
    hid = up.shape[1]
    vm = pl.BlockSpec(memory_space=pltpu.VMEM)
    shape = jax.ShapeDtypeStruct
    dma = pltpu.SemaphoreType.DMA
    slots = wide * cap
    return pl.pallas_call(
        functools.partial(experts_kernel, wide),
        in_specs=[vm] * len(operands),
        out_specs=[vm] * 6,
        out_shape=[shape((width, hid), F32), shape((1, hid), F32), shape((hid, width), F32), shape((1, width), F32),
                   shape((seq, width), BF16), shape((seq, width), BF16)],
        scratch_shapes=[
            pltpu.VMEM((seq, 2 * width), BF16), pltpu.VMEM((slots, 2 * width), BF16), pltpu.VMEM((slots, 2 * width), BF16),
            pltpu.VMEM((slots, hid), BF16), pltpu.VMEM((slots, hid), BF16),
            *[pltpu.VMEM((slots, width), BF16)] * 8,
            dma((wide,)), dma((wide,)), dma((3, wide)), dma((3, wide)), dma((3, wide)), dma((3, wide)), dma((2, wide)), dma((2, wide))],
        compiler_params=pltpu.CompilerParams(collective_id=2, has_side_effects=True, vmem_limit_bytes=60 << 20),
        name="experts",
    )(*operands)


def plain_device(
    tokens,
    segment_ids,
    routes,
    out_grad,
    mixer_gain,
    in_proj_x,
    in_proj_z,
    conv_weight,
    conv_bias,
    state_proj,
    step_proj,
    step_bias,
    log_rates,
    skip_gain,
    out_proj,
    expert_gain,
    router_weight,
    expert_up,
    up_bias,
    expert_down,
    down_bias,
):
    seq_len, model_width = tokens.shape
    conv_taps = conv_weight.shape[0]
    step_rank = step_proj.shape[0]
    experts = router_weight.shape[1]
    capacity = 5 * seq_len // (4 * experts)
    doc_ids = segment_ids[0]
    conv_masks = [same_document(doc_ids, offset)[:, None] for offset in range(conv_taps)]
    first_scale = lax.rsqrt(jnp.mean(tokens * tokens, axis=1, keepdims=True) + EPS)
    first_unit = tokens * first_scale
    normed = (first_unit * mixer_gain).astype(jnp.bfloat16)
    gathered_x, gathered_z, gathered_out = (
        lax.all_gather(in_proj_x, "wide", axis=0, tiled=True),
        lax.all_gather(in_proj_z, "wide", axis=0, tiled=True),
        lax.all_gather(out_proj, "wide", axis=0, tiled=True),
    )
    x_branch = multiply(normed, gathered_x)
    z_branch = multiply(normed, gathered_z)
    conv_sum = conv_bias + jnp.zeros_like(x_branch)
    for offset in range(conv_taps):
        conv_sum = conv_sum + conv_weight[conv_taps - 1 - offset] * conv_masks[
            offset
        ] * shifted_down(x_branch, offset)
    inner_act = jax.nn.silu(conv_sum).astype(jnp.bfloat16)
    wide_proj = jnp.pad(state_proj, ((0, 0), (0, LANES - state_proj.shape[1])))
    projected = lax.psum(multiply(inner_act, wide_proj), "tp")
    tall_proj = jnp.pad(step_proj, ((0, LANES - step_rank), (0, 0)))
    carry_mask = same_document(doc_ids, 1)[:, None]
    scan_out, step_size, states, starts = scan_fwd(
        projected, inner_act, carry_mask, tall_proj, step_bias[None], log_rates, skip_gain[None], step_rank
    )
    z_gate = jax.nn.silu(z_branch)
    gated = (scan_out * z_gate).astype(jnp.bfloat16)
    mixed = lax.psum(contract_cols(gated, gathered_out).astype(jnp.bfloat16), "tp").astype(
        jnp.float32
    )
    hidden = tokens + mixed
    second_scale = lax.rsqrt(jnp.mean(hidden * hidden, axis=1, keepdims=True) + EPS)
    second_unit = hidden * second_scale
    expert_in = (second_unit * expert_gain).astype(jnp.bfloat16)
    route_ids = routes[:, 0]
    chosen_int = (routes == jnp.arange(experts, dtype=jnp.int32)[None, :]).astype(jnp.int32)
    chosen = chosen_int.astype(jnp.float32)
    logits = multiply(expert_in, router_weight)
    gate = jax.nn.sigmoid(jnp.sum(logits * chosen, axis=1))
    rank_of = jnp.arange(seq_len, dtype=jnp.int32)
    earlier = (rank_of[:, None] > rank_of[None, :]).astype(jnp.bfloat16)
    position = jnp.sum(multiply(earlier, chosen.astype(jnp.bfloat16)) * chosen, axis=1).astype(jnp.int32)
    kept = position < capacity
    slots = jnp.where(kept, route_ids * capacity + position, experts * capacity)
    scaled_grad = (gate[:, None] * out_grad).astype(jnp.bfloat16)
    sent_width = expert_in.shape[1]
    send_in = (
        jnp.zeros((experts * capacity + 1, sent_width), jnp.bfloat16).at[slots].set(expert_in)[:-1]
    )
    send_grad = (
        jnp.zeros((experts * capacity + 1, sent_width), jnp.bfloat16)
        .at[slots]
        .set(scaled_grad)[:-1]
    )
    recv_in, recv_grad = (
        lax.all_to_all(
            send_in.reshape(experts, capacity, sent_width),
            "wide",
            split_axis=0,
            concat_axis=0,
            tiled=True,
        ),
        lax.all_to_all(
            send_grad.reshape(experts, capacity, sent_width),
            "wide",
            split_axis=0,
            concat_axis=0,
            tiled=True,
        ),
    )
    rows_in = recv_in.reshape(-1, model_width)
    rows_grad = recv_grad.reshape(-1, model_width)
    pre_act = multiply(rows_in, expert_up[0]) + up_bias[0]
    hidden_act = jax.nn.gelu(pre_act).astype(jnp.bfloat16)
    partial_out = multiply(hidden_act, expert_down[0])
    up_grad = contract_cols(rows_grad, expert_down[0])
    d_pre = jax.vjp(jax.nn.gelu, pre_act)[1](up_grad)[0].astype(jnp.bfloat16)
    partial_back = contract_cols(d_pre, expert_up[0])
    grad_down = contract_rows(hidden_act, rows_grad)
    grad_dbias = jnp.sum(rows_grad.astype(jnp.float32), axis=0)
    grad_up = contract_rows(rows_in, d_pre)
    grad_ubias = jnp.sum(d_pre.astype(jnp.float32), axis=0)
    out_sum, back_sum = (
        lax.psum(partial_out.astype(jnp.bfloat16), "tp").astype(jnp.float32),
        lax.psum(partial_back.astype(jnp.bfloat16), "tp").astype(jnp.float32),
    )
    bias_part = down_bias[0]
    outgoing = (out_sum + bias_part).astype(jnp.bfloat16).reshape(experts, capacity, -1)
    back_rows = back_sum.astype(jnp.bfloat16).reshape(experts, capacity, -1)
    incoming, arriving = (
        lax.all_to_all(outgoing, "wide", split_axis=0, concat_axis=0, tiled=True),
        lax.all_to_all(back_rows, "wide", split_axis=0, concat_axis=0, tiled=True),
    )
    safe_slots = jnp.minimum(slots, experts * capacity - 1)
    returned = jnp.where(
        kept[:, None], incoming.reshape(-1, model_width)[safe_slots].astype(jnp.float32), 0.0
    )
    result = hidden + gate[:, None] * returned
    d_gate = jnp.sum(out_grad * returned, axis=1)
    d_logit = (d_gate * gate * (1.0 - gate))[:, None] * chosen
    grad_router = jnp.dot(expert_in.astype(jnp.float32).T, d_logit, precision=HIGH)
    d_norm_two = jnp.dot(d_logit, router_weight.astype(jnp.float32).T, precision=HIGH)
    d_norm_two = d_norm_two + jnp.where(
        kept[:, None], arriving.reshape(-1, model_width)[safe_slots].astype(jnp.float32), 0.0
    )
    grad_second_gain = jnp.sum(d_norm_two * second_unit, axis=0)
    d_hidden = out_grad + rms_back(d_norm_two * expert_gain, second_unit, second_scale)
    d_mixed = d_hidden.astype(jnp.bfloat16)
    d_gated = multiply(d_mixed, gathered_out)
    grad_out = contract_rows(d_mixed, gated)
    d_scan = d_gated * z_gate
    d_z = (d_gated * scan_out * silu_slope(z_branch)).astype(jnp.bfloat16)
    d_step_pre, d_inner, d_proj, grad_step, grad_sbias, grad_rates, grad_skip = scan_bwd(
        projected, inner_act, carry_mask, step_size, states, starts, d_scan, tall_proj, log_rates, skip_gain[None], step_rank
    )
    grad_step, grad_sbias, grad_skip = grad_step[:step_rank], grad_sbias[0], grad_skip[0]
    d_projected = lax.psum(d_proj.astype(jnp.bfloat16), "tp")
    grad_state = contract_rows(inner_act, d_projected)[:, : state_proj.shape[1]]
    d_inner = d_inner + contract_cols(d_projected, wide_proj)
    d_conv = d_inner * silu_slope(conv_sum)
    grad_cbias = jnp.sum(d_conv, axis=0)
    conv_rows = []
    d_input = jnp.zeros_like(d_conv)
    for offset in range(conv_taps):
        conv_rows.append(
            jnp.sum(d_conv * conv_masks[offset] * shifted_down(x_branch, offset), axis=0)
        )
        d_input = d_input + conv_weight[conv_taps - 1 - offset] * shifted_up(
            conv_masks[offset] * d_conv, offset
        )
    grad_conv = jnp.stack(conv_rows[::-1])
    d_x_branch = d_input.astype(jnp.bfloat16)
    grad_in_x = contract_rows(normed, d_x_branch)
    grad_in_z = contract_rows(normed, d_z)
    d_normed = lax.psum(
        (contract_cols(d_x_branch, gathered_x) + contract_cols(d_z, gathered_z)).astype(
            jnp.bfloat16
        ),
        "tp",
    ).astype(jnp.float32)
    grad_first_gain = jnp.sum(d_normed * first_unit, axis=0)
    tokens_grad = d_hidden + rms_back(d_normed * mixer_gain, first_unit, first_scale)
    grad_in_x, grad_in_z, grad_out = (
        summed_on_arrival(grad_in_x.astype(jnp.bfloat16), "wide", 0),
        summed_on_arrival(grad_in_z.astype(jnp.bfloat16), "wide", 0),
        summed_on_arrival(grad_out.astype(jnp.bfloat16), "wide", 0),
    )
    (
        grad_first_gain,
        grad_conv,
        grad_cbias,
        grad_state,
        grad_step,
        grad_sbias,
        grad_rates,
        grad_skip,
        grad_second_gain,
        grad_router,
    ) = lax.psum(
        (
            grad_first_gain,
            grad_conv,
            grad_cbias,
            grad_state,
            grad_step,
            grad_sbias,
            grad_rates,
            grad_skip,
            grad_second_gain,
            grad_router,
        ),
        "wide",
    )
    return (
        result,
        tokens_grad,
        grad_first_gain,
        grad_in_x,
        grad_in_z,
        grad_conv,
        grad_cbias,
        grad_state,
        grad_step,
        grad_sbias,
        grad_rates,
        grad_skip,
        grad_out,
        grad_second_gain,
        grad_router,
        grad_up[None],
        grad_ubias[None],
        grad_down[None],
        grad_dbias[None],
    )


def fast_device(
    tokens,
    segment_ids,
    routes,
    out_grad,
    mixer_gain,
    in_proj_x,
    in_proj_z,
    conv_weight,
    conv_bias,
    state_proj,
    step_proj,
    step_bias,
    log_rates,
    skip_gain,
    out_proj,
    expert_gain,
    router_weight,
    expert_up,
    up_bias,
    expert_down,
    down_bias,
):
    seq_len, model_width = tokens.shape
    conv_taps = conv_weight.shape[0]
    step_rank = step_proj.shape[0]
    experts = router_weight.shape[1]
    capacity = 5 * seq_len // (4 * experts)
    doc_ids = segment_ids[0]
    conv_masks = [same_document(doc_ids, offset)[:, None] for offset in range(conv_taps)]
    first_scale = lax.rsqrt(jnp.mean(tokens * tokens, axis=1, keepdims=True) + EPS)
    first_unit = tokens * first_scale
    normed = (first_unit * mixer_gain).astype(jnp.bfloat16)
    gathered_x, gathered_z, gathered_out = (
        lax.all_gather(in_proj_x, "wide", axis=0, tiled=True),
        lax.all_gather(in_proj_z, "wide", axis=0, tiled=True),
        lax.all_gather(out_proj, "wide", axis=0, tiled=True),
    )
    x_branch = multiply(normed, gathered_x)
    z_branch = multiply(normed, gathered_z)
    conv_sum = conv_bias + jnp.zeros_like(x_branch)
    for offset in range(conv_taps):
        conv_sum = conv_sum + conv_weight[conv_taps - 1 - offset] * conv_masks[
            offset
        ] * shifted_down(x_branch, offset)
    inner_act = jax.nn.silu(conv_sum).astype(jnp.bfloat16)
    wide_proj = jnp.pad(state_proj, ((0, 0), (0, LANES - state_proj.shape[1])))
    projected = lax.psum(multiply(inner_act, wide_proj), "tp")
    tall_proj = jnp.pad(step_proj, ((0, LANES - step_rank), (0, 0)))
    carry_mask = same_document(doc_ids, 1)[:, None]
    scan_out, step_size, states, starts = scan_fwd(
        projected, inner_act, carry_mask, tall_proj, step_bias[None], log_rates, skip_gain[None], step_rank
    )
    z_gate = jax.nn.silu(z_branch)
    gated = (scan_out * z_gate).astype(jnp.bfloat16)
    mixed = lax.psum(contract_cols(gated, gathered_out).astype(jnp.bfloat16), "tp")
    wide = lax.axis_size("wide")
    chosen = (routes == jnp.arange(experts, dtype=jnp.int32)[None, :]).astype(jnp.float32)
    rank_of = jnp.arange(seq_len, dtype=jnp.int32)
    earlier = (rank_of[:, None] > rank_of[None, :]).astype(jnp.bfloat16)
    position = jnp.sum(multiply(earlier, chosen.astype(jnp.bfloat16)) * chosen, axis=1).astype(jnp.int32)
    slots = jnp.where(position < capacity, routes[:, 0] * capacity + position, experts * capacity)
    wide_router = jnp.pad(router_weight, ((0, 0), (0, LANES - experts)))
    grad_up, grad_ubias, grad_down, grad_dbias, arriving, returned = experts_block(
        wide, capacity, tokens, mixed, out_grad, slots[None], slots[:, None], routes, expert_gain[None], wide_router,
        expert_up[0], up_bias, expert_down[0], down_bias,
    )
    hidden = tokens + mixed.astype(jnp.float32)
    second_scale = lax.rsqrt(jnp.mean(hidden * hidden, axis=1, keepdims=True) + EPS)
    second_unit = hidden * second_scale
    expert_in = (second_unit * expert_gain).astype(jnp.bfloat16)
    logits = multiply(expert_in, router_weight)
    gate = jax.nn.sigmoid(jnp.sum(logits * chosen, axis=1))
    returned = returned.astype(jnp.float32)
    result = hidden + gate[:, None] * returned
    d_gate = jnp.sum(out_grad * returned, axis=1)
    d_logit = (d_gate * gate * (1.0 - gate))[:, None] * chosen
    grad_router = jnp.dot(d_logit.T, expert_in.astype(jnp.float32), precision=HIGH)
    d_norm_two = jnp.dot(d_logit, router_weight.astype(jnp.float32).T, precision=HIGH)
    d_norm_two = d_norm_two + arriving.astype(jnp.float32)
    grad_second_gain = jnp.sum(d_norm_two * second_unit, axis=0, keepdims=True)
    d_hidden = out_grad + rms_back(d_norm_two * expert_gain, second_unit, second_scale)
    d_mixed = d_hidden.astype(jnp.bfloat16)
    d_gated = multiply(d_mixed, gathered_out)
    d_scan = d_gated * z_gate
    d_z = (d_gated * scan_out * silu_slope(z_branch)).astype(jnp.bfloat16)
    d_step_pre, d_inner, d_proj, grad_step, grad_sbias, grad_rates, grad_skip = scan_bwd(
        projected, inner_act, carry_mask, step_size, states, starts, d_scan, tall_proj, log_rates, skip_gain[None], step_rank
    )
    grad_step = grad_step[:step_rank]
    masks = jnp.pad(jnp.concatenate(conv_masks, axis=1), ((0, 8), (0, 8 - conv_taps)))
    tokens_grad, grad_in_x, grad_in_z, grad_out, small = tail(
        wide, conv_taps, d_proj, d_inner, inner_act, x_branch, conv_sum, masks, wide_proj, conv_weight, normed, d_z,
        d_mixed, gated, gathered_x, gathered_z, tokens, first_scale, mixer_gain[None], d_hidden,
        grad_step, grad_sbias, grad_rates, grad_skip, grad_second_gain, grad_router,
    )
    (
        grad_first_gain, grad_conv, grad_cbias, grad_state, grad_step, grad_sbias, grad_rates, grad_skip, grad_second_gain, grad_router,
    ) = unpack(small, step_rank, log_rates.shape[0], experts, model_width)
    return (
        result,
        tokens_grad,
        grad_first_gain[0],
        grad_in_x,
        grad_in_z,
        grad_conv,
        grad_cbias[0],
        grad_state,
        grad_step,
        grad_sbias[0],
        grad_rates,
        grad_skip[0],
        grad_out,
        grad_second_gain[0],
        grad_router,
        grad_up[None],
        grad_ubias,
        grad_down[None],
        grad_dbias,
    )


def solution(mesh):
    in_specs = (
        P("wide", None),
        P("wide", None),
        P("wide", None),
        P("wide", None),
        P(),
        P("wide", "tp"),
        P("wide", "tp"),
        P(None, "tp"),
        P("tp"),
        P("tp", None),
        P(None, "tp"),
        P("tp"),
        P(None, "tp"),
        P("tp"),
        P("wide", "tp"),
        P(),
        P(),
        P("wide", None, "tp"),
        P("wide", "tp"),
        P("wide", "tp", None),
        P("wide", None),
    )
    out_specs = (
        P("wide", None),
        P("wide", None),
        P(),
        P("wide", "tp"),
        P("wide", "tp"),
        P(None, "tp"),
        P("tp"),
        P("tp", None),
        P(None, "tp"),
        P("tp"),
        P(None, "tp"),
        P("tp"),
        P("wide", "tp"),
        P(),
        P(),
        P("wide", None, "tp"),
        P("wide", "tp"),
        P("wide", "tp", None),
        P("wide", None),
    )
    wide, line = mesh.shape["wide"], mesh.shape["tp"]
    per_device = fast_device if line == 4 and wide == 8 else plain_device
    return jax.shard_map(
        per_device, mesh=mesh, in_specs=in_specs, out_specs=out_specs, check_vma=False
    )
```

```python
import functools

import jax
import jax.numpy as jnp
from jax import lax
from jax.experimental import pallas as pl
from jax.experimental.pallas import tpu as pltpu
from jax.sharding import PartitionSpec as P

EPS = 1e-05
HIGH = lax.Precision.HIGHEST


def in_blocks(shard, dim, size):
    before, after = (shard.shape[:dim], shard.shape[dim + 1 :])
    return jnp.moveaxis(shard.reshape(*before, size, -1, *after), dim, 0)


def summed_on_arrival(shard, axis, dim):
    size = lax.axis_size(axis)
    parts = lax.all_to_all(in_blocks(shard, dim, size), axis, 0, 0, tiled=True)
    return jnp.sum(parts.astype(jnp.float32), axis=0)


def multiply(left, right):
    return jnp.dot(left, right, preferred_element_type=jnp.float32)


def contract_rows(left, right):
    return lax.dot_general(
        left, right, (((0,), (0,)), ((), ())), preferred_element_type=jnp.float32
    )


def contract_cols(left, right):
    return lax.dot_general(
        left, right, (((1,), (1,)), ((), ())), preferred_element_type=jnp.float32
    )


def shifted_down(values, steps):
    if steps == 0:
        return values
    filler = jnp.zeros((steps,) + values.shape[1:], values.dtype)
    return jnp.concatenate([filler, values[:-steps]], axis=0)


def shifted_up(values, steps):
    if steps == 0:
        return values
    filler = jnp.zeros((steps,) + values.shape[1:], values.dtype)
    return jnp.concatenate([values[steps:], filler], axis=0)


def same_document(doc_ids, steps):
    if steps == 0:
        return jnp.ones(doc_ids.shape, jnp.float32)
    filler = jnp.full((steps,), -1, jnp.int32)
    earlier = jnp.concatenate([filler, doc_ids[:-steps]])
    return (earlier == doc_ids).astype(jnp.float32)


def silu_slope(values):
    logistic = jax.nn.sigmoid(values)
    return logistic * (1.0 + values * (1.0 - logistic))


def rms_back(grad_unit, unit, scale):
    return scale * (grad_unit - unit * jnp.mean(grad_unit * unit, axis=1, keepdims=True))


LOG2E = 1.4426950408889634
LANES = 128
F32, BF16 = jnp.float32, jnp.bfloat16
MESH = pl.DeviceIdType.MESH


def fold_rows(parts, masks):
    m4, m2, m1 = masks

    def join(a, b, m, shift):
        return jnp.where(m, a, b) + pltpu.roll(jnp.where(m, b, a), shift, 0)

    c = [join(parts[i], parts[i + 4], m4[i], 4) for i in range(4)]
    d = [join(c[i], c[i + 2], m2[i], 6) for i in range(2)]
    return join(d[0], d[1], m1, 7)


def fold_masks(width):
    sub = lax.broadcasted_iota(jnp.int32, (8, width), 0)
    m4 = [((sub - i) & 7) < 4 for i in range(4)]
    m2 = [((sub - i) & 2) == 0 for i in range(2)]
    m1 = (sub & 1) == 0
    return m4, m2, m1


def softplus(v):
    return jnp.maximum(v, 0.0) + jnp.log1p(jnp.exp(-jnp.abs(v)))


def row(ref, c, t, ns):
    one = ref[c, pl.ds(t, 8, stride=0), :]
    return jnp.concatenate([one] * (ns // 8), axis=0)


def spread(ref, value):
    for c in range(ref.shape[0]):
        ref[c] = value[:, c * LANES:(c + 1) * LANES]


def own_column(ns, rank):
    lane = lax.broadcasted_iota(jnp.int32, (ns, LANES), 1)
    n = lax.broadcasted_iota(jnp.int32, (ns, LANES), 0)
    return (lane == rank + n) | (lane == rank + ns + n)


def coefficient_rows(ns, rank, proj_ref, rows_s, wide_s):
    tb = proj_ref.shape[0]
    own = own_column(ns, rank)
    lane = lax.broadcasted_iota(jnp.int32, (LANES, 2 * LANES), 1)
    k = lax.broadcasted_iota(jnp.int32, (LANES, 2 * LANES), 0)
    pick = ((lane < LANES) & (k >= rank) & (k < rank + ns)) | ((lane >= LANES) & (k >= rank + ns) & (k < rank + 2 * ns))
    pick = jnp.where(pick, 1.0, 0.0).astype(BF16)

    def body(g, _):
        for j in range(16):
            t = g * 16 + j
            one = proj_ref[pl.ds(t, 8, stride=0), :]
            both = jnp.where(own, jnp.concatenate([one] * (ns // 8), axis=0), 0.0)
            rows_s[pl.ds(pl.multiple_of(j * ns, ns), ns), :] = both.astype(BF16)
        wide_s[pl.ds(pl.multiple_of(g * 16 * ns, 16 * ns), 16 * ns), :] = jnp.dot(rows_s[...], pick, preferred_element_type=F32)
        return 0

    lax.fori_loop(0, tb // 16, body, 0)


def scan_fwd_kernel(ns, rank, proj_ref, inner_ref, keep_ref, sproj_ref, sbias_ref, lr_ref, skip_ref,
                    scan_ref, step_ref, states_ref, starts_ref, state_s, stepd_s, drive_s, r2_s, rows_s, wide_s):
    tb, ch = inner_ref.shape
    groups = ch // LANES
    i = pl.program_id(0)

    @pl.when(i == 0)
    def _():
        state_s[...] = jnp.zeros_like(state_s)
        spread(r2_s, jnp.exp(lr_ref[...]) * (-LOG2E))

    step_in = proj_ref[...].astype(BF16)
    pre = jnp.dot(step_in, sproj_ref[...], preferred_element_type=F32) + sbias_ref[...]
    step = softplus(pre)
    step_ref[...] = step
    spread(stepd_s, jnp.where(keep_ref[...] > 0.0, step, 1e30))
    inner = inner_ref[...].astype(F32)
    spread(drive_s, step * inner)
    coefficient_rows(ns, rank, proj_ref, rows_s, wide_s)
    starts_ref[0] = state_s[...]
    masks = fold_masks(LANES)

    def body(g, state):
        state = list(state)
        parts = [[] for _ in range(groups)]
        for j in range(8):
            t = g * 8 + j
            here = pl.ds(pl.multiple_of(t * ns, ns), ns)
            in_b = wide_s[here, :LANES]
            out_b = wide_s[here, LANES:]
            for c in range(groups):
                cols = pl.ds(c * LANES, LANES)
                dec = jnp.exp2(row(stepd_s, c, t, ns) * r2_s[c])
                s = dec * state[c] + row(drive_s, c, t, ns) * in_b
                state[c] = s
                states_ref[here, cols] = s.astype(BF16)
                z = out_b * s
                parts[c].append(sum(z[8 * k:8 * k + 8] for k in range(ns // 8)))
        for c in range(groups):
            scan_ref[pl.ds(pl.multiple_of(g * 8, 8), 8), pl.ds(c * LANES, LANES)] = fold_rows(parts[c], masks)
        return tuple(state)

    start = tuple(state_s[:, c * LANES:(c + 1) * LANES] for c in range(groups))
    state = lax.fori_loop(0, tb // 8, body, start)
    for c in range(groups):
        state_s[:, c * LANES:(c + 1) * LANES] = state[c]
    scan_ref[...] += skip_ref[...] * inner


def scan_fwd(proj, inner, keep, sproj, sbias, log_rates, skip, rank):
    seq, ch = inner.shape
    ns = log_rates.shape[0]
    tb = LANES
    nb = seq // tb
    full = lambda a: pl.BlockSpec(a.shape, lambda i: (0,) * a.ndim)
    rows = pl.BlockSpec((tb, ch), lambda i: (i, 0))
    return pl.pallas_call(
        functools.partial(scan_fwd_kernel, ns, rank),
        grid=(nb,),
        in_specs=[pl.BlockSpec((tb, LANES), lambda i: (i, 0)), rows, pl.BlockSpec((tb, 1), lambda i: (i, 0)),
                  full(sproj), full(sbias), full(log_rates), full(skip)],
        out_specs=[rows, rows, pl.BlockSpec((tb * ns, ch), lambda i: (i, 0)), pl.BlockSpec((1, ns, ch), lambda i: (i, 0, 0))],
        out_shape=[jax.ShapeDtypeStruct((seq, ch), F32), jax.ShapeDtypeStruct((seq, ch), F32),
                   jax.ShapeDtypeStruct((seq * ns, ch), BF16), jax.ShapeDtypeStruct((nb, ns, ch), F32)],
        scratch_shapes=[pltpu.VMEM((ns, ch), F32)] + [pltpu.VMEM((ch // LANES, tb, LANES), F32)] * 2 + [pltpu.VMEM((ch // LANES, ns, LANES), F32),
                        pltpu.VMEM((16 * ns, LANES), BF16), pltpu.VMEM((tb * ns, 2 * LANES), F32)],
        compiler_params=pltpu.CompilerParams(vmem_limit_bytes=48 << 20),
        name="scan_fwd",
    )(proj, inner, keep, sproj, sbias, log_rates, skip)


def scan_bwd_kernel(ns, rank, proj_ref, inner_ref, keep_ref, step_ref, states_ref, starts_ref, dscan_ref, sproj_ref, lr_ref, skip_ref,
                    dpre_ref, dinner_ref, dproj_ref, gstep_ref, gsbias_ref, grates_ref, gskip_ref,
                    carry_s, stepd_s, drive_s, dscan_s, step_s, r2_s, coeff_s, exps_s, acc_s, rows_s, wide_s, sums_s):
    tb, ch = inner_ref.shape
    groups = ch // LANES
    i = pl.program_id(0)

    @pl.when(i == 0)
    def _():
        carry_s[...] = jnp.zeros_like(carry_s)
        acc_s[...] = jnp.zeros_like(acc_s)
        spread(r2_s, jnp.exp(lr_ref[...]) * (-LOG2E))
        gstep_ref[...] = jnp.zeros_like(gstep_ref)
        gsbias_ref[...] = jnp.zeros_like(gsbias_ref)
        gskip_ref[...] = jnp.zeros_like(gskip_ref)

    step = step_ref[...]
    inner = inner_ref[...].astype(F32)
    dscan = dscan_ref[...]
    spread(stepd_s, jnp.where(keep_ref[...] > 0.0, step, 1e30))
    spread(drive_s, step * inner)
    spread(dscan_s, dscan)
    spread(step_s, step)
    coefficient_rows(ns, rank, proj_ref, rows_s, wide_s)
    masks = fold_masks(LANES)
    steps = tb // 8

    def body(k, carry):
        later, acc = [list(v) for v in carry]
        g = steps - 1 - k
        cparts = [[None] * 8 for _ in range(groups)]
        eparts = [[None] * 8 for _ in range(groups)]
        last = pl.ds(pl.multiple_of((g * 8 + 7) * ns, ns), ns)
        now = [states_ref[last, pl.ds(c * LANES, LANES)].astype(F32) for c in range(groups)]
        for j in range(7, -1, -1):
            t = g * 8 + j
            here = pl.ds(pl.multiple_of(t * ns, ns), ns)
            prior = pl.ds(pl.multiple_of((t - 1 if j else jnp.maximum(t - 1, 0)) * ns, ns), ns)
            in_b = wide_s[here, :LANES]
            out_b = wide_s[here, LANES:]
            din = dout = None
            for c in range(groups):
                cols = pl.ds(c * LANES, LANES)
                before = states_ref[prior, cols].astype(F32)
                if j == 0:
                    before = jnp.where(jnp.full((ns, LANES), t, jnp.int32) == 0, starts_ref[0, :, cols], before)
                r2 = r2_s[c]
                dec = jnp.exp2(row(stepd_s, c, t, ns) * r2)
                ds = row(dscan_s, c, t, ns)
                d = later[c] + out_b * ds
                later[c] = dec * d
                dexp = later[c] * before
                e = dexp * r2
                cf = d * in_b
                cparts[c][j] = sum(cf[8 * q:8 * q + 8] for q in range(ns // 8))
                eparts[c][j] = sum(e[8 * q:8 * q + 8] for q in range(ns // 8))
                acc[c] = acc[c] + dexp * row(step_s, c, t, ns)
                a = d * row(drive_s, c, t, ns)
                b = now[c] * ds
                din = a if din is None else din + a
                dout = b if dout is None else dout + b
                now[c] = before
            sums_s[here, :LANES] = din.astype(BF16)
            sums_s[here, LANES:] = dout.astype(BF16)
        rows = pl.ds(pl.multiple_of(g * 8, 8), 8)
        for c in range(groups):
            cols = pl.ds(c * LANES, LANES)
            coeff_s[rows, cols] = fold_rows(cparts[c], masks)
            exps_s[rows, cols] = fold_rows(eparts[c], masks)
        return tuple(later), tuple(acc)

    pick = lambda ref: tuple(ref[:, c * LANES:(c + 1) * LANES] for c in range(groups))
    later, acc = lax.fori_loop(0, steps, body, (pick(carry_s), pick(acc_s)))
    for c in range(groups):
        carry_s[:, c * LANES:(c + 1) * LANES] = later[c]
        acc_s[:, c * LANES:(c + 1) * LANES] = acc[c]

    k = lax.broadcasted_iota(jnp.int32, (2 * LANES, LANES), 0)
    lane = lax.broadcasted_iota(jnp.int32, (2 * LANES, LANES), 1)
    into = ((k < LANES) & (lane >= rank) & (lane < rank + ns)) | ((k >= LANES) & (lane >= rank + ns) & (lane < rank + 2 * ns))
    into = jnp.where(into, 1.0, 0.0).astype(BF16)
    own = own_column(ns, rank)

    def gather(g, _):
        got = jnp.dot(sums_s[pl.ds(pl.multiple_of(g * 16 * ns, 16 * ns), 16 * ns), :], into, preferred_element_type=F32)
        for h in range(2):
            parts = []
            for j in range(8):
                one = jnp.where(own, got[(h * 8 + j) * ns:(h * 8 + j + 1) * ns], 0.0)
                parts.append(sum(one[8 * q:8 * q + 8] for q in range(ns // 8)))
            dproj_ref[pl.ds(pl.multiple_of(g * 16 + h * 8, 8), 8), :] = fold_rows(parts, masks)
        return 0

    lax.fori_loop(0, tb // 16, gather, 0)
    coeff = coeff_s[...]
    d_step = coeff * inner + exps_s[...] * (1.0 / LOG2E)
    d_pre = (d_step * (1.0 - jnp.exp(-step))).astype(BF16)
    dpre_ref[...] = d_pre
    dinner_ref[...] = dscan * skip_ref[...] + step * coeff
    step_in = proj_ref[...].astype(BF16)
    gstep_ref[...] += lax.dot_general(step_in, d_pre, (((0,), (0,)), ((), ())), preferred_element_type=F32)
    gsbias_ref[...] += jnp.sum(d_pre.astype(F32), axis=0, keepdims=True)
    gskip_ref[...] += jnp.sum(dscan * inner, axis=0, keepdims=True)
    dproj_ref[...] += lax.dot_general(d_pre, sproj_ref[...], (((1,), (1,)), ((), ())), preferred_element_type=F32)

    @pl.when(i == pl.num_programs(0) - 1)
    def _():
        grates_ref[...] = -jnp.exp(lr_ref[...]) * acc_s[...]


def scan_bwd(proj, inner, keep, step, states, starts, dscan, sproj, log_rates, skip, rank):
    seq, ch = inner.shape
    ns = log_rates.shape[0]
    tb = LANES
    nb = seq // tb
    full = lambda a: pl.BlockSpec(a.shape, lambda i: (0,) * a.ndim)
    rows = pl.BlockSpec((tb, ch), lambda i: (nb - 1 - i, 0))
    prow = pl.BlockSpec((tb, LANES), lambda i: (nb - 1 - i, 0))
    whole = lambda *s: pl.BlockSpec(s, lambda i: (0,) * len(s))
    shape = jax.ShapeDtypeStruct
    return pl.pallas_call(
        functools.partial(scan_bwd_kernel, ns, rank),
        grid=(nb,),
        in_specs=[prow, rows, pl.BlockSpec((tb, 1), lambda i: (nb - 1 - i, 0)), rows,
                  pl.BlockSpec((tb * ns, ch), lambda i: (nb - 1 - i, 0)), pl.BlockSpec((1, ns, ch), lambda i: (nb - 1 - i, 0, 0)),
                  rows, full(sproj), full(log_rates), full(skip)],
        out_specs=[rows, rows, prow, whole(LANES, ch), whole(1, ch), whole(ns, ch), whole(1, ch)],
        out_shape=[shape((seq, ch), BF16), shape((seq, ch), F32), shape((seq, LANES), F32), shape((LANES, ch), F32), shape((1, ch), F32),
                   shape((ns, ch), F32), shape((1, ch), F32)],
        scratch_shapes=[pltpu.VMEM((ns, ch), F32)] + [pltpu.VMEM((ch // LANES, tb, LANES), F32)] * 4 + [pltpu.VMEM((ch // LANES, ns, LANES), F32),
                        pltpu.VMEM((tb, ch), F32), pltpu.VMEM((tb, ch), F32), pltpu.VMEM((ns, ch), F32),
                        pltpu.VMEM((16 * ns, LANES), BF16), pltpu.VMEM((tb * ns, 2 * LANES), F32), pltpu.VMEM((tb * ns, 2 * LANES), BF16)],
        compiler_params=pltpu.CompilerParams(vmem_limit_bytes=48 << 20),
        name="scan_bwd",
    )(proj, inner, keep, step, states, starts, dscan, sproj, log_rates, skip)


def line_roles():
    me = lax.axis_index("tp")
    end = (me == 0) | (me == 3)
    mate = jnp.where(me < 2, 1 - me, 5 - me)
    return end, jnp.logical_not(end), mate, 3 - me


def greet(end, mid, mate, other, wide):
    barrier = pltpu.get_barrier_semaphore()
    me = lax.axis_index("wide")
    pl.semaphore_signal(barrier, inc=1, device_id={"tp": mate}, device_id_type=MESH)

    @pl.when(mid)
    def _():
        pl.semaphore_signal(barrier, inc=1, device_id={"tp": other}, device_id_type=MESH)

    for k in range(1, wide):
        pl.semaphore_signal(barrier, inc=1, device_id={"wide": lax.rem(me + k, wide)}, device_id_type=MESH)

    @pl.when(end)
    def _():
        pl.semaphore_wait(barrier, wide)

    @pl.when(mid)
    def _():
        pl.semaphore_wait(barrier, wide + 1)


class LineSum:
    def __init__(self, roles, rows, own, near, half, far, total, sends, arrivals):
        self.end, self.mid, self.mate, self.other = roles
        self.rows, self.own, self.near, self.half, self.far, self.total = rows, own, near, half, far, total
        self.sends, self.arrivals = sends, arrivals

    def part(self, ref, k):
        return ref.at[pl.ds(pl.multiple_of(k * self.rows, self.rows), self.rows)]

    def copy(self, source, target, hop, k, to):
        return pltpu.make_async_remote_copy(
            self.part(source, k), self.part(target, k), self.sends.at[hop, k], self.arrivals.at[hop, k],
            device_id={"tp": to}, device_id_type=MESH)

    def up(self, k):
        return self.copy(self.own, self.near, 0, k, self.mate)

    def across(self, k):
        return self.copy(self.half, self.far, 1, k, self.other)

    def down(self, k):
        return self.copy(self.total, self.total, 2, k, self.mate)

    def add(self, a, b, c, k):
        self.part(c, k)[...] = (self.part(a, k)[...].astype(F32) + self.part(b, k)[...].astype(F32)).astype(BF16)

    def first(self, k):
        self.up(k).wait_recv()
        self.add(self.own, self.near, self.half, k)
        self.across(k).start()

    def second(self, k):
        self.across(k).wait_recv()
        self.add(self.half, self.far, self.total, k)
        self.down(k).start()

    def sent(self, count):
        for k in range(count):
            @pl.when(self.end)
            def _():
                self.up(k).wait_send()

            @pl.when(self.mid)
            def _():
                self.across(k).wait_send()
                self.down(k).wait_send()


def line_scratch(rows, cols, blocks):
    return [pltpu.VMEM((rows, cols), BF16)] * 5 + [pltpu.SemaphoreType.DMA((3, blocks))] * 2


def tail_kernel(wide, taps, dproj_ref, dinner_ref, inner_ref, x_ref, csum_ref, masks_ref, wproj_ref, cw_ref, normed_ref, dz_ref,
                dmixed_ref, gated_ref, wx_ref, wz_ref, tokens_ref, scale_ref, gain_ref, dhidden_ref,
                gstep_ref, gsbias_ref, grates_ref, gskip_ref, gsecond_ref, grouter_ref,
                tgrad_ref, gx_ref, gz_ref, go_ref, small_ref,
                dp_own, dp_near, dp_half, dp_far, dp_total, dp_sends, dp_arrivals,
                dn_own, dn_near, dn_half, dn_far, dn_total, dn_sends, dn_arrivals,
                prod_s, inbox_s, prod_sends, prod_arrivals, pack_s, pack_in, pack_sends, pack_arrivals,
                dconv_s, dx_s, first_s):
    seq, ch = dinner_ref.shape
    width = tokens_ref.shape[1]
    tb = LANES
    nb = seq // tb
    me = lax.axis_index("wide")
    roles = line_roles()
    end, mid, mate, other = roles
    greet(*roles, wide)
    dp = LineSum(roles, seq, dp_own, dp_near, dp_half, dp_far, dp_total, dp_sends, dp_arrivals)
    dn = LineSum(roles, tb, dn_own, dn_near, dn_half, dn_far, dn_total, dn_sends, dn_arrivals)

    dp_own[...] = dproj_ref[...].astype(BF16)

    @pl.when(end)
    def _():
        dp.up(0).start()

    block = width // wide

    def deliver(which, k):
        to = lax.rem(me + k, wide)
        return pltpu.make_async_remote_copy(
            prod_s.at[which, pl.ds(pl.multiple_of(to * block, block), block)], inbox_s.at[which, k],
            prod_sends.at[which, k], prod_arrivals.at[which, k], device_id={"wide": to}, device_id_type=MESH)

    def product(which, left, right):
        def tile(j, _):
            cols = pl.ds(pl.multiple_of(j * LANES, LANES), LANES)
            got = lax.dot_general(left[:, cols], right[...], (((0,), (0,)), ((), ())), preferred_element_type=F32)
            prod_s[which, cols, :] = got.astype(BF16)
            return 0

        lax.fori_loop(0, width // LANES, tile, 0)
        for k in range(1, wide):
            deliver(which, k).start()

    product(0, dmixed_ref, gated_ref)

    @pl.when(mid)
    def _():
        dp.first(0)

    product(1, normed_ref, dz_ref)

    @pl.when(mid)
    def _():
        dp.second(0)

    @pl.when(end)
    def _():
        dp.down(0).wait_recv()

    pack_s[...] = jnp.zeros_like(pack_s)
    dconv_s[pl.ds(seq, 8), :] = jnp.zeros((8, ch), F32)
    first_s[...] = jnp.zeros_like(first_s)

    def rows_of(b):
        return pl.ds(pl.multiple_of(b * tb, tb), tb)

    def block_step(k, _):
        b = nb - 1 - k
        rows = rows_of(b)
        base = pl.multiple_of(b * tb, tb)
        d_inner = dinner_ref[rows, :] + lax.dot_general(
            dp_total[rows, :], wproj_ref[...], (((1,), (1,)), ((), ())), preferred_element_type=F32)
        csum = csum_ref[rows, :]
        logistic = 1.0 / (1.0 + jnp.exp(-csum))
        d_conv = d_inner * (logistic * (1.0 + csum * (1.0 - logistic)))
        dconv_s[rows, :] = d_conv
        prior = x_ref[pl.ds(pl.multiple_of(jnp.maximum(base - 8, 0), 8), 8), :]
        history = jnp.concatenate([prior, x_ref[rows, :]], axis=0)
        ahead = jnp.concatenate([d_conv, dconv_s[pl.ds(pl.multiple_of(base + tb, 8), 8), :]], axis=0)
        same = masks_ref[pl.ds(base, tb + 8), :]
        d_x = cw_ref[taps - 1:taps, :] * d_conv
        pack_s[0:1, :] += jnp.sum(d_conv, axis=0, keepdims=True)
        pack_s[8 - 1:8, :] += jnp.sum(d_conv * history[8:, :], axis=0, keepdims=True)
        for s in range(1, taps):
            linked = same[:, s:s + 1] * ahead
            d_x = d_x + cw_ref[taps - 1 - s:taps - s, :] * linked[s:s + tb, :]
            pack_s[7 - s:8 - s, :] += jnp.sum(linked[:tb, :] * history[8 - s:8 - s + tb, :], axis=0, keepdims=True)
        d_x = d_x.astype(BF16)
        dx_s[rows, :] = d_x
        both = lax.dot_general(d_x, wx_ref[...], (((1,), (1,)), ((), ())), preferred_element_type=F32)
        both = both + lax.dot_general(dz_ref[rows, :], wz_ref[...], (((1,), (1,)), ((), ())), preferred_element_type=F32)
        dn_own[rows, :] = both.astype(BF16)

        @pl.when(end)
        def _():
            dn.up(b).start()

        @pl.when(mid & (k > 0))
        def _():
            dn.first(b + 1)

        @pl.when(mid & (k > 1))
        def _():
            dn.second(b + 2)
        return 0

    lax.fori_loop(0, nb, block_step, 0)

    @pl.when(mid)
    def _():
        dn.second(1)
        dn.first(0)

    product(2, normed_ref, dx_s)
    state = lax.dot_general(dp_total[...], inner_ref[...], (((0,), (0,)), ((), ())), preferred_element_type=F32)

    @pl.when(mid)
    def _():
        dn.second(0)

    def finish(k, _):
        b = nb - 1 - k
        rows = rows_of(b)

        @pl.when(end)
        def _():
            dn.down(b).wait_recv()

        d_normed = dn_total[rows, :].astype(F32)
        scale = scale_ref[rows, :]
        unit = tokens_ref[rows, :] * scale
        through = d_normed * gain_ref[...]
        first_s[...] += jnp.sum(d_normed * unit, axis=0, keepdims=True)
        mean = jnp.mean(through * unit, axis=1, keepdims=True)
        tgrad_ref[rows, :] = dhidden_ref[rows, :] + scale * (through - unit * mean)
        return 0

    lax.fori_loop(0, nb, finish, 0)

    rank, states, experts = 48, grates_ref.shape[0], grouter_ref.shape[0]
    rank = gstep_ref.shape[0]
    pack_s[1:2, :] = gsbias_ref[...]
    pack_s[2:3, :] = gskip_ref[...]
    at = 8
    for ref in (grates_ref, gstep_ref):
        pack_s[at:at + ref.shape[0], :] = ref[...]
        at += ref.shape[0]
    held = rank + 2 * states
    pack_s[at:at + held, :] = state[:held, :]
    at += held
    halves = width // ch
    for h in range(halves):
        cols = slice(h * ch, (h + 1) * ch)
        pack_s[at + h:at + h + 1, :] = first_s[:, cols]
        pack_s[at + halves + h:at + halves + h + 1, :] = gsecond_ref[:, cols]
        pack_s[at + 8 + h * experts:at + 8 + (h + 1) * experts, :] = grouter_ref[:, cols]

    share = pack_s.shape[0] // wide

    def chunk(ref, i):
        return ref.at[pl.ds(pl.multiple_of(i * share, share), share)]

    def scatter(k):
        to = lax.rem(me + k, wide)
        return pltpu.make_async_remote_copy(chunk(pack_s, to), pack_in.at[k], pack_sends.at[0, k], pack_arrivals.at[0, k],
                                            device_id={"wide": to}, device_id_type=MESH)

    def spread_out(k):
        to = lax.rem(me + k, wide)
        return pltpu.make_async_remote_copy(chunk(small_ref, me), chunk(small_ref, me), pack_sends.at[1, k], pack_arrivals.at[1, k],
                                            device_id={"wide": to}, device_id_type=MESH)

    for k in range(1, wide):
        scatter(k).start()

    for which, ref in enumerate((go_ref, gz_ref, gx_ref)):
        total = prod_s[which, pl.ds(pl.multiple_of(me * block, block), block), :].astype(F32)
        for k in range(1, wide):
            deliver(which, k).wait_recv()
            total = total + inbox_s[which, k].astype(F32)
        ref[...] = total

    total = chunk(pack_s, me)[...]
    for k in range(1, wide):
        scatter(k).wait_recv()
        total = total + pack_in[k]
    chunk(small_ref, me)[...] = total
    for k in range(1, wide):
        spread_out(k).start()
    dp.sent(1)
    dn.sent(nb)
    for k in range(1, wide):
        for which in range(3):
            deliver(which, k).wait_send()
        scatter(k).wait_send()
    for k in range(1, wide):
        spread_out(k).wait_recv()
    for k in range(1, wide):
        spread_out(k).wait_send()


def pack_rows(rank, states, experts, width, ch, wide):
    rows = 8 + states + rank + (rank + 2 * states) + 8 + (width // ch) * experts
    return -(-rows // (8 * wide)) * (8 * wide)


def tail(wide, taps, *operands):
    (dproj, dinner, inner, x, csum, masks, wproj, cw, normed, dz, dmixed, gated, wx, wz, tokens, scale, gain, dhidden,
     gstep, gsbias, grates, gskip, gsecond, grouter) = operands
    seq, ch = dinner.shape
    width = tokens.shape[1]
    nb = seq // LANES
    packed = pack_rows(gstep.shape[0], grates.shape[0], grouter.shape[0], width, ch, wide)
    vm = pl.BlockSpec(memory_space=pltpu.VMEM)
    shape = jax.ShapeDtypeStruct
    dma = pltpu.SemaphoreType.DMA
    return pl.pallas_call(
        functools.partial(tail_kernel, wide, taps),
        in_specs=[vm] * len(operands),
        out_specs=[vm] * 5,
        out_shape=[shape((seq, width), F32)] + [shape((width // wide, ch), F32)] * 3 + [shape((packed, ch), F32)],
        scratch_shapes=[
            *line_scratch(seq, LANES, 1), *line_scratch(seq, width, nb),
            pltpu.VMEM((3, width, ch), BF16), pltpu.VMEM((3, wide, width // wide, ch), BF16), dma((3, wide)), dma((3, wide)),
            pltpu.VMEM((packed, ch), F32), pltpu.VMEM((wide, packed // wide, ch), F32), dma((2, wide)), dma((2, wide)),
            pltpu.VMEM((seq + 8, ch), F32), pltpu.VMEM((seq, ch), BF16), pltpu.VMEM((1, width), F32)],
        compiler_params=pltpu.CompilerParams(collective_id=1, has_side_effects=True, vmem_limit_bytes=56 << 20),
        name="mixer_tail",
    )(*operands)


def unpack_kernel(rank, states, small_ref, first_ref, cw_ref, cb_ref, state_ref, step_ref, sb_ref, rates_ref, skip_ref, second_ref, router_ref):
    ch = small_ref.shape[1]
    width, experts = router_ref.shape
    cb_ref[...] = small_ref[0:1, :]
    sb_ref[...] = small_ref[1:2, :]
    skip_ref[...] = small_ref[2:3, :]
    cw_ref[...] = small_ref[4:8, :]
    at = 8
    rates_ref[...] = small_ref[at:at + states, :]
    at += states
    step_ref[...] = small_ref[at:at + rank, :]
    at += rank
    held = rank + 2 * states
    state_ref[...] = small_ref[at:at + held, :].T
    at += held
    for h in range(width // ch):
        cols = slice(h * ch, (h + 1) * ch)
        first_ref[:, cols] = small_ref[at + h:at + h + 1, :]
        second_ref[:, cols] = small_ref[at + width // ch + h:at + width // ch + h + 1, :]
        router_ref[cols, :] = small_ref[at + 8 + h * experts:at + 8 + (h + 1) * experts, :].T


def unpack(small, rank, states, experts, width):
    ch = small.shape[1]
    shape = lambda *s: jax.ShapeDtypeStruct(s, F32)
    return pl.pallas_call(
        functools.partial(unpack_kernel, rank, states),
        out_shape=[shape(1, width), shape(4, ch), shape(1, ch), shape(ch, rank + 2 * states), shape(rank, ch), shape(1, ch), shape(states, ch),
                   shape(1, ch), shape(1, width), shape(width, experts)],
        name="unpack",
    )(small)


def gelu_pair(v):
    root = 0.7978845608028654
    square = v * v
    t = jnp.tanh(root * v * (1.0 + 0.044715 * square))
    half = 0.5 * (1.0 + t)
    slope = half + (0.5 * root) * v * (1.0 - t * t) * (1.0 + (3.0 * 0.044715) * square)
    return v * half, slope


def scan_mix_kernel(ns, rank, proj_ref, inner_ref, keep_ref, sproj_ref, sbias_ref, lr_ref, skip_ref, z_ref, wo_ref,
                    scan_ref, step_ref, states_ref, starts_ref, gated_ref, mixed_ref,
                    state_s, stepd_s, drive_s, r2_s, rows_s, wide_s, own_s, near_s, far_s, sends, arrivals):
    tb, ch = inner_ref.shape
    groups = ch // LANES
    i = pl.program_id(0)
    roles = line_roles()
    end, mid, mate, other = roles
    line = LineSum(roles, tb, own_s, near_s, own_s, far_s, far_s, sends, arrivals)
    steps = arrivals.shape[1]

    @pl.when(i == 0)
    def _():
        greet(*roles, 1)
        state_s[...] = jnp.zeros_like(state_s)
        spread(r2_s, jnp.exp(lr_ref[...]) * (-LOG2E))

    step_in = proj_ref[...].astype(BF16)
    pre = jnp.dot(step_in, sproj_ref[...], preferred_element_type=F32) + sbias_ref[...]
    step = softplus(pre)
    step_ref[...] = step
    spread(stepd_s, jnp.where(keep_ref[...] > 0.0, step, 1e30))
    inner = inner_ref[...].astype(F32)
    spread(drive_s, step * inner)
    coefficient_rows(ns, rank, proj_ref, rows_s, wide_s)
    starts_ref[0] = state_s[...]
    masks = fold_masks(LANES)

    def body(g, state):
        state = list(state)
        parts = [[] for _ in range(groups)]
        for j in range(8):
            t = g * 8 + j
            here = pl.ds(pl.multiple_of(t * ns, ns), ns)
            in_b = wide_s[here, :LANES]
            out_b = wide_s[here, LANES:]
            for c in range(groups):
                cols = pl.ds(c * LANES, LANES)
                dec = jnp.exp2(row(stepd_s, c, t, ns) * r2_s[c])
                s = dec * state[c] + row(drive_s, c, t, ns) * in_b
                state[c] = s
                states_ref[here, cols] = s.astype(BF16)
                z = out_b * s
                parts[c].append(sum(z[8 * k:8 * k + 8] for k in range(ns // 8)))
        for c in range(groups):
            scan_ref[pl.ds(pl.multiple_of(g * 8, 8), 8), pl.ds(c * LANES, LANES)] = fold_rows(parts[c], masks)
        return tuple(state)

    start = tuple(state_s[:, c * LANES:(c + 1) * LANES] for c in range(groups))
    state = lax.fori_loop(0, tb // 8, body, start)
    for c in range(groups):
        state_s[:, c * LANES:(c + 1) * LANES] = state[c]
    scan = scan_ref[...] + skip_ref[...] * inner
    scan_ref[...] = scan
    z = z_ref[...]
    gated = (scan * (z / (1.0 + jnp.exp(-z)))).astype(BF16)
    gated_ref[...] = gated
    here = pl.ds(pl.multiple_of(i * tb, tb), tb)
    own_s[here, :] = lax.dot_general(gated, wo_ref[...], (((1,), (1,)), ((), ())), preferred_element_type=F32).astype(BF16)

    @pl.when(end)
    def _():
        line.up(i).start()

    @pl.when(mid & (i > 0))
    def _():
        line.first(i - 1)

    @pl.when(mid & (i > 1))
    def _():
        line.second(i - 2)

    @pl.when(i == steps - 1)
    def _():
        @pl.when(mid)
        def _():
            line.first(steps - 1)
            line.second(steps - 2)
            line.second(steps - 1)

        @pl.when(end)
        def _():
            for k in range(steps):
                line.down(k).wait_recv()

        mixed_ref[...] = far_s[...]
        line.sent(steps)


def scan_mix(proj, inner, keep, sproj, sbias, log_rates, skip, z, wo, rank):
    seq, ch = inner.shape
    ns = log_rates.shape[0]
    tb = LANES
    nb = seq // tb
    width = wo.shape[0]
    full = lambda a: pl.BlockSpec(a.shape, lambda i: (0,) * a.ndim)
    rows = pl.BlockSpec((tb, ch), lambda i: (i, 0))
    return pl.pallas_call(
        functools.partial(scan_mix_kernel, ns, rank),
        grid=(nb,),
        in_specs=[pl.BlockSpec((tb, LANES), lambda i: (i, 0)), rows, pl.BlockSpec((tb, 1), lambda i: (i, 0)),
                  full(sproj), full(sbias), full(log_rates), full(skip), rows, full(wo)],
        out_specs=[rows, rows, pl.BlockSpec((tb * ns, ch), lambda i: (i, 0)), pl.BlockSpec((1, ns, ch), lambda i: (i, 0, 0)),
                   rows, pl.BlockSpec((seq, width), lambda i: (0, 0))],
        out_shape=[jax.ShapeDtypeStruct((seq, ch), F32), jax.ShapeDtypeStruct((seq, ch), F32),
                   jax.ShapeDtypeStruct((seq * ns, ch), BF16), jax.ShapeDtypeStruct((nb, ns, ch), F32),
                   jax.ShapeDtypeStruct((seq, ch), BF16), jax.ShapeDtypeStruct((seq, width), BF16)],
        scratch_shapes=[pltpu.VMEM((ns, ch), F32)] + [pltpu.VMEM((ch // LANES, tb, LANES), F32)] * 2 + [pltpu.VMEM((ch // LANES, ns, LANES), F32),
                        pltpu.VMEM((16 * ns, LANES), BF16), pltpu.VMEM((tb * ns, 2 * LANES), F32),
                        *[pltpu.VMEM((seq, width), BF16)] * 3, pltpu.SemaphoreType.DMA((3, nb)), pltpu.SemaphoreType.DMA((3, nb))],
        compiler_params=pltpu.CompilerParams(collective_id=4, has_side_effects=True, vmem_limit_bytes=48 << 20),
        name="scan_mix",
    )(proj, inner, keep, sproj, sbias, log_rates, skip, z, wo)


def experts_kernel(wide, tokens_ref, mixed_ref, ograd_ref, srow_ref, scol_ref, routes_ref, gain_ref, router_ref, up_ref, ub_ref, down_ref, db_ref,
                   gup_ref, gub_ref, gdown_ref, gdb_ref, back_ref, out_ref,
                   pay_s, send_s, inbox_s, act_s, dpre_s, b_own, b_near, b_far, o_own, o_near, o_far, ret_b, ret_o,
                   pay_sends, pay_arrivals, b_sends, b_arrivals, o_sends, o_arrivals, ret_sends, ret_arrivals):
    seq, width = tokens_ref.shape
    hid = up_ref.shape[1]
    cap = inbox_s.shape[0] // wide
    tb = LANES
    me = lax.axis_index("wide")
    roles = line_roles()
    end, mid, mate, other = roles
    greet(*roles, wide)
    back = LineSum(roles, cap, b_own, b_near, b_own, b_far, b_far, b_sends, b_arrivals)
    out = LineSum(roles, cap, o_own, o_near, o_own, o_far, o_far, o_sends, o_arrivals)

    def rows_of(b, size):
        return pl.ds(pl.multiple_of(b * size, size), size)

    lane = lax.broadcasted_iota(jnp.int32, (tb, LANES), 1)

    def prepare(b, _):
        rows = rows_of(b, tb)
        hidden = tokens_ref[rows, :] + mixed_ref[rows, :].astype(F32)
        scale = lax.rsqrt(jnp.mean(hidden * hidden, axis=1, keepdims=True) + EPS)
        expert_in = (hidden * scale * gain_ref[...]).astype(BF16)
        logits = jnp.dot(expert_in, router_ref[...], preferred_element_type=F32)
        logit = jnp.sum(jnp.where(lane == routes_ref[rows, :], logits, 0.0), axis=1, keepdims=True)
        gate = 1.0 / (1.0 + jnp.exp(-logit))
        pay_s[rows, :width] = expert_in
        pay_s[rows, width:] = (gate * ograd_ref[rows, :]).astype(BF16)
        return 0

    lax.fori_loop(0, seq // tb, prepare, 0)

    def payload(expert):
        ids = lax.broadcasted_iota(jnp.int32, (cap, seq), 0) + expert * cap
        chosen = jnp.where(ids == srow_ref[...], 1.0, 0.0).astype(BF16)
        return jnp.dot(chosen, pay_s[...], preferred_element_type=F32).astype(BF16)

    def dispatch(k):
        return pltpu.make_async_remote_copy(
            send_s.at[rows_of(k, cap)], inbox_s.at[rows_of(k, cap)], pay_sends.at[k], pay_arrivals.at[k],
            device_id={"wide": lax.rem(me + k, wide)}, device_id_type=MESH)

    def send(k, _):
        send_s[rows_of(k, cap), :] = payload(lax.rem(me + k, wide))
        dispatch(k).start()
        return 0

    lax.fori_loop(1, wide, send, 0)
    inbox_s[0:cap, :] = payload(me)

    def give_back(c, which, total, ret):
        return pltpu.make_async_remote_copy(
            total.at[rows_of(c, cap)], ret.at[rows_of(me, cap)], ret_sends.at[which, c], ret_arrivals.at[which, c],
            device_id={"wide": lax.rem(me + wide - c, wide)}, device_id_type=MESH)

    def return_chunk(c, which):
        total, ret = ((b_far, ret_b), (o_far, ret_o))[which]

        @pl.when(c == 0)
        def _():
            ret[rows_of(me, cap), :] = total[0:cap, :]

        @pl.when(c != 0)
        def _():
            give_back(c, which, total, ret).start()

    def back_second(c):
        back.second(c)
        return_chunk(c, 0)

    def out_second(c):
        out.across(c).wait_recv()
        part = rows_of(c, cap)
        o_far[part, :] = (o_own[part, :].astype(F32) + o_far[part, :].astype(F32) + db_ref[...]).astype(BF16)
        out.down(c).start()
        return_chunk(c, 1)

    gub_ref[...] = jnp.zeros_like(gub_ref)
    gdb_ref[...] = jnp.zeros_like(gdb_ref)
    turned = (((1,), (1,)), ((), ()))

    def compute(k, _):
        @pl.when(k > 0)
        def _():
            dispatch(k).wait_recv()

        part = rows_of(k, cap)
        rows_in = inbox_s[part, :width]
        rows_grad = inbox_s[part, width:]
        pre = jnp.dot(rows_in, up_ref[...], preferred_element_type=F32) + ub_ref[...]
        act, slope = gelu_pair(pre)
        act = act.astype(BF16)
        act_s[part, :] = act
        d_pre = (lax.dot_general(rows_grad, down_ref[...], turned, preferred_element_type=F32) * slope).astype(BF16)
        dpre_s[part, :] = d_pre
        b_own[part, :] = lax.dot_general(d_pre, up_ref[...], turned, preferred_element_type=F32).astype(BF16)

        @pl.when(end)
        def _():
            back.up(k).start()

        o_own[part, :] = jnp.dot(act, down_ref[...], preferred_element_type=F32).astype(BF16)
        gub_ref[...] += jnp.sum(d_pre.astype(F32), axis=0, keepdims=True)
        gdb_ref[...] += jnp.sum(rows_grad.astype(F32), axis=0, keepdims=True)

        @pl.when(mid & (k > 0))
        def _():
            back.first(k - 1)

        @pl.when(mid & (k > 1))
        def _():
            back_second(k - 2)
        return 0

    lax.fori_loop(0, wide, compute, 0)

    @pl.when(mid)
    def _():
        back.first(wide - 1)
        back_second(wide - 2)
        back_second(wide - 1)

    @pl.when(end)
    def _():
        for k in range(wide):
            out.up(k).start()

    tiles = hid // LANES
    across_rows = (((0,), (0,)), ((), ()))

    def tile(j, _):
        @pl.when(j < tiles)
        def _():
            cols = rows_of(j, LANES)
            gdown_ref[cols, :] = lax.dot_general(act_s[:, cols], inbox_s[:, width:], across_rows, preferred_element_type=F32)

        @pl.when(j >= tiles)
        def _():
            cols = rows_of(j - tiles, LANES)
            gup_ref[cols, :] = lax.dot_general(inbox_s[:, cols], dpre_s[...], across_rows, preferred_element_type=F32)

        @pl.when(end & (j < wide))
        def _():
            back.down(j).wait_recv()
            return_chunk(j, 0)

        @pl.when(mid & (j < wide))
        def _():
            out.first(j)

        @pl.when(mid & (j > 0) & (j <= wide))
        def _():
            out_second(j - 1)
        return 0

    lax.fori_loop(0, 2 * tiles, tile, 0)

    def combine(which, ref):
        ret = (ret_b, ret_o)[which]
        for c in range(1, wide):
            give_back(c, which, (b_far, o_far)[which], ret).wait_recv()

        def block(b, _):
            rows = rows_of(b, tb)
            ids = lax.broadcasted_iota(jnp.int32, (tb, wide * cap), 1)
            chosen = jnp.where(ids == scol_ref[rows, :], 1.0, 0.0).astype(BF16)
            ref[rows, :] = jnp.dot(chosen, ret[...], preferred_element_type=F32).astype(BF16)
            return 0

        lax.fori_loop(0, seq // tb, block, 0)

    combine(0, back_ref)

    @pl.when(end)
    def _():
        for k in range(wide):
            out.down(k).wait_recv()
            return_chunk(jnp.int32(k), 1)

    combine(1, out_ref)
    back.sent(wide)
    out.sent(wide)
    for k in range(1, wide):
        dispatch(k).wait_send()
        give_back(k, 0, b_far, ret_b).wait_send()
        give_back(k, 1, o_far, ret_o).wait_send()


def experts_block(wide, cap, *operands):
    tokens, mixed, ograd, srow, scol, routes, gain, router, up, ub, down, db = operands
    seq, width = tokens.shape
    hid = up.shape[1]
    vm = pl.BlockSpec(memory_space=pltpu.VMEM)
    shape = jax.ShapeDtypeStruct
    dma = pltpu.SemaphoreType.DMA
    slots = wide * cap
    return pl.pallas_call(
        functools.partial(experts_kernel, wide),
        in_specs=[vm] * len(operands),
        out_specs=[vm] * 6,
        out_shape=[shape((width, hid), F32), shape((1, hid), F32), shape((hid, width), F32), shape((1, width), F32),
                   shape((seq, width), BF16), shape((seq, width), BF16)],
        scratch_shapes=[
            pltpu.VMEM((seq, 2 * width), BF16), pltpu.VMEM((slots, 2 * width), BF16), pltpu.VMEM((slots, 2 * width), BF16),
            pltpu.VMEM((slots, hid), BF16), pltpu.VMEM((slots, hid), BF16),
            *[pltpu.VMEM((slots, width), BF16)] * 8,
            dma((wide,)), dma((wide,)), dma((3, wide)), dma((3, wide)), dma((3, wide)), dma((3, wide)), dma((2, wide)), dma((2, wide))],
        compiler_params=pltpu.CompilerParams(collective_id=2, has_side_effects=True, vmem_limit_bytes=60 << 20),
        name="experts",
    )(*operands)


def front_kernel(wide, taps, tokens_ref, gain_ref, inx_ref, inz_ref, outp_ref, cw_ref, cb_ref, wproj_ref, masks_ref,
                 scale_ref, normed_ref, x_ref, z_ref, csum_ref, inner_ref, proj_ref, wx_ref, wz_ref, wo_ref,
                 own_s, near_s, far_s, w_sends, w_arrivals, sends, arrivals):
    seq, width = tokens_ref.shape
    ch = x_ref.shape[1]
    block = inx_ref.shape[0]
    tb = LANES
    nb = seq // tb
    me = lax.axis_index("wide")
    roles = line_roles()
    end, mid, mate, other = roles
    greet(*roles, wide)
    line = LineSum(roles, 2 * tb, own_s, near_s, own_s, far_s, far_s, sends, arrivals)
    mine = pl.ds(pl.multiple_of(me * block, block), block)
    weights = ((inx_ref, wx_ref), (inz_ref, wz_ref), (outp_ref, wo_ref))

    def share(which, k):
        source, target = weights[which]
        return pltpu.make_async_remote_copy(source, target.at[mine], w_sends.at[which, k], w_arrivals.at[which, k],
                                            device_id={"wide": lax.rem(me + k, wide)}, device_id_type=MESH)

    for which in range(3):
        for k in range(1, wide):
            share(which, k).start()
    for source, target in weights:
        target[mine, :] = source[...]

    def rows_of(b):
        return pl.ds(pl.multiple_of(b * tb, tb), tb)

    def norm(b, _):
        rows = rows_of(b)
        tokens = tokens_ref[rows, :]
        scale = lax.rsqrt(jnp.mean(tokens * tokens, axis=1, keepdims=True) + EPS)
        scale_ref[rows, :] = scale
        normed_ref[rows, :] = (tokens * scale * gain_ref[...]).astype(BF16)
        return 0

    lax.fori_loop(0, nb, norm, 0)
    for k in range(1, wide):
        share(0, k).wait_recv()

    def step(b, _):
        rows = rows_of(b)
        base = pl.multiple_of(b * tb, tb)
        x = jnp.dot(normed_ref[rows, :], wx_ref[...], preferred_element_type=F32)
        x_ref[rows, :] = x
        prior = x_ref[pl.ds(pl.multiple_of(jnp.maximum(base - 8, 0), 8), 8), :]
        history = jnp.concatenate([prior, x], axis=0)
        same = masks_ref[rows, :]
        csum = cb_ref[...] + cw_ref[taps - 1:taps, :] * x
        for s in range(1, taps):
            csum = csum + cw_ref[taps - 1 - s:taps - s, :] * (same[:, s:s + 1] * history[8 - s:8 - s + tb, :])
        csum_ref[rows, :] = csum
        inner = (csum / (1.0 + jnp.exp(-csum))).astype(BF16)
        inner_ref[rows, :] = inner
        own_s[rows, :] = jnp.dot(inner, wproj_ref[...], preferred_element_type=F32).astype(BF16)

        @pl.when(end & (lax.rem(b, 2) == 1))
        def _():
            line.up(b // 2).start()
        return 0

    lax.fori_loop(0, nb, step, 0)
    steps = nb // 2

    @pl.when(mid)
    def _():
        line.first(0)
        for k in range(1, steps):
            line.first(k)
            line.second(k - 1)

    for k in range(1, wide):
        share(1, k).wait_recv()

    def gate(b, _):
        rows = rows_of(b)
        z_ref[rows, :] = jnp.dot(normed_ref[rows, :], wz_ref[...], preferred_element_type=F32)
        return 0

    lax.fori_loop(0, nb, gate, 0)

    @pl.when(mid)
    def _():
        line.second(steps - 1)

    @pl.when(end)
    def _():
        for k in range(steps):
            line.down(k).wait_recv()

    proj_ref[...] = far_s[...].astype(F32)
    line.sent(steps)
    for k in range(1, wide):
        share(2, k).wait_recv()
        for which in range(3):
            share(which, k).wait_send()


def front(wide, taps, *operands):
    tokens, gain, inx, inz, outp, cw, cb, wproj, masks = operands
    seq, width = tokens.shape
    ch = inx.shape[1]
    vm = pl.BlockSpec(memory_space=pltpu.VMEM)
    shape = jax.ShapeDtypeStruct
    dma = pltpu.SemaphoreType.DMA
    return pl.pallas_call(
        functools.partial(front_kernel, wide, taps),
        in_specs=[vm] * len(operands),
        out_specs=[vm] * 10,
        out_shape=[shape((seq, 1), F32), shape((seq, width), BF16), shape((seq, ch), F32), shape((seq, ch), F32), shape((seq, ch), F32),
                   shape((seq, ch), BF16), shape((seq, LANES), F32), *[shape((width, ch), BF16)] * 3],
        scratch_shapes=[*[pltpu.VMEM((seq, LANES), BF16)] * 3, dma((3, wide)), dma((3, wide)), dma((3, seq // LANES // 2)), dma((3, seq // LANES // 2))],
        compiler_params=pltpu.CompilerParams(collective_id=3, has_side_effects=True, vmem_limit_bytes=48 << 20),
        name="mixer_front",
    )(*operands)


def plain_device(
    tokens,
    segment_ids,
    routes,
    out_grad,
    mixer_gain,
    in_proj_x,
    in_proj_z,
    conv_weight,
    conv_bias,
    state_proj,
    step_proj,
    step_bias,
    log_rates,
    skip_gain,
    out_proj,
    expert_gain,
    router_weight,
    expert_up,
    up_bias,
    expert_down,
    down_bias,
):
    seq_len, model_width = tokens.shape
    conv_taps = conv_weight.shape[0]
    step_rank = step_proj.shape[0]
    experts = router_weight.shape[1]
    capacity = 5 * seq_len // (4 * experts)
    doc_ids = segment_ids[0]
    conv_masks = [same_document(doc_ids, offset)[:, None] for offset in range(conv_taps)]
    first_scale = lax.rsqrt(jnp.mean(tokens * tokens, axis=1, keepdims=True) + EPS)
    first_unit = tokens * first_scale
    normed = (first_unit * mixer_gain).astype(jnp.bfloat16)
    gathered_x, gathered_z, gathered_out = (
        lax.all_gather(in_proj_x, "wide", axis=0, tiled=True),
        lax.all_gather(in_proj_z, "wide", axis=0, tiled=True),
        lax.all_gather(out_proj, "wide", axis=0, tiled=True),
    )
    x_branch = multiply(normed, gathered_x)
    z_branch = multiply(normed, gathered_z)
    conv_sum = conv_bias + jnp.zeros_like(x_branch)
    for offset in range(conv_taps):
        conv_sum = conv_sum + conv_weight[conv_taps - 1 - offset] * conv_masks[
            offset
        ] * shifted_down(x_branch, offset)
    inner_act = jax.nn.silu(conv_sum).astype(jnp.bfloat16)
    wide_proj = jnp.pad(state_proj, ((0, 0), (0, LANES - state_proj.shape[1])))
    projected = lax.psum(multiply(inner_act, wide_proj), "tp")
    tall_proj = jnp.pad(step_proj, ((0, LANES - step_rank), (0, 0)))
    carry_mask = same_document(doc_ids, 1)[:, None]
    scan_out, step_size, states, starts = scan_fwd(
        projected, inner_act, carry_mask, tall_proj, step_bias[None], log_rates, skip_gain[None], step_rank
    )
    z_gate = jax.nn.silu(z_branch)
    gated = (scan_out * z_gate).astype(jnp.bfloat16)
    mixed = lax.psum(contract_cols(gated, gathered_out).astype(jnp.bfloat16), "tp").astype(
        jnp.float32
    )
    hidden = tokens + mixed
    second_scale = lax.rsqrt(jnp.mean(hidden * hidden, axis=1, keepdims=True) + EPS)
    second_unit = hidden * second_scale
    expert_in = (second_unit * expert_gain).astype(jnp.bfloat16)
    route_ids = routes[:, 0]
    chosen_int = (routes == jnp.arange(experts, dtype=jnp.int32)[None, :]).astype(jnp.int32)
    chosen = chosen_int.astype(jnp.float32)
    logits = multiply(expert_in, router_weight)
    gate = jax.nn.sigmoid(jnp.sum(logits * chosen, axis=1))
    rank_of = jnp.arange(seq_len, dtype=jnp.int32)
    earlier = (rank_of[:, None] > rank_of[None, :]).astype(jnp.bfloat16)
    position = jnp.sum(multiply(earlier, chosen.astype(jnp.bfloat16)) * chosen, axis=1).astype(jnp.int32)
    kept = position < capacity
    slots = jnp.where(kept, route_ids * capacity + position, experts * capacity)
    scaled_grad = (gate[:, None] * out_grad).astype(jnp.bfloat16)
    sent_width = expert_in.shape[1]
    send_in = (
        jnp.zeros((experts * capacity + 1, sent_width), jnp.bfloat16).at[slots].set(expert_in)[:-1]
    )
    send_grad = (
        jnp.zeros((experts * capacity + 1, sent_width), jnp.bfloat16)
        .at[slots]
        .set(scaled_grad)[:-1]
    )
    recv_in, recv_grad = (
        lax.all_to_all(
            send_in.reshape(experts, capacity, sent_width),
            "wide",
            split_axis=0,
            concat_axis=0,
            tiled=True,
        ),
        lax.all_to_all(
            send_grad.reshape(experts, capacity, sent_width),
            "wide",
            split_axis=0,
            concat_axis=0,
            tiled=True,
        ),
    )
    rows_in = recv_in.reshape(-1, model_width)
    rows_grad = recv_grad.reshape(-1, model_width)
    pre_act = multiply(rows_in, expert_up[0]) + up_bias[0]
    hidden_act = jax.nn.gelu(pre_act).astype(jnp.bfloat16)
    partial_out = multiply(hidden_act, expert_down[0])
    up_grad = contract_cols(rows_grad, expert_down[0])
    d_pre = jax.vjp(jax.nn.gelu, pre_act)[1](up_grad)[0].astype(jnp.bfloat16)
    partial_back = contract_cols(d_pre, expert_up[0])
    grad_down = contract_rows(hidden_act, rows_grad)
    grad_dbias = jnp.sum(rows_grad.astype(jnp.float32), axis=0)
    grad_up = contract_rows(rows_in, d_pre)
    grad_ubias = jnp.sum(d_pre.astype(jnp.float32), axis=0)
    out_sum, back_sum = (
        lax.psum(partial_out.astype(jnp.bfloat16), "tp").astype(jnp.float32),
        lax.psum(partial_back.astype(jnp.bfloat16), "tp").astype(jnp.float32),
    )
    bias_part = down_bias[0]
    outgoing = (out_sum + bias_part).astype(jnp.bfloat16).reshape(experts, capacity, -1)
    back_rows = back_sum.astype(jnp.bfloat16).reshape(experts, capacity, -1)
    incoming, arriving = (
        lax.all_to_all(outgoing, "wide", split_axis=0, concat_axis=0, tiled=True),
        lax.all_to_all(back_rows, "wide", split_axis=0, concat_axis=0, tiled=True),
    )
    safe_slots = jnp.minimum(slots, experts * capacity - 1)
    returned = jnp.where(
        kept[:, None], incoming.reshape(-1, model_width)[safe_slots].astype(jnp.float32), 0.0
    )
    result = hidden + gate[:, None] * returned
    d_gate = jnp.sum(out_grad * returned, axis=1)
    d_logit = (d_gate * gate * (1.0 - gate))[:, None] * chosen
    grad_router = jnp.dot(expert_in.astype(jnp.float32).T, d_logit, precision=HIGH)
    d_norm_two = jnp.dot(d_logit, router_weight.astype(jnp.float32).T, precision=HIGH)
    d_norm_two = d_norm_two + jnp.where(
        kept[:, None], arriving.reshape(-1, model_width)[safe_slots].astype(jnp.float32), 0.0
    )
    grad_second_gain = jnp.sum(d_norm_two * second_unit, axis=0)
    d_hidden = out_grad + rms_back(d_norm_two * expert_gain, second_unit, second_scale)
    d_mixed = d_hidden.astype(jnp.bfloat16)
    d_gated = multiply(d_mixed, gathered_out)
    grad_out = contract_rows(d_mixed, gated)
    d_scan = d_gated * z_gate
    d_z = (d_gated * scan_out * silu_slope(z_branch)).astype(jnp.bfloat16)
    d_step_pre, d_inner, d_proj, grad_step, grad_sbias, grad_rates, grad_skip = scan_bwd(
        projected, inner_act, carry_mask, step_size, states, starts, d_scan, tall_proj, log_rates, skip_gain[None], step_rank
    )
    grad_step, grad_sbias, grad_skip = grad_step[:step_rank], grad_sbias[0], grad_skip[0]
    d_projected = lax.psum(d_proj.astype(jnp.bfloat16), "tp")
    grad_state = contract_rows(inner_act, d_projected)[:, : state_proj.shape[1]]
    d_inner = d_inner + contract_cols(d_projected, wide_proj)
    d_conv = d_inner * silu_slope(conv_sum)
    grad_cbias = jnp.sum(d_conv, axis=0)
    conv_rows = []
    d_input = jnp.zeros_like(d_conv)
    for offset in range(conv_taps):
        conv_rows.append(
            jnp.sum(d_conv * conv_masks[offset] * shifted_down(x_branch, offset), axis=0)
        )
        d_input = d_input + conv_weight[conv_taps - 1 - offset] * shifted_up(
            conv_masks[offset] * d_conv, offset
        )
    grad_conv = jnp.stack(conv_rows[::-1])
    d_x_branch = d_input.astype(jnp.bfloat16)
    grad_in_x = contract_rows(normed, d_x_branch)
    grad_in_z = contract_rows(normed, d_z)
    d_normed = lax.psum(
        (contract_cols(d_x_branch, gathered_x) + contract_cols(d_z, gathered_z)).astype(
            jnp.bfloat16
        ),
        "tp",
    ).astype(jnp.float32)
    grad_first_gain = jnp.sum(d_normed * first_unit, axis=0)
    tokens_grad = d_hidden + rms_back(d_normed * mixer_gain, first_unit, first_scale)
    grad_in_x, grad_in_z, grad_out = (
        summed_on_arrival(grad_in_x.astype(jnp.bfloat16), "wide", 0),
        summed_on_arrival(grad_in_z.astype(jnp.bfloat16), "wide", 0),
        summed_on_arrival(grad_out.astype(jnp.bfloat16), "wide", 0),
    )
    (
        grad_first_gain,
        grad_conv,
        grad_cbias,
        grad_state,
        grad_step,
        grad_sbias,
        grad_rates,
        grad_skip,
        grad_second_gain,
        grad_router,
    ) = lax.psum(
        (
            grad_first_gain,
            grad_conv,
            grad_cbias,
            grad_state,
            grad_step,
            grad_sbias,
            grad_rates,
            grad_skip,
            grad_second_gain,
            grad_router,
        ),
        "wide",
    )
    return (
        result,
        tokens_grad,
        grad_first_gain,
        grad_in_x,
        grad_in_z,
        grad_conv,
        grad_cbias,
        grad_state,
        grad_step,
        grad_sbias,
        grad_rates,
        grad_skip,
        grad_out,
        grad_second_gain,
        grad_router,
        grad_up[None],
        grad_ubias[None],
        grad_down[None],
        grad_dbias[None],
    )


def fast_device(
    tokens,
    segment_ids,
    routes,
    out_grad,
    mixer_gain,
    in_proj_x,
    in_proj_z,
    conv_weight,
    conv_bias,
    state_proj,
    step_proj,
    step_bias,
    log_rates,
    skip_gain,
    out_proj,
    expert_gain,
    router_weight,
    expert_up,
    up_bias,
    expert_down,
    down_bias,
):
    seq_len, model_width = tokens.shape
    conv_taps = conv_weight.shape[0]
    step_rank = step_proj.shape[0]
    experts = router_weight.shape[1]
    capacity = 5 * seq_len // (4 * experts)
    doc_ids = segment_ids[0]
    conv_masks = [same_document(doc_ids, offset)[:, None] for offset in range(conv_taps)]
    masks = jnp.pad(jnp.concatenate(conv_masks, axis=1), ((0, 8), (0, 8 - conv_taps)))
    wide_proj = jnp.pad(state_proj, ((0, 0), (0, LANES - state_proj.shape[1])))
    tall_proj = jnp.pad(step_proj, ((0, LANES - step_rank), (0, 0)))
    wide = lax.axis_size("wide")
    first_scale, normed, x_branch, z_branch, conv_sum, inner_act, projected, gathered_x, gathered_z, gathered_out = front(
        wide, conv_taps, tokens, mixer_gain[None], in_proj_x, in_proj_z, out_proj, conv_weight, conv_bias[None], wide_proj, masks
    )
    carry_mask = same_document(doc_ids, 1)[:, None]
    scan_out, step_size, states, starts, gated, mixed = scan_mix(
        projected, inner_act, carry_mask, tall_proj, step_bias[None], log_rates, skip_gain[None], z_branch, gathered_out, step_rank
    )
    z_gate = jax.nn.silu(z_branch)
    chosen = (routes == jnp.arange(experts, dtype=jnp.int32)[None, :]).astype(jnp.float32)
    rank_of = jnp.arange(seq_len, dtype=jnp.int32)
    earlier = (rank_of[:, None] > rank_of[None, :]).astype(jnp.bfloat16)
    position = jnp.sum(multiply(earlier, chosen.astype(jnp.bfloat16)) * chosen, axis=1).astype(jnp.int32)
    slots = jnp.where(position < capacity, routes[:, 0] * capacity + position, experts * capacity)
    wide_router = jnp.pad(router_weight, ((0, 0), (0, LANES - experts)))
    grad_up, grad_ubias, grad_down, grad_dbias, arriving, returned = experts_block(
        wide, capacity, tokens, mixed, out_grad, slots[None], slots[:, None], routes, expert_gain[None], wide_router,
        expert_up[0], up_bias, expert_down[0], down_bias,
    )
    hidden = tokens + mixed.astype(jnp.float32)
    second_scale = lax.rsqrt(jnp.mean(hidden * hidden, axis=1, keepdims=True) + EPS)
    second_unit = hidden * second_scale
    expert_in = (second_unit * expert_gain).astype(jnp.bfloat16)
    logits = multiply(expert_in, router_weight)
    gate = jax.nn.sigmoid(jnp.sum(logits * chosen, axis=1))
    returned = returned.astype(jnp.float32)
    result = hidden + gate[:, None] * returned
    d_gate = jnp.sum(out_grad * returned, axis=1)
    d_logit = (d_gate * gate * (1.0 - gate))[:, None] * chosen
    grad_router = jnp.dot(d_logit.T, expert_in.astype(jnp.float32), precision=HIGH)
    d_norm_two = jnp.dot(d_logit, router_weight.astype(jnp.float32).T, precision=HIGH)
    d_norm_two = d_norm_two + arriving.astype(jnp.float32)
    grad_second_gain = jnp.sum(d_norm_two * second_unit, axis=0, keepdims=True)
    d_hidden = out_grad + rms_back(d_norm_two * expert_gain, second_unit, second_scale)
    d_mixed = d_hidden.astype(jnp.bfloat16)
    d_gated = multiply(d_mixed, gathered_out)
    d_scan = d_gated * z_gate
    d_z = (d_gated * scan_out * silu_slope(z_branch)).astype(jnp.bfloat16)
    d_step_pre, d_inner, d_proj, grad_step, grad_sbias, grad_rates, grad_skip = scan_bwd(
        projected, inner_act, carry_mask, step_size, states, starts, d_scan, tall_proj, log_rates, skip_gain[None], step_rank
    )
    grad_step = grad_step[:step_rank]
    tokens_grad, grad_in_x, grad_in_z, grad_out, small = tail(
        wide, conv_taps, d_proj, d_inner, inner_act, x_branch, conv_sum, masks, wide_proj, conv_weight, normed, d_z,
        d_mixed, gated, gathered_x, gathered_z, tokens, first_scale, mixer_gain[None], d_hidden,
        grad_step, grad_sbias, grad_rates, grad_skip, grad_second_gain, grad_router,
    )
    (
        grad_first_gain, grad_conv, grad_cbias, grad_state, grad_step, grad_sbias, grad_rates, grad_skip, grad_second_gain, grad_router,
    ) = unpack(small, step_rank, log_rates.shape[0], experts, model_width)
    return (
        result,
        tokens_grad,
        grad_first_gain[0],
        grad_in_x,
        grad_in_z,
        grad_conv,
        grad_cbias[0],
        grad_state,
        grad_step,
        grad_sbias[0],
        grad_rates,
        grad_skip[0],
        grad_out,
        grad_second_gain[0],
        grad_router,
        grad_up[None],
        grad_ubias,
        grad_down[None],
        grad_dbias,
    )


def solution(mesh):
    in_specs = (
        P("wide", None),
        P("wide", None),
        P("wide", None),
        P("wide", None),
        P(),
        P("wide", "tp"),
        P("wide", "tp"),
        P(None, "tp"),
        P("tp"),
        P("tp", None),
        P(None, "tp"),
        P("tp"),
        P(None, "tp"),
        P("tp"),
        P("wide", "tp"),
        P(),
        P(),
        P("wide", None, "tp"),
        P("wide", "tp"),
        P("wide", "tp", None),
        P("wide", None),
    )
    out_specs = (
        P("wide", None),
        P("wide", None),
        P(),
        P("wide", "tp"),
        P("wide", "tp"),
        P(None, "tp"),
        P("tp"),
        P("tp", None),
        P(None, "tp"),
        P("tp"),
        P(None, "tp"),
        P("tp"),
        P("wide", "tp"),
        P(),
        P(),
        P("wide", None, "tp"),
        P("wide", "tp"),
        P("wide", "tp", None),
        P("wide", None),
    )
    wide, line = mesh.shape["wide"], mesh.shape["tp"]
    per_device = fast_device if line == 4 and wide == 8 else plain_device
    return jax.shard_map(
        per_device, mesh=mesh, in_specs=in_specs, out_specs=out_specs, check_vma=False
    )
```

```python
import functools

import jax
import jax.numpy as jnp
from jax import lax
from jax.experimental import pallas as pl
from jax.experimental.pallas import tpu as pltpu
from jax.sharding import PartitionSpec as P

EPS = 1e-05
HIGH = lax.Precision.HIGHEST


def in_blocks(shard, dim, size):
    before, after = (shard.shape[:dim], shard.shape[dim + 1 :])
    return jnp.moveaxis(shard.reshape(*before, size, -1, *after), dim, 0)


def summed_on_arrival(shard, axis, dim):
    size = lax.axis_size(axis)
    parts = lax.all_to_all(in_blocks(shard, dim, size), axis, 0, 0, tiled=True)
    return jnp.sum(parts.astype(jnp.float32), axis=0)


def multiply(left, right):
    return jnp.dot(left, right, preferred_element_type=jnp.float32)


def contract_rows(left, right):
    return lax.dot_general(
        left, right, (((0,), (0,)), ((), ())), preferred_element_type=jnp.float32
    )


def contract_cols(left, right):
    return lax.dot_general(
        left, right, (((1,), (1,)), ((), ())), preferred_element_type=jnp.float32
    )


def shifted_down(values, steps):
    if steps == 0:
        return values
    filler = jnp.zeros((steps,) + values.shape[1:], values.dtype)
    return jnp.concatenate([filler, values[:-steps]], axis=0)


def shifted_up(values, steps):
    if steps == 0:
        return values
    filler = jnp.zeros((steps,) + values.shape[1:], values.dtype)
    return jnp.concatenate([values[steps:], filler], axis=0)


def same_document(doc_ids, steps):
    if steps == 0:
        return jnp.ones(doc_ids.shape, jnp.float32)
    filler = jnp.full((steps,), -1, jnp.int32)
    earlier = jnp.concatenate([filler, doc_ids[:-steps]])
    return (earlier == doc_ids).astype(jnp.float32)


def silu_slope(values):
    logistic = jax.nn.sigmoid(values)
    return logistic * (1.0 + values * (1.0 - logistic))


def rms_back(grad_unit, unit, scale):
    return scale * (grad_unit - unit * jnp.mean(grad_unit * unit, axis=1, keepdims=True))


LOG2E = 1.4426950408889634
LANES = 128
F32, BF16 = jnp.float32, jnp.bfloat16
MESH = pl.DeviceIdType.MESH


def fold_rows(parts, masks):
    m4, m2, m1 = masks

    def join(a, b, m, shift):
        return jnp.where(m, a, b) + pltpu.roll(jnp.where(m, b, a), shift, 0)

    c = [join(parts[i], parts[i + 4], m4[i], 4) for i in range(4)]
    d = [join(c[i], c[i + 2], m2[i], 6) for i in range(2)]
    return join(d[0], d[1], m1, 7)


def fold_masks(width):
    sub = lax.broadcasted_iota(jnp.int32, (8, width), 0)
    m4 = [((sub - i) & 7) < 4 for i in range(4)]
    m2 = [((sub - i) & 2) == 0 for i in range(2)]
    m1 = (sub & 1) == 0
    return m4, m2, m1


def softplus(v):
    return jnp.maximum(v, 0.0) + jnp.log1p(jnp.exp(-jnp.abs(v)))


def row(ref, c, t, ns):
    one = ref[c, pl.ds(t, 8, stride=0), :]
    return jnp.concatenate([one] * (ns // 8), axis=0)


def spread(ref, value):
    for c in range(ref.shape[0]):
        ref[c] = value[:, c * LANES:(c + 1) * LANES]


def own_column(ns, rank):
    lane = lax.broadcasted_iota(jnp.int32, (ns, LANES), 1)
    n = lax.broadcasted_iota(jnp.int32, (ns, LANES), 0)
    return (lane == rank + n) | (lane == rank + ns + n)


def coefficient_rows(ns, rank, proj_ref, rows_s, wide_s):
    tb = proj_ref.shape[0]
    own = own_column(ns, rank)
    lane = lax.broadcasted_iota(jnp.int32, (LANES, 2 * LANES), 1)
    k = lax.broadcasted_iota(jnp.int32, (LANES, 2 * LANES), 0)
    pick = ((lane < LANES) & (k >= rank) & (k < rank + ns)) | ((lane >= LANES) & (k >= rank + ns) & (k < rank + 2 * ns))
    pick = jnp.where(pick, 1.0, 0.0).astype(BF16)

    def body(g, _):
        for j in range(16):
            t = g * 16 + j
            one = proj_ref[pl.ds(t, 8, stride=0), :]
            both = jnp.where(own, jnp.concatenate([one] * (ns // 8), axis=0), 0.0)
            rows_s[pl.ds(pl.multiple_of(j * ns, ns), ns), :] = both.astype(BF16)
        wide_s[pl.ds(pl.multiple_of(g * 16 * ns, 16 * ns), 16 * ns), :] = jnp.dot(rows_s[...], pick, preferred_element_type=F32)
        return 0

    lax.fori_loop(0, tb // 16, body, 0)


def scan_fwd_kernel(ns, rank, proj_ref, inner_ref, keep_ref, sproj_ref, sbias_ref, lr_ref, skip_ref,
                    scan_ref, step_ref, states_ref, starts_ref, state_s, stepd_s, drive_s, r2_s, rows_s, wide_s):
    tb, ch = inner_ref.shape
    groups = ch // LANES
    i = pl.program_id(0)

    @pl.when(i == 0)
    def _():
        state_s[...] = jnp.zeros_like(state_s)
        spread(r2_s, jnp.exp(lr_ref[...]) * (-LOG2E))

    step_in = proj_ref[...].astype(BF16)
    pre = jnp.dot(step_in, sproj_ref[...], preferred_element_type=F32) + sbias_ref[...]
    step = softplus(pre)
    step_ref[...] = step
    spread(stepd_s, jnp.where(keep_ref[...] > 0.0, step, 1e30))
    inner = inner_ref[...].astype(F32)
    spread(drive_s, step * inner)
    coefficient_rows(ns, rank, proj_ref, rows_s, wide_s)
    starts_ref[0] = state_s[...]
    masks = fold_masks(LANES)

    def body(g, state):
        state = list(state)
        parts = [[] for _ in range(groups)]
        for j in range(8):
            t = g * 8 + j
            here = pl.ds(pl.multiple_of(t * ns, ns), ns)
            in_b = wide_s[here, :LANES]
            out_b = wide_s[here, LANES:]
            for c in range(groups):
                cols = pl.ds(c * LANES, LANES)
                dec = jnp.exp2(row(stepd_s, c, t, ns) * r2_s[c])
                s = dec * state[c] + row(drive_s, c, t, ns) * in_b
                state[c] = s
                states_ref[here, cols] = s.astype(BF16)
                z = out_b * s
                parts[c].append(sum(z[8 * k:8 * k + 8] for k in range(ns // 8)))
        for c in range(groups):
            scan_ref[pl.ds(pl.multiple_of(g * 8, 8), 8), pl.ds(c * LANES, LANES)] = fold_rows(parts[c], masks)
        return tuple(state)

    start = tuple(state_s[:, c * LANES:(c + 1) * LANES] for c in range(groups))
    state = lax.fori_loop(0, tb // 8, body, start)
    for c in range(groups):
        state_s[:, c * LANES:(c + 1) * LANES] = state[c]
    scan_ref[...] += skip_ref[...] * inner


def scan_fwd(proj, inner, keep, sproj, sbias, log_rates, skip, rank):
    seq, ch = inner.shape
    ns = log_rates.shape[0]
    tb = LANES
    nb = seq // tb
    full = lambda a: pl.BlockSpec(a.shape, lambda i: (0,) * a.ndim)
    rows = pl.BlockSpec((tb, ch), lambda i: (i, 0))
    return pl.pallas_call(
        functools.partial(scan_fwd_kernel, ns, rank),
        grid=(nb,),
        in_specs=[pl.BlockSpec((tb, LANES), lambda i: (i, 0)), rows, pl.BlockSpec((tb, 1), lambda i: (i, 0)),
                  full(sproj), full(sbias), full(log_rates), full(skip)],
        out_specs=[rows, rows, pl.BlockSpec((tb * ns, ch), lambda i: (i, 0)), pl.BlockSpec((1, ns, ch), lambda i: (i, 0, 0))],
        out_shape=[jax.ShapeDtypeStruct((seq, ch), F32), jax.ShapeDtypeStruct((seq, ch), F32),
                   jax.ShapeDtypeStruct((seq * ns, ch), BF16), jax.ShapeDtypeStruct((nb, ns, ch), F32)],
        scratch_shapes=[pltpu.VMEM((ns, ch), F32)] + [pltpu.VMEM((ch // LANES, tb, LANES), F32)] * 2 + [pltpu.VMEM((ch // LANES, ns, LANES), F32),
                        pltpu.VMEM((16 * ns, LANES), BF16), pltpu.VMEM((tb * ns, 2 * LANES), F32)],
        compiler_params=pltpu.CompilerParams(vmem_limit_bytes=48 << 20),
        name="scan_fwd",
    )(proj, inner, keep, sproj, sbias, log_rates, skip)


def scan_bwd_kernel(ns, rank, proj_ref, inner_ref, keep_ref, step_ref, states_ref, starts_ref, dscan_ref, sproj_ref, lr_ref, skip_ref,
                    dpre_ref, dinner_ref, dproj_ref, gstep_ref, gsbias_ref, grates_ref, gskip_ref,
                    carry_s, stepd_s, drive_s, dscan_s, step_s, r2_s, coeff_s, exps_s, acc_s, rows_s, wide_s, sums_s):
    tb, ch = inner_ref.shape
    groups = ch // LANES
    i = pl.program_id(0)

    @pl.when(i == 0)
    def _():
        carry_s[...] = jnp.zeros_like(carry_s)
        acc_s[...] = jnp.zeros_like(acc_s)
        spread(r2_s, jnp.exp(lr_ref[...]) * (-LOG2E))
        gstep_ref[...] = jnp.zeros_like(gstep_ref)
        gsbias_ref[...] = jnp.zeros_like(gsbias_ref)
        gskip_ref[...] = jnp.zeros_like(gskip_ref)

    step = step_ref[...]
    inner = inner_ref[...].astype(F32)
    dscan = dscan_ref[...]
    spread(stepd_s, jnp.where(keep_ref[...] > 0.0, step, 1e30))
    spread(drive_s, step * inner)
    spread(dscan_s, dscan)
    spread(step_s, step)
    coefficient_rows(ns, rank, proj_ref, rows_s, wide_s)
    masks = fold_masks(LANES)
    steps = tb // 8

    def body(k, carry):
        later, acc = [list(v) for v in carry]
        g = steps - 1 - k
        cparts = [[None] * 8 for _ in range(groups)]
        eparts = [[None] * 8 for _ in range(groups)]
        last = pl.ds(pl.multiple_of((g * 8 + 7) * ns, ns), ns)
        now = [states_ref[last, pl.ds(c * LANES, LANES)].astype(F32) for c in range(groups)]
        for j in range(7, -1, -1):
            t = g * 8 + j
            here = pl.ds(pl.multiple_of(t * ns, ns), ns)
            prior = pl.ds(pl.multiple_of((t - 1 if j else jnp.maximum(t - 1, 0)) * ns, ns), ns)
            in_b = wide_s[here, :LANES]
            out_b = wide_s[here, LANES:]
            din = dout = None
            for c in range(groups):
                cols = pl.ds(c * LANES, LANES)
                before = states_ref[prior, cols].astype(F32)
                if j == 0:
                    before = jnp.where(jnp.full((ns, LANES), t, jnp.int32) == 0, starts_ref[0, :, cols], before)
                r2 = r2_s[c]
                dec = jnp.exp2(row(stepd_s, c, t, ns) * r2)
                ds = row(dscan_s, c, t, ns)
                d = later[c] + out_b * ds
                later[c] = dec * d
                dexp = later[c] * before
                e = dexp * r2
                cf = d * in_b
                cparts[c][j] = sum(cf[8 * q:8 * q + 8] for q in range(ns // 8))
                eparts[c][j] = sum(e[8 * q:8 * q + 8] for q in range(ns // 8))
                acc[c] = acc[c] + dexp * row(step_s, c, t, ns)
                a = d * row(drive_s, c, t, ns)
                b = now[c] * ds
                din = a if din is None else din + a
                dout = b if dout is None else dout + b
                now[c] = before
            sums_s[here, :LANES] = din.astype(BF16)
            sums_s[here, LANES:] = dout.astype(BF16)
        rows = pl.ds(pl.multiple_of(g * 8, 8), 8)
        for c in range(groups):
            cols = pl.ds(c * LANES, LANES)
            coeff_s[rows, cols] = fold_rows(cparts[c], masks)
            exps_s[rows, cols] = fold_rows(eparts[c], masks)
        return tuple(later), tuple(acc)

    pick = lambda ref: tuple(ref[:, c * LANES:(c + 1) * LANES] for c in range(groups))
    later, acc = lax.fori_loop(0, steps, body, (pick(carry_s), pick(acc_s)))
    for c in range(groups):
        carry_s[:, c * LANES:(c + 1) * LANES] = later[c]
        acc_s[:, c * LANES:(c + 1) * LANES] = acc[c]

    k = lax.broadcasted_iota(jnp.int32, (2 * LANES, LANES), 0)
    lane = lax.broadcasted_iota(jnp.int32, (2 * LANES, LANES), 1)
    into = ((k < LANES) & (lane >= rank) & (lane < rank + ns)) | ((k >= LANES) & (lane >= rank + ns) & (lane < rank + 2 * ns))
    into = jnp.where(into, 1.0, 0.0).astype(BF16)
    own = own_column(ns, rank)

    def gather(g, _):
        got = jnp.dot(sums_s[pl.ds(pl.multiple_of(g * 16 * ns, 16 * ns), 16 * ns), :], into, preferred_element_type=F32)
        for h in range(2):
            parts = []
            for j in range(8):
                one = jnp.where(own, got[(h * 8 + j) * ns:(h * 8 + j + 1) * ns], 0.0)
                parts.append(sum(one[8 * q:8 * q + 8] for q in range(ns // 8)))
            dproj_ref[pl.ds(pl.multiple_of(g * 16 + h * 8, 8), 8), :] = fold_rows(parts, masks)
        return 0

    lax.fori_loop(0, tb // 16, gather, 0)
    coeff = coeff_s[...]
    d_step = coeff * inner + exps_s[...] * (1.0 / LOG2E)
    d_pre = (d_step * (1.0 - jnp.exp(-step))).astype(BF16)
    dpre_ref[...] = d_pre
    dinner_ref[...] = dscan * skip_ref[...] + step * coeff
    step_in = proj_ref[...].astype(BF16)
    gstep_ref[...] += lax.dot_general(step_in, d_pre, (((0,), (0,)), ((), ())), preferred_element_type=F32)
    gsbias_ref[...] += jnp.sum(d_pre.astype(F32), axis=0, keepdims=True)
    gskip_ref[...] += jnp.sum(dscan * inner, axis=0, keepdims=True)
    dproj_ref[...] += lax.dot_general(d_pre, sproj_ref[...], (((1,), (1,)), ((), ())), preferred_element_type=F32)

    @pl.when(i == pl.num_programs(0) - 1)
    def _():
        grates_ref[...] = -jnp.exp(lr_ref[...]) * acc_s[...]


def scan_bwd(proj, inner, keep, step, states, starts, dscan, sproj, log_rates, skip, rank):
    seq, ch = inner.shape
    ns = log_rates.shape[0]
    tb = LANES
    nb = seq // tb
    full = lambda a: pl.BlockSpec(a.shape, lambda i: (0,) * a.ndim)
    rows = pl.BlockSpec((tb, ch), lambda i: (nb - 1 - i, 0))
    prow = pl.BlockSpec((tb, LANES), lambda i: (nb - 1 - i, 0))
    whole = lambda *s: pl.BlockSpec(s, lambda i: (0,) * len(s))
    shape = jax.ShapeDtypeStruct
    return pl.pallas_call(
        functools.partial(scan_bwd_kernel, ns, rank),
        grid=(nb,),
        in_specs=[prow, rows, pl.BlockSpec((tb, 1), lambda i: (nb - 1 - i, 0)), rows,
                  pl.BlockSpec((tb * ns, ch), lambda i: (nb - 1 - i, 0)), pl.BlockSpec((1, ns, ch), lambda i: (nb - 1 - i, 0, 0)),
                  rows, full(sproj), full(log_rates), full(skip)],
        out_specs=[rows, rows, prow, whole(LANES, ch), whole(1, ch), whole(ns, ch), whole(1, ch)],
        out_shape=[shape((seq, ch), BF16), shape((seq, ch), F32), shape((seq, LANES), F32), shape((LANES, ch), F32), shape((1, ch), F32),
                   shape((ns, ch), F32), shape((1, ch), F32)],
        scratch_shapes=[pltpu.VMEM((ns, ch), F32)] + [pltpu.VMEM((ch // LANES, tb, LANES), F32)] * 4 + [pltpu.VMEM((ch // LANES, ns, LANES), F32),
                        pltpu.VMEM((tb, ch), F32), pltpu.VMEM((tb, ch), F32), pltpu.VMEM((ns, ch), F32),
                        pltpu.VMEM((16 * ns, LANES), BF16), pltpu.VMEM((tb * ns, 2 * LANES), F32), pltpu.VMEM((tb * ns, 2 * LANES), BF16)],
        compiler_params=pltpu.CompilerParams(vmem_limit_bytes=48 << 20),
        name="scan_bwd",
    )(proj, inner, keep, step, states, starts, dscan, sproj, log_rates, skip)


def as_row(ref):
    return ref[...].reshape(1, ref.shape[0])


def line_roles():
    me = lax.axis_index("tp")
    end = (me == 0) | (me == 3)
    mate = jnp.where(me < 2, 1 - me, 5 - me)
    return end, jnp.logical_not(end), mate, 3 - me


LINE = 4


def greet(wide):
    barrier = pltpu.get_barrier_semaphore()
    for axis, size in (("tp", LINE), ("wide", wide)):
        me = lax.axis_index(axis)
        for k in range(1, size):
            pl.semaphore_signal(barrier, inc=1, device_id={axis: lax.rem(me + k, size)}, device_id_type=MESH)
    pl.semaphore_wait(barrier, LINE + wide - 2)


class LineSum:
    def __init__(self, roles, rows, own, near, half, far, total, sends, arrivals):
        self.end, self.mid, self.mate, self.other = roles
        self.rows, self.own, self.near, self.half, self.far, self.total = rows, own, near, half, far, total
        self.sends, self.arrivals = sends, arrivals

    def part(self, ref, k):
        return ref.at[pl.ds(pl.multiple_of(k * self.rows, self.rows), self.rows)]

    def copy(self, source, target, hop, k, to):
        return pltpu.make_async_remote_copy(
            self.part(source, k), self.part(target, k), self.sends.at[hop, k], self.arrivals.at[hop, k],
            device_id={"tp": to}, device_id_type=MESH)

    def up(self, k):
        return self.copy(self.own, self.near, 0, k, self.mate)

    def across(self, k):
        return self.copy(self.half, self.far, 1, k, self.other)

    def down(self, k):
        return self.copy(self.total, self.total, 2, k, self.mate)

    def add(self, a, b, c, k):
        self.part(c, k)[...] = (self.part(a, k)[...].astype(F32) + self.part(b, k)[...].astype(F32)).astype(BF16)

    def first(self, k):
        self.up(k).wait_recv()
        self.add(self.own, self.near, self.half, k)
        self.across(k).start()

    def second(self, k):
        self.across(k).wait_recv()
        self.add(self.half, self.far, self.total, k)
        self.down(k).start()

    def sent(self, count):
        for k in range(count):
            @pl.when(self.end)
            def _():
                self.up(k).wait_send()

            @pl.when(self.mid)
            def _():
                self.across(k).wait_send()
                self.down(k).wait_send()


def tail_kernel(wide, taps_and_rank, dproj_ref, dinner_ref, inner_ref, x_ref, csum_ref, masks_ref, wproj_ref, cw_ref, normed_ref, dz_ref,
                dmixed_ref, gated_ref, wx_ref, wz_ref, tokens_ref, scale_ref,
                gstep_ref, gsbias_ref, grates_ref, gskip_ref, gsecond_ref, grow_ref,
                dn_ref, gx_ref, gz_ref, go_ref, small_ref,
                dp_own, dp_near, dp_total, dp_sends, dp_arrivals,
                dn_own, dn_near, dn_sends, dn_arrivals,
                prod_s, inbox_s, prod_sends, prod_arrivals, pack_s, pack_in, pack_sends, pack_arrivals,
                dconv_s, dx_s, first_s):
    taps, rank = taps_and_rank
    seq, ch = dinner_ref.shape
    width = tokens_ref.shape[1]
    tb = LANES
    nb = seq // tb
    me = lax.axis_index("wide")
    roles = line_roles()
    end, mid, mate, other = roles
    greet(wide)
    dp = LineSum(roles, seq, dp_own, dp_near, dp_own, dp_total, dp_total, dp_sends, dp_arrivals)
    dn = LineSum(roles, tb, dn_own, dn_near, dn_own, dn_ref, dn_ref, dn_sends, dn_arrivals)

    dp_own[...] = dproj_ref[...].astype(BF16)

    @pl.when(end)
    def _():
        dp.up(0).start()

    block = width // wide

    def deliver(which, k):
        to = lax.rem(me + k, wide)
        return pltpu.make_async_remote_copy(
            prod_s.at[which, pl.ds(pl.multiple_of(to * block, block), block)], inbox_s.at[which, k],
            prod_sends.at[which, k], prod_arrivals.at[which, k], device_id={"wide": to}, device_id_type=MESH)

    def product(which, left, right):
        def tile(j, _):
            cols = pl.ds(pl.multiple_of(j * LANES, LANES), LANES)
            got = lax.dot_general(left[:, cols], right[...], (((0,), (0,)), ((), ())), preferred_element_type=F32)
            prod_s[which, cols, :] = got.astype(BF16)
            return 0

        lax.fori_loop(0, width // LANES, tile, 0)
        for k in range(1, wide):
            deliver(which, k).start()

    product(0, dmixed_ref, gated_ref)

    @pl.when(mid)
    def _():
        dp.first(0)

    product(1, normed_ref, dz_ref)

    @pl.when(mid)
    def _():
        dp.second(0)

    @pl.when(end)
    def _():
        dp.down(0).wait_recv()

    pack_s[...] = jnp.zeros_like(pack_s)
    dconv_s[pl.ds(seq, 8), :] = jnp.zeros((8, ch), F32)
    first_s[...] = jnp.zeros_like(first_s)

    def rows_of(b):
        return pl.ds(pl.multiple_of(b * tb, tb), tb)

    def block_step(k, _):
        b = nb - 1 - k
        rows = rows_of(b)
        base = pl.multiple_of(b * tb, tb)
        d_inner = dinner_ref[rows, :] + lax.dot_general(
            dp_total[rows, :], wproj_ref[...], (((1,), (1,)), ((), ())), preferred_element_type=F32)
        csum = csum_ref[rows, :]
        logistic = 1.0 / (1.0 + jnp.exp(-csum))
        d_conv = d_inner * (logistic * (1.0 + csum * (1.0 - logistic)))
        dconv_s[rows, :] = d_conv
        prior = x_ref[pl.ds(pl.multiple_of(jnp.maximum(base - 8, 0), 8), 8), :]
        history = jnp.concatenate([prior, x_ref[rows, :]], axis=0)
        ahead = jnp.concatenate([d_conv, dconv_s[pl.ds(pl.multiple_of(base + tb, 8), 8), :]], axis=0)
        same = masks_ref[pl.ds(base, tb + 8), :]
        d_x = cw_ref[taps - 1:taps, :] * d_conv
        pack_s[0:1, :] += jnp.sum(d_conv, axis=0, keepdims=True)
        pack_s[8 - 1:8, :] += jnp.sum(d_conv * history[8:, :], axis=0, keepdims=True)
        for s in range(1, taps):
            linked = same[:, s:s + 1] * ahead
            d_x = d_x + cw_ref[taps - 1 - s:taps - s, :] * linked[s:s + tb, :]
            pack_s[7 - s:8 - s, :] += jnp.sum(linked[:tb, :] * history[8 - s:8 - s + tb, :], axis=0, keepdims=True)
        d_x = d_x.astype(BF16)
        dx_s[rows, :] = d_x
        both = lax.dot_general(d_x, wx_ref[...], (((1,), (1,)), ((), ())), preferred_element_type=F32)
        both = both + lax.dot_general(dz_ref[rows, :], wz_ref[...], (((1,), (1,)), ((), ())), preferred_element_type=F32)
        dn_own[rows, :] = both.astype(BF16)

        @pl.when(end)
        def _():
            dn.up(b).start()

        @pl.when(mid & (k > 0))
        def _():
            dn.first(b + 1)

        @pl.when(mid & (k > 1))
        def _():
            dn.second(b + 2)
        return 0

    lax.fori_loop(0, nb, block_step, 0)

    @pl.when(mid)
    def _():
        dn.second(1)
        dn.first(0)

    product(2, normed_ref, dx_s)
    state = lax.dot_general(dp_total[...], inner_ref[...], (((0,), (0,)), ((), ())), preferred_element_type=F32)

    @pl.when(mid)
    def _():
        dn.second(0)

    def finish(k, _):
        b = nb - 1 - k
        rows = rows_of(b)

        @pl.when(end)
        def _():
            dn.down(b).wait_recv()

        first_s[...] += jnp.sum(dn_ref[rows, :].astype(F32) * (tokens_ref[rows, :] * scale_ref[rows, :]), axis=0, keepdims=True)
        return 0

    lax.fori_loop(0, nb, finish, 0)

    states, experts = grates_ref.shape[0], wide
    pack_s[1:2, :] = gsbias_ref[...]
    pack_s[2:3, :] = gskip_ref[...]
    at = 8
    pack_s[at:at + states, :] = grates_ref[...]
    at += states
    pack_s[at:at + rank, :] = gstep_ref[0:rank, :]
    at += rank
    own_row = lax.broadcasted_iota(jnp.int32, (experts, ch), 0) == me
    held = rank + 2 * states
    pack_s[at:at + held, :] = state[:held, :]
    at += held
    halves = width // ch
    for h in range(halves):
        cols = slice(h * ch, (h + 1) * ch)
        pack_s[at + h:at + h + 1, :] = first_s[:, cols]
        pack_s[at + halves + h:at + halves + h + 1, :] = gsecond_ref[:, cols]
        pack_s[at + 8 + h * experts:at + 8 + (h + 1) * experts, :] = jnp.where(own_row, grow_ref[:, cols], 0.0)

    share = pack_s.shape[0] // wide

    def chunk(ref, i):
        return ref.at[pl.ds(pl.multiple_of(i * share, share), share)]

    def scatter(k):
        to = lax.rem(me + k, wide)
        return pltpu.make_async_remote_copy(chunk(pack_s, to), pack_in.at[k], pack_sends.at[0, k], pack_arrivals.at[0, k],
                                            device_id={"wide": to}, device_id_type=MESH)

    def spread_out(k):
        to = lax.rem(me + k, wide)
        return pltpu.make_async_remote_copy(chunk(small_ref, me), chunk(small_ref, me), pack_sends.at[1, k], pack_arrivals.at[1, k],
                                            device_id={"wide": to}, device_id_type=MESH)

    for k in range(1, wide):
        scatter(k).start()

    for which, ref in enumerate((go_ref, gz_ref, gx_ref)):
        total = prod_s[which, pl.ds(pl.multiple_of(me * block, block), block), :].astype(F32)
        for k in range(1, wide):
            deliver(which, k).wait_recv()
            total = total + inbox_s[which, k].astype(F32)
        ref[...] = total

    total = chunk(pack_s, me)[...]
    for k in range(1, wide):
        scatter(k).wait_recv()
        total = total + pack_in[k]
    chunk(small_ref, me)[...] = total
    for k in range(1, wide):
        spread_out(k).start()
    dp.sent(1)
    dn.sent(nb)
    for k in range(1, wide):
        for which in range(3):
            deliver(which, k).wait_send()
        scatter(k).wait_send()
    for k in range(1, wide):
        spread_out(k).wait_recv()
    for k in range(1, wide):
        spread_out(k).wait_send()


def pack_rows(rank, states, experts, width, ch, wide):
    rows = 8 + states + rank + (rank + 2 * states) + 8 + (width // ch) * experts
    return -(-rows // (8 * wide)) * (8 * wide)


def tail(wide, taps, rank, *operands):
    (dproj, dinner, inner, x, csum, masks, wproj, cw, normed, dz, dmixed, gated, wx, wz, tokens, scale,
     gstep, gsbias, grates, gskip, gsecond, grow) = operands
    seq, ch = dinner.shape
    width = tokens.shape[1]
    nb = seq // LANES
    packed = pack_rows(rank, grates.shape[0], wide, width, ch, wide)
    vm = pl.BlockSpec(memory_space=pltpu.VMEM)
    shape = jax.ShapeDtypeStruct
    dma = pltpu.SemaphoreType.DMA
    return pl.pallas_call(
        functools.partial(tail_kernel, wide, (taps, rank)),
        in_specs=[vm] * len(operands),
        out_specs=[vm] * 5,
        out_shape=[shape((seq, width), BF16)] + [shape((width // wide, ch), F32)] * 3 + [shape((packed, ch), F32)],
        scratch_shapes=[
            *[pltpu.VMEM((seq, LANES), BF16)] * 3, dma((3, 1)), dma((3, 1)),
            *[pltpu.VMEM((seq, width), BF16)] * 2, dma((3, nb)), dma((3, nb)),
            pltpu.VMEM((3, width, ch), BF16), pltpu.VMEM((3, wide, width // wide, ch), BF16), dma((3, wide)), dma((3, wide)),
            pltpu.VMEM((packed, ch), F32), pltpu.VMEM((wide, packed // wide, ch), F32), dma((2, wide)), dma((2, wide)),
            pltpu.VMEM((seq + 8, ch), F32), pltpu.VMEM((seq, ch), BF16), pltpu.VMEM((1, width), F32)],
        compiler_params=pltpu.CompilerParams(collective_id=1, has_side_effects=True, vmem_limit_bytes=56 << 20),
        name="mixer_tail",
    )(*operands)


def finish_kernel(rank, states, tokens_ref, mixed_ref, scol_ref, got_ref, dhidden_ref, dn_ref, scale_ref, gain_ref, small_ref,
                  gx_ref, gz_ref, go_ref, gup_ref, gdown_ref,
                  result_ref, tgrad_ref, first_ref, gx_out, gz_out, cw_ref, cb_ref, state_ref, step_ref, sb_ref, rates_ref, skip_ref, go_out,
                  second_ref, router_ref, gup_out, gdown_out, sems):
    i = pl.program_id(0)
    ch = small_ref.shape[1]
    width, experts = router_ref.shape
    pairs = ((gx_ref, gx_out), (gz_ref, gz_out), (go_ref, go_out), (gup_ref, gup_out), (gdown_ref, gdown_out))
    moves = [pltpu.make_async_copy(a, b, sems.at[n]) for n, (a, b) in enumerate(pairs)]

    @pl.when(i == 0)
    def _():
        for move in moves:
            move.start()
        flat = lambda r: small_ref[r:r + 1, :].reshape(ch)
        cb_ref[...] = flat(0)
        sb_ref[...] = flat(1)
        skip_ref[...] = flat(2)
        cw_ref[...] = small_ref[4:8, :]
        at = 8
        rates_ref[...] = small_ref[at:at + states, :]
        at += states
        step_ref[...] = small_ref[at:at + rank, :]
        at += rank
        held = rank + 2 * states
        state_ref[...] = small_ref[at:at + held, :].T
        at += held
        halves = width // ch
        for h in range(halves):
            cols = slice(h * ch, (h + 1) * ch)
            first_ref[cols] = flat(at + h)
            second_ref[cols] = flat(at + halves + h)
            router_ref[cols, :] = small_ref[at + 8 + h * experts:at + 8 + (h + 1) * experts, :].T

    ids = lax.broadcasted_iota(jnp.int32, (scol_ref.shape[0], got_ref.shape[0]), 1)
    chosen = jnp.where(ids == scol_ref[...], 1.0, 0.0).astype(BF16)
    tokens = tokens_ref[...]
    result_ref[...] = tokens + mixed_ref[...].astype(F32) + jnp.dot(chosen, got_ref[...], preferred_element_type=F32)
    scale = scale_ref[...]
    unit = tokens * scale
    through = dn_ref[...].astype(F32) * as_row(gain_ref)
    mean = jnp.mean(through * unit, axis=1, keepdims=True)
    tgrad_ref[...] = dhidden_ref[...] + scale * (through - unit * mean)

    @pl.when(i == pl.num_programs(0) - 1)
    def _():
        for move in moves:
            move.wait()


def finish(rank, states, experts, *operands):
    tokens, mixed, scol, got, dhidden, dn, scale, gain, small, gx, gz, go, gup, gdown = operands
    seq, width = tokens.shape
    ch = small.shape[1]
    tb = LANES
    row = lambda n: pl.BlockSpec((tb, n), lambda i: (i, 0))
    full = lambda a: pl.BlockSpec(a.shape, lambda i: (0,) * a.ndim)
    hbm = pl.BlockSpec(memory_space=pl.ANY)
    whole = lambda *s: pl.BlockSpec(s, lambda i: (0,) * len(s))
    sizes = [(width,), gx.shape, gz.shape, (4, ch), (ch,), (ch, rank + 2 * states), (rank, ch), (ch,), (states, ch), (ch,), go.shape,
             (width,), (width, experts), gup.shape, gdown.shape]
    copied = {1, 2, 10, 13, 14}
    return pl.pallas_call(
        functools.partial(finish_kernel, rank, states),
        grid=(seq // tb,),
        in_specs=[row(width), row(width), row(1), full(got), row(width), row(width), row(1), full(gain), full(small), *[hbm] * 5],
        out_specs=[row(width), row(width), *[hbm if n in copied else whole(*size) for n, size in enumerate(sizes)]],
        out_shape=[jax.ShapeDtypeStruct(size, F32) for size in [(seq, width), (seq, width), *sizes]],
        scratch_shapes=[pltpu.SemaphoreType.DMA((5,))],
        compiler_params=pltpu.CompilerParams(vmem_limit_bytes=40 << 20),
        name="finish",
    )(*operands)


def scan_back_kernel(ns, rank, wide, proj_ref, inner_ref, keep_ref, step_ref, states_ref, starts_ref, sproj_ref, lr_ref, skip_ref,
                     tokens_ref, mixed_ref, ograd_ref, scol_ref, ret_ref, gain_ref, z_ref, scan_ref, wo_ref, term_ref,
                     dinner_ref, dproj_ref, gstep_ref, gsbias_ref, grates_ref, gskip_ref, dhidden_ref, dmixed_ref, dz_ref, gsecond_ref, got_ref,
                    carry_s, stepd_s, drive_s, dscan_s, step_s, r2_s, coeff_s, exps_s, acc_s, rows_s, wide_s, sums_s, near_s, half_s, far_s, sends, arrivals, got_sends, got_arrivals):
    tb, ch = inner_ref.shape
    groups = ch // LANES
    i = pl.program_id(0)
    nb = pl.num_programs(0)
    me = lax.axis_index("wide")
    roles = line_roles()
    end, mid, mate, other = roles
    cap = term_ref.shape[0] // wide
    line = LineSum(roles, cap, term_ref, near_s, half_s, far_s, far_s, sends, arrivals)

    def slot_rows(c):
        return pl.ds(pl.multiple_of(c * cap, cap), cap)

    def give_back(c):
        return pltpu.make_async_remote_copy(
            far_s.at[slot_rows(c)], got_ref.at[slot_rows(me)], got_sends.at[c], got_arrivals.at[c],
            device_id={"wide": lax.rem(me + wide - c, wide)}, device_id_type=MESH)

    def return_chunk(c):
        @pl.when(c == 0)
        def _():
            here = pltpu.make_async_copy(far_s.at[slot_rows(0)], got_ref.at[slot_rows(me)], got_sends.at[0])
            here.start()
            here.wait()

        @pl.when(c != 0)
        def _():
            give_back(c).start()

    def second(c):
        line.second(c)
        return_chunk(c)

    def returned(c):
        line.down(c).wait_recv()
        return_chunk(c)

    @pl.when(i == 0)
    def _():
        greet(wide)

        @pl.when(end)
        def _():
            for c in range(wide):
                line.up(c).start()

        gsecond_ref[...] = jnp.zeros_like(gsecond_ref)
        carry_s[...] = jnp.zeros_like(carry_s)
        acc_s[...] = jnp.zeros_like(acc_s)
        spread(r2_s, jnp.exp(lr_ref[...]) * (-LOG2E))
        gstep_ref[...] = jnp.zeros_like(gstep_ref)
        gsbias_ref[...] = jnp.zeros_like(gsbias_ref)
        gskip_ref[...] = jnp.zeros_like(gskip_ref)

    step = step_ref[...]
    inner = inner_ref[...].astype(F32)
    tokens = tokens_ref[...]
    hidden = tokens + mixed_ref[...].astype(F32)
    scale = lax.rsqrt(jnp.mean(hidden * hidden, axis=1, keepdims=True) + EPS)
    unit = hidden * scale
    ids = lax.broadcasted_iota(jnp.int32, (tb, wide * cap), 1)
    chosen = jnp.where(ids == scol_ref[...], 1.0, 0.0).astype(BF16)
    d_norm_two = jnp.dot(chosen, ret_ref[...], preferred_element_type=F32)
    gsecond_ref[...] += jnp.sum(d_norm_two * unit, axis=0, keepdims=True)
    through = d_norm_two * as_row(gain_ref)
    d_hidden = ograd_ref[...] + scale * (through - unit * jnp.mean(through * unit, axis=1, keepdims=True))
    dhidden_ref[...] = d_hidden
    d_mixed = d_hidden.astype(BF16)
    dmixed_ref[...] = d_mixed
    d_gated = jnp.dot(d_mixed, wo_ref[...], preferred_element_type=F32)
    z = z_ref[...]
    logistic = 1.0 / (1.0 + jnp.exp(-z))
    dz_ref[...] = (d_gated * scan_ref[...] * (logistic * (1.0 + z * (1.0 - logistic)))).astype(BF16)
    dscan = d_gated * (z * logistic)
    spread(stepd_s, jnp.where(keep_ref[...] > 0.0, step, 1e30))
    spread(drive_s, step * inner)
    spread(dscan_s, dscan)
    spread(step_s, step)
    coefficient_rows(ns, rank, proj_ref, rows_s, wide_s)
    masks = fold_masks(LANES)
    steps = tb // 8

    def body(k, carry):
        later, acc = [list(v) for v in carry]
        g = steps - 1 - k
        cparts = [[None] * 8 for _ in range(groups)]
        eparts = [[None] * 8 for _ in range(groups)]
        last = pl.ds(pl.multiple_of((g * 8 + 7) * ns, ns), ns)
        now = [states_ref[last, pl.ds(c * LANES, LANES)].astype(F32) for c in range(groups)]
        for j in range(7, -1, -1):
            t = g * 8 + j
            here = pl.ds(pl.multiple_of(t * ns, ns), ns)
            prior = pl.ds(pl.multiple_of((t - 1 if j else jnp.maximum(t - 1, 0)) * ns, ns), ns)
            in_b = wide_s[here, :LANES]
            out_b = wide_s[here, LANES:]
            din = dout = None
            for c in range(groups):
                cols = pl.ds(c * LANES, LANES)
                before = states_ref[prior, cols].astype(F32)
                if j == 0:
                    before = jnp.where(jnp.full((ns, LANES), t, jnp.int32) == 0, starts_ref[0, :, cols], before)
                r2 = r2_s[c]
                dec = jnp.exp2(row(stepd_s, c, t, ns) * r2)
                ds = row(dscan_s, c, t, ns)
                d = later[c] + out_b * ds
                later[c] = dec * d
                dexp = later[c] * before
                e = dexp * r2
                cf = d * in_b
                cparts[c][j] = sum(cf[8 * q:8 * q + 8] for q in range(ns // 8))
                eparts[c][j] = sum(e[8 * q:8 * q + 8] for q in range(ns // 8))
                acc[c] = acc[c] + dexp * row(step_s, c, t, ns)
                a = d * row(drive_s, c, t, ns)
                b = now[c] * ds
                din = a if din is None else din + a
                dout = b if dout is None else dout + b
                now[c] = before
            sums_s[here, :LANES] = din.astype(BF16)
            sums_s[here, LANES:] = dout.astype(BF16)
        rows = pl.ds(pl.multiple_of(g * 8, 8), 8)
        for c in range(groups):
            cols = pl.ds(c * LANES, LANES)
            coeff_s[rows, cols] = fold_rows(cparts[c], masks)
            exps_s[rows, cols] = fold_rows(eparts[c], masks)
        return tuple(later), tuple(acc)

    pick = lambda ref: tuple(ref[:, c * LANES:(c + 1) * LANES] for c in range(groups))
    later, acc = lax.fori_loop(0, steps, body, (pick(carry_s), pick(acc_s)))
    for c in range(groups):
        carry_s[:, c * LANES:(c + 1) * LANES] = later[c]
        acc_s[:, c * LANES:(c + 1) * LANES] = acc[c]

    k = lax.broadcasted_iota(jnp.int32, (2 * LANES, LANES), 0)
    lane = lax.broadcasted_iota(jnp.int32, (2 * LANES, LANES), 1)
    into = ((k < LANES) & (lane >= rank) & (lane < rank + ns)) | ((k >= LANES) & (lane >= rank + ns) & (lane < rank + 2 * ns))
    into = jnp.where(into, 1.0, 0.0).astype(BF16)
    own = own_column(ns, rank)

    def gather(g, _):
        got = jnp.dot(sums_s[pl.ds(pl.multiple_of(g * 16 * ns, 16 * ns), 16 * ns), :], into, preferred_element_type=F32)
        for h in range(2):
            parts = []
            for j in range(8):
                one = jnp.where(own, got[(h * 8 + j) * ns:(h * 8 + j + 1) * ns], 0.0)
                parts.append(sum(one[8 * q:8 * q + 8] for q in range(ns // 8)))
            dproj_ref[pl.ds(pl.multiple_of(g * 16 + h * 8, 8), 8), :] = fold_rows(parts, masks)
        return 0

    lax.fori_loop(0, tb // 16, gather, 0)
    coeff = coeff_s[...]
    d_step = coeff * inner + exps_s[...] * (1.0 / LOG2E)
    d_pre = (d_step * (1.0 - jnp.exp(-step))).astype(BF16)
    dinner_ref[...] = dscan * as_row(skip_ref) + step * coeff
    step_in = proj_ref[...].astype(BF16)
    gstep_ref[...] += lax.dot_general(step_in, d_pre, (((0,), (0,)), ((), ())), preferred_element_type=F32)
    gsbias_ref[...] += jnp.sum(d_pre.astype(F32), axis=0, keepdims=True)
    gskip_ref[...] += jnp.sum(dscan * inner, axis=0, keepdims=True)
    dproj_ref[...] += lax.dot_general(d_pre, sproj_ref[...], (((1,), (1,)), ((), ())), preferred_element_type=F32)

    @pl.when(mid & (i < wide))
    def _():
        line.first(i)

    @pl.when(mid & (i > 0) & (i <= wide))
    def _():
        second(i - 1)

    @pl.when(end & (i > 1))
    def _():
        returned(i - 2)

    @pl.when(i == nb - 1)
    def _():
        grates_ref[...] = -jnp.exp(lr_ref[...]) * acc_s[...]

        @pl.when(mid)
        def _():
            second(wide - 1)

        @pl.when(end)
        def _():
            returned(wide - 2)
            returned(wide - 1)

        line.sent(wide)
        for c in range(1, wide):
            give_back(c).wait_recv()
            give_back(c).wait_send()


def scan_back(wide, proj, inner, keep, step, states, starts, sproj, log_rates, skip, tokens, mixed, ograd, scol, ret, gain, z, scan, wo, term, rank):
    seq, ch = inner.shape
    width = tokens.shape[1]
    ns = log_rates.shape[0]
    tb = LANES
    nb = seq // tb
    assert nb == wide
    full = lambda a: pl.BlockSpec(a.shape, lambda i: (0,) * a.ndim)
    row = lambda n: pl.BlockSpec((tb, n), lambda i: (nb - 1 - i, 0))
    whole = lambda *s: pl.BlockSpec(s, lambda i: (0,) * len(s))
    shape = jax.ShapeDtypeStruct
    dma = pltpu.SemaphoreType.DMA
    return pl.pallas_call(
        functools.partial(scan_back_kernel, ns, rank, wide),
        grid=(nb,),
        in_specs=[row(LANES), row(ch), row(1), row(ch),
                  pl.BlockSpec((tb * ns, ch), lambda i: (nb - 1 - i, 0)), pl.BlockSpec((1, ns, ch), lambda i: (nb - 1 - i, 0, 0)),
                  full(sproj), full(log_rates), full(skip), row(width), row(width), row(width), row(1), full(ret), full(gain),
                  row(ch), row(ch), full(wo), full(term)],
        out_specs=[row(ch), row(LANES), whole(LANES, ch), whole(1, ch), whole(ns, ch), whole(1, ch), row(width), row(width), row(ch),
                   whole(1, width), pl.BlockSpec(memory_space=pl.ANY)],
        out_shape=[shape((seq, ch), F32), shape((seq, LANES), F32), shape((LANES, ch), F32), shape((1, ch), F32),
                   shape((ns, ch), F32), shape((1, ch), F32), shape((seq, width), F32), shape((seq, width), BF16), shape((seq, ch), BF16),
                   shape((1, width), F32), shape(ret.shape, BF16)],
        scratch_shapes=[pltpu.VMEM((ns, ch), F32)] + [pltpu.VMEM((ch // LANES, tb, LANES), F32)] * 4 + [pltpu.VMEM((ch // LANES, ns, LANES), F32),
                        pltpu.VMEM((tb, ch), F32), pltpu.VMEM((tb, ch), F32), pltpu.VMEM((ns, ch), F32),
                        pltpu.VMEM((16 * ns, LANES), BF16), pltpu.VMEM((tb * ns, 2 * LANES), F32), pltpu.VMEM((tb * ns, 2 * LANES), BF16),
                        *[pltpu.VMEM(ret.shape, BF16)] * 3, dma((3, wide)), dma((3, wide)), dma((wide,)), dma((wide,))],
        compiler_params=pltpu.CompilerParams(collective_id=5, has_side_effects=True, vmem_limit_bytes=56 << 20),
        name="scan_back",
    )(proj, inner, keep, step, states, starts, sproj, log_rates, skip, tokens, mixed, ograd, scol, ret, gain, z, scan, wo, term)


def gelu_pair(v):
    root = 0.7978845608028654
    square = v * v
    t = jnp.tanh(root * v * (1.0 + 0.044715 * square))
    half = 0.5 * (1.0 + t)
    slope = half + (0.5 * root) * v * (1.0 - t * t) * (1.0 + (3.0 * 0.044715) * square)
    return v * half, slope


def scan_mix_kernel(ns, rank, wide, proj_ref, inner_ref, keep_ref, sproj_ref, sbias_ref, lr_ref, skip_ref, z_ref, wo_ref, ograd_ref, srow_ref,
                    scan_ref, step_ref, states_ref, starts_ref, gated_ref, mixed_ref, gin_ref,
                    state_s, stepd_s, drive_s, r2_s, rows_s, wide_s, own_s, near_s, far_s, sends, arrivals, grad_s, send_s, g_sends, g_arrivals):
    tb, ch = inner_ref.shape
    groups = ch // LANES
    i = pl.program_id(0)
    roles = line_roles()
    end, mid, mate, other = roles
    line = LineSum(roles, tb, own_s, near_s, own_s, far_s, far_s, sends, arrivals)
    steps = arrivals.shape[1]

    me = lax.axis_index("wide")
    cap = send_s.shape[0] // wide

    def slot_rows(k):
        return pl.ds(pl.multiple_of(k * cap, cap), cap)

    def dispatch(k):
        return pltpu.make_async_remote_copy(
            send_s.at[slot_rows(k)], gin_ref.at[slot_rows(k)], g_sends.at[k], g_arrivals.at[k],
            device_id={"wide": lax.rem(me + k, wide)}, device_id_type=MESH)

    own_rows = pltpu.make_async_copy(send_s.at[slot_rows(0)], gin_ref.at[slot_rows(0)], g_sends.at[0])

    @pl.when(i == 0)
    def _():
        greet(wide)
        grad_s[...] = ograd_ref[...].astype(BF16)
        state_s[...] = jnp.zeros_like(state_s)
        spread(r2_s, jnp.exp(lr_ref[...]) * (-LOG2E))

    @pl.when(i < wide)
    def _():
        ids = lax.broadcasted_iota(jnp.int32, (cap, grad_s.shape[0]), 0) + lax.rem(me + i, wide) * cap
        chosen = jnp.where(ids == srow_ref[...], 1.0, 0.0).astype(BF16)
        send_s[slot_rows(i), :] = jnp.dot(chosen, grad_s[...], preferred_element_type=F32).astype(BF16)

        @pl.when(i == 0)
        def _():
            own_rows.start()

        @pl.when(i > 0)
        def _():
            dispatch(i).start()

    step_in = proj_ref[...].astype(BF16)
    pre = jnp.dot(step_in, sproj_ref[...], preferred_element_type=F32) + as_row(sbias_ref)
    step = softplus(pre)
    step_ref[...] = step
    spread(stepd_s, jnp.where(keep_ref[...] > 0.0, step, 1e30))
    inner = inner_ref[...].astype(F32)
    spread(drive_s, step * inner)
    coefficient_rows(ns, rank, proj_ref, rows_s, wide_s)
    starts_ref[0] = state_s[...]
    masks = fold_masks(LANES)

    def body(g, state):
        state = list(state)
        parts = [[] for _ in range(groups)]
        for j in range(8):
            t = g * 8 + j
            here = pl.ds(pl.multiple_of(t * ns, ns), ns)
            in_b = wide_s[here, :LANES]
            out_b = wide_s[here, LANES:]
            for c in range(groups):
                cols = pl.ds(c * LANES, LANES)
                dec = jnp.exp2(row(stepd_s, c, t, ns) * r2_s[c])
                s = dec * state[c] + row(drive_s, c, t, ns) * in_b
                state[c] = s
                states_ref[here, cols] = s.astype(BF16)
                z = out_b * s
                parts[c].append(sum(z[8 * k:8 * k + 8] for k in range(ns // 8)))
        for c in range(groups):
            scan_ref[pl.ds(pl.multiple_of(g * 8, 8), 8), pl.ds(c * LANES, LANES)] = fold_rows(parts[c], masks)
        return tuple(state)

    start = tuple(state_s[:, c * LANES:(c + 1) * LANES] for c in range(groups))
    state = lax.fori_loop(0, tb // 8, body, start)
    for c in range(groups):
        state_s[:, c * LANES:(c + 1) * LANES] = state[c]
    scan = scan_ref[...] + as_row(skip_ref) * inner
    scan_ref[...] = scan
    z = z_ref[...]
    gated = (scan * (z / (1.0 + jnp.exp(-z)))).astype(BF16)
    gated_ref[...] = gated
    here = pl.ds(pl.multiple_of(i * tb, tb), tb)
    own_s[here, :] = lax.dot_general(gated, wo_ref[...], (((1,), (1,)), ((), ())), preferred_element_type=F32).astype(BF16)

    @pl.when(end)
    def _():
        line.up(i).start()

    @pl.when(mid & (i > 0))
    def _():
        line.first(i - 1)

    @pl.when(mid & (i > 1))
    def _():
        line.second(i - 2)

    @pl.when(i == steps - 1)
    def _():
        @pl.when(mid)
        def _():
            line.first(steps - 1)
            line.second(steps - 2)
            line.second(steps - 1)

        @pl.when(end)
        def _():
            for k in range(steps):
                line.down(k).wait_recv()

        mixed_ref[...] = far_s[...]
        line.sent(steps)
        own_rows.wait()
        for k in range(1, wide):
            dispatch(k).wait_recv()
            dispatch(k).wait_send()


def scan_mix(proj, inner, keep, sproj, sbias, log_rates, skip, z, wo, ograd, srow, rank, wide, cap):
    seq, ch = inner.shape
    ns = log_rates.shape[0]
    tb = LANES
    nb = seq // tb
    width = wo.shape[0]
    full = lambda a: pl.BlockSpec(a.shape, lambda i: (0,) * a.ndim)
    rows = pl.BlockSpec((tb, ch), lambda i: (i, 0))
    return pl.pallas_call(
        functools.partial(scan_mix_kernel, ns, rank, wide),
        grid=(nb,),
        in_specs=[pl.BlockSpec((tb, LANES), lambda i: (i, 0)), rows, pl.BlockSpec((tb, 1), lambda i: (i, 0)),
                  full(sproj), full(sbias), full(log_rates), full(skip), rows, full(wo), full(ograd), full(srow)],
        out_specs=[rows, rows, pl.BlockSpec((tb * ns, ch), lambda i: (i, 0)), pl.BlockSpec((1, ns, ch), lambda i: (i, 0, 0)),
                   rows, pl.BlockSpec((seq, width), lambda i: (0, 0)), pl.BlockSpec(memory_space=pl.ANY)],
        out_shape=[jax.ShapeDtypeStruct((seq, ch), F32), jax.ShapeDtypeStruct((seq, ch), F32),
                   jax.ShapeDtypeStruct((seq * ns, ch), BF16), jax.ShapeDtypeStruct((nb, ns, ch), F32),
                   jax.ShapeDtypeStruct((seq, ch), BF16), jax.ShapeDtypeStruct((seq, width), BF16),
                   jax.ShapeDtypeStruct((wide * cap, width), BF16)],
        scratch_shapes=[pltpu.VMEM((ns, ch), F32)] + [pltpu.VMEM((ch // LANES, tb, LANES), F32)] * 2 + [pltpu.VMEM((ch // LANES, ns, LANES), F32),
                        pltpu.VMEM((16 * ns, LANES), BF16), pltpu.VMEM((tb * ns, 2 * LANES), F32),
                        *[pltpu.VMEM((seq, width), BF16)] * 3, pltpu.SemaphoreType.DMA((3, nb)), pltpu.SemaphoreType.DMA((3, nb)),
                        pltpu.VMEM((seq, width), BF16), pltpu.VMEM((wide * cap, width), BF16),
                        pltpu.SemaphoreType.DMA((wide,)), pltpu.SemaphoreType.DMA((wide,))],
        compiler_params=pltpu.CompilerParams(collective_id=4, has_side_effects=True, vmem_limit_bytes=48 << 20),
        name="scan_mix",
    )(proj, inner, keep, sproj, sbias, log_rates, skip, z, wo, ograd, srow)


def experts_kernel(wide, tokens_ref, mixed_ref, gin_ref, srow_ref, gain_ref, router_ref, rt_ref, up_ref, ub_ref, down_ref, db_ref,
                   gup_ref, gub_ref, gdown_ref, gdb_ref, ret_ref, out_ref, grow_ref,
                   pay_s, send_s, inbox_s, rgrad_s, act_s, dpre_s, own_s, near_s, far_s, acc_s, column_s, rows_s,
                   pay_sends, pay_arrivals, sends, arrivals, ret_sends, ret_arrivals, r_sends, r_arrivals):
    seq, width = tokens_ref.shape
    hid = up_ref.shape[1]
    cap = inbox_s.shape[0] // wide
    tb = LANES
    me, rank = lax.axis_index("wide"), lax.axis_index("tp")
    roles = line_roles()
    end, mid, mate, other = roles
    greet(wide)
    back = LineSum(roles, cap, own_s, near_s, own_s, far_s, far_s, sends, arrivals)

    def rows_of(b, size):
        return pl.ds(pl.multiple_of(b * size, size), size)

    def prepare(b, _):
        rows = rows_of(b, tb)
        hidden = tokens_ref[rows, :] + mixed_ref[rows, :].astype(F32)
        scale = lax.rsqrt(jnp.mean(hidden * hidden, axis=1, keepdims=True) + EPS)
        pay_s[rows, :] = (hidden * scale * as_row(gain_ref)).astype(BF16)
        return 0

    lax.fori_loop(0, seq // tb, prepare, 0)

    def payload(expert):
        ids = lax.broadcasted_iota(jnp.int32, (cap, seq), 0) + expert * cap
        chosen = jnp.where(ids == srow_ref[...], 1.0, 0.0).astype(BF16)
        return jnp.dot(chosen, pay_s[...], preferred_element_type=F32).astype(BF16)

    def dispatch(k):
        return pltpu.make_async_remote_copy(
            send_s.at[rows_of(k, cap)], inbox_s.at[rows_of(k, cap)], pay_sends.at[k], pay_arrivals.at[k],
            device_id={"wide": lax.rem(me + k, wide)}, device_id_type=MESH)

    def send(k):
        send_s[rows_of(k, cap), :] = payload(lax.rem(me + k, wide))
        dispatch(k).start()

    ahead = wide // 2

    def send_first(k, _):
        send(k)
        return 0

    lax.fori_loop(1, ahead + 1, send_first, 0)
    inbox_s[0:cap, :] = payload(me)

    def give_back(c):
        return pltpu.make_async_remote_copy(
            far_s.at[rows_of(c, cap)], ret_ref.at[rows_of(me, cap)], ret_sends.at[c], ret_arrivals.at[c],
            device_id={"wide": lax.rem(me + wide - c, wide)}, device_id_type=MESH)

    def return_chunk(c):
        @pl.when(c == 0)
        def _():
            ret_ref[rows_of(me, cap), :] = far_s[0:cap, :]

        @pl.when(c != 0)
        def _():
            give_back(c).start()

    def second(c):
        back.second(c)
        return_chunk(c)

    gub_ref[...] = jnp.zeros_like(gub_ref)
    gdb_ref[...] = jnp.zeros_like(gdb_ref)
    acc_s[...] = jnp.zeros_like(acc_s)
    expert = lax.broadcasted_iota(jnp.int32, rt_ref.shape, 0)
    router_row = jnp.sum(jnp.where(expert == me, rt_ref[...], 0.0), axis=0, keepdims=True)
    column_s[...] = router_row
    lane = lax.broadcasted_iota(jnp.int32, (cap, LANES), 1)
    turned = (((1,), (1,)), ((), ()))

    def compute(k, _):
        @pl.when(k + ahead < wide - 1)
        def _():
            send(k + ahead + 1)

        @pl.when(k > 0)
        def _():
            dispatch(k).wait_recv()

        part = rows_of(k, cap)
        rows_in = inbox_s[part, :]
        rows_raw = gin_ref[part, :].astype(F32)
        logits = jnp.dot(rows_in, router_ref[...], preferred_element_type=F32)
        logit = jnp.sum(jnp.where(lane == me, logits, 0.0), axis=1, keepdims=True)
        gate = 1.0 / (1.0 + jnp.exp(-logit))
        rows_grad = (gate * rows_raw).astype(BF16)
        rgrad_s[part, :] = rows_grad
        pre = jnp.dot(rows_in, up_ref[...], preferred_element_type=F32) + ub_ref[...]
        act, slope = gelu_pair(pre)
        act = act.astype(BF16)
        act_s[part, :] = act
        d_pre = (lax.dot_general(rows_grad, down_ref[...], turned, preferred_element_type=F32) * slope).astype(BF16)
        dpre_s[part, :] = d_pre
        out = jnp.dot(act, down_ref[...], preferred_element_type=F32) + db_ref[...] * (1.0 / LINE)
        d_logit = jnp.sum(rows_raw * out, axis=1, keepdims=True) * (gate * (1.0 - gate))
        own_s[part, :] = (lax.dot_general(d_pre, up_ref[...], turned, preferred_element_type=F32) + d_logit * column_s[...]).astype(BF16)

        @pl.when(end)
        def _():
            back.up(k).start()

        out_ref[part, :] = (gate * out).astype(BF16)
        acc_s[...] += jnp.sum(d_logit * rows_in.astype(F32), axis=0, keepdims=True)
        gub_ref[...] += jnp.sum(d_pre.astype(F32), axis=0, keepdims=True)
        gdb_ref[...] += jnp.sum(rows_grad.astype(F32), axis=0, keepdims=True)

        @pl.when(mid & (k > 0))
        def _():
            back.first(k - 1)

        @pl.when(mid & (k > 1))
        def _():
            second(k - 2)
        return 0

    lax.fori_loop(0, wide, compute, 0)

    def term(k):
        return pltpu.make_async_remote_copy(rows_s.at[rank], rows_s.at[rank], r_sends.at[k], r_arrivals.at[k],
                                            device_id={"tp": lax.rem(rank + k, LINE)}, device_id_type=MESH)

    rows_s[rank] = jnp.broadcast_to(acc_s[...], (8, width))
    for k in range(1, LINE):
        term(k).start()

    @pl.when(mid)
    def _():
        back.first(wide - 1)
        second(wide - 2)

    tiles = hid // LANES
    across_rows = (((0,), (0,)), ((), ()))

    def tile(j, _):
        @pl.when(j < tiles)
        def _():
            cols = rows_of(j, LANES)
            gdown_ref[cols, :] = lax.dot_general(act_s[:, cols], rgrad_s[...], across_rows, preferred_element_type=F32)

        @pl.when(j >= tiles)
        def _():
            cols = rows_of(j - tiles, LANES)
            gup_ref[cols, :] = lax.dot_general(inbox_s[:, cols], dpre_s[...], across_rows, preferred_element_type=F32)

        @pl.when(end & (j < wide))
        def _():
            back.down(j).wait_recv()
            return_chunk(j)

        @pl.when(mid & (j == 0))
        def _():
            second(wide - 1)
        return 0

    lax.fori_loop(0, 2 * tiles, tile, 0)
    for k in range(1, LINE):
        term(k).wait_recv()
    grow_ref[...] = ((rows_s[0] + rows_s[1]) + rows_s[2]) + rows_s[3]
    for c in range(1, wide):
        give_back(c).wait_recv()
    back.sent(wide)
    for k in range(1, wide):
        dispatch(k).wait_send()
        give_back(k).wait_send()
    for k in range(1, LINE):
        term(k).wait_send()


def experts_block(wide, cap, *operands):
    tokens, mixed, gin, srow, gain, router, router_t, up, ub, down, db = operands
    seq, width = tokens.shape
    hid = up.shape[1]
    vm = pl.BlockSpec(memory_space=pltpu.VMEM)
    shape = jax.ShapeDtypeStruct
    dma = pltpu.SemaphoreType.DMA
    slots = wide * cap
    return pl.pallas_call(
        functools.partial(experts_kernel, wide),
        in_specs=[vm] * len(operands),
        out_specs=[vm] * 7,
        out_shape=[shape((width, hid), F32), shape((1, hid), F32), shape((hid, width), F32), shape((1, width), F32),
                   shape((slots, width), BF16), shape((slots, width), BF16), shape((8, width), F32)],
        scratch_shapes=[
            pltpu.VMEM((seq, width), BF16), *[pltpu.VMEM((slots, width), BF16)] * 3,
            pltpu.VMEM((slots, hid), BF16), pltpu.VMEM((slots, hid), BF16),
            *[pltpu.VMEM((slots, width), BF16)] * 3, pltpu.VMEM((1, width), F32), pltpu.VMEM((1, width), F32), pltpu.VMEM((LINE, 8, width), F32),
            dma((wide,)), dma((wide,)), dma((3, wide)), dma((3, wide)), dma((wide,)), dma((wide,)), dma((LINE,)), dma((LINE,))],
        compiler_params=pltpu.CompilerParams(collective_id=2, has_side_effects=True, vmem_limit_bytes=56 << 20),
        name="experts",
    )(*operands)


def front_kernel(wide, taps, tokens_ref, gain_ref, inx_ref, inz_ref, outp_ref, cw_ref, cb_ref, wproj_ref, masks_ref,
                 scale_ref, normed_ref, x_ref, z_ref, csum_ref, inner_ref, proj_ref, wx_ref, wz_ref, wo_ref,
                 own_s, near_s, far_s, w_sends, w_arrivals, sends, arrivals):
    seq, width = tokens_ref.shape
    ch = x_ref.shape[1]
    block = inx_ref.shape[0]
    tb = LANES
    nb = seq // tb
    me = lax.axis_index("wide")
    roles = line_roles()
    end, mid, mate, other = roles
    greet(wide)
    line = LineSum(roles, 2 * tb, own_s, near_s, own_s, far_s, far_s, sends, arrivals)
    mine = pl.ds(pl.multiple_of(me * block, block), block)
    weights = ((inx_ref, wx_ref), (inz_ref, wz_ref), (outp_ref, wo_ref))

    def share(which, k):
        source, target = weights[which]
        return pltpu.make_async_remote_copy(source, target.at[mine], w_sends.at[which, k], w_arrivals.at[which, k],
                                            device_id={"wide": lax.rem(me + k, wide)}, device_id_type=MESH)

    for which in range(3):
        for k in range(1, wide):
            share(which, k).start()
    for source, target in weights:
        target[mine, :] = source[...]

    def rows_of(b):
        return pl.ds(pl.multiple_of(b * tb, tb), tb)

    def norm(b, _):
        rows = rows_of(b)
        tokens = tokens_ref[rows, :]
        scale = lax.rsqrt(jnp.mean(tokens * tokens, axis=1, keepdims=True) + EPS)
        scale_ref[rows, :] = scale
        normed_ref[rows, :] = (tokens * scale * as_row(gain_ref)).astype(BF16)
        return 0

    lax.fori_loop(0, nb, norm, 0)
    for k in range(1, wide):
        share(0, k).wait_recv()

    def step(b, _):
        rows = rows_of(b)
        base = pl.multiple_of(b * tb, tb)
        x = jnp.dot(normed_ref[rows, :], wx_ref[...], preferred_element_type=F32)
        x_ref[rows, :] = x
        prior = x_ref[pl.ds(pl.multiple_of(jnp.maximum(base - 8, 0), 8), 8), :]
        history = jnp.concatenate([prior, x], axis=0)
        same = masks_ref[rows, :]
        csum = as_row(cb_ref) + cw_ref[taps - 1:taps, :] * x
        for s in range(1, taps):
            csum = csum + cw_ref[taps - 1 - s:taps - s, :] * (same[:, s:s + 1] * history[8 - s:8 - s + tb, :])
        csum_ref[rows, :] = csum
        inner = (csum / (1.0 + jnp.exp(-csum))).astype(BF16)
        inner_ref[rows, :] = inner
        own_s[rows, :] = jnp.dot(inner, wproj_ref[...], preferred_element_type=F32).astype(BF16)

        @pl.when(end & (lax.rem(b, 2) == 1))
        def _():
            line.up(b // 2).start()
        return 0

    lax.fori_loop(0, nb, step, 0)
    steps = nb // 2

    @pl.when(mid)
    def _():
        line.first(0)
        for k in range(1, steps):
            line.first(k)
            line.second(k - 1)

    for k in range(1, wide):
        share(1, k).wait_recv()

    def gate(b, _):
        rows = rows_of(b)
        z_ref[rows, :] = jnp.dot(normed_ref[rows, :], wz_ref[...], preferred_element_type=F32)
        return 0

    lax.fori_loop(0, nb, gate, 0)

    @pl.when(mid)
    def _():
        line.second(steps - 1)

    @pl.when(end)
    def _():
        for k in range(steps):
            line.down(k).wait_recv()

    proj_ref[...] = far_s[...].astype(F32)
    line.sent(steps)
    for k in range(1, wide):
        share(2, k).wait_recv()
        for which in range(3):
            share(which, k).wait_send()


def front(wide, taps, *operands):
    tokens, gain, inx, inz, outp, cw, cb, wproj, masks = operands
    seq, width = tokens.shape
    ch = inx.shape[1]
    vm = pl.BlockSpec(memory_space=pltpu.VMEM)
    shape = jax.ShapeDtypeStruct
    dma = pltpu.SemaphoreType.DMA
    return pl.pallas_call(
        functools.partial(front_kernel, wide, taps),
        in_specs=[vm] * len(operands),
        out_specs=[vm] * 10,
        out_shape=[shape((seq, 1), F32), shape((seq, width), BF16), shape((seq, ch), F32), shape((seq, ch), F32), shape((seq, ch), F32),
                   shape((seq, ch), BF16), shape((seq, LANES), F32), *[shape((width, ch), BF16)] * 3],
        scratch_shapes=[*[pltpu.VMEM((seq, LANES), BF16)] * 3, dma((3, wide)), dma((3, wide)), dma((3, seq // LANES // 2)), dma((3, seq // LANES // 2))],
        compiler_params=pltpu.CompilerParams(collective_id=3, has_side_effects=True, vmem_limit_bytes=48 << 20),
        name="mixer_front",
    )(*operands)


def plain_device(
    tokens,
    segment_ids,
    routes,
    out_grad,
    mixer_gain,
    in_proj_x,
    in_proj_z,
    conv_weight,
    conv_bias,
    state_proj,
    step_proj,
    step_bias,
    log_rates,
    skip_gain,
    out_proj,
    expert_gain,
    router_weight,
    expert_up,
    up_bias,
    expert_down,
    down_bias,
):
    seq_len, model_width = tokens.shape
    conv_taps = conv_weight.shape[0]
    step_rank = step_proj.shape[0]
    experts = router_weight.shape[1]
    capacity = 5 * seq_len // (4 * experts)
    doc_ids = segment_ids[0]
    conv_masks = [same_document(doc_ids, offset)[:, None] for offset in range(conv_taps)]
    first_scale = lax.rsqrt(jnp.mean(tokens * tokens, axis=1, keepdims=True) + EPS)
    first_unit = tokens * first_scale
    normed = (first_unit * mixer_gain).astype(jnp.bfloat16)
    gathered_x, gathered_z, gathered_out = (
        lax.all_gather(in_proj_x, "wide", axis=0, tiled=True),
        lax.all_gather(in_proj_z, "wide", axis=0, tiled=True),
        lax.all_gather(out_proj, "wide", axis=0, tiled=True),
    )
    x_branch = multiply(normed, gathered_x)
    z_branch = multiply(normed, gathered_z)
    conv_sum = conv_bias + jnp.zeros_like(x_branch)
    for offset in range(conv_taps):
        conv_sum = conv_sum + conv_weight[conv_taps - 1 - offset] * conv_masks[
            offset
        ] * shifted_down(x_branch, offset)
    inner_act = jax.nn.silu(conv_sum).astype(jnp.bfloat16)
    wide_proj = jnp.pad(state_proj, ((0, 0), (0, LANES - state_proj.shape[1])))
    projected = lax.psum(multiply(inner_act, wide_proj), "tp")
    tall_proj = jnp.pad(step_proj, ((0, LANES - step_rank), (0, 0)))
    carry_mask = same_document(doc_ids, 1)[:, None]
    scan_out, step_size, states, starts = scan_fwd(
        projected, inner_act, carry_mask, tall_proj, step_bias[None], log_rates, skip_gain[None], step_rank
    )
    z_gate = jax.nn.silu(z_branch)
    gated = (scan_out * z_gate).astype(jnp.bfloat16)
    mixed = lax.psum(contract_cols(gated, gathered_out).astype(jnp.bfloat16), "tp").astype(
        jnp.float32
    )
    hidden = tokens + mixed
    second_scale = lax.rsqrt(jnp.mean(hidden * hidden, axis=1, keepdims=True) + EPS)
    second_unit = hidden * second_scale
    expert_in = (second_unit * expert_gain).astype(jnp.bfloat16)
    route_ids = routes[:, 0]
    chosen_int = (routes == jnp.arange(experts, dtype=jnp.int32)[None, :]).astype(jnp.int32)
    chosen = chosen_int.astype(jnp.float32)
    logits = multiply(expert_in, router_weight)
    gate = jax.nn.sigmoid(jnp.sum(logits * chosen, axis=1))
    rank_of = jnp.arange(seq_len, dtype=jnp.int32)
    earlier = (rank_of[:, None] > rank_of[None, :]).astype(jnp.bfloat16)
    position = jnp.sum(multiply(earlier, chosen.astype(jnp.bfloat16)) * chosen, axis=1).astype(jnp.int32)
    kept = position < capacity
    slots = jnp.where(kept, route_ids * capacity + position, experts * capacity)
    scaled_grad = (gate[:, None] * out_grad).astype(jnp.bfloat16)
    sent_width = expert_in.shape[1]
    send_in = (
        jnp.zeros((experts * capacity + 1, sent_width), jnp.bfloat16).at[slots].set(expert_in)[:-1]
    )
    send_grad = (
        jnp.zeros((experts * capacity + 1, sent_width), jnp.bfloat16)
        .at[slots]
        .set(scaled_grad)[:-1]
    )
    recv_in, recv_grad = (
        lax.all_to_all(
            send_in.reshape(experts, capacity, sent_width),
            "wide",
            split_axis=0,
            concat_axis=0,
            tiled=True,
        ),
        lax.all_to_all(
            send_grad.reshape(experts, capacity, sent_width),
            "wide",
            split_axis=0,
            concat_axis=0,
            tiled=True,
        ),
    )
    rows_in = recv_in.reshape(-1, model_width)
    rows_grad = recv_grad.reshape(-1, model_width)
    pre_act = multiply(rows_in, expert_up[0]) + up_bias[0]
    hidden_act = jax.nn.gelu(pre_act).astype(jnp.bfloat16)
    partial_out = multiply(hidden_act, expert_down[0])
    up_grad = contract_cols(rows_grad, expert_down[0])
    d_pre = jax.vjp(jax.nn.gelu, pre_act)[1](up_grad)[0].astype(jnp.bfloat16)
    partial_back = contract_cols(d_pre, expert_up[0])
    grad_down = contract_rows(hidden_act, rows_grad)
    grad_dbias = jnp.sum(rows_grad.astype(jnp.float32), axis=0)
    grad_up = contract_rows(rows_in, d_pre)
    grad_ubias = jnp.sum(d_pre.astype(jnp.float32), axis=0)
    out_sum, back_sum = (
        lax.psum(partial_out.astype(jnp.bfloat16), "tp").astype(jnp.float32),
        lax.psum(partial_back.astype(jnp.bfloat16), "tp").astype(jnp.float32),
    )
    bias_part = down_bias[0]
    outgoing = (out_sum + bias_part).astype(jnp.bfloat16).reshape(experts, capacity, -1)
    back_rows = back_sum.astype(jnp.bfloat16).reshape(experts, capacity, -1)
    incoming, arriving = (
        lax.all_to_all(outgoing, "wide", split_axis=0, concat_axis=0, tiled=True),
        lax.all_to_all(back_rows, "wide", split_axis=0, concat_axis=0, tiled=True),
    )
    safe_slots = jnp.minimum(slots, experts * capacity - 1)
    returned = jnp.where(
        kept[:, None], incoming.reshape(-1, model_width)[safe_slots].astype(jnp.float32), 0.0
    )
    result = hidden + gate[:, None] * returned
    d_gate = jnp.sum(out_grad * returned, axis=1)
    d_logit = (d_gate * gate * (1.0 - gate))[:, None] * chosen
    grad_router = jnp.dot(expert_in.astype(jnp.float32).T, d_logit, precision=HIGH)
    d_norm_two = jnp.dot(d_logit, router_weight.astype(jnp.float32).T, precision=HIGH)
    d_norm_two = d_norm_two + jnp.where(
        kept[:, None], arriving.reshape(-1, model_width)[safe_slots].astype(jnp.float32), 0.0
    )
    grad_second_gain = jnp.sum(d_norm_two * second_unit, axis=0)
    d_hidden = out_grad + rms_back(d_norm_two * expert_gain, second_unit, second_scale)
    d_mixed = d_hidden.astype(jnp.bfloat16)
    d_gated = multiply(d_mixed, gathered_out)
    grad_out = contract_rows(d_mixed, gated)
    d_scan = d_gated * z_gate
    d_z = (d_gated * scan_out * silu_slope(z_branch)).astype(jnp.bfloat16)
    d_step_pre, d_inner, d_proj, grad_step, grad_sbias, grad_rates, grad_skip = scan_bwd(
        projected, inner_act, carry_mask, step_size, states, starts, d_scan, tall_proj, log_rates, skip_gain[None], step_rank
    )
    grad_step, grad_sbias, grad_skip = grad_step[:step_rank], grad_sbias[0], grad_skip[0]
    d_projected = lax.psum(d_proj.astype(jnp.bfloat16), "tp")
    grad_state = contract_rows(inner_act, d_projected)[:, : state_proj.shape[1]]
    d_inner = d_inner + contract_cols(d_projected, wide_proj)
    d_conv = d_inner * silu_slope(conv_sum)
    grad_cbias = jnp.sum(d_conv, axis=0)
    conv_rows = []
    d_input = jnp.zeros_like(d_conv)
    for offset in range(conv_taps):
        conv_rows.append(
            jnp.sum(d_conv * conv_masks[offset] * shifted_down(x_branch, offset), axis=0)
        )
        d_input = d_input + conv_weight[conv_taps - 1 - offset] * shifted_up(
            conv_masks[offset] * d_conv, offset
        )
    grad_conv = jnp.stack(conv_rows[::-1])
    d_x_branch = d_input.astype(jnp.bfloat16)
    grad_in_x = contract_rows(normed, d_x_branch)
    grad_in_z = contract_rows(normed, d_z)
    d_normed = lax.psum(
        (contract_cols(d_x_branch, gathered_x) + contract_cols(d_z, gathered_z)).astype(
            jnp.bfloat16
        ),
        "tp",
    ).astype(jnp.float32)
    grad_first_gain = jnp.sum(d_normed * first_unit, axis=0)
    tokens_grad = d_hidden + rms_back(d_normed * mixer_gain, first_unit, first_scale)
    grad_in_x, grad_in_z, grad_out = (
        summed_on_arrival(grad_in_x.astype(jnp.bfloat16), "wide", 0),
        summed_on_arrival(grad_in_z.astype(jnp.bfloat16), "wide", 0),
        summed_on_arrival(grad_out.astype(jnp.bfloat16), "wide", 0),
    )
    (
        grad_first_gain,
        grad_conv,
        grad_cbias,
        grad_state,
        grad_step,
        grad_sbias,
        grad_rates,
        grad_skip,
        grad_second_gain,
        grad_router,
    ) = lax.psum(
        (
            grad_first_gain,
            grad_conv,
            grad_cbias,
            grad_state,
            grad_step,
            grad_sbias,
            grad_rates,
            grad_skip,
            grad_second_gain,
            grad_router,
        ),
        "wide",
    )
    return (
        result,
        tokens_grad,
        grad_first_gain,
        grad_in_x,
        grad_in_z,
        grad_conv,
        grad_cbias,
        grad_state,
        grad_step,
        grad_sbias,
        grad_rates,
        grad_skip,
        grad_out,
        grad_second_gain,
        grad_router,
        grad_up[None],
        grad_ubias[None],
        grad_down[None],
        grad_dbias[None],
    )


def fast_device(
    tokens,
    segment_ids,
    routes,
    out_grad,
    mixer_gain,
    in_proj_x,
    in_proj_z,
    conv_weight,
    conv_bias,
    state_proj,
    step_proj,
    step_bias,
    log_rates,
    skip_gain,
    out_proj,
    expert_gain,
    router_weight,
    expert_up,
    up_bias,
    expert_down,
    down_bias,
):
    seq_len, model_width = tokens.shape
    conv_taps = conv_weight.shape[0]
    step_rank = step_proj.shape[0]
    experts = router_weight.shape[1]
    capacity = 5 * seq_len // (4 * experts)
    doc_ids = segment_ids[0]
    conv_masks = [same_document(doc_ids, offset)[:, None] for offset in range(conv_taps)]
    masks = jnp.pad(jnp.concatenate(conv_masks, axis=1), ((0, 8), (0, 8 - conv_taps)))
    wide_proj = jnp.pad(state_proj, ((0, 0), (0, LANES - state_proj.shape[1])))
    tall_proj = jnp.pad(step_proj, ((0, LANES - step_rank), (0, 0)))
    wide = lax.axis_size("wide")
    states = log_rates.shape[0]
    chosen = (routes == jnp.arange(experts, dtype=jnp.int32)[None, :]).astype(jnp.float32)
    rank_of = jnp.arange(seq_len, dtype=jnp.int32)
    earlier = (rank_of[:, None] > rank_of[None, :]).astype(jnp.bfloat16)
    position = jnp.sum(multiply(earlier, chosen.astype(jnp.bfloat16)) * chosen, axis=1).astype(jnp.int32)
    slots = jnp.where(position < capacity, routes[:, 0] * capacity + position, experts * capacity)
    slot_row, slot_col = slots[None], slots[:, None]
    wide_router = jnp.pad(router_weight, ((0, 0), (0, LANES - experts)))
    router_rows = router_weight.astype(jnp.float32).T
    carry_mask = same_document(doc_ids, 1)[:, None]

    first_scale, normed, x_branch, z_branch, conv_sum, inner_act, projected, gathered_x, gathered_z, gathered_out = front(
        wide, conv_taps, tokens, mixer_gain, in_proj_x, in_proj_z, out_proj, conv_weight, conv_bias, wide_proj, masks
    )
    scan_out, step_size, held, starts, gated, mixed, grads_in = scan_mix(
        projected, inner_act, carry_mask, tall_proj, step_bias, log_rates, skip_gain, z_branch, gathered_out, out_grad, slot_row,
        step_rank, wide, capacity,
    )
    grad_up, grad_ubias, grad_down, grad_dbias, returned, terms, router_grad = experts_block(
        wide, capacity, tokens, mixed, grads_in, slot_row, expert_gain, wide_router, router_rows,
        expert_up[0], up_bias, expert_down[0], down_bias,
    )
    d_inner, d_proj, grad_step, grad_sbias, grad_rates, grad_skip, d_hidden, d_mixed, d_z, grad_second, gated_out = scan_back(
        wide, projected, inner_act, carry_mask, step_size, held, starts, tall_proj, log_rates, skip_gain, tokens, mixed, out_grad,
        slot_col, returned, expert_gain, z_branch, scan_out, gathered_out, terms, step_rank,
    )
    d_normed, grad_in_x, grad_in_z, grad_out, small = tail(
        wide, conv_taps, step_rank, d_proj, d_inner, inner_act, x_branch, conv_sum, masks, wide_proj, conv_weight, normed, d_z,
        d_mixed, gated, gathered_x, gathered_z, tokens, first_scale, grad_step, grad_sbias, grad_rates, grad_skip, grad_second, router_grad,
    )
    outs = finish(
        step_rank, states, experts, tokens, mixed, slot_col, gated_out, d_hidden, d_normed, first_scale, mixer_gain, small,
        grad_in_x, grad_in_z, grad_out, grad_up, grad_down,
    )
    return (*outs[:15], outs[15][None], grad_ubias, outs[16][None], grad_dbias)


def solution(mesh):
    in_specs = (
        P("wide", None),
        P("wide", None),
        P("wide", None),
        P("wide", None),
        P(),
        P("wide", "tp"),
        P("wide", "tp"),
        P(None, "tp"),
        P("tp"),
        P("tp", None),
        P(None, "tp"),
        P("tp"),
        P(None, "tp"),
        P("tp"),
        P("wide", "tp"),
        P(),
        P(),
        P("wide", None, "tp"),
        P("wide", "tp"),
        P("wide", "tp", None),
        P("wide", None),
    )
    out_specs = (
        P("wide", None),
        P("wide", None),
        P(),
        P("wide", "tp"),
        P("wide", "tp"),
        P(None, "tp"),
        P("tp"),
        P("tp", None),
        P(None, "tp"),
        P("tp"),
        P(None, "tp"),
        P("tp"),
        P("wide", "tp"),
        P(),
        P(),
        P("wide", None, "tp"),
        P("wide", "tp"),
        P("wide", "tp", None),
        P("wide", None),
    )
    wide, line = mesh.shape["wide"], mesh.shape["tp"]
    per_device = fast_device if line == 4 and wide == 8 else plain_device
    return jax.shard_map(
        per_device, mesh=mesh, in_specs=in_specs, out_specs=out_specs, check_vma=False
    )
```

```python
import functools

import jax
import jax.numpy as jnp
from jax import lax
from jax.experimental import pallas as pl
from jax.experimental.pallas import tpu as pltpu
from jax.sharding import PartitionSpec as P

EPS = 1e-05
HIGH = lax.Precision.HIGHEST


def in_blocks(shard, dim, size):
    before, after = (shard.shape[:dim], shard.shape[dim + 1 :])
    return jnp.moveaxis(shard.reshape(*before, size, -1, *after), dim, 0)


def summed_on_arrival(shard, axis, dim):
    size = lax.axis_size(axis)
    parts = lax.all_to_all(in_blocks(shard, dim, size), axis, 0, 0, tiled=True)
    return jnp.sum(parts.astype(jnp.float32), axis=0)


def multiply(left, right):
    return jnp.dot(left, right, preferred_element_type=jnp.float32)


def contract_rows(left, right):
    return lax.dot_general(
        left, right, (((0,), (0,)), ((), ())), preferred_element_type=jnp.float32
    )


def contract_cols(left, right):
    return lax.dot_general(
        left, right, (((1,), (1,)), ((), ())), preferred_element_type=jnp.float32
    )


def shifted_down(values, steps):
    if steps == 0:
        return values
    filler = jnp.zeros((steps,) + values.shape[1:], values.dtype)
    return jnp.concatenate([filler, values[:-steps]], axis=0)


def shifted_up(values, steps):
    if steps == 0:
        return values
    filler = jnp.zeros((steps,) + values.shape[1:], values.dtype)
    return jnp.concatenate([values[steps:], filler], axis=0)


def same_document(doc_ids, steps):
    if steps == 0:
        return jnp.ones(doc_ids.shape, jnp.float32)
    filler = jnp.full((steps,), -1, jnp.int32)
    earlier = jnp.concatenate([filler, doc_ids[:-steps]])
    return (earlier == doc_ids).astype(jnp.float32)


def silu_slope(values):
    logistic = jax.nn.sigmoid(values)
    return logistic * (1.0 + values * (1.0 - logistic))


def rms_back(grad_unit, unit, scale):
    return scale * (grad_unit - unit * jnp.mean(grad_unit * unit, axis=1, keepdims=True))


LOG2E = 1.4426950408889634
LANES = 128
F32, BF16 = jnp.float32, jnp.bfloat16
MESH = pl.DeviceIdType.MESH


def fold_rows(parts, masks):
    m4, m2, m1 = masks

    def join(a, b, m, shift):
        return jnp.where(m, a, b) + pltpu.roll(jnp.where(m, b, a), shift, 0)

    c = [join(parts[i], parts[i + 4], m4[i], 4) for i in range(4)]
    d = [join(c[i], c[i + 2], m2[i], 6) for i in range(2)]
    return join(d[0], d[1], m1, 7)


def fold_masks(width):
    sub = lax.broadcasted_iota(jnp.int32, (8, width), 0)
    m4 = [((sub - i) & 7) < 4 for i in range(4)]
    m2 = [((sub - i) & 2) == 0 for i in range(2)]
    m1 = (sub & 1) == 0
    return m4, m2, m1


def softplus(v):
    return jnp.maximum(v, 0.0) + jnp.log1p(jnp.exp(-jnp.abs(v)))


def row(ref, c, t, ns):
    one = ref[c, pl.ds(t, 8, stride=0), :]
    return jnp.concatenate([one] * (ns // 8), axis=0)


def spread(ref, value):
    for c in range(ref.shape[0]):
        ref[c] = value[:, c * LANES:(c + 1) * LANES]


def own_column(ns, rank):
    lane = lax.broadcasted_iota(jnp.int32, (ns, LANES), 1)
    n = lax.broadcasted_iota(jnp.int32, (ns, LANES), 0)
    return (lane == rank + n) | (lane == rank + ns + n)


def coefficient_rows(ns, rank, proj_ref, first):
    own = own_column(ns, rank)
    lane = lax.broadcasted_iota(jnp.int32, (LANES, 2 * LANES), 1)
    k = lax.broadcasted_iota(jnp.int32, (LANES, 2 * LANES), 0)
    pick = ((lane < LANES) & (k >= rank) & (k < rank + ns)) | ((lane >= LANES) & (k >= rank + ns) & (k < rank + 2 * ns))
    pick = jnp.where(pick, 1.0, 0.0).astype(BF16)
    rows = []
    for j in range(8):
        one = proj_ref[pl.ds(first + j, 8, stride=0), :]
        rows.append(jnp.where(own, jnp.concatenate([one] * (ns // 8), axis=0), 0.0).astype(BF16))
    return jnp.dot(jnp.concatenate(rows, axis=0), pick, preferred_element_type=F32)


def forward_tokens(ns, rank, proj_ref, stepd_s, drive_s, r2_s, states_ref, scan_ref, state, wide_a, wide_b):
    tb = proj_ref.shape[0]
    groups = len(state)
    masks = fold_masks(LANES)

    def eight(first, wide, state):
        parts = [[] for _ in range(groups)]
        for j in range(8):
            t = first + j
            in_b = wide[j * ns:(j + 1) * ns, :LANES]
            out_b = wide[j * ns:(j + 1) * ns, LANES:]
            for c in range(groups):
                dec = jnp.exp2(row(stepd_s, c, t, ns) * r2_s[c])
                s = dec * state[c] + row(drive_s, c, t, ns) * in_b
                state[c] = s
                states_ref[pl.ds(pl.multiple_of(t * ns, ns), ns), pl.ds(c * LANES, LANES)] = s.astype(BF16)
                z = out_b * s
                parts[c].append(sum(z[8 * k:8 * k + 8] for k in range(ns // 8)))
        for c in range(groups):
            scan_ref[pl.ds(pl.multiple_of(first, 8), 8), pl.ds(c * LANES, LANES)] = fold_rows(parts[c], masks)
        return state

    def body(g, state):
        state = list(state)
        first = g * 16
        wide_b[...] = coefficient_rows(ns, rank, proj_ref, first + 8)
        state = eight(first, wide_a, state)
        wide_a[...] = coefficient_rows(ns, rank, proj_ref, jnp.minimum(first + 16, tb - 8))
        return tuple(eight(first + 8, wide_b, state))

    wide_a[...] = coefficient_rows(ns, rank, proj_ref, 0)
    return lax.fori_loop(0, tb // 16, body, state)


def backward_tokens(ns, rank, proj_ref, states_ref, starts_ref, stepd_s, drive_s, dscan_s, step_s, r2_s, coeff_s, exps_s, dproj_ref,
                    later, acc, wide_a, wide_b, sums_a, sums_b):
    tb = proj_ref.shape[0]
    groups = len(later)
    masks = fold_masks(LANES)
    own = own_column(ns, rank)
    k = lax.broadcasted_iota(jnp.int32, (2 * LANES, LANES), 0)
    lane = lax.broadcasted_iota(jnp.int32, (2 * LANES, LANES), 1)
    into = ((k < LANES) & (lane >= rank) & (lane < rank + ns)) | ((k >= LANES) & (lane >= rank + ns) & (lane < rank + 2 * ns))
    into = jnp.where(into, 1.0, 0.0).astype(BF16)

    def gather(sums, first):
        got = jnp.dot(sums[...], into, preferred_element_type=F32)
        parts = []
        for j in range(8):
            one = jnp.where(own, got[j * ns:(j + 1) * ns], 0.0)
            parts.append(sum(one[8 * q:8 * q + 8] for q in range(ns // 8)))
        dproj_ref[pl.ds(pl.multiple_of(first, 8), 8), :] = fold_rows(parts, masks)

    def eight(first, wide, sums, later, acc):
        cparts = [[None] * 8 for _ in range(groups)]
        eparts = [[None] * 8 for _ in range(groups)]
        last = pl.ds(pl.multiple_of((first + 7) * ns, ns), ns)
        now = [states_ref[last, pl.ds(c * LANES, LANES)].astype(F32) for c in range(groups)]
        for j in range(7, -1, -1):
            t = first + j
            prior = pl.ds(pl.multiple_of((t - 1 if j else jnp.maximum(t - 1, 0)) * ns, ns), ns)
            here = slice(j * ns, (j + 1) * ns)
            in_b = wide[here, :LANES]
            out_b = wide[here, LANES:]
            din = dout = None
            for c in range(groups):
                cols = pl.ds(c * LANES, LANES)
                before = states_ref[prior, cols].astype(F32)
                if j == 0:
                    before = jnp.where(jnp.full((ns, LANES), t, jnp.int32) == 0, starts_ref[0, :, cols], before)
                r2 = r2_s[c]
                dec = jnp.exp2(row(stepd_s, c, t, ns) * r2)
                ds = row(dscan_s, c, t, ns)
                d = later[c] + out_b * ds
                later[c] = dec * d
                dexp = later[c] * before
                e = dexp * r2
                cf = d * in_b
                cparts[c][j] = sum(cf[8 * q:8 * q + 8] for q in range(ns // 8))
                eparts[c][j] = sum(e[8 * q:8 * q + 8] for q in range(ns // 8))
                acc[c] = acc[c] + dexp * row(step_s, c, t, ns)
                a = d * row(drive_s, c, t, ns)
                b = now[c] * ds
                din = a if din is None else din + a
                dout = b if dout is None else dout + b
                now[c] = before
            sums[here, :LANES] = din.astype(BF16)
            sums[here, LANES:] = dout.astype(BF16)
        rows = pl.ds(pl.multiple_of(first, 8), 8)
        for c in range(groups):
            cols = pl.ds(c * LANES, LANES)
            coeff_s[rows, cols] = fold_rows(cparts[c], masks)
            exps_s[rows, cols] = fold_rows(eparts[c], masks)
        return later, acc

    def body(k, carry):
        later, acc = [list(v) for v in carry]
        first = tb - 16 - k * 16
        gather(sums_a, jnp.minimum(first + 16, tb - 8))
        wide_a[...] = coefficient_rows(ns, rank, proj_ref, first)
        later, acc = eight(first + 8, wide_b, sums_b, later, acc)
        gather(sums_b, first + 8)
        wide_b[...] = coefficient_rows(ns, rank, proj_ref, jnp.maximum(first - 8, 0))
        later, acc = eight(first, wide_a, sums_a, later, acc)
        return tuple(later), tuple(acc)

    wide_b[...] = coefficient_rows(ns, rank, proj_ref, tb - 8)
    sums_a[...] = jnp.zeros_like(sums_a)
    later, acc = lax.fori_loop(0, tb // 16, body, (later, acc))
    gather(sums_a, 0)
    return later, acc


def scan_fwd_kernel(ns, rank, proj_ref, inner_ref, keep_ref, sproj_ref, sbias_ref, lr_ref, skip_ref,
                    scan_ref, step_ref, states_ref, starts_ref, state_s, stepd_s, drive_s, r2_s, wide_a, wide_b):
    tb, ch = inner_ref.shape
    groups = ch // LANES
    i = pl.program_id(0)

    @pl.when(i == 0)
    def _():
        state_s[...] = jnp.zeros_like(state_s)
        spread(r2_s, jnp.exp(lr_ref[...]) * (-LOG2E))

    step_in = proj_ref[...].astype(BF16)
    pre = jnp.dot(step_in, sproj_ref[...], preferred_element_type=F32) + sbias_ref[...]
    step = softplus(pre)
    step_ref[...] = step
    spread(stepd_s, jnp.where(keep_ref[...] > 0.0, step, 1e30))
    inner = inner_ref[...].astype(F32)
    spread(drive_s, step * inner)
    starts_ref[0] = state_s[...]
    start = tuple(state_s[:, c * LANES:(c + 1) * LANES] for c in range(groups))
    state = forward_tokens(ns, rank, proj_ref, stepd_s, drive_s, r2_s, states_ref, scan_ref, start, wide_a, wide_b)
    for c in range(groups):
        state_s[:, c * LANES:(c + 1) * LANES] = state[c]
    scan_ref[...] += skip_ref[...] * inner


def scan_fwd(proj, inner, keep, sproj, sbias, log_rates, skip, rank):
    seq, ch = inner.shape
    ns = log_rates.shape[0]
    tb = LANES
    nb = seq // tb
    full = lambda a: pl.BlockSpec(a.shape, lambda i: (0,) * a.ndim)
    rows = pl.BlockSpec((tb, ch), lambda i: (i, 0))
    return pl.pallas_call(
        functools.partial(scan_fwd_kernel, ns, rank),
        grid=(nb,),
        in_specs=[pl.BlockSpec((tb, LANES), lambda i: (i, 0)), rows, pl.BlockSpec((tb, 1), lambda i: (i, 0)),
                  full(sproj), full(sbias), full(log_rates), full(skip)],
        out_specs=[rows, rows, pl.BlockSpec((tb * ns, ch), lambda i: (i, 0)), pl.BlockSpec((1, ns, ch), lambda i: (i, 0, 0))],
        out_shape=[jax.ShapeDtypeStruct((seq, ch), F32), jax.ShapeDtypeStruct((seq, ch), F32),
                   jax.ShapeDtypeStruct((seq * ns, ch), BF16), jax.ShapeDtypeStruct((nb, ns, ch), F32)],
        scratch_shapes=[pltpu.VMEM((ns, ch), F32)] + [pltpu.VMEM((ch // LANES, tb, LANES), F32)] * 2 + [pltpu.VMEM((ch // LANES, ns, LANES), F32),
                        *[pltpu.VMEM((8 * ns, 2 * LANES), F32)] * 2],
        compiler_params=pltpu.CompilerParams(vmem_limit_bytes=48 << 20),
        name="scan_fwd",
    )(proj, inner, keep, sproj, sbias, log_rates, skip)


def scan_bwd_kernel(ns, rank, proj_ref, inner_ref, keep_ref, step_ref, states_ref, starts_ref, dscan_ref, sproj_ref, lr_ref, skip_ref,
                    dpre_ref, dinner_ref, dproj_ref, gstep_ref, gsbias_ref, grates_ref, gskip_ref,
                    carry_s, stepd_s, drive_s, dscan_s, step_s, r2_s, coeff_s, exps_s, acc_s, wide_a, wide_b, sums_a, sums_b):
    tb, ch = inner_ref.shape
    groups = ch // LANES
    i = pl.program_id(0)

    @pl.when(i == 0)
    def _():
        carry_s[...] = jnp.zeros_like(carry_s)
        acc_s[...] = jnp.zeros_like(acc_s)
        spread(r2_s, jnp.exp(lr_ref[...]) * (-LOG2E))
        gstep_ref[...] = jnp.zeros_like(gstep_ref)
        gsbias_ref[...] = jnp.zeros_like(gsbias_ref)
        gskip_ref[...] = jnp.zeros_like(gskip_ref)

    step = step_ref[...]
    inner = inner_ref[...].astype(F32)
    dscan = dscan_ref[...]
    spread(stepd_s, jnp.where(keep_ref[...] > 0.0, step, 1e30))
    spread(drive_s, step * inner)
    spread(dscan_s, dscan)
    spread(step_s, step)
    pick = lambda ref: tuple(ref[:, c * LANES:(c + 1) * LANES] for c in range(groups))
    later, acc = backward_tokens(ns, rank, proj_ref, states_ref, starts_ref, stepd_s, drive_s, dscan_s, step_s, r2_s, coeff_s, exps_s,
                                 dproj_ref, pick(carry_s), pick(acc_s), wide_a, wide_b, sums_a, sums_b)
    for c in range(groups):
        carry_s[:, c * LANES:(c + 1) * LANES] = later[c]
        acc_s[:, c * LANES:(c + 1) * LANES] = acc[c]
    coeff = coeff_s[...]
    d_step = coeff * inner + exps_s[...] * (1.0 / LOG2E)
    d_pre = (d_step * (1.0 - jnp.exp(-step))).astype(BF16)
    dpre_ref[...] = d_pre
    dinner_ref[...] = dscan * skip_ref[...] + step * coeff
    step_in = proj_ref[...].astype(BF16)
    gstep_ref[...] += lax.dot_general(step_in, d_pre, (((0,), (0,)), ((), ())), preferred_element_type=F32)
    gsbias_ref[...] += jnp.sum(d_pre.astype(F32), axis=0, keepdims=True)
    gskip_ref[...] += jnp.sum(dscan * inner, axis=0, keepdims=True)
    dproj_ref[...] += lax.dot_general(d_pre, sproj_ref[...], (((1,), (1,)), ((), ())), preferred_element_type=F32)

    @pl.when(i == pl.num_programs(0) - 1)
    def _():
        grates_ref[...] = -jnp.exp(lr_ref[...]) * acc_s[...]


def scan_bwd(proj, inner, keep, step, states, starts, dscan, sproj, log_rates, skip, rank):
    seq, ch = inner.shape
    ns = log_rates.shape[0]
    tb = LANES
    nb = seq // tb
    full = lambda a: pl.BlockSpec(a.shape, lambda i: (0,) * a.ndim)
    rows = pl.BlockSpec((tb, ch), lambda i: (nb - 1 - i, 0))
    prow = pl.BlockSpec((tb, LANES), lambda i: (nb - 1 - i, 0))
    whole = lambda *s: pl.BlockSpec(s, lambda i: (0,) * len(s))
    shape = jax.ShapeDtypeStruct
    return pl.pallas_call(
        functools.partial(scan_bwd_kernel, ns, rank),
        grid=(nb,),
        in_specs=[prow, rows, pl.BlockSpec((tb, 1), lambda i: (nb - 1 - i, 0)), rows,
                  pl.BlockSpec((tb * ns, ch), lambda i: (nb - 1 - i, 0)), pl.BlockSpec((1, ns, ch), lambda i: (nb - 1 - i, 0, 0)),
                  rows, full(sproj), full(log_rates), full(skip)],
        out_specs=[rows, rows, prow, whole(LANES, ch), whole(1, ch), whole(ns, ch), whole(1, ch)],
        out_shape=[shape((seq, ch), BF16), shape((seq, ch), F32), shape((seq, LANES), F32), shape((LANES, ch), F32), shape((1, ch), F32),
                   shape((ns, ch), F32), shape((1, ch), F32)],
        scratch_shapes=[pltpu.VMEM((ns, ch), F32)] + [pltpu.VMEM((ch // LANES, tb, LANES), F32)] * 4 + [pltpu.VMEM((ch // LANES, ns, LANES), F32),
                        pltpu.VMEM((tb, ch), F32), pltpu.VMEM((tb, ch), F32), pltpu.VMEM((ns, ch), F32),
                        *[pltpu.VMEM((8 * ns, 2 * LANES), F32)] * 2, *[pltpu.VMEM((8 * ns, 2 * LANES), BF16)] * 2],
        compiler_params=pltpu.CompilerParams(vmem_limit_bytes=48 << 20),
        name="scan_bwd",
    )(proj, inner, keep, step, states, starts, dscan, sproj, log_rates, skip)


def as_row(ref):
    return ref[...].reshape(1, ref.shape[0])


def line_roles():
    me = lax.axis_index("tp")
    end = (me == 0) | (me == 3)
    mate = jnp.where(me < 2, 1 - me, 5 - me)
    return end, jnp.logical_not(end), mate, 3 - me


LINE = 4


def greet(wide):
    barrier = pltpu.get_barrier_semaphore()
    for axis, size in (("tp", LINE), ("wide", wide)):
        me = lax.axis_index(axis)
        for k in range(1, size):
            pl.semaphore_signal(barrier, inc=1, device_id={axis: lax.rem(me + k, size)}, device_id_type=MESH)
    pl.semaphore_wait(barrier, LINE + wide - 2)


class LineSum:
    def __init__(self, roles, rows, own, near, half, far, total, sends, arrivals):
        self.end, self.mid, self.mate, self.other = roles
        self.rows, self.own, self.near, self.half, self.far, self.total = rows, own, near, half, far, total
        self.sends, self.arrivals = sends, arrivals

    def part(self, ref, k):
        return ref.at[pl.ds(pl.multiple_of(k * self.rows, self.rows), self.rows)]

    def copy(self, source, target, hop, k, to):
        return pltpu.make_async_remote_copy(
            self.part(source, k), self.part(target, k), self.sends.at[hop, k], self.arrivals.at[hop, k],
            device_id={"tp": to}, device_id_type=MESH)

    def up(self, k):
        return self.copy(self.own, self.near, 0, k, self.mate)

    def across(self, k):
        return self.copy(self.half, self.far, 1, k, self.other)

    def down(self, k):
        return self.copy(self.total, self.total, 2, k, self.mate)

    def add(self, a, b, c, k):
        self.part(c, k)[...] = (self.part(a, k)[...].astype(F32) + self.part(b, k)[...].astype(F32)).astype(BF16)

    def first(self, k):
        self.up(k).wait_recv()
        self.add(self.own, self.near, self.half, k)
        self.across(k).start()

    def second(self, k):
        self.across(k).wait_recv()
        self.add(self.half, self.far, self.total, k)
        self.down(k).start()

    def sent(self, count):
        for k in range(count):
            @pl.when(self.end)
            def _():
                self.up(k).wait_send()

            @pl.when(self.mid)
            def _():
                self.across(k).wait_send()
                self.down(k).wait_send()


def pack_rows(rank, states, experts, width, ch, wide):
    rows = 8 + states + rank + (rank + 2 * states) + 8 + (width // ch) * experts
    return -(-rows // (8 * wide)) * (8 * wide)


def finish_kernel(rank, states, tokens_ref, mixed_ref, scol_ref, got_ref, dhidden_ref, dn_ref, scale_ref, gain_ref, small_ref,
                  gx_ref, gz_ref, go_ref, gup_ref, gdown_ref,
                  result_ref, tgrad_ref, first_ref, gx_out, gz_out, cw_ref, cb_ref, state_ref, step_ref, sb_ref, rates_ref, skip_ref, go_out,
                  second_ref, router_ref, gup_out, gdown_out, sems):
    i = pl.program_id(0)
    ch = small_ref.shape[1]
    width, experts = router_ref.shape
    pairs = ((gx_ref, gx_out), (gz_ref, gz_out), (go_ref, go_out), (gup_ref, gup_out), (gdown_ref, gdown_out))
    moves = [pltpu.make_async_copy(a, b, sems.at[n]) for n, (a, b) in enumerate(pairs)]

    @pl.when(i == 0)
    def _():
        for move in moves:
            move.start()
        flat = lambda r: small_ref[r:r + 1, :].reshape(ch)
        cb_ref[...] = flat(0)
        sb_ref[...] = flat(1)
        skip_ref[...] = flat(2)
        cw_ref[...] = small_ref[4:8, :]
        at = 8
        rates_ref[...] = small_ref[at:at + states, :]
        at += states
        step_ref[...] = small_ref[at:at + rank, :]
        at += rank
        held = rank + 2 * states
        state_ref[...] = small_ref[at:at + held, :].T
        at += held
        halves = width // ch
        for h in range(halves):
            cols = slice(h * ch, (h + 1) * ch)
            first_ref[cols] = flat(at + h)
            second_ref[cols] = flat(at + halves + h)
            router_ref[cols, :] = small_ref[at + 8 + h * experts:at + 8 + (h + 1) * experts, :].T

    ids = lax.broadcasted_iota(jnp.int32, (scol_ref.shape[0], got_ref.shape[0]), 1)
    chosen = jnp.where(ids == scol_ref[...], 1.0, 0.0).astype(BF16)
    tokens = tokens_ref[...]
    result_ref[...] = tokens + mixed_ref[...].astype(F32) + jnp.dot(chosen, got_ref[...], preferred_element_type=F32)
    scale = scale_ref[...]
    unit = tokens * scale
    through = dn_ref[...].astype(F32) * as_row(gain_ref)
    mean = jnp.mean(through * unit, axis=1, keepdims=True)
    tgrad_ref[...] = dhidden_ref[...] + scale * (through - unit * mean)

    @pl.when(i == pl.num_programs(0) - 1)
    def _():
        for move in moves:
            move.wait()


def finish(rank, states, experts, *operands):
    tokens, mixed, scol, got, dhidden, dn, scale, gain, small, gx, gz, go, gup, gdown = operands
    seq, width = tokens.shape
    ch = small.shape[1]
    tb = LANES
    row = lambda n: pl.BlockSpec((tb, n), lambda i: (i, 0))
    full = lambda a: pl.BlockSpec(a.shape, lambda i: (0,) * a.ndim)
    hbm = pl.BlockSpec(memory_space=pl.ANY)
    whole = lambda *s: pl.BlockSpec(s, lambda i: (0,) * len(s))
    sizes = [(width,), gx.shape, gz.shape, (4, ch), (ch,), (ch, rank + 2 * states), (rank, ch), (ch,), (states, ch), (ch,), go.shape,
             (width,), (width, experts), gup.shape, gdown.shape]
    copied = {1, 2, 10, 13, 14}
    return pl.pallas_call(
        functools.partial(finish_kernel, rank, states),
        grid=(seq // tb,),
        in_specs=[row(width), row(width), row(1), full(got), row(width), row(width), row(1), full(gain), full(small), *[hbm] * 5],
        out_specs=[row(width), row(width), *[hbm if n in copied else whole(*size) for n, size in enumerate(sizes)]],
        out_shape=[jax.ShapeDtypeStruct(size, F32) for size in [(seq, width), (seq, width), *sizes]],
        scratch_shapes=[pltpu.SemaphoreType.DMA((5,))],
        compiler_params=pltpu.CompilerParams(vmem_limit_bytes=40 << 20),
        name="finish",
    )(*operands)


def mixer_back_kernel(ns, rank, wide, taps, proj_ref, keep_ref, step_ref, states_ref, starts_ref, tokens_ref, mixed_ref, ograd_ref, scol_ref, z_ref, scan_ref,
                      inner_ref, sproj_ref, lr_ref, skip_ref, ret_ref, gain_ref, wo_ref, term_ref,
                      x_ref, csum_ref, masks_ref, wproj_ref, cw_ref, normed_ref, gated_ref, wx_ref, wz_ref, first_gain_ref, grow_ref,
                      dhidden_ref, dn_ref, gx_ref, gz_ref, go_ref, small_ref, got_ref,
                      carry_s, stepd_s, drive_s, dscan_s, step_s, r2_s, coeff_s, exps_s, acc_s, dproj_s, wide_a, wide_b, sums_a, sums_b,
                      near_s, half_s, far_s, sends, arrivals, got_sends, got_arrivals,
                      dp_own, dp_near, dp_far, dp_sends, dp_arrivals, dn_own, dn_near, dn_far, dn_sends, dn_arrivals,
                      prod_s, inbox_s, prod_sends, prod_arrivals, pack_s, pack_in, small_s, pack_sends, pack_arrivals,
                      dinner_s, dmixed_s, dz_s, dconv_s, dx_s, gstep_s, state_s, first_s, second_s):
    seq, ch = inner_ref.shape
    width = normed_ref.shape[1]
    tb = LANES
    nb = seq // tb
    groups = ch // LANES
    i = pl.program_id(0)
    me = lax.axis_index("wide")
    roles = line_roles()
    end, mid, mate, other = roles
    cap = term_ref.shape[0] // wide
    line = LineSum(roles, cap, term_ref, near_s, half_s, far_s, far_s, sends, arrivals)
    dp = LineSum(roles, tb, dp_own, dp_near, dp_own, dp_far, dp_far, dp_sends, dp_arrivals)
    dn = LineSum(roles, tb, dn_own, dn_near, dn_own, dn_far, dn_far, dn_sends, dn_arrivals)
    block = width // wide
    turned = (((1,), (1,)), ((), ()))
    across_rows = (((0,), (0,)), ((), ()))

    def slot_rows(c):
        return pl.ds(pl.multiple_of(c * cap, cap), cap)

    def rows_of(b):
        return pl.ds(pl.multiple_of(b * tb, tb), tb)

    def give_back(c):
        return pltpu.make_async_remote_copy(
            far_s.at[slot_rows(c)], got_ref.at[slot_rows(me)], got_sends.at[c], got_arrivals.at[c],
            device_id={"wide": lax.rem(me + wide - c, wide)}, device_id_type=MESH)

    def return_chunk(c):
        @pl.when(c == 0)
        def _():
            here = pltpu.make_async_copy(far_s.at[slot_rows(0)], got_ref.at[slot_rows(me)], got_sends.at[0])
            here.start()
            here.wait()

        @pl.when(c != 0)
        def _():
            give_back(c).start()

    def deliver(which, k):
        to = lax.rem(me + k, wide)
        return pltpu.make_async_remote_copy(
            prod_s.at[which, pl.ds(pl.multiple_of(to * block, block), block)], inbox_s.at[which, k],
            prod_sends.at[which, k], prod_arrivals.at[which, k], device_id={"wide": to}, device_id_type=MESH)

    def product(which, left, right):
        def tile(j, _):
            cols = pl.ds(pl.multiple_of(j * LANES, LANES), LANES)
            got = lax.dot_general(left[:, cols], right[...], across_rows, preferred_element_type=F32)
            prod_s[which, cols, :] = got.astype(BF16)
            return 0

        lax.fori_loop(0, width // LANES, tile, 0)
        for k in range(1, wide):
            deliver(which, k).start()

    @pl.when(i == 0)
    def _():
        greet(wide)
        for ref in (carry_s, acc_s, gstep_s, state_s, first_s, second_s, pack_s):
            ref[...] = jnp.zeros_like(ref)
        dconv_s[pl.ds(seq, 8), :] = jnp.zeros((8, ch), F32)
        spread(r2_s, jnp.exp(lr_ref[...]) * (-LOG2E))

    @pl.when(end & (i < wide))
    def _():
        line.up(i).start()

    def scan_block():
        b = nb - 1 - i
        rows = rows_of(b)
        step = step_ref[...]
        inner = inner_ref[rows, :].astype(F32)
        hidden = tokens_ref[...] + mixed_ref[...].astype(F32)
        scale = lax.rsqrt(jnp.mean(hidden * hidden, axis=1, keepdims=True) + EPS)
        unit = hidden * scale
        ids = lax.broadcasted_iota(jnp.int32, (tb, wide * cap), 1)
        chosen = jnp.where(ids == scol_ref[...], 1.0, 0.0).astype(BF16)
        d_norm_two = jnp.dot(chosen, ret_ref[...], preferred_element_type=F32)
        second_s[...] += jnp.sum(d_norm_two * unit, axis=0, keepdims=True)
        through = d_norm_two * as_row(gain_ref)
        d_hidden = ograd_ref[...] + scale * (through - unit * jnp.mean(through * unit, axis=1, keepdims=True))
        dhidden_ref[...] = d_hidden
        d_mixed = d_hidden.astype(BF16)
        dmixed_s[rows, :] = d_mixed
        d_gated = jnp.dot(d_mixed, wo_ref[...], preferred_element_type=F32)
        z = z_ref[...]
        logistic = 1.0 / (1.0 + jnp.exp(-z))
        dz_s[rows, :] = (d_gated * scan_ref[...] * (logistic * (1.0 + z * (1.0 - logistic)))).astype(BF16)
        dscan = d_gated * (z * logistic)
        spread(stepd_s, jnp.where(keep_ref[...] > 0.0, step, 1e30))
        spread(drive_s, step * inner)
        spread(dscan_s, dscan)
        spread(step_s, step)
        pick = lambda ref: tuple(ref[:, c * LANES:(c + 1) * LANES] for c in range(groups))
        later, acc = backward_tokens(ns, rank, proj_ref, states_ref, starts_ref, stepd_s, drive_s, dscan_s, step_s, r2_s, coeff_s, exps_s,
                                     dproj_s, pick(carry_s), pick(acc_s), wide_a, wide_b, sums_a, sums_b)
        for c in range(groups):
            carry_s[:, c * LANES:(c + 1) * LANES] = later[c]
            acc_s[:, c * LANES:(c + 1) * LANES] = acc[c]
        coeff = coeff_s[...]
        d_step = coeff * inner + exps_s[...] * (1.0 / LOG2E)
        d_pre = (d_step * (1.0 - jnp.exp(-step))).astype(BF16)
        dinner_s[rows, :] = dscan * as_row(skip_ref) + step * coeff
        step_in = proj_ref[...].astype(BF16)
        gstep_s[...] += lax.dot_general(step_in, d_pre, across_rows, preferred_element_type=F32)
        pack_s[1:2, :] += jnp.sum(d_pre.astype(F32), axis=0, keepdims=True)
        pack_s[2:3, :] += jnp.sum(dscan * inner, axis=0, keepdims=True)
        both = dproj_s[...] + lax.dot_general(d_pre, sproj_ref[...], turned, preferred_element_type=F32)
        dp_own[rows, :] = both.astype(BF16)

        @pl.when(end)
        def _():
            dp.up(b).start()

    def conv_block(k):
        b = nb - 1 - k
        rows = rows_of(b)
        base = pl.multiple_of(b * tb, tb)

        @pl.when(end)
        def _():
            dp.down(b).wait_recv()

        d_proj = dp_far[rows, :]
        state_s[...] += lax.dot_general(d_proj, inner_ref[rows, :], across_rows, preferred_element_type=F32)
        d_inner = dinner_s[rows, :] + lax.dot_general(d_proj, wproj_ref[...], turned, preferred_element_type=F32)
        csum = csum_ref[rows, :]
        logistic = 1.0 / (1.0 + jnp.exp(-csum))
        d_conv = d_inner * (logistic * (1.0 + csum * (1.0 - logistic)))
        prior = x_ref[pl.ds(pl.multiple_of(jnp.maximum(base - 8, 0), 8), 8), :]
        history = jnp.concatenate([prior, x_ref[rows, :]], axis=0)
        ahead = jnp.concatenate([d_conv, dconv_s[pl.ds(pl.multiple_of(base + tb, 8), 8), :]], axis=0)
        dconv_s[rows, :] = d_conv
        same = masks_ref[pl.ds(base, tb + 8), :]
        d_x = cw_ref[taps - 1:taps, :] * d_conv
        pack_s[0:1, :] += jnp.sum(d_conv, axis=0, keepdims=True)
        pack_s[8 - 1:8, :] += jnp.sum(d_conv * history[8:, :], axis=0, keepdims=True)
        for s in range(1, taps):
            linked = same[:, s:s + 1] * ahead
            d_x = d_x + cw_ref[taps - 1 - s:taps - s, :] * linked[s:s + tb, :]
            pack_s[7 - s:8 - s, :] += jnp.sum(linked[:tb, :] * history[8 - s:8 - s + tb, :], axis=0, keepdims=True)
        d_x = d_x.astype(BF16)
        dx_s[rows, :] = d_x
        both = lax.dot_general(d_x, wx_ref[...], turned, preferred_element_type=F32)
        both = both + lax.dot_general(dz_s[rows, :], wz_ref[...], turned, preferred_element_type=F32)
        dn_own[rows, :] = both.astype(BF16)

        @pl.when(end)
        def _():
            dn.up(b).start()

    def last_block(k):
        b = nb - 1 - k
        rows = rows_of(b)

        @pl.when(end)
        def _():
            dn.down(b).wait_recv()

        d_normed = dn_far[rows, :]
        dn_ref[...] = d_normed
        first_s[...] += jnp.sum(d_normed.astype(F32) * normed_ref[rows, :].astype(F32), axis=0, keepdims=True)

    def at_step(lag, count, work):
        @pl.when((i >= lag) & (i < lag + count))
        def _():
            work(i - lag)

    def on_mid(lag, count, work):
        @pl.when(mid & (i >= lag) & (i < lag + count))
        def _():
            work(i - lag)

    def line_second(c):
        line.second(c)
        return_chunk(c)

    def line_down(c):
        line.down(c).wait_recv()
        return_chunk(c)

    at_step(0, nb, lambda k: scan_block())
    on_mid(1, nb, lambda k: dp.first(nb - 1 - k))
    on_mid(2, nb, lambda k: dp.second(nb - 1 - k))
    at_step(3, nb, conv_block)
    on_mid(4, nb, lambda k: dn.first(nb - 1 - k))
    on_mid(5, nb, lambda k: dn.second(nb - 1 - k))
    on_mid(1, wide, line.first)
    on_mid(2, wide, line_second)

    @pl.when(end & (i >= 3) & (i < 3 + wide))
    def _():
        line_down(i - 3)

    at_step(nb, 1, lambda k: product(0, dmixed_s, gated_ref))
    at_step(nb + 1, 1, lambda k: product(1, normed_ref, dz_s))
    at_step(nb + 2, 1, lambda k: product(2, normed_ref, dx_s))
    at_step(6, nb, last_block)

    @pl.when(i == pl.num_programs(0) - 1)
    def _():
        at = 8
        pack_s[at:at + ns, :] = -jnp.exp(lr_ref[...]) * acc_s[...]
        at += ns
        pack_s[at:at + rank, :] = gstep_s[0:rank, :]
        at += rank
        held = rank + 2 * ns
        pack_s[at:at + held, :] = state_s[0:held, :]
        at += held
        halves = width // ch
        own_row = lax.broadcasted_iota(jnp.int32, (wide, ch), 0) == me
        first = first_s[...] / as_row(first_gain_ref)
        for h in range(halves):
            cols = slice(h * ch, (h + 1) * ch)
            pack_s[at + h:at + h + 1, :] = first[:, cols]
            pack_s[at + halves + h:at + halves + h + 1, :] = second_s[:, cols]
            pack_s[at + 8 + h * wide:at + 8 + (h + 1) * wide, :] = jnp.where(own_row, grow_ref[:, cols], 0.0)
        share = pack_s.shape[0] // wide

        def chunk(ref, n):
            return ref.at[pl.ds(pl.multiple_of(n * share, share), share)]

        def scatter(k):
            to = lax.rem(me + k, wide)
            return pltpu.make_async_remote_copy(chunk(pack_s, to), pack_in.at[k], pack_sends.at[0, k], pack_arrivals.at[0, k],
                                                device_id={"wide": to}, device_id_type=MESH)

        def spread_out(k):
            to = lax.rem(me + k, wide)
            return pltpu.make_async_remote_copy(chunk(small_s, me), chunk(small_s, me), pack_sends.at[1, k], pack_arrivals.at[1, k],
                                                device_id={"wide": to}, device_id_type=MESH)

        for k in range(1, wide):
            scatter(k).start()
        for which, ref in enumerate((go_ref, gz_ref, gx_ref)):
            total = prod_s[which, pl.ds(pl.multiple_of(me * block, block), block), :].astype(F32)
            for k in range(1, wide):
                deliver(which, k).wait_recv()
                total = total + inbox_s[which, k].astype(F32)
            ref[...] = total
        total = chunk(pack_s, me)[...]
        for k in range(1, wide):
            scatter(k).wait_recv()
            total = total + pack_in[k]
        chunk(small_s, me)[...] = total
        for k in range(1, wide):
            spread_out(k).start()
        line.sent(wide)
        dp.sent(nb)
        dn.sent(nb)
        for k in range(1, wide):
            give_back(k).wait_recv()
            give_back(k).wait_send()
            for which in range(3):
                deliver(which, k).wait_send()
            scatter(k).wait_send()
        for k in range(1, wide):
            spread_out(k).wait_recv()
        small_ref[...] = small_s[...]
        for k in range(1, wide):
            spread_out(k).wait_send()


def mixer_back(wide, taps, rank, by_rows, whole_ones):
    proj, keep, step, states, starts, tokens, mixed, ograd, scol, z, scan = by_rows
    inner, log_rates, ret = whole_ones[0], whole_ones[2], whole_ones[4]
    seq, ch = inner.shape
    width = tokens.shape[1]
    ns = log_rates.shape[0]
    tb = LANES
    nb = seq // tb
    packed = pack_rows(rank, ns, wide, width, ch, wide)
    back = lambda i: jnp.maximum(nb - 1 - i, 0)
    final = lambda i: nb - 1 - jnp.maximum(i - 6, 0)
    row = lambda n, size=tb: pl.BlockSpec((size, n), lambda i: (back(i), 0))
    full = lambda a: pl.BlockSpec(a.shape, lambda i: (0,) * a.ndim, pipeline_mode=pl.Buffered(1))
    whole = lambda *s: pl.BlockSpec(s, lambda i: (0,) * len(s))
    shape = jax.ShapeDtypeStruct
    dma = pltpu.SemaphoreType.DMA
    vm = pltpu.VMEM
    return pl.pallas_call(
        functools.partial(mixer_back_kernel, ns, rank, wide, taps),
        grid=(nb + 6,),
        in_specs=[row(LANES), row(1), row(ch), row(ch, tb * ns), pl.BlockSpec((1, ns, ch), lambda i: (back(i), 0, 0)),
                  row(width), row(width), row(width), row(1), row(ch), row(ch), *[full(a) for a in whole_ones]],
        out_specs=[row(width), pl.BlockSpec((tb, width), lambda i: (final(i), 0)), *[whole(width // wide, ch)] * 3, whole(packed, ch),
                   pl.BlockSpec(memory_space=pl.ANY)],
        out_shape=[shape((seq, width), F32), shape((seq, width), BF16), *[shape((width // wide, ch), F32)] * 3, shape((packed, ch), F32),
                   shape(ret.shape, BF16)],
        scratch_shapes=[
            vm((ns, ch), F32), *[vm((ch // LANES, tb, LANES), F32)] * 4, vm((ch // LANES, ns, LANES), F32), vm((tb, ch), F32), vm((tb, ch), F32),
            vm((ns, ch), F32), vm((tb, LANES), F32), *[vm((8 * ns, 2 * LANES), F32)] * 2, *[vm((8 * ns, 2 * LANES), BF16)] * 2,
            *[vm(ret.shape, BF16)] * 3, dma((3, wide)), dma((3, wide)), dma((wide,)), dma((wide,)),
            *[vm((seq, LANES), BF16)] * 3, dma((3, nb)), dma((3, nb)), *[vm((seq, width), BF16)] * 3, dma((3, nb)), dma((3, nb)),
            vm((3, width, ch), BF16), vm((3, wide, width // wide, ch), BF16), dma((3, wide)), dma((3, wide)),
            vm((packed, ch), F32), vm((wide, packed // wide, ch), F32), vm((packed, ch), F32), dma((2, wide)), dma((2, wide)),
            vm((seq, ch), F32), vm((seq, width), BF16), vm((seq, ch), BF16), vm((seq + 8, ch), F32), vm((seq, ch), BF16),
            vm((LANES, ch), F32), vm((LANES, ch), F32), vm((1, width), F32), vm((1, width), F32)],
        compiler_params=pltpu.CompilerParams(collective_id=1, has_side_effects=True, vmem_limit_bytes=60 << 20),
        name="mixer_back",
    )(*by_rows, *whole_ones)


def gelu_pair(v):
    root = 0.7978845608028654
    square = v * v
    t = jnp.tanh(root * v * (1.0 + 0.044715 * square))
    half = 0.5 * (1.0 + t)
    slope = half + (0.5 * root) * v * (1.0 - t * t) * (1.0 + (3.0 * 0.044715) * square)
    return v * half, slope


def scan_mix_kernel(ns, rank, wide, proj_ref, inner_ref, keep_ref, sproj_ref, sbias_ref, lr_ref, skip_ref, z_ref, wo_ref, ograd_ref, srow_ref,
                    scan_ref, step_ref, states_ref, starts_ref, gated_ref, mixed_ref, gin_ref,
                    state_s, stepd_s, drive_s, r2_s, wide_a, wide_b, own_s, near_s, far_s, sends, arrivals, grad_s, send_s, g_sends, g_arrivals):
    tb, ch = inner_ref.shape
    groups = ch // LANES
    i = pl.program_id(0)
    roles = line_roles()
    end, mid, mate, other = roles
    line = LineSum(roles, tb, own_s, near_s, own_s, far_s, far_s, sends, arrivals)
    steps = arrivals.shape[1]

    me = lax.axis_index("wide")
    cap = send_s.shape[0] // wide

    def slot_rows(k):
        return pl.ds(pl.multiple_of(k * cap, cap), cap)

    def dispatch(k):
        return pltpu.make_async_remote_copy(
            send_s.at[slot_rows(k)], gin_ref.at[slot_rows(k)], g_sends.at[k], g_arrivals.at[k],
            device_id={"wide": lax.rem(me + k, wide)}, device_id_type=MESH)

    own_rows = pltpu.make_async_copy(send_s.at[slot_rows(0)], gin_ref.at[slot_rows(0)], g_sends.at[0])

    @pl.when(i == 0)
    def _():
        greet(wide)
        grad_s[...] = ograd_ref[...].astype(BF16)
        state_s[...] = jnp.zeros_like(state_s)
        spread(r2_s, jnp.exp(lr_ref[...]) * (-LOG2E))

    @pl.when(i < wide)
    def _():
        ids = lax.broadcasted_iota(jnp.int32, (cap, grad_s.shape[0]), 0) + lax.rem(me + i, wide) * cap
        chosen = jnp.where(ids == srow_ref[...], 1.0, 0.0).astype(BF16)
        send_s[slot_rows(i), :] = jnp.dot(chosen, grad_s[...], preferred_element_type=F32).astype(BF16)

        @pl.when(i == 0)
        def _():
            own_rows.start()

        @pl.when(i > 0)
        def _():
            dispatch(i).start()

    step_in = proj_ref[...].astype(BF16)
    pre = jnp.dot(step_in, sproj_ref[...], preferred_element_type=F32) + as_row(sbias_ref)
    step = softplus(pre)
    step_ref[...] = step
    spread(stepd_s, jnp.where(keep_ref[...] > 0.0, step, 1e30))
    inner = inner_ref[...].astype(F32)
    spread(drive_s, step * inner)
    starts_ref[0] = state_s[...]
    start = tuple(state_s[:, c * LANES:(c + 1) * LANES] for c in range(groups))
    state = forward_tokens(ns, rank, proj_ref, stepd_s, drive_s, r2_s, states_ref, scan_ref, start, wide_a, wide_b)
    for c in range(groups):
        state_s[:, c * LANES:(c + 1) * LANES] = state[c]
    scan = scan_ref[...] + as_row(skip_ref) * inner
    scan_ref[...] = scan
    z = z_ref[...]
    gated = (scan * (z / (1.0 + jnp.exp(-z)))).astype(BF16)
    gated_ref[...] = gated
    here = pl.ds(pl.multiple_of(i * tb, tb), tb)
    own_s[here, :] = lax.dot_general(gated, wo_ref[...], (((1,), (1,)), ((), ())), preferred_element_type=F32).astype(BF16)

    @pl.when(end)
    def _():
        line.up(i).start()

    @pl.when(mid & (i > 0))
    def _():
        line.first(i - 1)

    @pl.when(mid & (i > 1))
    def _():
        line.second(i - 2)

    @pl.when(i == steps - 1)
    def _():
        @pl.when(mid)
        def _():
            line.first(steps - 1)
            line.second(steps - 2)
            line.second(steps - 1)

        @pl.when(end)
        def _():
            for k in range(steps):
                line.down(k).wait_recv()

        mixed_ref[...] = far_s[...]
        line.sent(steps)
        own_rows.wait()
        for k in range(1, wide):
            dispatch(k).wait_recv()
            dispatch(k).wait_send()


def scan_mix(proj, inner, keep, sproj, sbias, log_rates, skip, z, wo, ograd, srow, rank, wide, cap):
    seq, ch = inner.shape
    ns = log_rates.shape[0]
    tb = LANES
    nb = seq // tb
    width = wo.shape[0]
    full = lambda a: pl.BlockSpec(a.shape, lambda i: (0,) * a.ndim)
    rows = pl.BlockSpec((tb, ch), lambda i: (i, 0))
    return pl.pallas_call(
        functools.partial(scan_mix_kernel, ns, rank, wide),
        grid=(nb,),
        in_specs=[pl.BlockSpec((tb, LANES), lambda i: (i, 0)), rows, pl.BlockSpec((tb, 1), lambda i: (i, 0)),
                  full(sproj), full(sbias), full(log_rates), full(skip), rows, full(wo), full(ograd), full(srow)],
        out_specs=[rows, rows, pl.BlockSpec((tb * ns, ch), lambda i: (i, 0)), pl.BlockSpec((1, ns, ch), lambda i: (i, 0, 0)),
                   rows, pl.BlockSpec((seq, width), lambda i: (0, 0)), pl.BlockSpec(memory_space=pl.ANY)],
        out_shape=[jax.ShapeDtypeStruct((seq, ch), F32), jax.ShapeDtypeStruct((seq, ch), F32),
                   jax.ShapeDtypeStruct((seq * ns, ch), BF16), jax.ShapeDtypeStruct((nb, ns, ch), F32),
                   jax.ShapeDtypeStruct((seq, ch), BF16), jax.ShapeDtypeStruct((seq, width), BF16),
                   jax.ShapeDtypeStruct((wide * cap, width), BF16)],
        scratch_shapes=[pltpu.VMEM((ns, ch), F32)] + [pltpu.VMEM((ch // LANES, tb, LANES), F32)] * 2 + [pltpu.VMEM((ch // LANES, ns, LANES), F32),
                        *[pltpu.VMEM((8 * ns, 2 * LANES), F32)] * 2,
                        *[pltpu.VMEM((seq, width), BF16)] * 3, pltpu.SemaphoreType.DMA((3, nb)), pltpu.SemaphoreType.DMA((3, nb)),
                        pltpu.VMEM((seq, width), BF16), pltpu.VMEM((wide * cap, width), BF16),
                        pltpu.SemaphoreType.DMA((wide,)), pltpu.SemaphoreType.DMA((wide,))],
        compiler_params=pltpu.CompilerParams(collective_id=4, has_side_effects=True, vmem_limit_bytes=48 << 20),
        name="scan_mix",
    )(proj, inner, keep, sproj, sbias, log_rates, skip, z, wo, ograd, srow)


def experts_kernel(wide, tokens_ref, mixed_ref, gin_ref, srow_ref, gain_ref, router_ref, rt_ref, up_ref, ub_ref, down_ref, db_ref,
                   gup_ref, gub_ref, gdown_ref, gdb_ref, ret_ref, out_ref, grow_ref,
                   pay_s, send_s, inbox_s, rgrad_s, act_s, dpre_s, own_s, near_s, far_s, acc_s, column_s, rows_s,
                   pay_sends, pay_arrivals, sends, arrivals, ret_sends, ret_arrivals, r_sends, r_arrivals):
    seq, width = tokens_ref.shape
    hid = up_ref.shape[1]
    cap = inbox_s.shape[0] // wide
    tb = LANES
    me, rank = lax.axis_index("wide"), lax.axis_index("tp")
    roles = line_roles()
    end, mid, mate, other = roles
    greet(wide)
    back = LineSum(roles, cap, own_s, near_s, own_s, far_s, far_s, sends, arrivals)

    def rows_of(b, size):
        return pl.ds(pl.multiple_of(b * size, size), size)

    def prepare(b, _):
        rows = rows_of(b, tb)
        hidden = tokens_ref[rows, :] + mixed_ref[rows, :].astype(F32)
        scale = lax.rsqrt(jnp.mean(hidden * hidden, axis=1, keepdims=True) + EPS)
        pay_s[rows, :] = (hidden * scale * as_row(gain_ref)).astype(BF16)
        return 0

    lax.fori_loop(0, seq // tb, prepare, 0)

    def payload(expert):
        ids = lax.broadcasted_iota(jnp.int32, (cap, seq), 0) + expert * cap
        chosen = jnp.where(ids == srow_ref[...], 1.0, 0.0).astype(BF16)
        return jnp.dot(chosen, pay_s[...], preferred_element_type=F32).astype(BF16)

    def dispatch(k):
        return pltpu.make_async_remote_copy(
            send_s.at[rows_of(k, cap)], inbox_s.at[rows_of(k, cap)], pay_sends.at[k], pay_arrivals.at[k],
            device_id={"wide": lax.rem(me + k, wide)}, device_id_type=MESH)

    def send(k):
        send_s[rows_of(k, cap), :] = payload(lax.rem(me + k, wide))
        dispatch(k).start()

    ahead = wide // 2

    def send_first(k, _):
        send(k)
        return 0

    lax.fori_loop(1, ahead + 1, send_first, 0)
    inbox_s[0:cap, :] = payload(me)

    def give_back(c):
        return pltpu.make_async_remote_copy(
            far_s.at[rows_of(c, cap)], ret_ref.at[rows_of(me, cap)], ret_sends.at[c], ret_arrivals.at[c],
            device_id={"wide": lax.rem(me + wide - c, wide)}, device_id_type=MESH)

    def return_chunk(c):
        @pl.when(c == 0)
        def _():
            ret_ref[rows_of(me, cap), :] = far_s[0:cap, :]

        @pl.when(c != 0)
        def _():
            give_back(c).start()

    def second(c):
        back.second(c)
        return_chunk(c)

    gub_ref[...] = jnp.zeros_like(gub_ref)
    gdb_ref[...] = jnp.zeros_like(gdb_ref)
    acc_s[...] = jnp.zeros_like(acc_s)
    expert = lax.broadcasted_iota(jnp.int32, rt_ref.shape, 0)
    router_row = jnp.sum(jnp.where(expert == me, rt_ref[...], 0.0), axis=0, keepdims=True)
    column_s[...] = router_row
    lane = lax.broadcasted_iota(jnp.int32, (cap, LANES), 1)
    turned = (((1,), (1,)), ((), ()))

    def compute(k, _):
        @pl.when(k + ahead < wide - 1)
        def _():
            send(k + ahead + 1)

        @pl.when(k > 0)
        def _():
            dispatch(k).wait_recv()

        part = rows_of(k, cap)
        rows_in = inbox_s[part, :]
        rows_raw = gin_ref[part, :].astype(F32)
        logits = jnp.dot(rows_in, router_ref[...], preferred_element_type=F32)
        logit = jnp.sum(jnp.where(lane == me, logits, 0.0), axis=1, keepdims=True)
        gate = 1.0 / (1.0 + jnp.exp(-logit))
        rows_grad = (gate * rows_raw).astype(BF16)
        rgrad_s[part, :] = rows_grad
        pre = jnp.dot(rows_in, up_ref[...], preferred_element_type=F32) + ub_ref[...]
        act, slope = gelu_pair(pre)
        act = act.astype(BF16)
        act_s[part, :] = act
        d_pre = (lax.dot_general(rows_grad, down_ref[...], turned, preferred_element_type=F32) * slope).astype(BF16)
        dpre_s[part, :] = d_pre
        out = jnp.dot(act, down_ref[...], preferred_element_type=F32) + db_ref[...] * (1.0 / LINE)
        d_logit = jnp.sum(rows_raw * out, axis=1, keepdims=True) * (gate * (1.0 - gate))
        own_s[part, :] = (lax.dot_general(d_pre, up_ref[...], turned, preferred_element_type=F32) + d_logit * column_s[...]).astype(BF16)

        @pl.when(end)
        def _():
            back.up(k).start()

        out_ref[part, :] = (gate * out).astype(BF16)
        acc_s[...] += jnp.sum(d_logit * rows_in.astype(F32), axis=0, keepdims=True)
        gub_ref[...] += jnp.sum(d_pre.astype(F32), axis=0, keepdims=True)
        gdb_ref[...] += jnp.sum(rows_grad.astype(F32), axis=0, keepdims=True)

        @pl.when(mid & (k > 0))
        def _():
            back.first(k - 1)

        @pl.when(mid & (k > 1))
        def _():
            second(k - 2)
        return 0

    lax.fori_loop(0, wide, compute, 0)

    def term(k):
        return pltpu.make_async_remote_copy(rows_s.at[rank], rows_s.at[rank], r_sends.at[k], r_arrivals.at[k],
                                            device_id={"tp": lax.rem(rank + k, LINE)}, device_id_type=MESH)

    rows_s[rank] = jnp.broadcast_to(acc_s[...], (8, width))
    for k in range(1, LINE):
        term(k).start()

    @pl.when(mid)
    def _():
        back.first(wide - 1)
        second(wide - 2)

    tiles = hid // LANES
    across_rows = (((0,), (0,)), ((), ()))

    def tile(j, _):
        @pl.when(j < tiles)
        def _():
            cols = rows_of(j, LANES)
            gdown_ref[cols, :] = lax.dot_general(act_s[:, cols], rgrad_s[...], across_rows, preferred_element_type=F32)

        @pl.when(j >= tiles)
        def _():
            cols = rows_of(j - tiles, LANES)
            gup_ref[cols, :] = lax.dot_general(inbox_s[:, cols], dpre_s[...], across_rows, preferred_element_type=F32)

        @pl.when(end & (j < wide))
        def _():
            back.down(j).wait_recv()
            return_chunk(j)

        @pl.when(mid & (j == 0))
        def _():
            second(wide - 1)
        return 0

    lax.fori_loop(0, 2 * tiles, tile, 0)
    for k in range(1, LINE):
        term(k).wait_recv()
    grow_ref[...] = ((rows_s[0] + rows_s[1]) + rows_s[2]) + rows_s[3]
    for c in range(1, wide):
        give_back(c).wait_recv()
    back.sent(wide)
    for k in range(1, wide):
        dispatch(k).wait_send()
        give_back(k).wait_send()
    for k in range(1, LINE):
        term(k).wait_send()


def experts_block(wide, cap, *operands):
    tokens, mixed, gin, srow, gain, router, router_t, up, ub, down, db = operands
    seq, width = tokens.shape
    hid = up.shape[1]
    vm = pl.BlockSpec(memory_space=pltpu.VMEM)
    shape = jax.ShapeDtypeStruct
    dma = pltpu.SemaphoreType.DMA
    slots = wide * cap
    return pl.pallas_call(
        functools.partial(experts_kernel, wide),
        in_specs=[vm] * len(operands),
        out_specs=[vm] * 7,
        out_shape=[shape((width, hid), F32), shape((1, hid), F32), shape((hid, width), F32), shape((1, width), F32),
                   shape((slots, width), BF16), shape((slots, width), BF16), shape((8, width), F32)],
        scratch_shapes=[
            pltpu.VMEM((seq, width), BF16), *[pltpu.VMEM((slots, width), BF16)] * 3,
            pltpu.VMEM((slots, hid), BF16), pltpu.VMEM((slots, hid), BF16),
            *[pltpu.VMEM((slots, width), BF16)] * 3, pltpu.VMEM((1, width), F32), pltpu.VMEM((1, width), F32), pltpu.VMEM((LINE, 8, width), F32),
            dma((wide,)), dma((wide,)), dma((3, wide)), dma((3, wide)), dma((wide,)), dma((wide,)), dma((LINE,)), dma((LINE,))],
        compiler_params=pltpu.CompilerParams(collective_id=2, has_side_effects=True, vmem_limit_bytes=56 << 20),
        name="experts",
    )(*operands)


def front_kernel(wide, taps, tokens_ref, gain_ref, inx_ref, inz_ref, outp_ref, cw_ref, cb_ref, wproj_ref, masks_ref,
                 scale_ref, normed_ref, x_ref, z_ref, csum_ref, inner_ref, proj_ref, wx_ref, wz_ref, wo_ref,
                 own_s, near_s, far_s, w_sends, w_arrivals, sends, arrivals):
    seq, width = tokens_ref.shape
    ch = x_ref.shape[1]
    block = inx_ref.shape[0]
    tb = LANES
    nb = seq // tb
    me = lax.axis_index("wide")
    roles = line_roles()
    end, mid, mate, other = roles
    greet(wide)
    line = LineSum(roles, 2 * tb, own_s, near_s, own_s, far_s, far_s, sends, arrivals)
    mine = pl.ds(pl.multiple_of(me * block, block), block)
    weights = ((inx_ref, wx_ref), (inz_ref, wz_ref), (outp_ref, wo_ref))

    def share(which, k):
        source, target = weights[which]
        return pltpu.make_async_remote_copy(source, target.at[mine], w_sends.at[which, k], w_arrivals.at[which, k],
                                            device_id={"wide": lax.rem(me + k, wide)}, device_id_type=MESH)

    for which in range(3):
        for k in range(1, wide):
            share(which, k).start()
    for source, target in weights:
        target[mine, :] = source[...]

    def rows_of(b):
        return pl.ds(pl.multiple_of(b * tb, tb), tb)

    def norm(b, _):
        rows = rows_of(b)
        tokens = tokens_ref[rows, :]
        scale = lax.rsqrt(jnp.mean(tokens * tokens, axis=1, keepdims=True) + EPS)
        scale_ref[rows, :] = scale
        normed_ref[rows, :] = (tokens * scale * as_row(gain_ref)).astype(BF16)
        return 0

    lax.fori_loop(0, nb, norm, 0)
    for k in range(1, wide):
        share(0, k).wait_recv()

    def step(b, _):
        rows = rows_of(b)
        base = pl.multiple_of(b * tb, tb)
        x = jnp.dot(normed_ref[rows, :], wx_ref[...], preferred_element_type=F32)
        x_ref[rows, :] = x
        prior = x_ref[pl.ds(pl.multiple_of(jnp.maximum(base - 8, 0), 8), 8), :]
        history = jnp.concatenate([prior, x], axis=0)
        same = masks_ref[rows, :]
        csum = as_row(cb_ref) + cw_ref[taps - 1:taps, :] * x
        for s in range(1, taps):
            csum = csum + cw_ref[taps - 1 - s:taps - s, :] * (same[:, s:s + 1] * history[8 - s:8 - s + tb, :])
        csum_ref[rows, :] = csum
        inner = (csum / (1.0 + jnp.exp(-csum))).astype(BF16)
        inner_ref[rows, :] = inner
        own_s[rows, :] = jnp.dot(inner, wproj_ref[...], preferred_element_type=F32).astype(BF16)

        @pl.when(end & (lax.rem(b, 2) == 1))
        def _():
            line.up(b // 2).start()
        return 0

    lax.fori_loop(0, nb, step, 0)
    steps = nb // 2

    @pl.when(mid)
    def _():
        line.first(0)
        for k in range(1, steps):
            line.first(k)
            line.second(k - 1)

    for k in range(1, wide):
        share(1, k).wait_recv()

    def gate(b, _):
        rows = rows_of(b)
        z_ref[rows, :] = jnp.dot(normed_ref[rows, :], wz_ref[...], preferred_element_type=F32)
        return 0

    lax.fori_loop(0, nb, gate, 0)

    @pl.when(mid)
    def _():
        line.second(steps - 1)

    @pl.when(end)
    def _():
        for k in range(steps):
            line.down(k).wait_recv()

    proj_ref[...] = far_s[...].astype(F32)
    line.sent(steps)
    for k in range(1, wide):
        share(2, k).wait_recv()
        for which in range(3):
            share(which, k).wait_send()


def front(wide, taps, *operands):
    tokens, gain, inx, inz, outp, cw, cb, wproj, masks = operands
    seq, width = tokens.shape
    ch = inx.shape[1]
    vm = pl.BlockSpec(memory_space=pltpu.VMEM)
    shape = jax.ShapeDtypeStruct
    dma = pltpu.SemaphoreType.DMA
    return pl.pallas_call(
        functools.partial(front_kernel, wide, taps),
        in_specs=[vm] * len(operands),
        out_specs=[vm] * 10,
        out_shape=[shape((seq, 1), F32), shape((seq, width), BF16), shape((seq, ch), F32), shape((seq, ch), F32), shape((seq, ch), F32),
                   shape((seq, ch), BF16), shape((seq, LANES), F32), *[shape((width, ch), BF16)] * 3],
        scratch_shapes=[*[pltpu.VMEM((seq, LANES), BF16)] * 3, dma((3, wide)), dma((3, wide)), dma((3, seq // LANES // 2)), dma((3, seq // LANES // 2))],
        compiler_params=pltpu.CompilerParams(collective_id=3, has_side_effects=True, vmem_limit_bytes=48 << 20),
        name="mixer_front",
    )(*operands)


def plain_device(
    tokens,
    segment_ids,
    routes,
    out_grad,
    mixer_gain,
    in_proj_x,
    in_proj_z,
    conv_weight,
    conv_bias,
    state_proj,
    step_proj,
    step_bias,
    log_rates,
    skip_gain,
    out_proj,
    expert_gain,
    router_weight,
    expert_up,
    up_bias,
    expert_down,
    down_bias,
):
    seq_len, model_width = tokens.shape
    conv_taps = conv_weight.shape[0]
    step_rank = step_proj.shape[0]
    experts = router_weight.shape[1]
    capacity = 5 * seq_len // (4 * experts)
    doc_ids = segment_ids[0]
    conv_masks = [same_document(doc_ids, offset)[:, None] for offset in range(conv_taps)]
    first_scale = lax.rsqrt(jnp.mean(tokens * tokens, axis=1, keepdims=True) + EPS)
    first_unit = tokens * first_scale
    normed = (first_unit * mixer_gain).astype(jnp.bfloat16)
    gathered_x, gathered_z, gathered_out = (
        lax.all_gather(in_proj_x, "wide", axis=0, tiled=True),
        lax.all_gather(in_proj_z, "wide", axis=0, tiled=True),
        lax.all_gather(out_proj, "wide", axis=0, tiled=True),
    )
    x_branch = multiply(normed, gathered_x)
    z_branch = multiply(normed, gathered_z)
    conv_sum = conv_bias + jnp.zeros_like(x_branch)
    for offset in range(conv_taps):
        conv_sum = conv_sum + conv_weight[conv_taps - 1 - offset] * conv_masks[
            offset
        ] * shifted_down(x_branch, offset)
    inner_act = jax.nn.silu(conv_sum).astype(jnp.bfloat16)
    wide_proj = jnp.pad(state_proj, ((0, 0), (0, LANES - state_proj.shape[1])))
    projected = lax.psum(multiply(inner_act, wide_proj), "tp")
    tall_proj = jnp.pad(step_proj, ((0, LANES - step_rank), (0, 0)))
    carry_mask = same_document(doc_ids, 1)[:, None]
    scan_out, step_size, states, starts = scan_fwd(
        projected, inner_act, carry_mask, tall_proj, step_bias[None], log_rates, skip_gain[None], step_rank
    )
    z_gate = jax.nn.silu(z_branch)
    gated = (scan_out * z_gate).astype(jnp.bfloat16)
    mixed = lax.psum(contract_cols(gated, gathered_out).astype(jnp.bfloat16), "tp").astype(
        jnp.float32
    )
    hidden = tokens + mixed
    second_scale = lax.rsqrt(jnp.mean(hidden * hidden, axis=1, keepdims=True) + EPS)
    second_unit = hidden * second_scale
    expert_in = (second_unit * expert_gain).astype(jnp.bfloat16)
    route_ids = routes[:, 0]
    chosen_int = (routes == jnp.arange(experts, dtype=jnp.int32)[None, :]).astype(jnp.int32)
    chosen = chosen_int.astype(jnp.float32)
    logits = multiply(expert_in, router_weight)
    gate = jax.nn.sigmoid(jnp.sum(logits * chosen, axis=1))
    rank_of = jnp.arange(seq_len, dtype=jnp.int32)
    earlier = (rank_of[:, None] > rank_of[None, :]).astype(jnp.bfloat16)
    position = jnp.sum(multiply(earlier, chosen.astype(jnp.bfloat16)) * chosen, axis=1).astype(jnp.int32)
    kept = position < capacity
    slots = jnp.where(kept, route_ids * capacity + position, experts * capacity)
    scaled_grad = (gate[:, None] * out_grad).astype(jnp.bfloat16)
    sent_width = expert_in.shape[1]
    send_in = (
        jnp.zeros((experts * capacity + 1, sent_width), jnp.bfloat16).at[slots].set(expert_in)[:-1]
    )
    send_grad = (
        jnp.zeros((experts * capacity + 1, sent_width), jnp.bfloat16)
        .at[slots]
        .set(scaled_grad)[:-1]
    )
    recv_in, recv_grad = (
        lax.all_to_all(
            send_in.reshape(experts, capacity, sent_width),
            "wide",
            split_axis=0,
            concat_axis=0,
            tiled=True,
        ),
        lax.all_to_all(
            send_grad.reshape(experts, capacity, sent_width),
            "wide",
            split_axis=0,
            concat_axis=0,
            tiled=True,
        ),
    )
    rows_in = recv_in.reshape(-1, model_width)
    rows_grad = recv_grad.reshape(-1, model_width)
    pre_act = multiply(rows_in, expert_up[0]) + up_bias[0]
    hidden_act = jax.nn.gelu(pre_act).astype(jnp.bfloat16)
    partial_out = multiply(hidden_act, expert_down[0])
    up_grad = contract_cols(rows_grad, expert_down[0])
    d_pre = jax.vjp(jax.nn.gelu, pre_act)[1](up_grad)[0].astype(jnp.bfloat16)
    partial_back = contract_cols(d_pre, expert_up[0])
    grad_down = contract_rows(hidden_act, rows_grad)
    grad_dbias = jnp.sum(rows_grad.astype(jnp.float32), axis=0)
    grad_up = contract_rows(rows_in, d_pre)
    grad_ubias = jnp.sum(d_pre.astype(jnp.float32), axis=0)
    out_sum, back_sum = (
        lax.psum(partial_out.astype(jnp.bfloat16), "tp").astype(jnp.float32),
        lax.psum(partial_back.astype(jnp.bfloat16), "tp").astype(jnp.float32),
    )
    bias_part = down_bias[0]
    outgoing = (out_sum + bias_part).astype(jnp.bfloat16).reshape(experts, capacity, -1)
    back_rows = back_sum.astype(jnp.bfloat16).reshape(experts, capacity, -1)
    incoming, arriving = (
        lax.all_to_all(outgoing, "wide", split_axis=0, concat_axis=0, tiled=True),
        lax.all_to_all(back_rows, "wide", split_axis=0, concat_axis=0, tiled=True),
    )
    safe_slots = jnp.minimum(slots, experts * capacity - 1)
    returned = jnp.where(
        kept[:, None], incoming.reshape(-1, model_width)[safe_slots].astype(jnp.float32), 0.0
    )
    result = hidden + gate[:, None] * returned
    d_gate = jnp.sum(out_grad * returned, axis=1)
    d_logit = (d_gate * gate * (1.0 - gate))[:, None] * chosen
    grad_router = jnp.dot(expert_in.astype(jnp.float32).T, d_logit, precision=HIGH)
    d_norm_two = jnp.dot(d_logit, router_weight.astype(jnp.float32).T, precision=HIGH)
    d_norm_two = d_norm_two + jnp.where(
        kept[:, None], arriving.reshape(-1, model_width)[safe_slots].astype(jnp.float32), 0.0
    )
    grad_second_gain = jnp.sum(d_norm_two * second_unit, axis=0)
    d_hidden = out_grad + rms_back(d_norm_two * expert_gain, second_unit, second_scale)
    d_mixed = d_hidden.astype(jnp.bfloat16)
    d_gated = multiply(d_mixed, gathered_out)
    grad_out = contract_rows(d_mixed, gated)
    d_scan = d_gated * z_gate
    d_z = (d_gated * scan_out * silu_slope(z_branch)).astype(jnp.bfloat16)
    d_step_pre, d_inner, d_proj, grad_step, grad_sbias, grad_rates, grad_skip = scan_bwd(
        projected, inner_act, carry_mask, step_size, states, starts, d_scan, tall_proj, log_rates, skip_gain[None], step_rank
    )
    grad_step, grad_sbias, grad_skip = grad_step[:step_rank], grad_sbias[0], grad_skip[0]
    d_projected = lax.psum(d_proj.astype(jnp.bfloat16), "tp")
    grad_state = contract_rows(inner_act, d_projected)[:, : state_proj.shape[1]]
    d_inner = d_inner + contract_cols(d_projected, wide_proj)
    d_conv = d_inner * silu_slope(conv_sum)
    grad_cbias = jnp.sum(d_conv, axis=0)
    conv_rows = []
    d_input = jnp.zeros_like(d_conv)
    for offset in range(conv_taps):
        conv_rows.append(
            jnp.sum(d_conv * conv_masks[offset] * shifted_down(x_branch, offset), axis=0)
        )
        d_input = d_input + conv_weight[conv_taps - 1 - offset] * shifted_up(
            conv_masks[offset] * d_conv, offset
        )
    grad_conv = jnp.stack(conv_rows[::-1])
    d_x_branch = d_input.astype(jnp.bfloat16)
    grad_in_x = contract_rows(normed, d_x_branch)
    grad_in_z = contract_rows(normed, d_z)
    d_normed = lax.psum(
        (contract_cols(d_x_branch, gathered_x) + contract_cols(d_z, gathered_z)).astype(
            jnp.bfloat16
        ),
        "tp",
    ).astype(jnp.float32)
    grad_first_gain = jnp.sum(d_normed * first_unit, axis=0)
    tokens_grad = d_hidden + rms_back(d_normed * mixer_gain, first_unit, first_scale)
    grad_in_x, grad_in_z, grad_out = (
        summed_on_arrival(grad_in_x.astype(jnp.bfloat16), "wide", 0),
        summed_on_arrival(grad_in_z.astype(jnp.bfloat16), "wide", 0),
        summed_on_arrival(grad_out.astype(jnp.bfloat16), "wide", 0),
    )
    (
        grad_first_gain,
        grad_conv,
        grad_cbias,
        grad_state,
        grad_step,
        grad_sbias,
        grad_rates,
        grad_skip,
        grad_second_gain,
        grad_router,
    ) = lax.psum(
        (
            grad_first_gain,
            grad_conv,
            grad_cbias,
            grad_state,
            grad_step,
            grad_sbias,
            grad_rates,
            grad_skip,
            grad_second_gain,
            grad_router,
        ),
        "wide",
    )
    return (
        result,
        tokens_grad,
        grad_first_gain,
        grad_in_x,
        grad_in_z,
        grad_conv,
        grad_cbias,
        grad_state,
        grad_step,
        grad_sbias,
        grad_rates,
        grad_skip,
        grad_out,
        grad_second_gain,
        grad_router,
        grad_up[None],
        grad_ubias[None],
        grad_down[None],
        grad_dbias[None],
    )


def fast_device(
    tokens,
    segment_ids,
    routes,
    out_grad,
    mixer_gain,
    in_proj_x,
    in_proj_z,
    conv_weight,
    conv_bias,
    state_proj,
    step_proj,
    step_bias,
    log_rates,
    skip_gain,
    out_proj,
    expert_gain,
    router_weight,
    expert_up,
    up_bias,
    expert_down,
    down_bias,
):
    seq_len, model_width = tokens.shape
    conv_taps = conv_weight.shape[0]
    step_rank = step_proj.shape[0]
    experts = router_weight.shape[1]
    capacity = 5 * seq_len // (4 * experts)
    doc_ids = segment_ids[0]
    conv_masks = [same_document(doc_ids, offset)[:, None] for offset in range(conv_taps)]
    masks = jnp.pad(jnp.concatenate(conv_masks, axis=1), ((0, 8), (0, 8 - conv_taps)))
    wide_proj = jnp.pad(state_proj, ((0, 0), (0, LANES - state_proj.shape[1])))
    tall_proj = jnp.pad(step_proj, ((0, LANES - step_rank), (0, 0)))
    wide = lax.axis_size("wide")
    states = log_rates.shape[0]
    chosen = (routes == jnp.arange(experts, dtype=jnp.int32)[None, :]).astype(jnp.float32)
    rank_of = jnp.arange(seq_len, dtype=jnp.int32)
    earlier = (rank_of[:, None] > rank_of[None, :]).astype(jnp.bfloat16)
    position = jnp.sum(multiply(earlier, chosen.astype(jnp.bfloat16)) * chosen, axis=1).astype(jnp.int32)
    slots = jnp.where(position < capacity, routes[:, 0] * capacity + position, experts * capacity)
    slot_row, slot_col = slots[None], slots[:, None]
    wide_router = jnp.pad(router_weight, ((0, 0), (0, LANES - experts)))
    router_rows = router_weight.astype(jnp.float32).T
    carry_mask = same_document(doc_ids, 1)[:, None]

    first_scale, normed, x_branch, z_branch, conv_sum, inner_act, projected, gathered_x, gathered_z, gathered_out = front(
        wide, conv_taps, tokens, mixer_gain, in_proj_x, in_proj_z, out_proj, conv_weight, conv_bias, wide_proj, masks
    )
    scan_out, step_size, held, starts, gated, mixed, grads_in = scan_mix(
        projected, inner_act, carry_mask, tall_proj, step_bias, log_rates, skip_gain, z_branch, gathered_out, out_grad, slot_row,
        step_rank, wide, capacity,
    )
    grad_up, grad_ubias, grad_down, grad_dbias, returned, terms, router_grad = experts_block(
        wide, capacity, tokens, mixed, grads_in, slot_row, expert_gain, wide_router, router_rows,
        expert_up[0], up_bias, expert_down[0], down_bias,
    )
    d_hidden, d_normed, grad_in_x, grad_in_z, grad_out, small, gated_out = mixer_back(
        wide, conv_taps, step_rank,
        (projected, carry_mask, step_size, held, starts, tokens, mixed, out_grad, slot_col, z_branch, scan_out),
        (inner_act, tall_proj, log_rates, skip_gain, returned, expert_gain, gathered_out, terms, x_branch, conv_sum, masks, wide_proj,
         conv_weight, normed, gated, gathered_x, gathered_z, mixer_gain, router_grad),
    )
    outs = finish(
        step_rank, states, experts, tokens, mixed, slot_col, gated_out, d_hidden, d_normed, first_scale, mixer_gain, small,
        grad_in_x, grad_in_z, grad_out, grad_up, grad_down,
    )
    return (*outs[:15], outs[15][None], grad_ubias, outs[16][None], grad_dbias)


def solution(mesh):
    in_specs = (
        P("wide", None),
        P("wide", None),
        P("wide", None),
        P("wide", None),
        P(),
        P("wide", "tp"),
        P("wide", "tp"),
        P(None, "tp"),
        P("tp"),
        P("tp", None),
        P(None, "tp"),
        P("tp"),
        P(None, "tp"),
        P("tp"),
        P("wide", "tp"),
        P(),
        P(),
        P("wide", None, "tp"),
        P("wide", "tp"),
        P("wide", "tp", None),
        P("wide", None),
    )
    out_specs = (
        P("wide", None),
        P("wide", None),
        P(),
        P("wide", "tp"),
        P("wide", "tp"),
        P(None, "tp"),
        P("tp"),
        P("tp", None),
        P(None, "tp"),
        P("tp"),
        P(None, "tp"),
        P("tp"),
        P("wide", "tp"),
        P(),
        P(),
        P("wide", None, "tp"),
        P("wide", "tp"),
        P("wide", "tp", None),
        P("wide", None),
    )
    wide, line = mesh.shape["wide"], mesh.shape["tp"]
    per_device = fast_device if line == 4 and wide == 8 else plain_device
    return jax.shard_map(
        per_device, mesh=mesh, in_specs=in_specs, out_specs=out_specs, check_vma=False
    )
```

```python
import functools

import jax
import jax.numpy as jnp
from jax import lax
from jax.experimental import pallas as pl
from jax.experimental.pallas import tpu as pltpu
from jax.sharding import PartitionSpec as P

EPS = 1e-05
HIGH = lax.Precision.HIGHEST


def in_blocks(shard, dim, size):
    before, after = (shard.shape[:dim], shard.shape[dim + 1 :])
    return jnp.moveaxis(shard.reshape(*before, size, -1, *after), dim, 0)


def summed_on_arrival(shard, axis, dim):
    size = lax.axis_size(axis)
    parts = lax.all_to_all(in_blocks(shard, dim, size), axis, 0, 0, tiled=True)
    return jnp.sum(parts.astype(jnp.float32), axis=0)


def multiply(left, right):
    return jnp.dot(left, right, preferred_element_type=jnp.float32)


def contract_rows(left, right):
    return lax.dot_general(
        left, right, (((0,), (0,)), ((), ())), preferred_element_type=jnp.float32
    )


def contract_cols(left, right):
    return lax.dot_general(
        left, right, (((1,), (1,)), ((), ())), preferred_element_type=jnp.float32
    )


def shifted_down(values, steps):
    if steps == 0:
        return values
    filler = jnp.zeros((steps,) + values.shape[1:], values.dtype)
    return jnp.concatenate([filler, values[:-steps]], axis=0)


def shifted_up(values, steps):
    if steps == 0:
        return values
    filler = jnp.zeros((steps,) + values.shape[1:], values.dtype)
    return jnp.concatenate([values[steps:], filler], axis=0)


def same_document(doc_ids, steps):
    if steps == 0:
        return jnp.ones(doc_ids.shape, jnp.float32)
    filler = jnp.full((steps,), -1, jnp.int32)
    earlier = jnp.concatenate([filler, doc_ids[:-steps]])
    return (earlier == doc_ids).astype(jnp.float32)


def silu_slope(values):
    logistic = jax.nn.sigmoid(values)
    return logistic * (1.0 + values * (1.0 - logistic))


def rms_back(grad_unit, unit, scale):
    return scale * (grad_unit - unit * jnp.mean(grad_unit * unit, axis=1, keepdims=True))


LOG2E = 1.4426950408889634
LANES = 128
F32, BF16 = jnp.float32, jnp.bfloat16
MESH = pl.DeviceIdType.MESH


def fold_rows(parts, masks):
    m4, m2, m1 = masks

    def join(a, b, m, shift):
        return jnp.where(m, a, b) + pltpu.roll(jnp.where(m, b, a), shift, 0)

    c = [join(parts[i], parts[i + 4], m4[i], 4) for i in range(4)]
    d = [join(c[i], c[i + 2], m2[i], 6) for i in range(2)]
    return join(d[0], d[1], m1, 7)


def fold_masks(width):
    sub = lax.broadcasted_iota(jnp.int32, (8, width), 0)
    m4 = [((sub - i) & 7) < 4 for i in range(4)]
    m2 = [((sub - i) & 2) == 0 for i in range(2)]
    m1 = (sub & 1) == 0
    return m4, m2, m1


def softplus(v):
    return jnp.maximum(v, 0.0) + jnp.log1p(jnp.exp(-jnp.abs(v)))


def row(ref, c, t, ns):
    one = ref[c, pl.ds(t, 8, stride=0), :]
    return jnp.concatenate([one] * (ns // 8), axis=0)


def spread(ref, value):
    for c in range(ref.shape[0]):
        ref[c] = value[:, c * LANES:(c + 1) * LANES]


def own_column(ns, rank):
    lane = lax.broadcasted_iota(jnp.int32, (ns, LANES), 1)
    n = lax.broadcasted_iota(jnp.int32, (ns, LANES), 0)
    return (lane == rank + n) | (lane == rank + ns + n)


def coefficient_rows(ns, rank, proj_ref, first):
    own = own_column(ns, rank)
    lane = lax.broadcasted_iota(jnp.int32, (LANES, 2 * LANES), 1)
    k = lax.broadcasted_iota(jnp.int32, (LANES, 2 * LANES), 0)
    pick = ((lane < LANES) & (k >= rank) & (k < rank + ns)) | ((lane >= LANES) & (k >= rank + ns) & (k < rank + 2 * ns))
    pick = jnp.where(pick, 1.0, 0.0).astype(BF16)
    rows = []
    for j in range(8):
        one = proj_ref[pl.ds(first + j, 8, stride=0), :]
        rows.append(jnp.where(own, jnp.concatenate([one] * (ns // 8), axis=0), 0.0).astype(BF16))
    return jnp.dot(jnp.concatenate(rows, axis=0), pick, preferred_element_type=F32)


def forward_tokens(ns, rank, proj_ref, stepd_s, drive_s, r2_s, states_ref, scan_ref, state, wide_a, wide_b):
    tb = proj_ref.shape[0]
    groups = len(state)
    masks = fold_masks(LANES)

    def eight(first, wide, state):
        parts = [[] for _ in range(groups)]
        for j in range(8):
            t = first + j
            in_b = wide[j * ns:(j + 1) * ns, :LANES]
            out_b = wide[j * ns:(j + 1) * ns, LANES:]
            for c in range(groups):
                dec = jnp.exp2(row(stepd_s, c, t, ns) * r2_s[c])
                s = dec * state[c] + row(drive_s, c, t, ns) * in_b
                state[c] = s
                states_ref[pl.ds(pl.multiple_of(t * ns, ns), ns), pl.ds(c * LANES, LANES)] = s.astype(BF16)
                z = out_b * s
                parts[c].append(sum(z[8 * k:8 * k + 8] for k in range(ns // 8)))
        for c in range(groups):
            scan_ref[pl.ds(pl.multiple_of(first, 8), 8), pl.ds(c * LANES, LANES)] = fold_rows(parts[c], masks)
        return state

    def body(g, state):
        state = list(state)
        first = g * 16
        wide_b[...] = coefficient_rows(ns, rank, proj_ref, first + 8)
        state = eight(first, wide_a, state)
        wide_a[...] = coefficient_rows(ns, rank, proj_ref, jnp.minimum(first + 16, tb - 8))
        return tuple(eight(first + 8, wide_b, state))

    wide_a[...] = coefficient_rows(ns, rank, proj_ref, 0)
    return lax.fori_loop(0, tb // 16, body, state)


def backward_tokens(ns, rank, proj_ref, states_ref, starts_ref, stepd_s, drive_s, dscan_s, step_s, r2_s, coeff_s, exps_s, dproj_ref,
                    later, acc, wide_a, wide_b, sums_a, sums_b):
    tb = proj_ref.shape[0]
    groups = len(later)
    masks = fold_masks(LANES)
    own = own_column(ns, rank)
    k = lax.broadcasted_iota(jnp.int32, (2 * LANES, LANES), 0)
    lane = lax.broadcasted_iota(jnp.int32, (2 * LANES, LANES), 1)
    into = ((k < LANES) & (lane >= rank) & (lane < rank + ns)) | ((k >= LANES) & (lane >= rank + ns) & (lane < rank + 2 * ns))
    into = jnp.where(into, 1.0, 0.0).astype(BF16)

    def gather(sums, first):
        got = jnp.dot(sums[...], into, preferred_element_type=F32)
        parts = []
        for j in range(8):
            one = jnp.where(own, got[j * ns:(j + 1) * ns], 0.0)
            parts.append(sum(one[8 * q:8 * q + 8] for q in range(ns // 8)))
        dproj_ref[pl.ds(pl.multiple_of(first, 8), 8), :] = fold_rows(parts, masks)

    def eight(first, wide, sums, later, acc):
        cparts = [[None] * 8 for _ in range(groups)]
        eparts = [[None] * 8 for _ in range(groups)]
        last = pl.ds(pl.multiple_of((first + 7) * ns, ns), ns)
        now = [states_ref[last, pl.ds(c * LANES, LANES)].astype(F32) for c in range(groups)]
        for j in range(7, -1, -1):
            t = first + j
            prior = pl.ds(pl.multiple_of((t - 1 if j else jnp.maximum(t - 1, 0)) * ns, ns), ns)
            here = slice(j * ns, (j + 1) * ns)
            in_b = wide[here, :LANES]
            out_b = wide[here, LANES:]
            din = dout = None
            for c in range(groups):
                cols = pl.ds(c * LANES, LANES)
                before = states_ref[prior, cols].astype(F32)
                if j == 0:
                    before = jnp.where(jnp.full((ns, LANES), t, jnp.int32) == 0, starts_ref[0, :, cols], before)
                r2 = r2_s[c]
                dec = jnp.exp2(row(stepd_s, c, t, ns) * r2)
                ds = row(dscan_s, c, t, ns)
                d = later[c] + out_b * ds
                later[c] = dec * d
                dexp = later[c] * before
                e = dexp * r2
                cf = d * in_b
                cparts[c][j] = sum(cf[8 * q:8 * q + 8] for q in range(ns // 8))
                eparts[c][j] = sum(e[8 * q:8 * q + 8] for q in range(ns // 8))
                acc[c] = acc[c] + dexp * row(step_s, c, t, ns)
                a = d * row(drive_s, c, t, ns)
                b = now[c] * ds
                din = a if din is None else din + a
                dout = b if dout is None else dout + b
                now[c] = before
            sums[here, :LANES] = din.astype(BF16)
            sums[here, LANES:] = dout.astype(BF16)
        rows = pl.ds(pl.multiple_of(first, 8), 8)
        for c in range(groups):
            cols = pl.ds(c * LANES, LANES)
            coeff_s[rows, cols] = fold_rows(cparts[c], masks)
            exps_s[rows, cols] = fold_rows(eparts[c], masks)
        return later, acc

    def body(k, carry):
        later, acc = [list(v) for v in carry]
        first = tb - 16 - k * 16
        gather(sums_a, jnp.minimum(first + 16, tb - 8))
        wide_a[...] = coefficient_rows(ns, rank, proj_ref, first)
        later, acc = eight(first + 8, wide_b, sums_b, later, acc)
        gather(sums_b, first + 8)
        wide_b[...] = coefficient_rows(ns, rank, proj_ref, jnp.maximum(first - 8, 0))
        later, acc = eight(first, wide_a, sums_a, later, acc)
        return tuple(later), tuple(acc)

    wide_b[...] = coefficient_rows(ns, rank, proj_ref, tb - 8)
    sums_a[...] = jnp.zeros_like(sums_a)
    later, acc = lax.fori_loop(0, tb // 16, body, (later, acc))
    gather(sums_a, 0)
    return later, acc


def scan_fwd_kernel(ns, rank, proj_ref, inner_ref, keep_ref, sproj_ref, sbias_ref, lr_ref, skip_ref,
                    scan_ref, step_ref, states_ref, starts_ref, state_s, stepd_s, drive_s, r2_s, wide_a, wide_b):
    tb, ch = inner_ref.shape
    groups = ch // LANES
    i = pl.program_id(0)

    @pl.when(i == 0)
    def _():
        state_s[...] = jnp.zeros_like(state_s)
        spread(r2_s, jnp.exp(lr_ref[...]) * (-LOG2E))

    step_in = proj_ref[...].astype(BF16)
    pre = jnp.dot(step_in, sproj_ref[...], preferred_element_type=F32) + sbias_ref[...]
    step = softplus(pre)
    step_ref[...] = step
    spread(stepd_s, jnp.where(keep_ref[...] > 0.0, step, 1e30))
    inner = inner_ref[...].astype(F32)
    spread(drive_s, step * inner)
    starts_ref[0] = state_s[...]
    start = tuple(state_s[:, c * LANES:(c + 1) * LANES] for c in range(groups))
    state = forward_tokens(ns, rank, proj_ref, stepd_s, drive_s, r2_s, states_ref, scan_ref, start, wide_a, wide_b)
    for c in range(groups):
        state_s[:, c * LANES:(c + 1) * LANES] = state[c]
    scan_ref[...] += skip_ref[...] * inner


def scan_fwd(proj, inner, keep, sproj, sbias, log_rates, skip, rank):
    seq, ch = inner.shape
    ns = log_rates.shape[0]
    tb = LANES
    nb = seq // tb
    full = lambda a: pl.BlockSpec(a.shape, lambda i: (0,) * a.ndim)
    rows = pl.BlockSpec((tb, ch), lambda i: (i, 0))
    return pl.pallas_call(
        functools.partial(scan_fwd_kernel, ns, rank),
        grid=(nb,),
        in_specs=[pl.BlockSpec((tb, LANES), lambda i: (i, 0)), rows, pl.BlockSpec((tb, 1), lambda i: (i, 0)),
                  full(sproj), full(sbias), full(log_rates), full(skip)],
        out_specs=[rows, rows, pl.BlockSpec((tb * ns, ch), lambda i: (i, 0)), pl.BlockSpec((1, ns, ch), lambda i: (i, 0, 0))],
        out_shape=[jax.ShapeDtypeStruct((seq, ch), F32), jax.ShapeDtypeStruct((seq, ch), F32),
                   jax.ShapeDtypeStruct((seq * ns, ch), BF16), jax.ShapeDtypeStruct((nb, ns, ch), F32)],
        scratch_shapes=[pltpu.VMEM((ns, ch), F32)] + [pltpu.VMEM((ch // LANES, tb, LANES), F32)] * 2 + [pltpu.VMEM((ch // LANES, ns, LANES), F32),
                        *[pltpu.VMEM((8 * ns, 2 * LANES), F32)] * 2],
        compiler_params=pltpu.CompilerParams(vmem_limit_bytes=48 << 20),
        name="scan_fwd",
    )(proj, inner, keep, sproj, sbias, log_rates, skip)


def scan_bwd_kernel(ns, rank, proj_ref, inner_ref, keep_ref, step_ref, states_ref, starts_ref, dscan_ref, sproj_ref, lr_ref, skip_ref,
                    dpre_ref, dinner_ref, dproj_ref, gstep_ref, gsbias_ref, grates_ref, gskip_ref,
                    carry_s, stepd_s, drive_s, dscan_s, step_s, r2_s, coeff_s, exps_s, acc_s, wide_a, wide_b, sums_a, sums_b):
    tb, ch = inner_ref.shape
    groups = ch // LANES
    i = pl.program_id(0)

    @pl.when(i == 0)
    def _():
        carry_s[...] = jnp.zeros_like(carry_s)
        acc_s[...] = jnp.zeros_like(acc_s)
        spread(r2_s, jnp.exp(lr_ref[...]) * (-LOG2E))
        gstep_ref[...] = jnp.zeros_like(gstep_ref)
        gsbias_ref[...] = jnp.zeros_like(gsbias_ref)
        gskip_ref[...] = jnp.zeros_like(gskip_ref)

    step = step_ref[...]
    inner = inner_ref[...].astype(F32)
    dscan = dscan_ref[...]
    spread(stepd_s, jnp.where(keep_ref[...] > 0.0, step, 1e30))
    spread(drive_s, step * inner)
    spread(dscan_s, dscan)
    spread(step_s, step)
    pick = lambda ref: tuple(ref[:, c * LANES:(c + 1) * LANES] for c in range(groups))
    later, acc = backward_tokens(ns, rank, proj_ref, states_ref, starts_ref, stepd_s, drive_s, dscan_s, step_s, r2_s, coeff_s, exps_s,
                                 dproj_ref, pick(carry_s), pick(acc_s), wide_a, wide_b, sums_a, sums_b)
    for c in range(groups):
        carry_s[:, c * LANES:(c + 1) * LANES] = later[c]
        acc_s[:, c * LANES:(c + 1) * LANES] = acc[c]
    coeff = coeff_s[...]
    d_step = coeff * inner + exps_s[...] * (1.0 / LOG2E)
    d_pre = (d_step * (1.0 - jnp.exp(-step))).astype(BF16)
    dpre_ref[...] = d_pre
    dinner_ref[...] = dscan * skip_ref[...] + step * coeff
    step_in = proj_ref[...].astype(BF16)
    gstep_ref[...] += lax.dot_general(step_in, d_pre, (((0,), (0,)), ((), ())), preferred_element_type=F32)
    gsbias_ref[...] += jnp.sum(d_pre.astype(F32), axis=0, keepdims=True)
    gskip_ref[...] += jnp.sum(dscan * inner, axis=0, keepdims=True)
    dproj_ref[...] += lax.dot_general(d_pre, sproj_ref[...], (((1,), (1,)), ((), ())), preferred_element_type=F32)

    @pl.when(i == pl.num_programs(0) - 1)
    def _():
        grates_ref[...] = -jnp.exp(lr_ref[...]) * acc_s[...]


def scan_bwd(proj, inner, keep, step, states, starts, dscan, sproj, log_rates, skip, rank):
    seq, ch = inner.shape
    ns = log_rates.shape[0]
    tb = LANES
    nb = seq // tb
    full = lambda a: pl.BlockSpec(a.shape, lambda i: (0,) * a.ndim)
    rows = pl.BlockSpec((tb, ch), lambda i: (nb - 1 - i, 0))
    prow = pl.BlockSpec((tb, LANES), lambda i: (nb - 1 - i, 0))
    whole = lambda *s: pl.BlockSpec(s, lambda i: (0,) * len(s))
    shape = jax.ShapeDtypeStruct
    return pl.pallas_call(
        functools.partial(scan_bwd_kernel, ns, rank),
        grid=(nb,),
        in_specs=[prow, rows, pl.BlockSpec((tb, 1), lambda i: (nb - 1 - i, 0)), rows,
                  pl.BlockSpec((tb * ns, ch), lambda i: (nb - 1 - i, 0)), pl.BlockSpec((1, ns, ch), lambda i: (nb - 1 - i, 0, 0)),
                  rows, full(sproj), full(log_rates), full(skip)],
        out_specs=[rows, rows, prow, whole(LANES, ch), whole(1, ch), whole(ns, ch), whole(1, ch)],
        out_shape=[shape((seq, ch), BF16), shape((seq, ch), F32), shape((seq, LANES), F32), shape((LANES, ch), F32), shape((1, ch), F32),
                   shape((ns, ch), F32), shape((1, ch), F32)],
        scratch_shapes=[pltpu.VMEM((ns, ch), F32)] + [pltpu.VMEM((ch // LANES, tb, LANES), F32)] * 4 + [pltpu.VMEM((ch // LANES, ns, LANES), F32),
                        pltpu.VMEM((tb, ch), F32), pltpu.VMEM((tb, ch), F32), pltpu.VMEM((ns, ch), F32),
                        *[pltpu.VMEM((8 * ns, 2 * LANES), F32)] * 2, *[pltpu.VMEM((8 * ns, 2 * LANES), BF16)] * 2],
        compiler_params=pltpu.CompilerParams(vmem_limit_bytes=48 << 20),
        name="scan_bwd",
    )(proj, inner, keep, step, states, starts, dscan, sproj, log_rates, skip)


def tall(ref):
    value = ref[...]
    return jnp.concatenate([value, jnp.zeros((LANES - value.shape[0], value.shape[1]), value.dtype)], axis=0)


def as_row(ref):
    return ref[...].reshape(1, ref.shape[0])


def line_roles():
    me = lax.axis_index("tp")
    end = (me == 0) | (me == 3)
    mate = jnp.where(me < 2, 1 - me, 5 - me)
    return end, jnp.logical_not(end), mate, 3 - me


LINE = 4
PIECES, SLOT_PIECES = 2, 2
MIX_BEHIND, SLOT_BEHIND, DN_BEHIND = 2, 2, 2
OUT_STEPS = (0, 1, 2, 3, 4, 5, 6, 7)


def greet(wide):
    barrier = pltpu.get_barrier_semaphore()
    for axis, size in (("tp", LINE), ("wide", wide)):
        me = lax.axis_index(axis)
        for k in range(1, size):
            pl.semaphore_signal(barrier, inc=1, device_id={axis: lax.rem(me + k, size)}, device_id_type=MESH)
    pl.semaphore_wait(barrier, LINE + wide - 2)


class LineSum:
    def __init__(self, roles, rows, pieces, own, near, half, far, sends, arrivals, behind=None, last=None):
        self.end, self.mid, self.mate, self.other = roles
        self.rows, self.pieces = rows // pieces, pieces
        self.behind = pieces if behind is None else behind
        self.last = last
        self.own, self.near, self.half, self.far = own, near, half, far
        self.sends, self.arrivals = sends, arrivals

    def part(self, ref, n):
        return ref.at[pl.ds(pl.multiple_of(n * self.rows, self.rows), self.rows)]

    def copy(self, source, target, hop, n, to):
        return pltpu.make_async_remote_copy(
            self.part(source, n), self.part(target, n), self.sends.at[hop, n], self.arrivals.at[hop, n],
            device_id={"tp": to}, device_id_type=MESH)

    def up(self, n):
        return self.copy(self.own, self.near, 0, n, self.mate)

    def across(self, n):
        return self.copy(self.half, self.far, 1, n, self.other)

    def down(self, n):
        return self.copy(self.far, self.far, 2, n, self.mate)

    def add(self, a, b, c, n):
        self.part(c, n)[...] = (self.part(a, n)[...].astype(F32) + self.part(b, n)[...].astype(F32)).astype(BF16)

    def each(self, k):
        return [k * self.pieces + j for j in range(self.pieces)]

    def start(self, k):
        for n in self.each(k):
            self.up(n).start()

    def first(self, n):
        self.up(n).wait_recv()
        self.add(self.own, self.near, self.half, n)
        self.across(n).start()

    def second(self, n):
        self.across(n).wait_recv()
        self.add(self.half, self.far, self.far, n)
        self.down(n).start()

    def place(self, m):
        if self.last is None:
            return m
        return (self.last - m // self.pieces) * self.pieces + m % self.pieces

    def flow(self, k, done=None):
        for j in range(self.pieces):
            m = k * self.pieces + j
            self.first(self.place(m))

            @pl.when(m >= self.behind)
            def _():
                self.second(self.place(m - self.behind))
                if done and (j - self.behind) % self.pieces == self.pieces - 1:
                    done(self.place(m - self.behind) // self.pieces)

    def flush(self, count, done=None):
        for m in range(count * self.pieces - self.behind, count * self.pieces):
            self.second(self.place(m))
            if done and m % self.pieces == self.pieces - 1:
                done(jnp.int32(self.place(m) // self.pieces))

    def arrived(self, k):
        for n in self.each(k):
            self.down(n).wait_recv()

    def sent(self, count):
        def block(n, _):
            @pl.when(self.end)
            def _():
                self.up(n).wait_send()

            @pl.when(self.mid)
            def _():
                self.across(n).wait_send()
                self.down(n).wait_send()
            return 0

        lax.fori_loop(0, count * self.pieces, block, 0)


def pack_rows(rank, states, experts, width, ch, wide):
    rows = 8 + states + rank + (rank + 2 * states) + 8 + (width // ch) * experts
    return -(-rows // (8 * wide)) * (8 * wide)


def finish_kernel(rank, states, tokens_ref, mixed_ref, scol_ref, got_ref, dhidden_ref, dn_ref, scale_ref, gain_ref, small_ref,
                  gx_ref, gz_ref, go_ref, gup_ref, gdown_ref, gub_ref, gdb_ref,
                  result_ref, tgrad_ref, first_ref, gx_out, gz_out, cw_ref, cb_ref, state_ref, step_ref, sb_ref, rates_ref, skip_ref, go_out,
                  second_ref, router_ref, gup_out, gub_out, gdown_out, gdb_out):
    i = pl.program_id(0)
    ch = small_ref.shape[1]
    width, experts = router_ref.shape
    gup_out[0] = gup_ref[...]
    gdown_out[0] = gdown_ref[...]

    @pl.when(i == 0)
    def _():
        for ref, out in ((gx_ref, gx_out), (gz_ref, gz_out), (go_ref, go_out), (gub_ref, gub_out), (gdb_ref, gdb_out)):
            out[...] = ref[...]
        flat = lambda r: small_ref[r:r + 1, :].reshape(ch)
        cb_ref[...] = flat(0)
        sb_ref[...] = flat(1)
        skip_ref[...] = flat(2)
        cw_ref[...] = small_ref[4:8, :]
        at = 8
        rates_ref[...] = small_ref[at:at + states, :]
        at += states
        step_ref[...] = small_ref[at:at + rank, :]
        at += rank
        held = rank + 2 * states
        state_ref[...] = small_ref[at:at + held, :].T
        at += held
        halves = width // ch
        for h in range(halves):
            cols = slice(h * ch, (h + 1) * ch)
            first_ref[cols] = flat(at + h)
            second_ref[cols] = flat(at + halves + h)
            router_ref[cols, :] = small_ref[at + 8 + h * experts:at + 8 + (h + 1) * experts, :].T

    ids = lax.broadcasted_iota(jnp.int32, (scol_ref.shape[0], got_ref.shape[0]), 1)
    chosen = jnp.where(ids == scol_ref[...], 1.0, 0.0).astype(BF16)
    tokens = tokens_ref[...]
    result_ref[...] = tokens + mixed_ref[...].astype(F32) + jnp.dot(chosen, got_ref[...], preferred_element_type=F32)
    scale = scale_ref[...]
    unit = tokens * scale
    through = dn_ref[...].astype(F32) * as_row(gain_ref)
    mean = jnp.mean(through * unit, axis=1, keepdims=True)
    tgrad_ref[...] = dhidden_ref[...] + scale * (through - unit * mean)


def finish(rank, states, experts, *operands):
    tokens, mixed, scol, got, dhidden, dn, scale, gain, small, gx, gz, go, gup, gdown, gub, gdb = operands
    seq, width = tokens.shape
    ch = small.shape[1]
    tb = LANES
    row = lambda n: pl.BlockSpec((tb, n), lambda i: (i, 0))
    full = lambda a: pl.BlockSpec(a.shape, lambda i: (0,) * a.ndim)
    whole = lambda *s: pl.BlockSpec(s, lambda i: (0,) * len(s))
    sizes = [(width,), gx.shape, gz.shape, (4, ch), (ch,), (ch, rank + 2 * states), (rank, ch), (ch,), (states, ch), (ch,), go.shape,
             (width,), (width, experts), (1, *gup.shape), gub.shape, (1, *gdown.shape), gdb.shape]
    nb = seq // tb
    piece = lambda a: pl.BlockSpec((a.shape[0] // nb, a.shape[1]), lambda i: (i, 0))
    placed = lambda size: pl.BlockSpec((1, size[1] // nb, size[2]), lambda i: (0, i, 0)) if len(size) == 3 else whole(*size)
    return pl.pallas_call(
        functools.partial(finish_kernel, rank, states),
        grid=(seq // tb,),
        in_specs=[row(width), row(width), row(1), full(got), row(width), row(width), row(1), full(gain), full(small), full(gx), full(gz), full(go), piece(gup), piece(gdown), full(gub), full(gdb)],
        out_specs=[row(width), row(width), *[placed(size) for size in sizes]],
        out_shape=[jax.ShapeDtypeStruct(size, F32) for size in [(seq, width), (seq, width), *sizes]],
        compiler_params=pltpu.CompilerParams(vmem_limit_bytes=62 << 20),
        name="finish",
    )(*operands)


def mixer_back_kernel(ns, rank, wide, taps, proj_ref, keep_ref, step_ref, states_ref, starts_ref, tokens_ref, mixed_ref, ograd_ref, scol_ref, z_ref, scan_ref,
                      inner_ref, sproj_ref, lr_ref, skip_ref, ret_ref, gain_ref, wo_ref, term_ref,
                      x_ref, csum_ref, masks_ref, wproj_ref, cw_ref, normed_ref, gated_ref, wx_ref, wz_ref, first_gain_ref, grow_ref,
                      dhidden_ref, dn_ref, gx_ref, gz_ref, go_ref, small_ref, got_ref,
                      carry_s, stepd_s, drive_s, dscan_s, step_s, r2_s, coeff_s, exps_s, acc_s, dproj_s, wide_a, wide_b, sums_a, sums_b,
                      near_s, half_s, far_s, sends, arrivals, got_sends, got_arrivals,
                      dp_own, dp_near, dp_far, dp_sends, dp_arrivals, dn_own, dn_near, dn_far, dn_sends, dn_arrivals,
                      prod_s, inbox_s, prod_sends, prod_arrivals, pack_s, pack_in, small_s, pack_sends, pack_arrivals,
                      dinner_s, dmixed_s, dz_s, dconv_s, dx_s, gstep_s, state_s, first_s, second_s, dscan_all, gains_s):
    seq, ch = inner_ref.shape
    width = normed_ref.shape[1]
    tb = LANES
    nb = seq // tb
    groups = ch // LANES
    i = pl.program_id(0)
    me = lax.axis_index("wide")
    roles = line_roles()
    end, mid, mate, other = roles
    cap = term_ref.shape[0] // wide
    line = LineSum(roles, cap, SLOT_PIECES, term_ref, near_s, half_s, far_s, sends, arrivals)
    dp = LineSum(roles, tb, 1, dp_own, dp_near, dp_own, dp_far, dp_sends, dp_arrivals, last=nb - 1)
    dn = LineSum(roles, tb, PIECES, dn_own, dn_near, dn_own, dn_far, dn_sends, dn_arrivals, behind=DN_BEHIND, last=nb - 1)
    block = width // wide
    turned = (((1,), (1,)), ((), ()))
    across_rows = (((0,), (0,)), ((), ()))

    def slot_rows(c):
        return pl.ds(pl.multiple_of(c * cap, cap), cap)

    def rows_of(b):
        return pl.ds(pl.multiple_of(b * tb, tb), tb)

    def give_back(c):
        return pltpu.make_async_remote_copy(
            far_s.at[slot_rows(c)], got_ref.at[slot_rows(me)], got_sends.at[c], got_arrivals.at[c],
            device_id={"wide": lax.rem(me + wide - c, wide)}, device_id_type=MESH)

    def return_chunk(c):
        @pl.when(c == 0)
        def _():
            here = pltpu.make_async_copy(far_s.at[slot_rows(0)], got_ref.at[slot_rows(me)], got_sends.at[0])
            here.start()
            here.wait()

        @pl.when(c != 0)
        def _():
            give_back(c).start()

    def deliver(which, k):
        to = lax.rem(me + k, wide)
        return pltpu.make_async_remote_copy(
            prod_s.at[which, pl.ds(pl.multiple_of(to * block, block), block)], inbox_s.at[which, k],
            prod_sends.at[which, k], prod_arrivals.at[which, k], device_id={"wide": to}, device_id_type=MESH)

    def product(which, left, right):
        def tile(j, _):
            cols = pl.ds(pl.multiple_of(j * LANES, LANES), LANES)
            got = lax.dot_general(left[:, cols], right[...], across_rows, preferred_element_type=F32)
            prod_s[which, cols, :] = got.astype(BF16)
            return 0

        lax.fori_loop(0, width // LANES, tile, 0)
        for k in range(1, wide):
            deliver(which, k).start()

    @pl.when(i == 0)
    def _():
        greet(wide)
        for ref in (carry_s, acc_s, gstep_s, state_s, first_s, second_s, pack_s):
            ref[...] = jnp.zeros_like(ref)
        dconv_s[pl.ds(seq, 8), :] = jnp.zeros((8, ch), F32)
        spread(r2_s, jnp.exp(lr_ref[...]) * (-LOG2E))

    def at_out_steps(role, lag, work):
        for c, step in enumerate(OUT_STEPS):
            @pl.when(role & (i == step + lag))
            def _():
                work(jnp.int32(c))

    at_out_steps(end, 0, line.start)

    def glue(g):
        part = tokens_ref.shape[0]
        rows = pl.ds(pl.multiple_of((seq // part - 1 - g) * part, part), part)
        hidden = tokens_ref[...] + mixed_ref[...].astype(F32)
        scale = lax.rsqrt(jnp.mean(hidden * hidden, axis=1, keepdims=True) + EPS)
        unit = hidden * scale
        ids = lax.broadcasted_iota(jnp.int32, (part, wide * cap), 1)
        chosen = jnp.where(ids == scol_ref[...], 1.0, 0.0).astype(BF16)
        d_norm_two = jnp.dot(chosen, ret_ref[...], preferred_element_type=F32)
        second_s[...] += jnp.sum(d_norm_two * unit, axis=0, keepdims=True)
        through = d_norm_two * as_row(gain_ref)
        d_hidden = ograd_ref[...] + scale * (through - unit * jnp.mean(through * unit, axis=1, keepdims=True))
        dhidden_ref[...] = d_hidden
        d_mixed = d_hidden.astype(BF16)
        dmixed_s[rows, :] = d_mixed
        d_gated = jnp.dot(d_mixed, wo_ref[...], preferred_element_type=F32)
        z = z_ref[...]
        logistic = 1.0 / (1.0 + jnp.exp(-z))
        dz_s[rows, :] = (d_gated * scan_ref[...] * (logistic * (1.0 + z * (1.0 - logistic)))).astype(BF16)
        dscan_all[rows, :] = d_gated * (z * logistic)

    def scan_block():
        b = nb - 1 - i
        rows = rows_of(b)
        step = step_ref[...]
        inner = inner_ref[rows, :].astype(F32)
        dscan = dscan_all[rows, :]
        spread(stepd_s, jnp.where(keep_ref[...] > 0.0, step, 1e30))
        spread(drive_s, step * inner)
        spread(dscan_s, dscan)
        spread(step_s, step)
        pick = lambda ref: tuple(ref[:, c * LANES:(c + 1) * LANES] for c in range(groups))
        later, acc = backward_tokens(ns, rank, proj_ref, states_ref, starts_ref, stepd_s, drive_s, dscan_s, step_s, r2_s, coeff_s, exps_s,
                                     dproj_s, pick(carry_s), pick(acc_s), wide_a, wide_b, sums_a, sums_b)
        for c in range(groups):
            carry_s[:, c * LANES:(c + 1) * LANES] = later[c]
            acc_s[:, c * LANES:(c + 1) * LANES] = acc[c]
        coeff = coeff_s[...]
        d_step = coeff * inner + exps_s[...] * (1.0 / LOG2E)
        d_pre = (d_step * (1.0 - jnp.exp(-step))).astype(BF16)
        dinner_s[rows, :] = dscan * as_row(skip_ref) + step * coeff
        step_in = proj_ref[...].astype(BF16)
        gstep_s[...] += lax.dot_general(step_in, d_pre, across_rows, preferred_element_type=F32)
        pack_s[1:2, :] += jnp.sum(d_pre.astype(F32), axis=0, keepdims=True)
        pack_s[2:3, :] += jnp.sum(dscan * inner, axis=0, keepdims=True)
        both = dproj_s[...] + lax.dot_general(d_pre, tall(sproj_ref), turned, preferred_element_type=F32)
        dp_own[rows, :] = both.astype(BF16)

        @pl.when(end)
        def _():
            dp.start(b)

    def conv_block(k):
        b = nb - 1 - k
        rows = rows_of(b)
        base = pl.multiple_of(b * tb, tb)

        @pl.when(end)
        def _():
            dp.arrived(b)

        d_proj = dp_far[rows, :]
        state_s[...] += lax.dot_general(d_proj, inner_ref[rows, :], across_rows, preferred_element_type=F32)
        d_inner = dinner_s[rows, :] + lax.dot_general(d_proj[:, :wproj_ref.shape[1]], wproj_ref[...], turned, preferred_element_type=F32)
        csum = csum_ref[rows, :]
        logistic = 1.0 / (1.0 + jnp.exp(-csum))
        d_conv = d_inner * (logistic * (1.0 + csum * (1.0 - logistic)))
        prior = x_ref[pl.ds(pl.multiple_of(jnp.maximum(base - 8, 0), 8), 8), :]
        history = jnp.concatenate([prior, x_ref[rows, :]], axis=0)
        ahead = jnp.concatenate([d_conv, dconv_s[pl.ds(pl.multiple_of(base + tb, 8), 8), :]], axis=0)
        dconv_s[rows, :] = d_conv
        same = masks_ref[pl.ds(base, tb + 8), :]
        d_x = cw_ref[taps - 1:taps, :] * d_conv
        pack_s[0:1, :] += jnp.sum(d_conv, axis=0, keepdims=True)
        pack_s[8 - 1:8, :] += jnp.sum(d_conv * history[8:, :], axis=0, keepdims=True)
        for s in range(1, taps):
            linked = same[:, s:s + 1] * ahead
            d_x = d_x + cw_ref[taps - 1 - s:taps - s, :] * linked[s:s + tb, :]
            pack_s[7 - s:8 - s, :] += jnp.sum(linked[:tb, :] * history[8 - s:8 - s + tb, :], axis=0, keepdims=True)
        d_x = d_x.astype(BF16)
        dx_s[rows, :] = d_x
        both = lax.dot_general(d_x, wx_ref[...], turned, preferred_element_type=F32)
        both = both + lax.dot_general(dz_s[rows, :], wz_ref[...], turned, preferred_element_type=F32)
        dn_own[rows, :] = both.astype(BF16)

        @pl.when(end)
        def _():
            dn.start(b)

    def last_block(k):
        b = nb - 1 - k
        rows = rows_of(b)

        @pl.when(end)
        def _():
            dn.arrived(b)

        d_normed = dn_far[rows, :]
        dn_ref[...] = d_normed
        first_s[...] += jnp.sum(d_normed.astype(F32) * normed_ref[rows, :].astype(F32), axis=0, keepdims=True)

    def at_step(lag, count, work):
        @pl.when((i >= lag) & (i < lag + count))
        def _():
            work(i - lag)

    def on_mid(lag, count, work):
        @pl.when(mid & (i >= lag) & (i < lag + count))
        def _():
            work(i - lag)

    def line_down(c):
        line.arrived(c)
        return_chunk(c)

    parts = seq // tokens_ref.shape[0]
    at_step(0, parts, glue)
    at_step(parts, 1, lambda k: product(0, dmixed_s, gated_ref))
    at_step(parts + 1, 1, lambda k: product(1, normed_ref, dz_s))
    at_step(0, nb, lambda k: scan_block())
    on_mid(1, nb, dp.flow)
    on_mid(nb + 1, 1, lambda k: dp.flush(nb))
    at_step(3, nb, conv_block)
    on_mid(4, nb, dn.flow)
    on_mid(nb + 4, 1, lambda k: dn.flush(nb))
    at_out_steps(mid, 1, lambda c: line.flow(c, return_chunk))
    on_mid(OUT_STEPS[-1] + 2, 1, lambda k: line.flush(wide, return_chunk))

    at_out_steps(end, 3, line_down)
    at_step(nb + 2, 1, lambda k: product(2, normed_ref, dx_s))
    at_step(6, nb, last_block)

    share = pack_s.shape[0] // wide
    halves = width // ch
    gains_at = 8 + ns + rank + rank + 2 * ns

    def chunk(ref, n):
        return ref.at[pl.ds(pl.multiple_of(n * share, share), share)]

    def scatter(k):
        to = lax.rem(me + k, wide)
        return pltpu.make_async_remote_copy(chunk(pack_s, to), pack_in.at[k], pack_sends.at[0, k], pack_arrivals.at[0, k],
                                            device_id={"wide": to}, device_id_type=MESH)

    def spread_out(k):
        to = lax.rem(me + k, wide)
        return pltpu.make_async_remote_copy(chunk(small_s, me), chunk(small_s, me), pack_sends.at[1, k], pack_arrivals.at[1, k],
                                            device_id={"wide": to}, device_id_type=MESH)

    def gain_term(k):
        to = lax.rem(me + k, wide)
        return pltpu.make_async_remote_copy(gains_s.at[me], gains_s.at[me], pack_sends.at[2, k], pack_arrivals.at[2, k],
                                            device_id={"wide": to}, device_id_type=MESH)

    def collect(which, ref):
        total = prod_s[which, pl.ds(pl.multiple_of(me * block, block), block), :].astype(F32)
        for k in range(1, wide):
            deliver(which, k).wait_recv()
            total = total + inbox_s[which, k].astype(F32)
        ref[...] = total

    @pl.when(i == nb + 3)
    def _():
        at = 8
        pack_s[at:at + ns, :] = -jnp.exp(lr_ref[...]) * acc_s[...]
        at += ns
        pack_s[at:at + rank, :] = gstep_s[0:rank, :]
        at += rank
        held = rank + 2 * ns
        pack_s[at:at + held, :] = state_s[0:held, :]
        own_row = lax.broadcasted_iota(jnp.int32, (wide, ch), 0) == me
        for h in range(halves):
            cols = slice(h * ch, (h + 1) * ch)
            pack_s[gains_at + halves + h:gains_at + halves + h + 1, :] = second_s[:, cols]
            pack_s[gains_at + 8 + h * wide:gains_at + 8 + (h + 1) * wide, :] = jnp.where(own_row, grow_ref[:, cols], 0.0)
        for k in range(1, wide):
            scatter(k).start()
        collect(0, go_ref)

    @pl.when(i == nb + 4)
    def _():
        total = chunk(pack_s, me)[...]
        for k in range(1, wide):
            scatter(k).wait_recv()
            total = total + pack_in[k]
        chunk(small_s, me)[...] = total
        for k in range(1, wide):
            spread_out(k).start()
        collect(1, gz_ref)

    @pl.when(i == pl.num_programs(0) - 1)
    def _():
        gains_s[me] = jnp.broadcast_to(first_s[...] / as_row(first_gain_ref), (8, width))
        for k in range(1, wide):
            gain_term(k).start()
        collect(2, gx_ref)
        line.sent(wide)
        dp.sent(nb)
        dn.sent(nb)
        for k in range(1, wide):
            spread_out(k).wait_recv()
        small_ref[...] = small_s[...]
        for k in range(1, wide):
            gain_term(k).wait_recv()
        first = gains_s[0, 0:1, :]
        for n in range(1, wide):
            first = first + gains_s[n, 0:1, :]
        for h in range(halves):
            small_ref[gains_at + h:gains_at + h + 1, :] = first[:, h * ch:(h + 1) * ch]
        for k in range(1, wide):
            give_back(k).wait_recv()
            give_back(k).wait_send()
            for which in range(3):
                deliver(which, k).wait_send()
            scatter(k).wait_send()
            spread_out(k).wait_send()
            gain_term(k).wait_send()


def mixer_back(wide, taps, rank, by_rows, whole_ones):
    proj, keep, step, states, starts, tokens, mixed, ograd, scol, z, scan = by_rows
    inner, log_rates, ret = whole_ones[0], whole_ones[2], whole_ones[4]
    seq, ch = inner.shape
    width = tokens.shape[1]
    ns = log_rates.shape[0]
    tb = LANES
    nb = seq // tb
    packed = pack_rows(rank, ns, wide, width, ch, wide)
    back = lambda i: jnp.maximum(nb - 1 - i, 0)
    early = lambda i: jnp.maximum(nb // 2 - 1 - i, 0)
    final = lambda i: nb - 1 - jnp.maximum(i - 6, 0)
    row = lambda n, size=tb: pl.BlockSpec((size, n), lambda i: (back(i), 0))
    full = lambda a: pl.BlockSpec(a.shape, lambda i: (0,) * a.ndim, pipeline_mode=pl.Buffered(1))
    whole = lambda *s: pl.BlockSpec(s, lambda i: (0,) * len(s))
    shape = jax.ShapeDtypeStruct
    dma = pltpu.SemaphoreType.DMA
    vm = pltpu.VMEM
    return pl.pallas_call(
        functools.partial(mixer_back_kernel, ns, rank, wide, taps),
        grid=(nb + 6,),
        in_specs=[row(LANES), row(1), row(ch), row(ch, tb * ns), pl.BlockSpec((1, ns, ch), lambda i: (back(i), 0, 0)),
                  *[pl.BlockSpec((2 * tb, n), lambda i: (early(i), 0)) for n in (width, width, width, 1, ch, ch)], *[full(a) for a in whole_ones]],
        out_specs=[pl.BlockSpec((2 * tb, width), lambda i: (early(i), 0)), pl.BlockSpec((tb, width), lambda i: (final(i), 0)), *[whole(width // wide, ch)] * 3, whole(packed, ch),
                   pl.BlockSpec(memory_space=pl.ANY)],
        out_shape=[shape((seq, width), F32), shape((seq, width), BF16), *[shape((width // wide, ch), F32)] * 3, shape((packed, ch), F32),
                   shape(ret.shape, BF16)],
        scratch_shapes=[
            vm((ns, ch), F32), *[vm((ch // LANES, tb, LANES), F32)] * 4, vm((ch // LANES, ns, LANES), F32), vm((tb, ch), F32), vm((tb, ch), F32),
            vm((ns, ch), F32), vm((tb, LANES), F32), *[vm((8 * ns, 2 * LANES), F32)] * 2, *[vm((8 * ns, 2 * LANES), BF16)] * 2,
            *[vm(ret.shape, BF16)] * 3, *[dma((3, wide * SLOT_PIECES))] * 2, dma((wide,)), dma((wide,)),
            *[vm((seq, LANES), BF16)] * 3, dma((3, nb)), dma((3, nb)), *[vm((seq, width), BF16)] * 3, *[dma((3, nb * PIECES))] * 2,
            vm((3, width, ch), BF16), vm((3, wide, width // wide, ch), BF16), dma((3, wide)), dma((3, wide)),
            vm((packed, ch), F32), vm((wide, packed // wide, ch), F32), vm((packed, ch), F32), dma((3, wide)), dma((3, wide)),
            vm((seq, ch), F32), vm((seq, width), BF16), vm((seq, ch), BF16), vm((seq + 8, ch), F32), vm((seq, ch), BF16),
            vm((LANES, ch), F32), vm((LANES, ch), F32), vm((1, width), F32), vm((1, width), F32),
            vm((seq, ch), F32), vm((wide, 8, width), F32)],
        compiler_params=pltpu.CompilerParams(collective_id=1, has_side_effects=True, vmem_limit_bytes=60 << 20),
        name="mixer_back",
    )(*by_rows, *whole_ones)


def gelu_pair(v):
    root = 0.7978845608028654
    square = v * v
    t = jnp.tanh(root * v * (1.0 + 0.044715 * square))
    half = 0.5 * (1.0 + t)
    slope = half + (0.5 * root) * v * (1.0 - t * t) * (1.0 + (3.0 * 0.044715) * square)
    return v * half, slope


def scan_mix_kernel(ns, rank, wide, proj_ref, inner_ref, keep_ref, sproj_ref, sbias_ref, lr_ref, skip_ref, z_ref, wo_ref, ograd_ref, srow_ref,
                    scan_ref, step_ref, states_ref, starts_ref, gated_ref, mixed_ref, gin_ref,
                    state_s, stepd_s, drive_s, r2_s, wide_a, wide_b, own_s, near_s, far_s, sends, arrivals, grad_s, send_s, g_sends, g_arrivals):
    tb, ch = inner_ref.shape
    groups = ch // LANES
    i = pl.program_id(0)
    roles = line_roles()
    end, mid, mate, other = roles
    line = LineSum(roles, tb, PIECES, own_s, near_s, own_s, far_s, sends, arrivals, behind=MIX_BEHIND)
    steps = pl.num_programs(0)
    seq_blocks = own_s.shape[0] // tb

    me = lax.axis_index("wide")
    cap = send_s.shape[0] // wide

    def slot_rows(k):
        return pl.ds(pl.multiple_of(k * cap, cap), cap)

    def dispatch(k):
        return pltpu.make_async_remote_copy(
            send_s.at[slot_rows(k)], gin_ref.at[slot_rows(k)], g_sends.at[k], g_arrivals.at[k],
            device_id={"wide": lax.rem(me + k, wide)}, device_id_type=MESH)

    own_rows = pltpu.make_async_copy(send_s.at[slot_rows(0)], gin_ref.at[slot_rows(0)], g_sends.at[0])

    @pl.when(i == 0)
    def _():
        greet(wide)
        grad_s[...] = ograd_ref[...].astype(BF16)
        state_s[...] = jnp.zeros_like(state_s)
        spread(r2_s, jnp.exp(lr_ref[...]) * (-LOG2E))

    @pl.when(i < wide)
    def _():
        ids = lax.broadcasted_iota(jnp.int32, (cap, grad_s.shape[0]), 0) + lax.rem(me + i, wide) * cap
        chosen = jnp.where(ids == srow_ref[...], 1.0, 0.0).astype(BF16)
        send_s[slot_rows(i), :] = jnp.dot(chosen, grad_s[...], preferred_element_type=F32).astype(BF16)

        @pl.when(i == 0)
        def _():
            own_rows.start()

        @pl.when(i > 0)
        def _():
            dispatch(i).start()

    step_in = proj_ref[...].astype(BF16)
    pre = jnp.dot(step_in, tall(sproj_ref), preferred_element_type=F32) + as_row(sbias_ref)
    step = softplus(pre)
    step_ref[...] = step
    spread(stepd_s, jnp.where(keep_ref[...] > 0.0, step, 1e30))
    inner = inner_ref[...].astype(F32)
    spread(drive_s, step * inner)
    starts_ref[0] = state_s[...]
    start = tuple(state_s[:, c * LANES:(c + 1) * LANES] for c in range(groups))
    state = forward_tokens(ns, rank, proj_ref, stepd_s, drive_s, r2_s, states_ref, scan_ref, start, wide_a, wide_b)
    for c in range(groups):
        state_s[:, c * LANES:(c + 1) * LANES] = state[c]
    scan = scan_ref[...] + as_row(skip_ref) * inner
    scan_ref[...] = scan
    z = z_ref[...]
    gated = (scan * (z / (1.0 + jnp.exp(-z)))).astype(BF16)
    gated_ref[...] = gated
    here = pl.ds(pl.multiple_of(i * tb, tb), tb)
    own_s[here, :] = lax.dot_general(gated, wo_ref[...], (((1,), (1,)), ((), ())), preferred_element_type=F32).astype(BF16)

    @pl.when(end)
    def _():
        line.start(i)

    @pl.when(mid & (i > 0))
    def _():
        line.flow(i - 1)

    @pl.when(i == steps - 1)
    def _():
        @pl.when(mid)
        def _():
            line.flow(i)
            line.flush(seq_blocks)

        @pl.when(end)
        def _():
            for k in range(steps):
                line.arrived(k)

        mixed_ref[...] = far_s[...]
        line.sent(steps)
        own_rows.wait()
        for k in range(1, wide):
            dispatch(k).wait_recv()
            dispatch(k).wait_send()


def scan_mix(proj, inner, keep, sproj, sbias, log_rates, skip, z, wo, ograd, srow, rank, wide, cap):
    seq, ch = inner.shape
    ns = log_rates.shape[0]
    tb = LANES
    nb = seq // tb
    width = wo.shape[0]
    full = lambda a: pl.BlockSpec(a.shape, lambda i: (0,) * a.ndim)
    rows = pl.BlockSpec((tb, ch), lambda i: (i, 0))
    return pl.pallas_call(
        functools.partial(scan_mix_kernel, ns, rank, wide),
        grid=(nb,),
        in_specs=[pl.BlockSpec((tb, LANES), lambda i: (i, 0)), rows, pl.BlockSpec((tb, 1), lambda i: (i, 0)),
                  full(sproj), full(sbias), full(log_rates), full(skip), rows, full(wo), full(ograd), full(srow)],
        out_specs=[rows, rows, pl.BlockSpec((tb * ns, ch), lambda i: (i, 0)), pl.BlockSpec((1, ns, ch), lambda i: (i, 0, 0)),
                   rows, pl.BlockSpec((seq, width), lambda i: (0, 0)), pl.BlockSpec(memory_space=pl.ANY)],
        out_shape=[jax.ShapeDtypeStruct((seq, ch), F32), jax.ShapeDtypeStruct((seq, ch), F32),
                   jax.ShapeDtypeStruct((seq * ns, ch), BF16), jax.ShapeDtypeStruct((nb, ns, ch), F32),
                   jax.ShapeDtypeStruct((seq, ch), BF16), jax.ShapeDtypeStruct((seq, width), BF16),
                   jax.ShapeDtypeStruct((wide * cap, width), BF16)],
        scratch_shapes=[pltpu.VMEM((ns, ch), F32)] + [pltpu.VMEM((ch // LANES, tb, LANES), F32)] * 2 + [pltpu.VMEM((ch // LANES, ns, LANES), F32),
                        *[pltpu.VMEM((8 * ns, 2 * LANES), F32)] * 2,
                        *[pltpu.VMEM((seq, width), BF16)] * 3, *[pltpu.SemaphoreType.DMA((3, nb * PIECES))] * 2,
                        pltpu.VMEM((seq, width), BF16), pltpu.VMEM((wide * cap, width), BF16),
                        pltpu.SemaphoreType.DMA((wide,)), pltpu.SemaphoreType.DMA((wide,))],
        compiler_params=pltpu.CompilerParams(collective_id=4, has_side_effects=True, vmem_limit_bytes=48 << 20),
        name="scan_mix",
    )(proj, inner, keep, sproj, sbias, log_rates, skip, z, wo, ograd, srow)


def experts_kernel(wide, tokens_ref, mixed_ref, gin_ref, srow_ref, gain_ref, router_ref, up_ref, ub_ref, down_ref, db_ref,
                   gup_ref, gub_ref, gdown_ref, gdb_ref, ret_ref, out_ref, grow_ref,
                   pay_s, send_s, inbox_s, rgrad_s, act_s, dpre_s, own_s, near_s, far_s, acc_s, column_s, rows_s,
                   pay_sends, pay_arrivals, sends, arrivals, ret_sends, ret_arrivals, r_sends, r_arrivals):
    seq, width = tokens_ref.shape
    hid = up_ref.shape[1]
    cap = inbox_s.shape[0] // wide
    tb = LANES
    me, rank = lax.axis_index("wide"), lax.axis_index("tp")
    roles = line_roles()
    end, mid, mate, other = roles
    greet(wide)
    back = LineSum(roles, cap, SLOT_PIECES, own_s, near_s, own_s, far_s, sends, arrivals, behind=SLOT_BEHIND)

    def rows_of(b, size):
        return pl.ds(pl.multiple_of(b * size, size), size)

    def prepare(b, _):
        rows = rows_of(b, tb)
        hidden = tokens_ref[rows, :] + mixed_ref[rows, :].astype(F32)
        scale = lax.rsqrt(jnp.mean(hidden * hidden, axis=1, keepdims=True) + EPS)
        pay_s[rows, :] = (hidden * scale * as_row(gain_ref)).astype(BF16)
        return 0

    lax.fori_loop(0, seq // tb, prepare, 0)

    def payload(expert):
        ids = lax.broadcasted_iota(jnp.int32, (cap, seq), 0) + expert * cap
        chosen = jnp.where(ids == srow_ref[...], 1.0, 0.0).astype(BF16)
        return jnp.dot(chosen, pay_s[...], preferred_element_type=F32).astype(BF16)

    def dispatch(k):
        return pltpu.make_async_remote_copy(
            send_s.at[rows_of(k, cap)], inbox_s.at[rows_of(k, cap)], pay_sends.at[k], pay_arrivals.at[k],
            device_id={"wide": lax.rem(me + k, wide)}, device_id_type=MESH)

    def send(k):
        send_s[rows_of(k, cap), :] = payload(lax.rem(me + k, wide))
        dispatch(k).start()

    ahead = 2

    def send_first(k, _):
        send(k)
        return 0

    lax.fori_loop(1, ahead + 1, send_first, 0)
    inbox_s[0:cap, :] = payload(me)

    def give_back(c):
        return pltpu.make_async_remote_copy(
            far_s.at[rows_of(c, cap)], ret_ref.at[rows_of(me, cap)], ret_sends.at[c], ret_arrivals.at[c],
            device_id={"wide": lax.rem(me + wide - c, wide)}, device_id_type=MESH)

    def return_chunk(c):
        @pl.when(c == 0)
        def _():
            ret_ref[rows_of(me, cap), :] = far_s[0:cap, :]

        @pl.when(c != 0)
        def _():
            give_back(c).start()

    gub_ref[...] = jnp.zeros_like(gub_ref)
    gdb_ref[...] = jnp.zeros_like(gdb_ref)
    acc_s[...] = jnp.zeros_like(acc_s)
    turned = (((1,), (1,)), ((), ()))
    mine = jnp.where(lax.broadcasted_iota(jnp.int32, (8, wide), 1) == me, 1.0, 0.0).astype(BF16)
    column_s[...] = lax.dot_general(mine, router_ref[...], turned, preferred_element_type=F32)[0:1, :]
    lane = lax.broadcasted_iota(jnp.int32, (cap, wide), 1)

    def compute(k, _):
        @pl.when(k + ahead < wide - 1)
        def _():
            send(k + ahead + 1)

        @pl.when(k > 0)
        def _():
            dispatch(k).wait_recv()

        part = rows_of(k, cap)
        rows_in = inbox_s[part, :]
        rows_raw = gin_ref[part, :].astype(F32)
        logits = jnp.dot(rows_in, router_ref[...], preferred_element_type=F32)
        logit = jnp.sum(jnp.where(lane == me, logits, 0.0), axis=1, keepdims=True)
        gate = 1.0 / (1.0 + jnp.exp(-logit))
        rows_grad = (gate * rows_raw).astype(BF16)
        rgrad_s[part, :] = rows_grad
        pre = jnp.dot(rows_in, up_ref[...], preferred_element_type=F32) + ub_ref[...]
        act, slope = gelu_pair(pre)
        act = act.astype(BF16)
        act_s[part, :] = act
        d_pre = (lax.dot_general(rows_grad, down_ref[...], turned, preferred_element_type=F32) * slope).astype(BF16)
        dpre_s[part, :] = d_pre
        out = jnp.dot(act, down_ref[...], preferred_element_type=F32) + db_ref[...] * (1.0 / LINE)
        d_logit = jnp.sum(rows_raw * out, axis=1, keepdims=True) * (gate * (1.0 - gate))
        own_s[part, :] = (lax.dot_general(d_pre, up_ref[...], turned, preferred_element_type=F32) + d_logit * column_s[...]).astype(BF16)

        @pl.when(end)
        def _():
            back.start(k)

        out_ref[part, :] = (gate * out).astype(BF16)
        acc_s[...] += jnp.sum(d_logit * rows_in.astype(F32), axis=0, keepdims=True)
        gub_ref[...] += jnp.sum(d_pre.astype(F32), axis=0, keepdims=True)
        gdb_ref[...] += jnp.sum(rows_grad.astype(F32), axis=0, keepdims=True)

        @pl.when(mid & (k > 0))
        def _():
            back.flow(k - 1, return_chunk)
        return 0

    lax.fori_loop(0, wide, compute, 0)

    def term(k):
        return pltpu.make_async_remote_copy(rows_s.at[rank], rows_s.at[rank], r_sends.at[k], r_arrivals.at[k],
                                            device_id={"tp": lax.rem(rank + k, LINE)}, device_id_type=MESH)

    rows_s[rank] = jnp.broadcast_to(acc_s[...], (8, width))
    for k in range(1, LINE):
        term(k).start()

    @pl.when(mid)
    def _():
        back.flow(jnp.int32(wide - 1), return_chunk)

    tiles = hid // LANES
    across_rows = (((0,), (0,)), ((), ()))

    def tile(j, _):
        @pl.when(j < tiles)
        def _():
            cols = rows_of(j, LANES)
            gdown_ref[cols, :] = lax.dot_general(act_s[:, cols], rgrad_s[...], across_rows, preferred_element_type=F32)

        @pl.when(j >= tiles)
        def _():
            cols = rows_of(j - tiles, LANES)
            gup_ref[cols, :] = lax.dot_general(inbox_s[:, cols], dpre_s[...], across_rows, preferred_element_type=F32)

        @pl.when(end & (j < wide))
        def _():
            back.arrived(j)
            return_chunk(j)

        @pl.when(mid & (j == 1))
        def _():
            back.flush(wide, return_chunk)
        return 0

    lax.fori_loop(0, 2 * tiles, tile, 0)
    for k in range(1, LINE):
        term(k).wait_recv()
    grow_ref[...] = ((rows_s[0] + rows_s[1]) + rows_s[2]) + rows_s[3]
    for c in range(1, wide):
        give_back(c).wait_recv()
    back.sent(wide)
    for k in range(1, wide):
        dispatch(k).wait_send()
        give_back(k).wait_send()
    for k in range(1, LINE):
        term(k).wait_send()


def experts_block(wide, cap, *operands):
    tokens, mixed, gin, srow, gain, router, up, ub, down, db = operands
    seq, width = tokens.shape
    hid = up.shape[1]
    vm = pl.BlockSpec(memory_space=pltpu.VMEM)
    shape = jax.ShapeDtypeStruct
    dma = pltpu.SemaphoreType.DMA
    slots = wide * cap
    return pl.pallas_call(
        functools.partial(experts_kernel, wide),
        in_specs=[vm] * len(operands),
        out_specs=[vm] * 7,
        out_shape=[shape((width, hid), F32), shape((1, hid), F32), shape((hid, width), F32), shape((1, width), F32),
                   shape((slots, width), BF16), shape((slots, width), BF16), shape((8, width), F32)],
        scratch_shapes=[
            pltpu.VMEM((seq, width), BF16), *[pltpu.VMEM((slots, width), BF16)] * 3,
            pltpu.VMEM((slots, hid), BF16), pltpu.VMEM((slots, hid), BF16),
            *[pltpu.VMEM((slots, width), BF16)] * 3, pltpu.VMEM((1, width), F32), pltpu.VMEM((1, width), F32), pltpu.VMEM((LINE, 8, width), F32),
            dma((wide,)), dma((wide,)), *[dma((3, wide * SLOT_PIECES))] * 2, dma((wide,)), dma((wide,)), dma((LINE,)), dma((LINE,))],
        compiler_params=pltpu.CompilerParams(collective_id=2, has_side_effects=True, vmem_limit_bytes=56 << 20),
        name="experts",
    )(*operands)


def front_kernel(wide, taps, tokens_ref, gain_ref, inx_ref, inz_ref, outp_ref, cw_ref, cb_ref, wproj_ref, masks_ref,
                 scale_ref, normed_ref, x_ref, z_ref, csum_ref, inner_ref, proj_ref, wx_ref, wz_ref, wo_ref,
                 own_s, near_s, far_s, w_sends, w_arrivals, sends, arrivals):
    seq, width = tokens_ref.shape
    ch = x_ref.shape[1]
    block = inx_ref.shape[0]
    tb = LANES
    nb = seq // tb
    me = lax.axis_index("wide")
    roles = line_roles()
    end, mid, mate, other = roles
    greet(wide)
    line = LineSum(roles, 2 * tb, 1, own_s, near_s, own_s, far_s, sends, arrivals)
    mine = pl.ds(pl.multiple_of(me * block, block), block)
    weights = ((inx_ref, wx_ref), (inz_ref, wz_ref), (outp_ref, wo_ref))

    def share(which, k):
        source, target = weights[which]
        return pltpu.make_async_remote_copy(source, target.at[mine], w_sends.at[which, k], w_arrivals.at[which, k],
                                            device_id={"wide": lax.rem(me + k, wide)}, device_id_type=MESH)

    for which in range(3):
        for k in range(1, wide):
            share(which, k).start()
    for source, target in weights:
        target[mine, :] = source[...]

    def rows_of(b):
        return pl.ds(pl.multiple_of(b * tb, tb), tb)

    def norm(b, _):
        rows = rows_of(b)
        tokens = tokens_ref[rows, :]
        scale = lax.rsqrt(jnp.mean(tokens * tokens, axis=1, keepdims=True) + EPS)
        scale_ref[rows, :] = scale
        normed_ref[rows, :] = (tokens * scale * as_row(gain_ref)).astype(BF16)
        return 0

    own_s[...] = jnp.zeros_like(own_s)
    lax.fori_loop(0, nb, norm, 0)
    for k in range(1, wide):
        share(0, k).wait_recv()

    def step(b, _):
        rows = rows_of(b)
        base = pl.multiple_of(b * tb, tb)
        x = jnp.dot(normed_ref[rows, :], wx_ref[...], preferred_element_type=F32)
        x_ref[rows, :] = x
        prior = x_ref[pl.ds(pl.multiple_of(jnp.maximum(base - 8, 0), 8), 8), :]
        history = jnp.concatenate([prior, x], axis=0)
        same = masks_ref[rows, :]
        csum = as_row(cb_ref) + cw_ref[taps - 1:taps, :] * x
        for s in range(1, taps):
            csum = csum + cw_ref[taps - 1 - s:taps - s, :] * (same[:, s:s + 1] * history[8 - s:8 - s + tb, :])
        csum_ref[rows, :] = csum
        inner = (csum / (1.0 + jnp.exp(-csum))).astype(BF16)
        inner_ref[rows, :] = inner
        own_s[rows, :wproj_ref.shape[1]] = jnp.dot(inner, wproj_ref[...], preferred_element_type=F32).astype(BF16)

        @pl.when(end & (lax.rem(b, 2) == 1))
        def _():
            line.start(b // 2)
        return 0

    lax.fori_loop(0, nb, step, 0)
    steps = nb // 2

    @pl.when(mid)
    def _():
        for k in range(steps):
            line.flow(jnp.int32(k))

    for k in range(1, wide):
        share(1, k).wait_recv()

    def gate(b, _):
        rows = rows_of(b)
        z_ref[rows, :] = jnp.dot(normed_ref[rows, :], wz_ref[...], preferred_element_type=F32)
        return 0

    lax.fori_loop(0, nb, gate, 0)

    @pl.when(mid)
    def _():
        line.flush(steps)

    @pl.when(end)
    def _():
        for k in range(steps):
            line.arrived(k)

    proj_ref[...] = far_s[...].astype(F32)
    line.sent(steps)
    for k in range(1, wide):
        share(2, k).wait_recv()
        for which in range(3):
            share(which, k).wait_send()


def front(wide, taps, *operands):
    tokens, gain, inx, inz, outp, cw, cb, wproj, masks = operands
    seq, width = tokens.shape
    ch = inx.shape[1]
    vm = pl.BlockSpec(memory_space=pltpu.VMEM)
    shape = jax.ShapeDtypeStruct
    dma = pltpu.SemaphoreType.DMA
    return pl.pallas_call(
        functools.partial(front_kernel, wide, taps),
        in_specs=[vm] * len(operands),
        out_specs=[vm] * 10,
        out_shape=[shape((seq, 1), F32), shape((seq, width), BF16), shape((seq, ch), F32), shape((seq, ch), F32), shape((seq, ch), F32),
                   shape((seq, ch), BF16), shape((seq, LANES), F32), *[shape((width, ch), BF16)] * 3],
        scratch_shapes=[*[pltpu.VMEM((seq, LANES), BF16)] * 3, dma((3, wide)), dma((3, wide)), dma((3, seq // LANES // 2)), dma((3, seq // LANES // 2))],
        compiler_params=pltpu.CompilerParams(collective_id=3, has_side_effects=True, vmem_limit_bytes=48 << 20),
        name="mixer_front",
    )(*operands)


def plain_device(
    tokens,
    segment_ids,
    routes,
    out_grad,
    mixer_gain,
    in_proj_x,
    in_proj_z,
    conv_weight,
    conv_bias,
    state_proj,
    step_proj,
    step_bias,
    log_rates,
    skip_gain,
    out_proj,
    expert_gain,
    router_weight,
    expert_up,
    up_bias,
    expert_down,
    down_bias,
):
    seq_len, model_width = tokens.shape
    conv_taps = conv_weight.shape[0]
    step_rank = step_proj.shape[0]
    experts = router_weight.shape[1]
    capacity = 5 * seq_len // (4 * experts)
    doc_ids = segment_ids[0]
    conv_masks = [same_document(doc_ids, offset)[:, None] for offset in range(conv_taps)]
    first_scale = lax.rsqrt(jnp.mean(tokens * tokens, axis=1, keepdims=True) + EPS)
    first_unit = tokens * first_scale
    normed = (first_unit * mixer_gain).astype(jnp.bfloat16)
    gathered_x, gathered_z, gathered_out = (
        lax.all_gather(in_proj_x, "wide", axis=0, tiled=True),
        lax.all_gather(in_proj_z, "wide", axis=0, tiled=True),
        lax.all_gather(out_proj, "wide", axis=0, tiled=True),
    )
    x_branch = multiply(normed, gathered_x)
    z_branch = multiply(normed, gathered_z)
    conv_sum = conv_bias + jnp.zeros_like(x_branch)
    for offset in range(conv_taps):
        conv_sum = conv_sum + conv_weight[conv_taps - 1 - offset] * conv_masks[
            offset
        ] * shifted_down(x_branch, offset)
    inner_act = jax.nn.silu(conv_sum).astype(jnp.bfloat16)
    wide_proj = jnp.pad(state_proj, ((0, 0), (0, LANES - state_proj.shape[1])))
    projected = lax.psum(multiply(inner_act, wide_proj), "tp")
    tall_proj = jnp.pad(step_proj, ((0, LANES - step_rank), (0, 0)))
    carry_mask = same_document(doc_ids, 1)[:, None]
    scan_out, step_size, states, starts = scan_fwd(
        projected, inner_act, carry_mask, tall_proj, step_bias[None], log_rates, skip_gain[None], step_rank
    )
    z_gate = jax.nn.silu(z_branch)
    gated = (scan_out * z_gate).astype(jnp.bfloat16)
    mixed = lax.psum(contract_cols(gated, gathered_out).astype(jnp.bfloat16), "tp").astype(
        jnp.float32
    )
    hidden = tokens + mixed
    second_scale = lax.rsqrt(jnp.mean(hidden * hidden, axis=1, keepdims=True) + EPS)
    second_unit = hidden * second_scale
    expert_in = (second_unit * expert_gain).astype(jnp.bfloat16)
    route_ids = routes[:, 0]
    chosen_int = (routes == jnp.arange(experts, dtype=jnp.int32)[None, :]).astype(jnp.int32)
    chosen = chosen_int.astype(jnp.float32)
    logits = multiply(expert_in, router_weight)
    gate = jax.nn.sigmoid(jnp.sum(logits * chosen, axis=1))
    rank_of = jnp.arange(seq_len, dtype=jnp.int32)
    earlier = (rank_of[:, None] > rank_of[None, :]).astype(jnp.bfloat16)
    position = jnp.sum(multiply(earlier, chosen.astype(jnp.bfloat16)) * chosen, axis=1).astype(jnp.int32)
    kept = position < capacity
    slots = jnp.where(kept, route_ids * capacity + position, experts * capacity)
    scaled_grad = (gate[:, None] * out_grad).astype(jnp.bfloat16)
    sent_width = expert_in.shape[1]
    send_in = (
        jnp.zeros((experts * capacity + 1, sent_width), jnp.bfloat16).at[slots].set(expert_in)[:-1]
    )
    send_grad = (
        jnp.zeros((experts * capacity + 1, sent_width), jnp.bfloat16)
        .at[slots]
        .set(scaled_grad)[:-1]
    )
    recv_in, recv_grad = (
        lax.all_to_all(
            send_in.reshape(experts, capacity, sent_width),
            "wide",
            split_axis=0,
            concat_axis=0,
            tiled=True,
        ),
        lax.all_to_all(
            send_grad.reshape(experts, capacity, sent_width),
            "wide",
            split_axis=0,
            concat_axis=0,
            tiled=True,
        ),
    )
    rows_in = recv_in.reshape(-1, model_width)
    rows_grad = recv_grad.reshape(-1, model_width)
    pre_act = multiply(rows_in, expert_up[0]) + up_bias[0]
    hidden_act = jax.nn.gelu(pre_act).astype(jnp.bfloat16)
    partial_out = multiply(hidden_act, expert_down[0])
    up_grad = contract_cols(rows_grad, expert_down[0])
    d_pre = jax.vjp(jax.nn.gelu, pre_act)[1](up_grad)[0].astype(jnp.bfloat16)
    partial_back = contract_cols(d_pre, expert_up[0])
    grad_down = contract_rows(hidden_act, rows_grad)
    grad_dbias = jnp.sum(rows_grad.astype(jnp.float32), axis=0)
    grad_up = contract_rows(rows_in, d_pre)
    grad_ubias = jnp.sum(d_pre.astype(jnp.float32), axis=0)
    out_sum, back_sum = (
        lax.psum(partial_out.astype(jnp.bfloat16), "tp").astype(jnp.float32),
        lax.psum(partial_back.astype(jnp.bfloat16), "tp").astype(jnp.float32),
    )
    bias_part = down_bias[0]
    outgoing = (out_sum + bias_part).astype(jnp.bfloat16).reshape(experts, capacity, -1)
    back_rows = back_sum.astype(jnp.bfloat16).reshape(experts, capacity, -1)
    incoming, arriving = (
        lax.all_to_all(outgoing, "wide", split_axis=0, concat_axis=0, tiled=True),
        lax.all_to_all(back_rows, "wide", split_axis=0, concat_axis=0, tiled=True),
    )
    safe_slots = jnp.minimum(slots, experts * capacity - 1)
    returned = jnp.where(
        kept[:, None], incoming.reshape(-1, model_width)[safe_slots].astype(jnp.float32), 0.0
    )
    result = hidden + gate[:, None] * returned
    d_gate = jnp.sum(out_grad * returned, axis=1)
    d_logit = (d_gate * gate * (1.0 - gate))[:, None] * chosen
    grad_router = jnp.dot(expert_in.astype(jnp.float32).T, d_logit, precision=HIGH)
    d_norm_two = jnp.dot(d_logit, router_weight.astype(jnp.float32).T, precision=HIGH)
    d_norm_two = d_norm_two + jnp.where(
        kept[:, None], arriving.reshape(-1, model_width)[safe_slots].astype(jnp.float32), 0.0
    )
    grad_second_gain = jnp.sum(d_norm_two * second_unit, axis=0)
    d_hidden = out_grad + rms_back(d_norm_two * expert_gain, second_unit, second_scale)
    d_mixed = d_hidden.astype(jnp.bfloat16)
    d_gated = multiply(d_mixed, gathered_out)
    grad_out = contract_rows(d_mixed, gated)
    d_scan = d_gated * z_gate
    d_z = (d_gated * scan_out * silu_slope(z_branch)).astype(jnp.bfloat16)
    d_step_pre, d_inner, d_proj, grad_step, grad_sbias, grad_rates, grad_skip = scan_bwd(
        projected, inner_act, carry_mask, step_size, states, starts, d_scan, tall_proj, log_rates, skip_gain[None], step_rank
    )
    grad_step, grad_sbias, grad_skip = grad_step[:step_rank], grad_sbias[0], grad_skip[0]
    d_projected = lax.psum(d_proj.astype(jnp.bfloat16), "tp")
    grad_state = contract_rows(inner_act, d_projected)[:, : state_proj.shape[1]]
    d_inner = d_inner + contract_cols(d_projected, wide_proj)
    d_conv = d_inner * silu_slope(conv_sum)
    grad_cbias = jnp.sum(d_conv, axis=0)
    conv_rows = []
    d_input = jnp.zeros_like(d_conv)
    for offset in range(conv_taps):
        conv_rows.append(
            jnp.sum(d_conv * conv_masks[offset] * shifted_down(x_branch, offset), axis=0)
        )
        d_input = d_input + conv_weight[conv_taps - 1 - offset] * shifted_up(
            conv_masks[offset] * d_conv, offset
        )
    grad_conv = jnp.stack(conv_rows[::-1])
    d_x_branch = d_input.astype(jnp.bfloat16)
    grad_in_x = contract_rows(normed, d_x_branch)
    grad_in_z = contract_rows(normed, d_z)
    d_normed = lax.psum(
        (contract_cols(d_x_branch, gathered_x) + contract_cols(d_z, gathered_z)).astype(
            jnp.bfloat16
        ),
        "tp",
    ).astype(jnp.float32)
    grad_first_gain = jnp.sum(d_normed * first_unit, axis=0)
    tokens_grad = d_hidden + rms_back(d_normed * mixer_gain, first_unit, first_scale)
    grad_in_x, grad_in_z, grad_out = (
        summed_on_arrival(grad_in_x.astype(jnp.bfloat16), "wide", 0),
        summed_on_arrival(grad_in_z.astype(jnp.bfloat16), "wide", 0),
        summed_on_arrival(grad_out.astype(jnp.bfloat16), "wide", 0),
    )
    (
        grad_first_gain,
        grad_conv,
        grad_cbias,
        grad_state,
        grad_step,
        grad_sbias,
        grad_rates,
        grad_skip,
        grad_second_gain,
        grad_router,
    ) = lax.psum(
        (
            grad_first_gain,
            grad_conv,
            grad_cbias,
            grad_state,
            grad_step,
            grad_sbias,
            grad_rates,
            grad_skip,
            grad_second_gain,
            grad_router,
        ),
        "wide",
    )
    return (
        result,
        tokens_grad,
        grad_first_gain,
        grad_in_x,
        grad_in_z,
        grad_conv,
        grad_cbias,
        grad_state,
        grad_step,
        grad_sbias,
        grad_rates,
        grad_skip,
        grad_out,
        grad_second_gain,
        grad_router,
        grad_up[None],
        grad_ubias[None],
        grad_down[None],
        grad_dbias[None],
    )


def fast_device(
    tokens,
    segment_ids,
    routes,
    out_grad,
    mixer_gain,
    in_proj_x,
    in_proj_z,
    conv_weight,
    conv_bias,
    state_proj,
    step_proj,
    step_bias,
    log_rates,
    skip_gain,
    out_proj,
    expert_gain,
    router_weight,
    expert_up,
    up_bias,
    expert_down,
    down_bias,
):
    seq_len, model_width = tokens.shape
    conv_taps = conv_weight.shape[0]
    step_rank = step_proj.shape[0]
    experts = router_weight.shape[1]
    capacity = 5 * seq_len // (4 * experts)
    doc_ids = segment_ids[0]
    conv_masks = [same_document(doc_ids, offset)[:, None] for offset in range(conv_taps)]
    masks = jnp.pad(jnp.concatenate(conv_masks, axis=1), ((0, 8), (0, 8 - conv_taps)))
    wide = lax.axis_size("wide")
    states = log_rates.shape[0]
    chosen = (routes == jnp.arange(experts, dtype=jnp.int32)[None, :]).astype(jnp.float32)
    rank_of = jnp.arange(seq_len, dtype=jnp.int32)
    earlier = (rank_of[:, None] > rank_of[None, :]).astype(jnp.bfloat16)
    position = jnp.sum(multiply(earlier, chosen.astype(jnp.bfloat16)) * chosen, axis=1).astype(jnp.int32)
    slots = jnp.where(position < capacity, routes[:, 0] * capacity + position, experts * capacity)
    slot_row, slot_col = slots[None], slots[:, None]
    carry_mask = same_document(doc_ids, 1)[:, None]

    first_scale, normed, x_branch, z_branch, conv_sum, inner_act, projected, gathered_x, gathered_z, gathered_out = front(
        wide, conv_taps, tokens, mixer_gain, in_proj_x, in_proj_z, out_proj, conv_weight, conv_bias, state_proj, masks
    )
    scan_out, step_size, held, starts, gated, mixed, grads_in = scan_mix(
        projected, inner_act, carry_mask, step_proj, step_bias, log_rates, skip_gain, z_branch, gathered_out, out_grad, slot_row,
        step_rank, wide, capacity,
    )
    grad_up, grad_ubias, grad_down, grad_dbias, returned, terms, router_grad = experts_block(
        wide, capacity, tokens, mixed, grads_in, slot_row, expert_gain, router_weight,
        expert_up[0], up_bias, expert_down[0], down_bias,
    )
    d_hidden, d_normed, grad_in_x, grad_in_z, grad_out, small, gated_out = mixer_back(
        wide, conv_taps, step_rank,
        (projected, carry_mask, step_size, held, starts, tokens, mixed, out_grad, slot_col, z_branch, scan_out),
        (inner_act, step_proj, log_rates, skip_gain, returned, expert_gain, gathered_out, terms, x_branch, conv_sum, masks, state_proj,
         conv_weight, normed, gated, gathered_x, gathered_z, mixer_gain, router_grad),
    )
    outs = finish(
        step_rank, states, experts, tokens, mixed, slot_col, gated_out, d_hidden, d_normed, first_scale, mixer_gain, small,
        grad_in_x, grad_in_z, grad_out, grad_up, grad_down, grad_ubias, grad_dbias,
    )
    return tuple(outs)


def solution(mesh):
    in_specs = (
        P("wide", None),
        P("wide", None),
        P("wide", None),
        P("wide", None),
        P(),
        P("wide", "tp"),
        P("wide", "tp"),
        P(None, "tp"),
        P("tp"),
        P("tp", None),
        P(None, "tp"),
        P("tp"),
        P(None, "tp"),
        P("tp"),
        P("wide", "tp"),
        P(),
        P(),
        P("wide", None, "tp"),
        P("wide", "tp"),
        P("wide", "tp", None),
        P("wide", None),
    )
    out_specs = (
        P("wide", None),
        P("wide", None),
        P(),
        P("wide", "tp"),
        P("wide", "tp"),
        P(None, "tp"),
        P("tp"),
        P("tp", None),
        P(None, "tp"),
        P("tp"),
        P(None, "tp"),
        P("tp"),
        P("wide", "tp"),
        P(),
        P(),
        P("wide", None, "tp"),
        P("wide", "tp"),
        P("wide", "tp", None),
        P("wide", None),
    )
    wide, line = mesh.shape["wide"], mesh.shape["tp"]
    per_device = fast_device if line == 4 and wide == 8 else plain_device
    return jax.shard_map(
        per_device, mesh=mesh, in_specs=in_specs, out_specs=out_specs, check_vma=False
    )
```

```python
import functools

import jax
import jax.numpy as jnp
from jax import lax
from jax.experimental import pallas as pl
from jax.experimental.pallas import tpu as pltpu
from jax.sharding import PartitionSpec as P

EPS = 1e-05
HIGH = lax.Precision.HIGHEST


def in_blocks(shard, dim, size):
    before, after = (shard.shape[:dim], shard.shape[dim + 1 :])
    return jnp.moveaxis(shard.reshape(*before, size, -1, *after), dim, 0)


def summed_on_arrival(shard, axis, dim):
    size = lax.axis_size(axis)
    parts = lax.all_to_all(in_blocks(shard, dim, size), axis, 0, 0, tiled=True)
    return jnp.sum(parts.astype(jnp.float32), axis=0)


def multiply(left, right):
    return jnp.dot(left, right, preferred_element_type=jnp.float32)


def contract_rows(left, right):
    return lax.dot_general(
        left, right, (((0,), (0,)), ((), ())), preferred_element_type=jnp.float32
    )


def contract_cols(left, right):
    return lax.dot_general(
        left, right, (((1,), (1,)), ((), ())), preferred_element_type=jnp.float32
    )


def shifted_down(values, steps):
    if steps == 0:
        return values
    filler = jnp.zeros((steps,) + values.shape[1:], values.dtype)
    return jnp.concatenate([filler, values[:-steps]], axis=0)


def shifted_up(values, steps):
    if steps == 0:
        return values
    filler = jnp.zeros((steps,) + values.shape[1:], values.dtype)
    return jnp.concatenate([values[steps:], filler], axis=0)


def same_document(doc_ids, steps):
    if steps == 0:
        return jnp.ones(doc_ids.shape, jnp.float32)
    filler = jnp.full((steps,), -1, jnp.int32)
    earlier = jnp.concatenate([filler, doc_ids[:-steps]])
    return (earlier == doc_ids).astype(jnp.float32)


def silu_slope(values):
    logistic = jax.nn.sigmoid(values)
    return logistic * (1.0 + values * (1.0 - logistic))


def rms_back(grad_unit, unit, scale):
    return scale * (grad_unit - unit * jnp.mean(grad_unit * unit, axis=1, keepdims=True))


LOG2E = 1.4426950408889634
LANES = 128
F32, BF16 = jnp.float32, jnp.bfloat16
MESH = pl.DeviceIdType.MESH


def fold_rows(parts, masks):
    m4, m2, m1 = masks

    def join(a, b, m, shift):
        return jnp.where(m, a, b) + pltpu.roll(jnp.where(m, b, a), shift, 0)

    c = [join(parts[i], parts[i + 4], m4[i], 4) for i in range(4)]
    d = [join(c[i], c[i + 2], m2[i], 6) for i in range(2)]
    return join(d[0], d[1], m1, 7)


def fold_masks(width):
    sub = lax.broadcasted_iota(jnp.int32, (8, width), 0)
    m4 = [((sub - i) & 7) < 4 for i in range(4)]
    m2 = [((sub - i) & 2) == 0 for i in range(2)]
    m1 = (sub & 1) == 0
    return m4, m2, m1


def softplus(v):
    return jnp.maximum(v, 0.0) + jnp.log1p(jnp.exp(-jnp.abs(v)))


def row(ref, c, t, ns):
    one = ref[c, pl.ds(t, 8, stride=0), :]
    return jnp.concatenate([one] * (ns // 8), axis=0)


def spread(ref, value):
    for c in range(ref.shape[0]):
        ref[c] = value[:, c * LANES:(c + 1) * LANES]


def own_column(ns, rank):
    lane = lax.broadcasted_iota(jnp.int32, (ns, LANES), 1)
    n = lax.broadcasted_iota(jnp.int32, (ns, LANES), 0)
    return (lane == rank + n) | (lane == rank + ns + n)


def coefficient_rows(ns, rank, proj_ref, first):
    own = own_column(ns, rank)
    lane = lax.broadcasted_iota(jnp.int32, (LANES, 2 * LANES), 1)
    k = lax.broadcasted_iota(jnp.int32, (LANES, 2 * LANES), 0)
    pick = ((lane < LANES) & (k >= rank) & (k < rank + ns)) | ((lane >= LANES) & (k >= rank + ns) & (k < rank + 2 * ns))
    pick = jnp.where(pick, 1.0, 0.0).astype(BF16)
    rows = []
    for j in range(8):
        one = proj_ref[pl.ds(first + j, 8, stride=0), :]
        rows.append(jnp.where(own, jnp.concatenate([one] * (ns // 8), axis=0), 0.0).astype(BF16))
    return jnp.dot(jnp.concatenate(rows, axis=0), pick, preferred_element_type=F32)


def forward_tokens(ns, rank, proj_ref, stepd_s, drive_s, r2_s, states_ref, scan_ref, state, wide_a, wide_b):
    tb = proj_ref.shape[0]
    groups = len(state)
    masks = fold_masks(LANES)

    def eight(first, wide, state):
        parts = [[] for _ in range(groups)]
        for j in range(8):
            t = first + j
            in_b = wide[j * ns:(j + 1) * ns, :LANES]
            out_b = wide[j * ns:(j + 1) * ns, LANES:]
            for c in range(groups):
                dec = jnp.exp2(row(stepd_s, c, t, ns) * r2_s[c])
                s = dec * state[c] + row(drive_s, c, t, ns) * in_b
                state[c] = s
                states_ref[pl.ds(pl.multiple_of(t * ns, ns), ns), pl.ds(c * LANES, LANES)] = s.astype(BF16)
                z = out_b * s
                parts[c].append(sum(z[8 * k:8 * k + 8] for k in range(ns // 8)))
        for c in range(groups):
            scan_ref[pl.ds(pl.multiple_of(first, 8), 8), pl.ds(c * LANES, LANES)] = fold_rows(parts[c], masks)
        return state

    def body(g, state):
        state = list(state)
        first = g * 16
        wide_b[...] = coefficient_rows(ns, rank, proj_ref, first + 8)
        state = eight(first, wide_a, state)
        wide_a[...] = coefficient_rows(ns, rank, proj_ref, jnp.minimum(first + 16, tb - 8))
        return tuple(eight(first + 8, wide_b, state))

    wide_a[...] = coefficient_rows(ns, rank, proj_ref, 0)
    return lax.fori_loop(0, tb // 16, body, state)


def backward_tokens(ns, rank, proj_ref, states_ref, starts_ref, stepd_s, drive_s, dscan_s, step_s, r2_s, coeff_s, exps_s, dproj_ref,
                    later, acc, wide_a, wide_b, sums_a, sums_b):
    tb = proj_ref.shape[0]
    groups = len(later)
    masks = fold_masks(LANES)
    own = own_column(ns, rank)
    k = lax.broadcasted_iota(jnp.int32, (2 * LANES, LANES), 0)
    lane = lax.broadcasted_iota(jnp.int32, (2 * LANES, LANES), 1)
    into = ((k < LANES) & (lane >= rank) & (lane < rank + ns)) | ((k >= LANES) & (lane >= rank + ns) & (lane < rank + 2 * ns))
    into = jnp.where(into, 1.0, 0.0).astype(BF16)

    def gather(sums, first):
        got = jnp.dot(sums[...], into, preferred_element_type=F32)
        parts = []
        for j in range(8):
            one = jnp.where(own, got[j * ns:(j + 1) * ns], 0.0)
            parts.append(sum(one[8 * q:8 * q + 8] for q in range(ns // 8)))
        dproj_ref[pl.ds(pl.multiple_of(first, 8), 8), :] = fold_rows(parts, masks)

    def eight(first, wide, sums, later, acc):
        cparts = [[None] * 8 for _ in range(groups)]
        eparts = [[None] * 8 for _ in range(groups)]
        last = pl.ds(pl.multiple_of((first + 7) * ns, ns), ns)
        now = [states_ref[last, pl.ds(c * LANES, LANES)].astype(F32) for c in range(groups)]
        for j in range(7, -1, -1):
            t = first + j
            prior = pl.ds(pl.multiple_of((t - 1 if j else jnp.maximum(t - 1, 0)) * ns, ns), ns)
            here = slice(j * ns, (j + 1) * ns)
            in_b = wide[here, :LANES]
            out_b = wide[here, LANES:]
            din = dout = None
            for c in range(groups):
                cols = pl.ds(c * LANES, LANES)
                before = states_ref[prior, cols].astype(F32)
                if j == 0:
                    before = jnp.where(jnp.full((ns, LANES), t, jnp.int32) == 0, starts_ref[0, :, cols], before)
                r2 = r2_s[c]
                dec = jnp.exp2(row(stepd_s, c, t, ns) * r2)
                ds = row(dscan_s, c, t, ns)
                d = later[c] + out_b * ds
                later[c] = dec * d
                dexp = later[c] * before
                e = dexp * r2
                cf = d * in_b
                cparts[c][j] = sum(cf[8 * q:8 * q + 8] for q in range(ns // 8))
                eparts[c][j] = sum(e[8 * q:8 * q + 8] for q in range(ns // 8))
                acc[c] = acc[c] + dexp * row(step_s, c, t, ns)
                a = d * row(drive_s, c, t, ns)
                b = now[c] * ds
                din = a if din is None else din + a
                dout = b if dout is None else dout + b
                now[c] = before
            sums[here, :LANES] = din.astype(BF16)
            sums[here, LANES:] = dout.astype(BF16)
        rows = pl.ds(pl.multiple_of(first, 8), 8)
        for c in range(groups):
            cols = pl.ds(c * LANES, LANES)
            coeff_s[rows, cols] = fold_rows(cparts[c], masks)
            exps_s[rows, cols] = fold_rows(eparts[c], masks)
        return later, acc

    def body(k, carry):
        later, acc = [list(v) for v in carry]
        first = tb - 16 - k * 16
        gather(sums_a, jnp.minimum(first + 16, tb - 8))
        wide_a[...] = coefficient_rows(ns, rank, proj_ref, first)
        later, acc = eight(first + 8, wide_b, sums_b, later, acc)
        gather(sums_b, first + 8)
        wide_b[...] = coefficient_rows(ns, rank, proj_ref, jnp.maximum(first - 8, 0))
        later, acc = eight(first, wide_a, sums_a, later, acc)
        return tuple(later), tuple(acc)

    wide_b[...] = coefficient_rows(ns, rank, proj_ref, tb - 8)
    sums_a[...] = jnp.zeros_like(sums_a)
    later, acc = lax.fori_loop(0, tb // 16, body, (later, acc))
    gather(sums_a, 0)
    return later, acc


def scan_fwd_kernel(ns, rank, proj_ref, inner_ref, keep_ref, sproj_ref, sbias_ref, lr_ref, skip_ref,
                    scan_ref, step_ref, states_ref, starts_ref, state_s, stepd_s, drive_s, r2_s, wide_a, wide_b):
    tb, ch = inner_ref.shape
    groups = ch // LANES
    i = pl.program_id(0)

    @pl.when(i == 0)
    def _():
        state_s[...] = jnp.zeros_like(state_s)
        spread(r2_s, jnp.exp(lr_ref[...]) * (-LOG2E))

    step_in = proj_ref[...].astype(BF16)
    pre = jnp.dot(step_in, sproj_ref[...], preferred_element_type=F32) + sbias_ref[...]
    step = softplus(pre)
    step_ref[...] = step
    spread(stepd_s, jnp.where(keep_ref[...] > 0.0, step, 1e30))
    inner = inner_ref[...].astype(F32)
    spread(drive_s, step * inner)
    starts_ref[0] = state_s[...]
    start = tuple(state_s[:, c * LANES:(c + 1) * LANES] for c in range(groups))
    state = forward_tokens(ns, rank, proj_ref, stepd_s, drive_s, r2_s, states_ref, scan_ref, start, wide_a, wide_b)
    for c in range(groups):
        state_s[:, c * LANES:(c + 1) * LANES] = state[c]
    scan_ref[...] += skip_ref[...] * inner


def scan_fwd(proj, inner, keep, sproj, sbias, log_rates, skip, rank):
    seq, ch = inner.shape
    ns = log_rates.shape[0]
    tb = LANES
    nb = seq // tb
    full = lambda a: pl.BlockSpec(a.shape, lambda i: (0,) * a.ndim)
    rows = pl.BlockSpec((tb, ch), lambda i: (i, 0))
    return pl.pallas_call(
        functools.partial(scan_fwd_kernel, ns, rank),
        grid=(nb,),
        in_specs=[pl.BlockSpec((tb, LANES), lambda i: (i, 0)), rows, pl.BlockSpec((tb, 1), lambda i: (i, 0)),
                  full(sproj), full(sbias), full(log_rates), full(skip)],
        out_specs=[rows, rows, pl.BlockSpec((tb * ns, ch), lambda i: (i, 0)), pl.BlockSpec((1, ns, ch), lambda i: (i, 0, 0))],
        out_shape=[jax.ShapeDtypeStruct((seq, ch), F32), jax.ShapeDtypeStruct((seq, ch), F32),
                   jax.ShapeDtypeStruct((seq * ns, ch), BF16), jax.ShapeDtypeStruct((nb, ns, ch), F32)],
        scratch_shapes=[pltpu.VMEM((ns, ch), F32)] + [pltpu.VMEM((ch // LANES, tb, LANES), F32)] * 2 + [pltpu.VMEM((ch // LANES, ns, LANES), F32),
                        *[pltpu.VMEM((8 * ns, 2 * LANES), F32)] * 2],
        compiler_params=pltpu.CompilerParams(vmem_limit_bytes=48 << 20),
        name="scan_fwd",
    )(proj, inner, keep, sproj, sbias, log_rates, skip)


def scan_bwd_kernel(ns, rank, proj_ref, inner_ref, keep_ref, step_ref, states_ref, starts_ref, dscan_ref, sproj_ref, lr_ref, skip_ref,
                    dpre_ref, dinner_ref, dproj_ref, gstep_ref, gsbias_ref, grates_ref, gskip_ref,
                    carry_s, stepd_s, drive_s, dscan_s, step_s, r2_s, coeff_s, exps_s, acc_s, wide_a, wide_b, sums_a, sums_b):
    tb, ch = inner_ref.shape
    groups = ch // LANES
    i = pl.program_id(0)

    @pl.when(i == 0)
    def _():
        carry_s[...] = jnp.zeros_like(carry_s)
        acc_s[...] = jnp.zeros_like(acc_s)
        spread(r2_s, jnp.exp(lr_ref[...]) * (-LOG2E))
        gstep_ref[...] = jnp.zeros_like(gstep_ref)
        gsbias_ref[...] = jnp.zeros_like(gsbias_ref)
        gskip_ref[...] = jnp.zeros_like(gskip_ref)

    step = step_ref[...]
    inner = inner_ref[...].astype(F32)
    dscan = dscan_ref[...]
    spread(stepd_s, jnp.where(keep_ref[...] > 0.0, step, 1e30))
    spread(drive_s, step * inner)
    spread(dscan_s, dscan)
    spread(step_s, step)
    pick = lambda ref: tuple(ref[:, c * LANES:(c + 1) * LANES] for c in range(groups))
    later, acc = backward_tokens(ns, rank, proj_ref, states_ref, starts_ref, stepd_s, drive_s, dscan_s, step_s, r2_s, coeff_s, exps_s,
                                 dproj_ref, pick(carry_s), pick(acc_s), wide_a, wide_b, sums_a, sums_b)
    for c in range(groups):
        carry_s[:, c * LANES:(c + 1) * LANES] = later[c]
        acc_s[:, c * LANES:(c + 1) * LANES] = acc[c]
    coeff = coeff_s[...]
    d_step = coeff * inner + exps_s[...] * (1.0 / LOG2E)
    d_pre = (d_step * (1.0 - jnp.exp(-step))).astype(BF16)
    dpre_ref[...] = d_pre
    dinner_ref[...] = dscan * skip_ref[...] + step * coeff
    step_in = proj_ref[...].astype(BF16)
    gstep_ref[...] += lax.dot_general(step_in, d_pre, (((0,), (0,)), ((), ())), preferred_element_type=F32)
    gsbias_ref[...] += jnp.sum(d_pre.astype(F32), axis=0, keepdims=True)
    gskip_ref[...] += jnp.sum(dscan * inner, axis=0, keepdims=True)
    dproj_ref[...] += lax.dot_general(d_pre, sproj_ref[...], (((1,), (1,)), ((), ())), preferred_element_type=F32)

    @pl.when(i == pl.num_programs(0) - 1)
    def _():
        grates_ref[...] = -jnp.exp(lr_ref[...]) * acc_s[...]


def scan_bwd(proj, inner, keep, step, states, starts, dscan, sproj, log_rates, skip, rank):
    seq, ch = inner.shape
    ns = log_rates.shape[0]
    tb = LANES
    nb = seq // tb
    full = lambda a: pl.BlockSpec(a.shape, lambda i: (0,) * a.ndim)
    rows = pl.BlockSpec((tb, ch), lambda i: (nb - 1 - i, 0))
    prow = pl.BlockSpec((tb, LANES), lambda i: (nb - 1 - i, 0))
    whole = lambda *s: pl.BlockSpec(s, lambda i: (0,) * len(s))
    shape = jax.ShapeDtypeStruct
    return pl.pallas_call(
        functools.partial(scan_bwd_kernel, ns, rank),
        grid=(nb,),
        in_specs=[prow, rows, pl.BlockSpec((tb, 1), lambda i: (nb - 1 - i, 0)), rows,
                  pl.BlockSpec((tb * ns, ch), lambda i: (nb - 1 - i, 0)), pl.BlockSpec((1, ns, ch), lambda i: (nb - 1 - i, 0, 0)),
                  rows, full(sproj), full(log_rates), full(skip)],
        out_specs=[rows, rows, prow, whole(LANES, ch), whole(1, ch), whole(ns, ch), whole(1, ch)],
        out_shape=[shape((seq, ch), BF16), shape((seq, ch), F32), shape((seq, LANES), F32), shape((LANES, ch), F32), shape((1, ch), F32),
                   shape((ns, ch), F32), shape((1, ch), F32)],
        scratch_shapes=[pltpu.VMEM((ns, ch), F32)] + [pltpu.VMEM((ch // LANES, tb, LANES), F32)] * 4 + [pltpu.VMEM((ch // LANES, ns, LANES), F32),
                        pltpu.VMEM((tb, ch), F32), pltpu.VMEM((tb, ch), F32), pltpu.VMEM((ns, ch), F32),
                        *[pltpu.VMEM((8 * ns, 2 * LANES), F32)] * 2, *[pltpu.VMEM((8 * ns, 2 * LANES), BF16)] * 2],
        compiler_params=pltpu.CompilerParams(vmem_limit_bytes=48 << 20),
        name="scan_bwd",
    )(proj, inner, keep, step, states, starts, dscan, sproj, log_rates, skip)


def tall(ref):
    value = ref[...]
    return jnp.concatenate([value, jnp.zeros((LANES - value.shape[0], value.shape[1]), value.dtype)], axis=0)


def as_row(ref):
    return ref[...].reshape(1, ref.shape[0])


def line_roles():
    me = lax.axis_index("tp")
    end = (me == 0) | (me == 3)
    mate = jnp.where(me < 2, 1 - me, 5 - me)
    return end, jnp.logical_not(end), mate, 3 - me


LINE = 4
PIECES, SLOT_PIECES = 2, 2
MIX_BEHIND, SLOT_BEHIND, DN_BEHIND = 2, 2, 2
OUT_STEPS = (0, 1, 2, 3, 4, 5, 6, 7)


def greet(wide):
    barrier = pltpu.get_barrier_semaphore()
    for axis, size in (("tp", LINE), ("wide", wide)):
        me = lax.axis_index(axis)
        for k in range(1, size):
            pl.semaphore_signal(barrier, inc=1, device_id={axis: lax.rem(me + k, size)}, device_id_type=MESH)
    pl.semaphore_wait(barrier, LINE + wide - 2)


class LineSum:
    def __init__(self, roles, rows, pieces, own, near, half, far, sends, arrivals, behind=None, last=None):
        self.end, self.mid, self.mate, self.other = roles
        self.rows, self.pieces = rows // pieces, pieces
        self.behind = pieces if behind is None else behind
        self.last = last
        self.own, self.near, self.half, self.far = own, near, half, far
        self.sends, self.arrivals = sends, arrivals

    def part(self, ref, n):
        return ref.at[pl.ds(pl.multiple_of(n * self.rows, self.rows), self.rows)]

    def copy(self, source, target, hop, n, to):
        return pltpu.make_async_remote_copy(
            self.part(source, n), self.part(target, n), self.sends.at[hop, n], self.arrivals.at[hop, n],
            device_id={"tp": to}, device_id_type=MESH)

    def up(self, n):
        return self.copy(self.own, self.near, 0, n, self.mate)

    def across(self, n):
        return self.copy(self.half, self.far, 1, n, self.other)

    def down(self, n):
        return self.copy(self.far, self.far, 2, n, self.mate)

    def add(self, a, b, c, n):
        self.part(c, n)[...] = (self.part(a, n)[...].astype(F32) + self.part(b, n)[...].astype(F32)).astype(BF16)

    def each(self, k):
        return [k * self.pieces + j for j in range(self.pieces)]

    def start(self, k):
        for n in self.each(k):
            self.up(n).start()

    def first(self, n):
        self.up(n).wait_recv()
        self.add(self.own, self.near, self.half, n)
        self.across(n).start()

    def second(self, n):
        self.across(n).wait_recv()
        self.add(self.half, self.far, self.far, n)
        self.down(n).start()

    def place(self, m):
        if self.last is None:
            return m
        return (self.last - m // self.pieces) * self.pieces + m % self.pieces

    def flow(self, k, done=None):
        for j in range(self.pieces):
            m = k * self.pieces + j
            self.first(self.place(m))

            @pl.when(m >= self.behind)
            def _():
                self.second(self.place(m - self.behind))
                if done and (j - self.behind) % self.pieces == self.pieces - 1:
                    done(self.place(m - self.behind) // self.pieces)

    def flush(self, count, done=None):
        for m in range(count * self.pieces - self.behind, count * self.pieces):
            self.second(self.place(m))
            if done and m % self.pieces == self.pieces - 1:
                done(jnp.int32(self.place(m) // self.pieces))

    def arrived(self, k):
        for n in self.each(k):
            self.down(n).wait_recv()

    def sent(self, count):
        def block(n, _):
            @pl.when(self.end)
            def _():
                self.up(n).wait_send()

            @pl.when(self.mid)
            def _():
                self.across(n).wait_send()
                self.down(n).wait_send()
            return 0

        lax.fori_loop(0, count * self.pieces, block, 0)


def pack_rows(rank, states, experts, width, ch, wide):
    rows = 8 + states + rank + (rank + 2 * states) + 8 + (width // ch) * experts
    return -(-rows // (8 * wide)) * (8 * wide)


def finish_kernel(rank, states, tokens_ref, mixed_ref, scol_ref, got_ref, dhidden_ref, dn_ref, scale_ref, gain_ref, small_ref,
                  gx_ref, gz_ref, go_ref, gup_ref, gdown_ref, gub_ref, gdb_ref,
                  result_ref, tgrad_ref, first_ref, gx_out, gz_out, cw_ref, cb_ref, state_ref, step_ref, sb_ref, rates_ref, skip_ref, go_out,
                  second_ref, router_ref, gup_out, gub_out, gdown_out, gdb_out):
    i = pl.program_id(0)
    ch = small_ref.shape[1]
    experts, width = router_ref.shape
    gup_out[0] = gup_ref[...]
    gdown_out[0] = gdown_ref[...]

    @pl.when(i == 0)
    def _():
        for ref, out in ((gx_ref, gx_out), (gz_ref, gz_out), (go_ref, go_out), (gub_ref, gub_out), (gdb_ref, gdb_out)):
            out[...] = ref[...]
        flat = lambda r: small_ref[r:r + 1, :].reshape(ch)
        cb_ref[...] = flat(0)
        sb_ref[...] = flat(1)
        skip_ref[...] = flat(2)
        cw_ref[...] = small_ref[4:8, :]
        at = 8
        rates_ref[...] = small_ref[at:at + states, :]
        at += states
        step_ref[...] = small_ref[at:at + rank, :]
        at += rank
        held = rank + 2 * states
        state_ref[...] = small_ref[at:at + held, :]
        at += held
        halves = width // ch
        for h in range(halves):
            cols = slice(h * ch, (h + 1) * ch)
            first_ref[cols] = flat(at + h)
            second_ref[cols] = flat(at + halves + h)
            router_ref[:, cols] = small_ref[at + 8 + h * experts:at + 8 + (h + 1) * experts, :]

    ids = lax.broadcasted_iota(jnp.int32, (scol_ref.shape[0], got_ref.shape[0]), 1)
    chosen = jnp.where(ids == scol_ref[...], 1.0, 0.0).astype(BF16)
    tokens = tokens_ref[...]
    result_ref[...] = tokens + mixed_ref[...].astype(F32) + jnp.dot(chosen, got_ref[...], preferred_element_type=F32)
    scale = scale_ref[...]
    unit = tokens * scale
    through = dn_ref[...].astype(F32) * as_row(gain_ref)
    mean = jnp.mean(through * unit, axis=1, keepdims=True)
    tgrad_ref[...] = dhidden_ref[...] + scale * (through - unit * mean)


def finish(rank, states, experts, *operands):
    tokens, mixed, scol, got, dhidden, dn, scale, gain, small, gx, gz, go, gup, gdown, gub, gdb = operands
    seq, width = tokens.shape
    ch = small.shape[1]
    tb = 2 * LANES
    row = lambda n: pl.BlockSpec((tb, n), lambda i: (i, 0))
    full = lambda a: pl.BlockSpec(a.shape, lambda i: (0,) * a.ndim)
    whole = lambda *s: pl.BlockSpec(s, lambda i: (0,) * len(s))
    sizes = [(width,), gx.shape, gz.shape, (4, ch), (ch,), (rank + 2 * states, ch), (rank, ch), (ch,), (states, ch), (ch,), go.shape,
             (width,), (experts, width), (1, *gup.shape), gub.shape, (1, *gdown.shape), gdb.shape]
    nb = seq // tb
    piece = lambda a: pl.BlockSpec((a.shape[0] // nb, a.shape[1]), lambda i: (i, 0))
    placed = lambda size: pl.BlockSpec((1, size[1] // nb, size[2]), lambda i: (0, i, 0)) if len(size) == 3 else whole(*size)
    return pl.pallas_call(
        functools.partial(finish_kernel, rank, states),
        grid=(seq // tb,),
        in_specs=[row(width), row(width), row(1), full(got), row(width), row(width), row(1), full(gain), full(small), full(gx), full(gz), full(go), piece(gup), piece(gdown), full(gub), full(gdb)],
        out_specs=[row(width), row(width), *[placed(size) for size in sizes]],
        out_shape=[jax.ShapeDtypeStruct(size, F32) for size in [(seq, width), (seq, width), *sizes]],
        compiler_params=pltpu.CompilerParams(vmem_limit_bytes=62 << 20),
        name="finish",
    )(*operands)


def mixer_back_kernel(ns, rank, wide, taps, proj_ref, keep_ref, step_ref, states_ref, starts_ref, tokens_ref, mixed_ref, ograd_ref, scol_ref, z_ref, scan_ref,
                      inner_ref, sproj_ref, lr_ref, skip_ref, ret_ref, gain_ref, wo_ref, term_ref,
                      x_ref, csum_ref, masks_ref, wproj_ref, cw_ref, normed_ref, gated_ref, wx_ref, wz_ref, first_gain_ref, grow_ref,
                      dhidden_ref, dn_ref, gx_ref, gz_ref, go_ref, small_ref, got_ref,
                      carry_s, stepd_s, drive_s, dscan_s, step_s, r2_s, coeff_s, exps_s, acc_s, dproj_s, wide_a, wide_b, sums_a, sums_b,
                      near_s, half_s, far_s, sends, arrivals, got_sends, got_arrivals,
                      dp_own, dp_near, dp_far, dp_sends, dp_arrivals, dn_own, dn_near, dn_far, dn_sends, dn_arrivals,
                      prod_s, inbox_s, prod_sends, prod_arrivals, pack_s, pack_in, small_s, pack_sends, pack_arrivals,
                      dinner_s, dmixed_s, dz_s, dconv_s, dx_s, gstep_s, state_s, first_s, second_s, dscan_all, gains_s):
    seq, ch = inner_ref.shape
    width = normed_ref.shape[1]
    tb = LANES
    nb = seq // tb
    groups = ch // LANES
    i = pl.program_id(0)
    me = lax.axis_index("wide")
    roles = line_roles()
    end, mid, mate, other = roles
    cap = term_ref.shape[0] // wide
    line = LineSum(roles, cap, SLOT_PIECES, term_ref, near_s, half_s, far_s, sends, arrivals)
    dp = LineSum(roles, tb, 1, dp_own, dp_near, dp_own, dp_far, dp_sends, dp_arrivals, last=nb - 1)
    dn = LineSum(roles, tb, PIECES, dn_own, dn_near, dn_own, dn_far, dn_sends, dn_arrivals, behind=DN_BEHIND, last=nb - 1)
    block = width // wide
    turned = (((1,), (1,)), ((), ()))
    across_rows = (((0,), (0,)), ((), ()))

    def slot_rows(c):
        return pl.ds(pl.multiple_of(c * cap, cap), cap)

    def rows_of(b):
        return pl.ds(pl.multiple_of(b * tb, tb), tb)

    def give_back(c):
        return pltpu.make_async_remote_copy(
            far_s.at[slot_rows(c)], got_ref.at[slot_rows(me)], got_sends.at[c], got_arrivals.at[c],
            device_id={"wide": lax.rem(me + wide - c, wide)}, device_id_type=MESH)

    def return_chunk(c):
        @pl.when(c == 0)
        def _():
            here = pltpu.make_async_copy(far_s.at[slot_rows(0)], got_ref.at[slot_rows(me)], got_sends.at[0])
            here.start()
            here.wait()

        @pl.when(c != 0)
        def _():
            give_back(c).start()

    def deliver(which, k):
        to = lax.rem(me + k, wide)
        return pltpu.make_async_remote_copy(
            prod_s.at[which, pl.ds(pl.multiple_of(to * block, block), block)], inbox_s.at[which, k],
            prod_sends.at[which, k], prod_arrivals.at[which, k], device_id={"wide": to}, device_id_type=MESH)

    def product(which, left, right):
        def tile(j, _):
            cols = pl.ds(pl.multiple_of(j * LANES, LANES), LANES)
            got = lax.dot_general(left[:, cols], right[...], across_rows, preferred_element_type=F32)
            prod_s[which, cols, :] = got.astype(BF16)
            return 0

        lax.fori_loop(0, width // LANES, tile, 0)
        for k in range(1, wide):
            deliver(which, k).start()

    @pl.when(i == 0)
    def _():
        greet(wide)
        for ref in (carry_s, acc_s, gstep_s, state_s, first_s, second_s, pack_s):
            ref[...] = jnp.zeros_like(ref)
        dconv_s[pl.ds(seq, 8), :] = jnp.zeros((8, ch), F32)
        spread(r2_s, jnp.exp(lr_ref[...]) * (-LOG2E))

    def at_out_steps(role, lag, work):
        for c, step in enumerate(OUT_STEPS):
            @pl.when(role & (i == step + lag))
            def _():
                work(jnp.int32(c))

    at_out_steps(end, 0, line.start)

    def glue(g):
        part = tokens_ref.shape[0]
        rows = pl.ds(pl.multiple_of((seq // part - 1 - g) * part, part), part)
        hidden = tokens_ref[...] + mixed_ref[...].astype(F32)
        scale = lax.rsqrt(jnp.mean(hidden * hidden, axis=1, keepdims=True) + EPS)
        unit = hidden * scale
        ids = lax.broadcasted_iota(jnp.int32, (part, wide * cap), 1)
        chosen = jnp.where(ids == scol_ref[...], 1.0, 0.0).astype(BF16)
        d_norm_two = jnp.dot(chosen, ret_ref[...], preferred_element_type=F32)
        second_s[...] += jnp.sum(d_norm_two * unit, axis=0, keepdims=True)
        through = d_norm_two * as_row(gain_ref)
        d_hidden = ograd_ref[...] + scale * (through - unit * jnp.mean(through * unit, axis=1, keepdims=True))
        dhidden_ref[...] = d_hidden
        d_mixed = d_hidden.astype(BF16)
        dmixed_s[rows, :] = d_mixed
        d_gated = jnp.dot(d_mixed, wo_ref[...], preferred_element_type=F32)
        z = z_ref[...]
        logistic = 1.0 / (1.0 + jnp.exp(-z))
        dz_s[rows, :] = (d_gated * scan_ref[...] * (logistic * (1.0 + z * (1.0 - logistic)))).astype(BF16)
        dscan_all[rows, :] = d_gated * (z * logistic)

    def scan_block():
        b = nb - 1 - i
        rows = rows_of(b)
        step = step_ref[...]
        inner = inner_ref[rows, :].astype(F32)
        dscan = dscan_all[rows, :]
        spread(stepd_s, jnp.where(keep_ref[...] > 0.0, step, 1e30))
        spread(drive_s, step * inner)
        spread(dscan_s, dscan)
        spread(step_s, step)
        pick = lambda ref: tuple(ref[:, c * LANES:(c + 1) * LANES] for c in range(groups))
        later, acc = backward_tokens(ns, rank, proj_ref, states_ref, starts_ref, stepd_s, drive_s, dscan_s, step_s, r2_s, coeff_s, exps_s,
                                     dproj_s, pick(carry_s), pick(acc_s), wide_a, wide_b, sums_a, sums_b)
        for c in range(groups):
            carry_s[:, c * LANES:(c + 1) * LANES] = later[c]
            acc_s[:, c * LANES:(c + 1) * LANES] = acc[c]
        coeff = coeff_s[...]
        d_step = coeff * inner + exps_s[...] * (1.0 / LOG2E)
        d_pre = (d_step * (1.0 - jnp.exp(-step))).astype(BF16)
        dinner_s[rows, :] = dscan * as_row(skip_ref) + step * coeff
        step_in = proj_ref[...].astype(BF16)
        gstep_s[...] += lax.dot_general(step_in, d_pre, across_rows, preferred_element_type=F32)
        pack_s[1:2, :] += jnp.sum(d_pre.astype(F32), axis=0, keepdims=True)
        pack_s[2:3, :] += jnp.sum(dscan * inner, axis=0, keepdims=True)
        both = dproj_s[...] + lax.dot_general(d_pre, tall(sproj_ref), turned, preferred_element_type=F32)
        dp_own[rows, :] = both.astype(BF16)

        @pl.when(end)
        def _():
            dp.start(b)

    def conv_block(k):
        b = nb - 1 - k
        rows = rows_of(b)
        base = pl.multiple_of(b * tb, tb)

        @pl.when(end)
        def _():
            dp.arrived(b)

        d_proj = dp_far[rows, :]
        state_s[...] += lax.dot_general(d_proj, inner_ref[rows, :], across_rows, preferred_element_type=F32)
        d_inner = dinner_s[rows, :] + jnp.dot(d_proj[:, :wproj_ref.shape[0]], wproj_ref[...], preferred_element_type=F32)
        csum = csum_ref[rows, :]
        logistic = 1.0 / (1.0 + jnp.exp(-csum))
        d_conv = d_inner * (logistic * (1.0 + csum * (1.0 - logistic)))
        prior = x_ref[pl.ds(pl.multiple_of(jnp.maximum(base - 8, 0), 8), 8), :]
        history = jnp.concatenate([prior, x_ref[rows, :]], axis=0)
        ahead = jnp.concatenate([d_conv, dconv_s[pl.ds(pl.multiple_of(base + tb, 8), 8), :]], axis=0)
        dconv_s[rows, :] = d_conv
        same = masks_ref[pl.ds(base, tb + 8), :]
        d_x = cw_ref[taps - 1:taps, :] * d_conv
        pack_s[0:1, :] += jnp.sum(d_conv, axis=0, keepdims=True)
        pack_s[8 - 1:8, :] += jnp.sum(d_conv * history[8:, :], axis=0, keepdims=True)
        for s in range(1, taps):
            linked = same[:, s:s + 1] * ahead
            d_x = d_x + cw_ref[taps - 1 - s:taps - s, :] * linked[s:s + tb, :]
            pack_s[7 - s:8 - s, :] += jnp.sum(linked[:tb, :] * history[8 - s:8 - s + tb, :], axis=0, keepdims=True)
        d_x = d_x.astype(BF16)
        dx_s[rows, :] = d_x
        both = lax.dot_general(d_x, wx_ref[...], turned, preferred_element_type=F32)
        both = both + lax.dot_general(dz_s[rows, :], wz_ref[...], turned, preferred_element_type=F32)
        dn_own[rows, :] = both.astype(BF16)

        @pl.when(end)
        def _():
            dn.start(b)

    def last_block(k):
        b = nb - 1 - k
        rows = rows_of(b)

        @pl.when(end)
        def _():
            dn.arrived(b)

        d_normed = dn_far[rows, :]
        dn_ref[...] = d_normed
        first_s[...] += jnp.sum(d_normed.astype(F32) * normed_ref[rows, :].astype(F32), axis=0, keepdims=True)

    def at_step(lag, count, work):
        @pl.when((i >= lag) & (i < lag + count))
        def _():
            work(i - lag)

    def on_mid(lag, count, work):
        @pl.when(mid & (i >= lag) & (i < lag + count))
        def _():
            work(i - lag)

    def line_down(c):
        line.arrived(c)
        return_chunk(c)

    parts = seq // tokens_ref.shape[0]
    at_step(0, parts, glue)
    at_step(parts, 1, lambda k: product(0, dmixed_s, gated_ref))
    at_step(parts + 1, 1, lambda k: product(1, normed_ref, dz_s))
    at_step(0, nb, lambda k: scan_block())
    on_mid(1, nb, dp.flow)
    on_mid(nb + 1, 1, lambda k: dp.flush(nb))
    at_step(3, nb, conv_block)
    on_mid(4, nb, dn.flow)
    on_mid(nb + 4, 1, lambda k: dn.flush(nb))
    at_out_steps(mid, 1, lambda c: line.flow(c, return_chunk))
    on_mid(OUT_STEPS[-1] + 2, 1, lambda k: line.flush(wide, return_chunk))

    at_out_steps(end, 3, line_down)
    at_step(nb + 2, 1, lambda k: product(2, normed_ref, dx_s))
    at_step(6, nb, last_block)

    share = pack_s.shape[0] // wide
    halves = width // ch
    gains_at = 8 + ns + rank + rank + 2 * ns

    def chunk(ref, n):
        return ref.at[pl.ds(pl.multiple_of(n * share, share), share)]

    def scatter(k):
        to = lax.rem(me + k, wide)
        return pltpu.make_async_remote_copy(chunk(pack_s, to), pack_in.at[k], pack_sends.at[0, k], pack_arrivals.at[0, k],
                                            device_id={"wide": to}, device_id_type=MESH)

    def spread_out(k):
        to = lax.rem(me + k, wide)
        return pltpu.make_async_remote_copy(chunk(small_s, me), chunk(small_s, me), pack_sends.at[1, k], pack_arrivals.at[1, k],
                                            device_id={"wide": to}, device_id_type=MESH)

    def gain_term(k):
        to = lax.rem(me + k, wide)
        return pltpu.make_async_remote_copy(gains_s.at[me], gains_s.at[me], pack_sends.at[2, k], pack_arrivals.at[2, k],
                                            device_id={"wide": to}, device_id_type=MESH)

    def collect(which, ref):
        total = prod_s[which, pl.ds(pl.multiple_of(me * block, block), block), :].astype(F32)
        for k in range(1, wide):
            deliver(which, k).wait_recv()
            total = total + inbox_s[which, k].astype(F32)
        ref[...] = total

    @pl.when(i == nb + 3)
    def _():
        at = 8
        pack_s[at:at + ns, :] = -jnp.exp(lr_ref[...]) * acc_s[...]
        at += ns
        pack_s[at:at + rank, :] = gstep_s[0:rank, :]
        at += rank
        held = rank + 2 * ns
        pack_s[at:at + held, :] = state_s[0:held, :]
        own_row = lax.broadcasted_iota(jnp.int32, (wide, ch), 0) == me
        for h in range(halves):
            cols = slice(h * ch, (h + 1) * ch)
            pack_s[gains_at + halves + h:gains_at + halves + h + 1, :] = second_s[:, cols]
            pack_s[gains_at + 8 + h * wide:gains_at + 8 + (h + 1) * wide, :] = jnp.where(own_row, grow_ref[:, cols], 0.0)
        for k in range(1, wide):
            scatter(k).start()
        collect(0, go_ref)

    @pl.when(i == nb + 4)
    def _():
        total = chunk(pack_s, me)[...]
        for k in range(1, wide):
            scatter(k).wait_recv()
            total = total + pack_in[k]
        chunk(small_s, me)[...] = total
        for k in range(1, wide):
            spread_out(k).start()
        collect(1, gz_ref)

    @pl.when(i == pl.num_programs(0) - 1)
    def _():
        gains_s[me] = jnp.broadcast_to(first_s[...] / as_row(first_gain_ref), (8, width))
        for k in range(1, wide):
            gain_term(k).start()
        collect(2, gx_ref)
        line.sent(wide)
        dp.sent(nb)
        dn.sent(nb)
        for k in range(1, wide):
            spread_out(k).wait_recv()
        small_ref[...] = small_s[...]
        for k in range(1, wide):
            gain_term(k).wait_recv()
        first = gains_s[0, 0:1, :]
        for n in range(1, wide):
            first = first + gains_s[n, 0:1, :]
        for h in range(halves):
            small_ref[gains_at + h:gains_at + h + 1, :] = first[:, h * ch:(h + 1) * ch]
        for k in range(1, wide):
            give_back(k).wait_recv()
            give_back(k).wait_send()
            for which in range(3):
                deliver(which, k).wait_send()
            scatter(k).wait_send()
            spread_out(k).wait_send()
            gain_term(k).wait_send()


def mixer_back(wide, taps, rank, by_rows, whole_ones):
    proj, keep, step, states, starts, tokens, mixed, ograd, scol, z, scan = by_rows
    inner, log_rates, ret = whole_ones[0], whole_ones[2], whole_ones[4]
    seq, ch = inner.shape
    width = tokens.shape[1]
    ns = log_rates.shape[0]
    tb = LANES
    nb = seq // tb
    packed = pack_rows(rank, ns, wide, width, ch, wide)
    back = lambda i: jnp.maximum(nb - 1 - i, 0)
    early = lambda i: jnp.maximum(nb // 2 - 1 - i, 0)
    final = lambda i: nb - 1 - jnp.maximum(i - 6, 0)
    row = lambda n, size=tb: pl.BlockSpec((size, n), lambda i: (back(i), 0))
    full = lambda a: pl.BlockSpec(a.shape, lambda i: (0,) * a.ndim, pipeline_mode=pl.Buffered(1))
    whole = lambda *s: pl.BlockSpec(s, lambda i: (0,) * len(s))
    shape = jax.ShapeDtypeStruct
    dma = pltpu.SemaphoreType.DMA
    vm = pltpu.VMEM
    return pl.pallas_call(
        functools.partial(mixer_back_kernel, ns, rank, wide, taps),
        grid=(nb + 6,),
        in_specs=[row(LANES), row(1), row(ch), row(ch, tb * ns), pl.BlockSpec((1, ns, ch), lambda i: (back(i), 0, 0)),
                  *[pl.BlockSpec((2 * tb, n), lambda i: (early(i), 0)) for n in (width, width, width, 1, ch, ch)], *[full(a) for a in whole_ones]],
        out_specs=[pl.BlockSpec((2 * tb, width), lambda i: (early(i), 0)), pl.BlockSpec((tb, width), lambda i: (final(i), 0)), *[whole(width // wide, ch)] * 3, whole(packed, ch),
                   pl.BlockSpec(memory_space=pl.ANY)],
        out_shape=[shape((seq, width), F32), shape((seq, width), BF16), *[shape((width // wide, ch), F32)] * 3, shape((packed, ch), F32),
                   shape(ret.shape, BF16)],
        scratch_shapes=[
            vm((ns, ch), F32), *[vm((ch // LANES, tb, LANES), F32)] * 4, vm((ch // LANES, ns, LANES), F32), vm((tb, ch), F32), vm((tb, ch), F32),
            vm((ns, ch), F32), vm((tb, LANES), F32), *[vm((8 * ns, 2 * LANES), F32)] * 2, *[vm((8 * ns, 2 * LANES), BF16)] * 2,
            *[vm(ret.shape, BF16)] * 3, *[dma((3, wide * SLOT_PIECES))] * 2, dma((wide,)), dma((wide,)),
            *[vm((seq, LANES), BF16)] * 3, dma((3, nb)), dma((3, nb)), *[vm((seq, width), BF16)] * 3, *[dma((3, nb * PIECES))] * 2,
            vm((3, width, ch), BF16), vm((3, wide, width // wide, ch), BF16), dma((3, wide)), dma((3, wide)),
            vm((packed, ch), F32), vm((wide, packed // wide, ch), F32), vm((packed, ch), F32), dma((3, wide)), dma((3, wide)),
            vm((seq, ch), F32), vm((seq, width), BF16), vm((seq, ch), BF16), vm((seq + 8, ch), F32), vm((seq, ch), BF16),
            vm((LANES, ch), F32), vm((LANES, ch), F32), vm((1, width), F32), vm((1, width), F32),
            vm((seq, ch), F32), vm((wide, 8, width), F32)],
        compiler_params=pltpu.CompilerParams(collective_id=1, has_side_effects=True, vmem_limit_bytes=62 << 20),
        name="mixer_back",
    )(*by_rows, *whole_ones)


def gelu_pair(v):
    root = 0.7978845608028654
    square = v * v
    t = jnp.tanh(root * v * (1.0 + 0.044715 * square))
    half = 0.5 * (1.0 + t)
    slope = half + (0.5 * root) * v * (1.0 - t * t) * (1.0 + (3.0 * 0.044715) * square)
    return v * half, slope


def scan_mix_kernel(ns, rank, wide, proj_ref, inner_ref, keep_ref, sproj_ref, sbias_ref, lr_ref, skip_ref, z_ref, wo_ref, ograd_ref, srow_ref,
                    scan_ref, step_ref, states_ref, starts_ref, gated_ref, mixed_ref, gin_ref,
                    state_s, stepd_s, drive_s, r2_s, wide_a, wide_b, own_s, near_s, far_s, sends, arrivals, grad_s, send_s, g_sends, g_arrivals):
    tb, ch = inner_ref.shape
    groups = ch // LANES
    i = pl.program_id(0)
    roles = line_roles()
    end, mid, mate, other = roles
    line = LineSum(roles, tb, PIECES, own_s, near_s, own_s, far_s, sends, arrivals, behind=MIX_BEHIND)
    steps = pl.num_programs(0)
    seq_blocks = own_s.shape[0] // tb

    me = lax.axis_index("wide")
    cap = send_s.shape[0] // wide

    def slot_rows(k):
        return pl.ds(pl.multiple_of(k * cap, cap), cap)

    def dispatch(k):
        return pltpu.make_async_remote_copy(
            send_s.at[slot_rows(k)], gin_ref.at[slot_rows(k)], g_sends.at[k], g_arrivals.at[k],
            device_id={"wide": lax.rem(me + k, wide)}, device_id_type=MESH)

    own_rows = pltpu.make_async_copy(send_s.at[slot_rows(0)], gin_ref.at[slot_rows(0)], g_sends.at[0])

    @pl.when(i == 0)
    def _():
        greet(wide)
        state_s[...] = jnp.zeros_like(state_s)
        spread(r2_s, jnp.exp(lr_ref[...]) * (-LOG2E))

    step_in = proj_ref[...].astype(BF16)
    pre = jnp.dot(step_in, tall(sproj_ref), preferred_element_type=F32) + as_row(sbias_ref)
    step = softplus(pre)
    step_ref[...] = step
    spread(stepd_s, jnp.where(keep_ref[...] > 0.0, step, 1e30))
    inner = inner_ref[...].astype(F32)
    spread(drive_s, step * inner)
    starts_ref[0] = state_s[...]
    start = tuple(state_s[:, c * LANES:(c + 1) * LANES] for c in range(groups))
    state = forward_tokens(ns, rank, proj_ref, stepd_s, drive_s, r2_s, states_ref, scan_ref, start, wide_a, wide_b)
    for c in range(groups):
        state_s[:, c * LANES:(c + 1) * LANES] = state[c]
    scan = scan_ref[...] + as_row(skip_ref) * inner
    scan_ref[...] = scan
    z = z_ref[...]
    gated = (scan * (z / (1.0 + jnp.exp(-z)))).astype(BF16)
    gated_ref[...] = gated
    here = pl.ds(pl.multiple_of(i * tb, tb), tb)
    own_s[here, :] = lax.dot_general(gated, wo_ref[...], (((1,), (1,)), ((), ())), preferred_element_type=F32).astype(BF16)

    @pl.when(end)
    def _():
        line.start(i)

    @pl.when(i < wide)
    def _():
        @pl.when(i == 0)
        def _():
            grad_s[...] = ograd_ref[...].astype(BF16)

        ids = lax.broadcasted_iota(jnp.int32, (cap, grad_s.shape[0]), 0) + lax.rem(me + i, wide) * cap
        chosen = jnp.where(ids == srow_ref[...], 1.0, 0.0).astype(BF16)
        send_s[slot_rows(i), :] = jnp.dot(chosen, grad_s[...], preferred_element_type=F32).astype(BF16)

        @pl.when(i == 0)
        def _():
            own_rows.start()

        @pl.when(i > 0)
        def _():
            dispatch(i).start()

    @pl.when(mid & (i > 0))
    def _():
        line.flow(i - 1)

    @pl.when(i == steps - 1)
    def _():
        @pl.when(mid)
        def _():
            line.flow(i)
            line.flush(seq_blocks)

        @pl.when(end)
        def _():
            for k in range(steps):
                line.arrived(k)

        mixed_ref[...] = far_s[...]
        line.sent(steps)
        own_rows.wait()
        for k in range(1, wide):
            dispatch(k).wait_recv()
            dispatch(k).wait_send()


def scan_mix(proj, inner, keep, sproj, sbias, log_rates, skip, z, wo, ograd, srow, rank, wide, cap):
    seq, ch = inner.shape
    ns = log_rates.shape[0]
    tb = LANES
    nb = seq // tb
    width = wo.shape[0]
    full = lambda a: pl.BlockSpec(a.shape, lambda i: (0,) * a.ndim)
    rows = pl.BlockSpec((tb, ch), lambda i: (i, 0))
    return pl.pallas_call(
        functools.partial(scan_mix_kernel, ns, rank, wide),
        grid=(nb,),
        in_specs=[pl.BlockSpec((tb, LANES), lambda i: (i, 0)), rows, pl.BlockSpec((tb, 1), lambda i: (i, 0)),
                  full(sproj), full(sbias), full(log_rates), full(skip), rows, full(wo), full(ograd), full(srow)],
        out_specs=[rows, rows, pl.BlockSpec((tb * ns, ch), lambda i: (i, 0)), pl.BlockSpec((1, ns, ch), lambda i: (i, 0, 0)),
                   rows, pl.BlockSpec((seq, width), lambda i: (0, 0)), pl.BlockSpec(memory_space=pl.ANY)],
        out_shape=[jax.ShapeDtypeStruct((seq, ch), F32), jax.ShapeDtypeStruct((seq, ch), F32),
                   jax.ShapeDtypeStruct((seq * ns, ch), BF16), jax.ShapeDtypeStruct((nb, ns, ch), F32),
                   jax.ShapeDtypeStruct((seq, ch), BF16), jax.ShapeDtypeStruct((seq, width), BF16),
                   jax.ShapeDtypeStruct((wide * cap, width), BF16)],
        scratch_shapes=[pltpu.VMEM((ns, ch), F32)] + [pltpu.VMEM((ch // LANES, tb, LANES), F32)] * 2 + [pltpu.VMEM((ch // LANES, ns, LANES), F32),
                        *[pltpu.VMEM((8 * ns, 2 * LANES), F32)] * 2,
                        *[pltpu.VMEM((seq, width), BF16)] * 3, *[pltpu.SemaphoreType.DMA((3, nb * PIECES))] * 2,
                        pltpu.VMEM((seq, width), BF16), pltpu.VMEM((wide * cap, width), BF16),
                        pltpu.SemaphoreType.DMA((wide,)), pltpu.SemaphoreType.DMA((wide,))],
        compiler_params=pltpu.CompilerParams(collective_id=4, has_side_effects=True, vmem_limit_bytes=62 << 20),
        name="scan_mix",
    )(proj, inner, keep, sproj, sbias, log_rates, skip, z, wo, ograd, srow)


def experts_kernel(wide, tokens_ref, mixed_ref, gin_ref, srow_ref, gain_ref, router_ref, up_ref, ub_ref, down_ref, db_ref,
                   gup_ref, gub_ref, gdown_ref, gdb_ref, ret_ref, out_ref, grow_ref,
                   pay_s, send_s, inbox_s, rgrad_s, act_s, dpre_s, own_s, near_s, far_s, acc_s, column_s, rows_s,
                   pay_sends, pay_arrivals, sends, arrivals, ret_sends, ret_arrivals, r_sends, r_arrivals):
    seq, width = tokens_ref.shape
    hid = up_ref.shape[1]
    cap = inbox_s.shape[0] // wide
    tb = LANES
    me, rank = lax.axis_index("wide"), lax.axis_index("tp")
    roles = line_roles()
    end, mid, mate, other = roles
    greet(wide)
    back = LineSum(roles, cap, SLOT_PIECES, own_s, near_s, own_s, far_s, sends, arrivals, behind=SLOT_BEHIND)

    def rows_of(b, size):
        return pl.ds(pl.multiple_of(b * size, size), size)

    def prepare(b, _):
        rows = rows_of(b, tb)
        hidden = tokens_ref[rows, :] + mixed_ref[rows, :].astype(F32)
        scale = lax.rsqrt(jnp.mean(hidden * hidden, axis=1, keepdims=True) + EPS)
        pay_s[rows, :] = (hidden * scale * as_row(gain_ref)).astype(BF16)
        return 0

    lax.fori_loop(0, seq // tb, prepare, 0)

    def payload(expert):
        ids = lax.broadcasted_iota(jnp.int32, (cap, seq), 0) + expert * cap
        chosen = jnp.where(ids == srow_ref[...], 1.0, 0.0).astype(BF16)
        return jnp.dot(chosen, pay_s[...], preferred_element_type=F32).astype(BF16)

    def dispatch(k):
        return pltpu.make_async_remote_copy(
            send_s.at[rows_of(k, cap)], inbox_s.at[rows_of(k, cap)], pay_sends.at[k], pay_arrivals.at[k],
            device_id={"wide": lax.rem(me + k, wide)}, device_id_type=MESH)

    def send(k):
        send_s[rows_of(k, cap), :] = payload(lax.rem(me + k, wide))
        dispatch(k).start()

    ahead = 2

    def send_first(k, _):
        send(k)
        return 0

    lax.fori_loop(1, ahead + 1, send_first, 0)
    inbox_s[0:cap, :] = payload(me)

    def give_back(c):
        return pltpu.make_async_remote_copy(
            far_s.at[rows_of(c, cap)], ret_ref.at[rows_of(me, cap)], ret_sends.at[c], ret_arrivals.at[c],
            device_id={"wide": lax.rem(me + wide - c, wide)}, device_id_type=MESH)

    def return_chunk(c):
        @pl.when(c == 0)
        def _():
            ret_ref[rows_of(me, cap), :] = far_s[0:cap, :]

        @pl.when(c != 0)
        def _():
            give_back(c).start()

    gub_ref[...] = jnp.zeros_like(gub_ref)
    gdb_ref[...] = jnp.zeros_like(gdb_ref)
    acc_s[...] = jnp.zeros_like(acc_s)
    turned = (((1,), (1,)), ((), ()))
    mine = lax.broadcasted_iota(jnp.int32, router_ref.shape, 0) == me
    column_s[...] = jnp.sum(jnp.where(mine, router_ref[...].astype(F32), 0.0), axis=0, keepdims=True)
    lane = lax.broadcasted_iota(jnp.int32, (cap, wide), 1)

    def compute(k, _):
        @pl.when(k + ahead < wide - 1)
        def _():
            send(k + ahead + 1)

        @pl.when(k > 0)
        def _():
            dispatch(k).wait_recv()

        part = rows_of(k, cap)
        rows_in = inbox_s[part, :]
        rows_raw = gin_ref[part, :].astype(F32)
        logits = lax.dot_general(rows_in, router_ref[...], turned, preferred_element_type=F32)
        logit = jnp.sum(jnp.where(lane == me, logits, 0.0), axis=1, keepdims=True)
        gate = 1.0 / (1.0 + jnp.exp(-logit))
        rows_grad = (gate * rows_raw).astype(BF16)
        rgrad_s[part, :] = rows_grad
        pre = jnp.dot(rows_in, up_ref[...], preferred_element_type=F32) + ub_ref[...]
        act, slope = gelu_pair(pre)
        act = act.astype(BF16)
        act_s[part, :] = act
        d_pre = (lax.dot_general(rows_grad, down_ref[...], turned, preferred_element_type=F32) * slope).astype(BF16)
        dpre_s[part, :] = d_pre
        out = jnp.dot(act, down_ref[...], preferred_element_type=F32) + db_ref[...] * (1.0 / LINE)
        d_logit = jnp.sum(rows_raw * out, axis=1, keepdims=True) * (gate * (1.0 - gate))
        own_s[part, :] = (lax.dot_general(d_pre, up_ref[...], turned, preferred_element_type=F32) + d_logit * column_s[...]).astype(BF16)

        @pl.when(end)
        def _():
            back.start(k)

        out_ref[part, :] = (gate * out).astype(BF16)
        acc_s[...] += jnp.sum(d_logit * rows_in.astype(F32), axis=0, keepdims=True)
        gub_ref[...] += jnp.sum(d_pre.astype(F32), axis=0, keepdims=True)
        gdb_ref[...] += jnp.sum(rows_grad.astype(F32), axis=0, keepdims=True)

        @pl.when(mid & (k > 0))
        def _():
            back.flow(k - 1, return_chunk)
        return 0

    lax.fori_loop(0, wide, compute, 0)

    def term(k):
        return pltpu.make_async_remote_copy(rows_s.at[rank], rows_s.at[rank], r_sends.at[k], r_arrivals.at[k],
                                            device_id={"tp": lax.rem(rank + k, LINE)}, device_id_type=MESH)

    rows_s[rank] = jnp.broadcast_to(acc_s[...], (8, width))
    for k in range(1, LINE):
        term(k).start()

    @pl.when(mid)
    def _():
        back.flow(jnp.int32(wide - 1), return_chunk)

    tiles = hid // LANES
    across_rows = (((0,), (0,)), ((), ()))

    def tile(j, _):
        @pl.when(j < tiles)
        def _():
            cols = rows_of(j, LANES)
            gdown_ref[cols, :] = lax.dot_general(act_s[:, cols], rgrad_s[...], across_rows, preferred_element_type=F32)

        @pl.when(j >= tiles)
        def _():
            cols = rows_of(j - tiles, LANES)
            gup_ref[cols, :] = lax.dot_general(inbox_s[:, cols], dpre_s[...], across_rows, preferred_element_type=F32)

        @pl.when(end & (j < wide))
        def _():
            back.arrived(j)
            return_chunk(j)

        @pl.when(mid & (j == 1))
        def _():
            back.flush(wide, return_chunk)
        return 0

    lax.fori_loop(0, 2 * tiles, tile, 0)
    for k in range(1, LINE):
        term(k).wait_recv()
    grow_ref[...] = ((rows_s[0] + rows_s[1]) + rows_s[2]) + rows_s[3]
    for c in range(1, wide):
        give_back(c).wait_recv()
    back.sent(wide)
    for k in range(1, wide):
        dispatch(k).wait_send()
        give_back(k).wait_send()
    for k in range(1, LINE):
        term(k).wait_send()


def experts_block(wide, cap, *operands):
    tokens, mixed, gin, srow, gain, router, up, ub, down, db = operands
    seq, width = tokens.shape
    hid = up.shape[1]
    vm = pl.BlockSpec(memory_space=pltpu.VMEM)
    shape = jax.ShapeDtypeStruct
    dma = pltpu.SemaphoreType.DMA
    slots = wide * cap
    return pl.pallas_call(
        functools.partial(experts_kernel, wide),
        in_specs=[vm] * len(operands),
        out_specs=[vm] * 7,
        out_shape=[shape((width, hid), F32), shape((1, hid), F32), shape((hid, width), F32), shape((1, width), F32),
                   shape((slots, width), BF16), shape((slots, width), BF16), shape((8, width), F32)],
        scratch_shapes=[
            pltpu.VMEM((seq, width), BF16), *[pltpu.VMEM((slots, width), BF16)] * 3,
            pltpu.VMEM((slots, hid), BF16), pltpu.VMEM((slots, hid), BF16),
            *[pltpu.VMEM((slots, width), BF16)] * 3, pltpu.VMEM((1, width), F32), pltpu.VMEM((1, width), F32), pltpu.VMEM((LINE, 8, width), F32),
            dma((wide,)), dma((wide,)), *[dma((3, wide * SLOT_PIECES))] * 2, dma((wide,)), dma((wide,)), dma((LINE,)), dma((LINE,))],
        compiler_params=pltpu.CompilerParams(collective_id=2, has_side_effects=True, vmem_limit_bytes=62 << 20),
        name="experts",
    )(*operands)


def front_kernel(wide, taps, tokens_ref, gain_ref, inx_ref, inz_ref, outp_ref, cw_ref, cb_ref, wproj_ref, masks_ref,
                 scale_ref, normed_ref, x_ref, z_ref, csum_ref, inner_ref, proj_ref, wx_ref, wz_ref, wo_ref,
                 own_s, near_s, far_s, w_sends, w_arrivals, sends, arrivals):
    seq, width = tokens_ref.shape
    ch = x_ref.shape[1]
    block = inx_ref.shape[0]
    tb = LANES
    nb = seq // tb
    me = lax.axis_index("wide")
    roles = line_roles()
    end, mid, mate, other = roles
    greet(wide)
    line = LineSum(roles, 2 * tb, 1, own_s, near_s, own_s, far_s, sends, arrivals)
    mine = pl.ds(pl.multiple_of(me * block, block), block)
    weights = ((inx_ref, wx_ref), (inz_ref, wz_ref), (outp_ref, wo_ref))

    def share(which, k):
        source, target = weights[which]
        return pltpu.make_async_remote_copy(source, target.at[mine], w_sends.at[which, k], w_arrivals.at[which, k],
                                            device_id={"wide": lax.rem(me + k, wide)}, device_id_type=MESH)

    for which in range(3):
        for k in range(1, wide):
            share(which, k).start()
    for source, target in weights:
        target[mine, :] = source[...]

    def rows_of(b):
        return pl.ds(pl.multiple_of(b * tb, tb), tb)

    def norm(b, _):
        rows = rows_of(b)
        tokens = tokens_ref[rows, :]
        scale = lax.rsqrt(jnp.mean(tokens * tokens, axis=1, keepdims=True) + EPS)
        scale_ref[rows, :] = scale
        normed_ref[rows, :] = (tokens * scale * as_row(gain_ref)).astype(BF16)
        return 0

    own_s[...] = jnp.zeros_like(own_s)
    lax.fori_loop(0, nb, norm, 0)
    for k in range(1, wide):
        share(0, k).wait_recv()

    def step(b, _):
        rows = rows_of(b)
        base = pl.multiple_of(b * tb, tb)
        x = jnp.dot(normed_ref[rows, :], wx_ref[...], preferred_element_type=F32)
        x_ref[rows, :] = x
        prior = x_ref[pl.ds(pl.multiple_of(jnp.maximum(base - 8, 0), 8), 8), :]
        history = jnp.concatenate([prior, x], axis=0)
        same = masks_ref[rows, :]
        csum = as_row(cb_ref) + cw_ref[taps - 1:taps, :] * x
        for s in range(1, taps):
            csum = csum + cw_ref[taps - 1 - s:taps - s, :] * (same[:, s:s + 1] * history[8 - s:8 - s + tb, :])
        csum_ref[rows, :] = csum
        inner = (csum / (1.0 + jnp.exp(-csum))).astype(BF16)
        inner_ref[rows, :] = inner
        own_s[rows, :wproj_ref.shape[0]] = lax.dot_general(
            inner, wproj_ref[...], (((1,), (1,)), ((), ())), preferred_element_type=F32).astype(BF16)

        @pl.when(end & (lax.rem(b, 2) == 1))
        def _():
            line.start(b // 2)
        return 0

    lax.fori_loop(0, nb, step, 0)
    steps = nb // 2

    @pl.when(mid)
    def _():
        for k in range(steps):
            line.flow(jnp.int32(k))

    for k in range(1, wide):
        share(1, k).wait_recv()

    def gate(b, _):
        rows = rows_of(b)
        z_ref[rows, :] = jnp.dot(normed_ref[rows, :], wz_ref[...], preferred_element_type=F32)
        return 0

    lax.fori_loop(0, nb, gate, 0)

    @pl.when(mid)
    def _():
        line.flush(steps)

    @pl.when(end)
    def _():
        for k in range(steps):
            line.arrived(k)

    proj_ref[...] = far_s[...].astype(F32)
    line.sent(steps)
    for k in range(1, wide):
        share(2, k).wait_recv()
        for which in range(3):
            share(which, k).wait_send()


def front(wide, taps, *operands):
    tokens, gain, inx, inz, outp, cw, cb, wproj, masks = operands
    seq, width = tokens.shape
    ch = inx.shape[1]
    vm = pl.BlockSpec(memory_space=pltpu.VMEM)
    shape = jax.ShapeDtypeStruct
    dma = pltpu.SemaphoreType.DMA
    return pl.pallas_call(
        functools.partial(front_kernel, wide, taps),
        in_specs=[vm] * len(operands),
        out_specs=[vm] * 10,
        out_shape=[shape((seq, 1), F32), shape((seq, width), BF16), shape((seq, ch), F32), shape((seq, ch), F32), shape((seq, ch), F32),
                   shape((seq, ch), BF16), shape((seq, LANES), F32), *[shape((width, ch), BF16)] * 3],
        scratch_shapes=[*[pltpu.VMEM((seq, LANES), BF16)] * 3, dma((3, wide)), dma((3, wide)), dma((3, seq // LANES // 2)), dma((3, seq // LANES // 2))],
        compiler_params=pltpu.CompilerParams(collective_id=3, has_side_effects=True, vmem_limit_bytes=62 << 20),
        name="mixer_front",
    )(*operands)


def plain_device(
    tokens,
    segment_ids,
    routes,
    out_grad,
    mixer_gain,
    in_proj_x,
    in_proj_z,
    conv_weight,
    conv_bias,
    state_proj,
    step_proj,
    step_bias,
    log_rates,
    skip_gain,
    out_proj,
    expert_gain,
    router_weight,
    expert_up,
    up_bias,
    expert_down,
    down_bias,
):
    seq_len, model_width = tokens.shape
    conv_taps = conv_weight.shape[0]
    step_rank = step_proj.shape[0]
    experts = router_weight.shape[1]
    capacity = 5 * seq_len // (4 * experts)
    doc_ids = segment_ids[0]
    conv_masks = [same_document(doc_ids, offset)[:, None] for offset in range(conv_taps)]
    first_scale = lax.rsqrt(jnp.mean(tokens * tokens, axis=1, keepdims=True) + EPS)
    first_unit = tokens * first_scale
    normed = (first_unit * mixer_gain).astype(jnp.bfloat16)
    gathered_x, gathered_z, gathered_out = (
        lax.all_gather(in_proj_x, "wide", axis=0, tiled=True),
        lax.all_gather(in_proj_z, "wide", axis=0, tiled=True),
        lax.all_gather(out_proj, "wide", axis=0, tiled=True),
    )
    x_branch = multiply(normed, gathered_x)
    z_branch = multiply(normed, gathered_z)
    conv_sum = conv_bias + jnp.zeros_like(x_branch)
    for offset in range(conv_taps):
        conv_sum = conv_sum + conv_weight[conv_taps - 1 - offset] * conv_masks[
            offset
        ] * shifted_down(x_branch, offset)
    inner_act = jax.nn.silu(conv_sum).astype(jnp.bfloat16)
    wide_proj = jnp.pad(state_proj, ((0, 0), (0, LANES - state_proj.shape[1])))
    projected = lax.psum(multiply(inner_act, wide_proj), "tp")
    tall_proj = jnp.pad(step_proj, ((0, LANES - step_rank), (0, 0)))
    carry_mask = same_document(doc_ids, 1)[:, None]
    scan_out, step_size, states, starts = scan_fwd(
        projected, inner_act, carry_mask, tall_proj, step_bias[None], log_rates, skip_gain[None], step_rank
    )
    z_gate = jax.nn.silu(z_branch)
    gated = (scan_out * z_gate).astype(jnp.bfloat16)
    mixed = lax.psum(contract_cols(gated, gathered_out).astype(jnp.bfloat16), "tp").astype(
        jnp.float32
    )
    hidden = tokens + mixed
    second_scale = lax.rsqrt(jnp.mean(hidden * hidden, axis=1, keepdims=True) + EPS)
    second_unit = hidden * second_scale
    expert_in = (second_unit * expert_gain).astype(jnp.bfloat16)
    route_ids = routes[:, 0]
    chosen_int = (routes == jnp.arange(experts, dtype=jnp.int32)[None, :]).astype(jnp.int32)
    chosen = chosen_int.astype(jnp.float32)
    logits = multiply(expert_in, router_weight)
    gate = jax.nn.sigmoid(jnp.sum(logits * chosen, axis=1))
    rank_of = jnp.arange(seq_len, dtype=jnp.int32)
    earlier = (rank_of[:, None] > rank_of[None, :]).astype(jnp.bfloat16)
    position = jnp.sum(multiply(earlier, chosen.astype(jnp.bfloat16)) * chosen, axis=1).astype(jnp.int32)
    kept = position < capacity
    slots = jnp.where(kept, route_ids * capacity + position, experts * capacity)
    scaled_grad = (gate[:, None] * out_grad).astype(jnp.bfloat16)
    sent_width = expert_in.shape[1]
    send_in = (
        jnp.zeros((experts * capacity + 1, sent_width), jnp.bfloat16).at[slots].set(expert_in)[:-1]
    )
    send_grad = (
        jnp.zeros((experts * capacity + 1, sent_width), jnp.bfloat16)
        .at[slots]
        .set(scaled_grad)[:-1]
    )
    recv_in, recv_grad = (
        lax.all_to_all(
            send_in.reshape(experts, capacity, sent_width),
            "wide",
            split_axis=0,
            concat_axis=0,
            tiled=True,
        ),
        lax.all_to_all(
            send_grad.reshape(experts, capacity, sent_width),
            "wide",
            split_axis=0,
            concat_axis=0,
            tiled=True,
        ),
    )
    rows_in = recv_in.reshape(-1, model_width)
    rows_grad = recv_grad.reshape(-1, model_width)
    pre_act = multiply(rows_in, expert_up[0]) + up_bias[0]
    hidden_act = jax.nn.gelu(pre_act).astype(jnp.bfloat16)
    partial_out = multiply(hidden_act, expert_down[0])
    up_grad = contract_cols(rows_grad, expert_down[0])
    d_pre = jax.vjp(jax.nn.gelu, pre_act)[1](up_grad)[0].astype(jnp.bfloat16)
    partial_back = contract_cols(d_pre, expert_up[0])
    grad_down = contract_rows(hidden_act, rows_grad)
    grad_dbias = jnp.sum(rows_grad.astype(jnp.float32), axis=0)
    grad_up = contract_rows(rows_in, d_pre)
    grad_ubias = jnp.sum(d_pre.astype(jnp.float32), axis=0)
    out_sum, back_sum = (
        lax.psum(partial_out.astype(jnp.bfloat16), "tp").astype(jnp.float32),
        lax.psum(partial_back.astype(jnp.bfloat16), "tp").astype(jnp.float32),
    )
    bias_part = down_bias[0]
    outgoing = (out_sum + bias_part).astype(jnp.bfloat16).reshape(experts, capacity, -1)
    back_rows = back_sum.astype(jnp.bfloat16).reshape(experts, capacity, -1)
    incoming, arriving = (
        lax.all_to_all(outgoing, "wide", split_axis=0, concat_axis=0, tiled=True),
        lax.all_to_all(back_rows, "wide", split_axis=0, concat_axis=0, tiled=True),
    )
    safe_slots = jnp.minimum(slots, experts * capacity - 1)
    returned = jnp.where(
        kept[:, None], incoming.reshape(-1, model_width)[safe_slots].astype(jnp.float32), 0.0
    )
    result = hidden + gate[:, None] * returned
    d_gate = jnp.sum(out_grad * returned, axis=1)
    d_logit = (d_gate * gate * (1.0 - gate))[:, None] * chosen
    grad_router = jnp.dot(expert_in.astype(jnp.float32).T, d_logit, precision=HIGH)
    d_norm_two = jnp.dot(d_logit, router_weight.astype(jnp.float32).T, precision=HIGH)
    d_norm_two = d_norm_two + jnp.where(
        kept[:, None], arriving.reshape(-1, model_width)[safe_slots].astype(jnp.float32), 0.0
    )
    grad_second_gain = jnp.sum(d_norm_two * second_unit, axis=0)
    d_hidden = out_grad + rms_back(d_norm_two * expert_gain, second_unit, second_scale)
    d_mixed = d_hidden.astype(jnp.bfloat16)
    d_gated = multiply(d_mixed, gathered_out)
    grad_out = contract_rows(d_mixed, gated)
    d_scan = d_gated * z_gate
    d_z = (d_gated * scan_out * silu_slope(z_branch)).astype(jnp.bfloat16)
    d_step_pre, d_inner, d_proj, grad_step, grad_sbias, grad_rates, grad_skip = scan_bwd(
        projected, inner_act, carry_mask, step_size, states, starts, d_scan, tall_proj, log_rates, skip_gain[None], step_rank
    )
    grad_step, grad_sbias, grad_skip = grad_step[:step_rank], grad_sbias[0], grad_skip[0]
    d_projected = lax.psum(d_proj.astype(jnp.bfloat16), "tp")
    grad_state = contract_rows(inner_act, d_projected)[:, : state_proj.shape[1]]
    d_inner = d_inner + contract_cols(d_projected, wide_proj)
    d_conv = d_inner * silu_slope(conv_sum)
    grad_cbias = jnp.sum(d_conv, axis=0)
    conv_rows = []
    d_input = jnp.zeros_like(d_conv)
    for offset in range(conv_taps):
        conv_rows.append(
            jnp.sum(d_conv * conv_masks[offset] * shifted_down(x_branch, offset), axis=0)
        )
        d_input = d_input + conv_weight[conv_taps - 1 - offset] * shifted_up(
            conv_masks[offset] * d_conv, offset
        )
    grad_conv = jnp.stack(conv_rows[::-1])
    d_x_branch = d_input.astype(jnp.bfloat16)
    grad_in_x = contract_rows(normed, d_x_branch)
    grad_in_z = contract_rows(normed, d_z)
    d_normed = lax.psum(
        (contract_cols(d_x_branch, gathered_x) + contract_cols(d_z, gathered_z)).astype(
            jnp.bfloat16
        ),
        "tp",
    ).astype(jnp.float32)
    grad_first_gain = jnp.sum(d_normed * first_unit, axis=0)
    tokens_grad = d_hidden + rms_back(d_normed * mixer_gain, first_unit, first_scale)
    grad_in_x, grad_in_z, grad_out = (
        summed_on_arrival(grad_in_x.astype(jnp.bfloat16), "wide", 0),
        summed_on_arrival(grad_in_z.astype(jnp.bfloat16), "wide", 0),
        summed_on_arrival(grad_out.astype(jnp.bfloat16), "wide", 0),
    )
    (
        grad_first_gain,
        grad_conv,
        grad_cbias,
        grad_state,
        grad_step,
        grad_sbias,
        grad_rates,
        grad_skip,
        grad_second_gain,
        grad_router,
    ) = lax.psum(
        (
            grad_first_gain,
            grad_conv,
            grad_cbias,
            grad_state,
            grad_step,
            grad_sbias,
            grad_rates,
            grad_skip,
            grad_second_gain,
            grad_router,
        ),
        "wide",
    )
    return (
        result,
        tokens_grad,
        grad_first_gain,
        grad_in_x,
        grad_in_z,
        grad_conv,
        grad_cbias,
        grad_state,
        grad_step,
        grad_sbias,
        grad_rates,
        grad_skip,
        grad_out,
        grad_second_gain,
        grad_router,
        grad_up[None],
        grad_ubias[None],
        grad_down[None],
        grad_dbias[None],
    )


def fast_device(
    tokens,
    segment_ids,
    routes,
    out_grad,
    mixer_gain,
    in_proj_x,
    in_proj_z,
    conv_weight,
    conv_bias,
    state_proj,
    step_proj,
    step_bias,
    log_rates,
    skip_gain,
    out_proj,
    expert_gain,
    router_weight,
    expert_up,
    up_bias,
    expert_down,
    down_bias,
):
    seq_len, model_width = tokens.shape
    conv_taps = conv_weight.shape[0]
    step_rank = step_proj.shape[0]
    experts = router_weight.shape[1]
    capacity = 5 * seq_len // (4 * experts)
    doc_ids = segment_ids[0]
    conv_masks = [same_document(doc_ids, offset)[:, None] for offset in range(conv_taps)]
    masks = jnp.pad(jnp.concatenate(conv_masks, axis=1), ((0, 8), (0, 8 - conv_taps)))
    wide = lax.axis_size("wide")
    states = log_rates.shape[0]
    chosen = (routes == jnp.arange(experts, dtype=jnp.int32)[None, :]).astype(jnp.float32)
    rank_of = jnp.arange(seq_len, dtype=jnp.int32)
    earlier = (rank_of[:, None] > rank_of[None, :]).astype(jnp.bfloat16)
    position = jnp.sum(multiply(earlier, chosen.astype(jnp.bfloat16)) * chosen, axis=1).astype(jnp.int32)
    slots = jnp.where(position < capacity, routes[:, 0] * capacity + position, experts * capacity)
    slot_row, slot_col = slots[None], slots[:, None]
    carry_mask = same_document(doc_ids, 1)[:, None]

    first_scale, normed, x_branch, z_branch, conv_sum, inner_act, projected, gathered_x, gathered_z, gathered_out = front(
        wide, conv_taps, tokens, mixer_gain, in_proj_x, in_proj_z, out_proj, conv_weight, conv_bias, state_proj.T, masks
    )
    scan_out, step_size, held, starts, gated, mixed, grads_in = scan_mix(
        projected, inner_act, carry_mask, step_proj, step_bias, log_rates, skip_gain, z_branch, gathered_out, out_grad, slot_row,
        step_rank, wide, capacity,
    )
    grad_up, grad_ubias, grad_down, grad_dbias, returned, terms, router_grad = experts_block(
        wide, capacity, tokens, mixed, grads_in, slot_row, expert_gain, router_weight.T,
        expert_up[0], up_bias, expert_down[0], down_bias,
    )
    d_hidden, d_normed, grad_in_x, grad_in_z, grad_out, small, gated_out = mixer_back(
        wide, conv_taps, step_rank,
        (projected, carry_mask, step_size, held, starts, tokens, mixed, out_grad, slot_col, z_branch, scan_out),
        (inner_act, step_proj, log_rates, skip_gain, returned, expert_gain, gathered_out, terms, x_branch, conv_sum, masks, state_proj.T,
         conv_weight, normed, gated, gathered_x, gathered_z, mixer_gain, router_grad),
    )
    outs = finish(
        step_rank, states, experts, tokens, mixed, slot_col, gated_out, d_hidden, d_normed, first_scale, mixer_gain, small,
        grad_in_x, grad_in_z, grad_out, grad_up, grad_down, grad_ubias, grad_dbias,
    )
    return tuple(out.T if n in (7, 14) else out for n, out in enumerate(outs))


def solution(mesh):
    in_specs = (
        P("wide", None),
        P("wide", None),
        P("wide", None),
        P("wide", None),
        P(),
        P("wide", "tp"),
        P("wide", "tp"),
        P(None, "tp"),
        P("tp"),
        P("tp", None),
        P(None, "tp"),
        P("tp"),
        P(None, "tp"),
        P("tp"),
        P("wide", "tp"),
        P(),
        P(),
        P("wide", None, "tp"),
        P("wide", "tp"),
        P("wide", "tp", None),
        P("wide", None),
    )
    out_specs = (
        P("wide", None),
        P("wide", None),
        P(),
        P("wide", "tp"),
        P("wide", "tp"),
        P(None, "tp"),
        P("tp"),
        P("tp", None),
        P(None, "tp"),
        P("tp"),
        P(None, "tp"),
        P("tp"),
        P("wide", "tp"),
        P(),
        P(),
        P("wide", None, "tp"),
        P("wide", "tp"),
        P("wide", "tp", None),
        P("wide", None),
    )
    wide, line = mesh.shape["wide"], mesh.shape["tp"]
    per_device = fast_device if line == 4 and wide == 8 else plain_device
    return jax.shard_map(
        per_device, mesh=mesh, in_specs=in_specs, out_specs=out_specs, check_vma=False
    )
```

```python
import functools

import jax
import jax.numpy as jnp
from jax import lax
from jax.experimental import pallas as pl
from jax.experimental.pallas import tpu as pltpu
from jax.sharding import PartitionSpec as P

EPS = 1e-05
HIGH = lax.Precision.HIGHEST


def in_blocks(shard, dim, size):
    before, after = (shard.shape[:dim], shard.shape[dim + 1 :])
    return jnp.moveaxis(shard.reshape(*before, size, -1, *after), dim, 0)


def summed_on_arrival(shard, axis, dim):
    size = lax.axis_size(axis)
    parts = lax.all_to_all(in_blocks(shard, dim, size), axis, 0, 0, tiled=True)
    return jnp.sum(parts.astype(jnp.float32), axis=0)


def multiply(left, right):
    return jnp.dot(left, right, preferred_element_type=jnp.float32)


def contract_rows(left, right):
    return lax.dot_general(
        left, right, (((0,), (0,)), ((), ())), preferred_element_type=jnp.float32
    )


def contract_cols(left, right):
    return lax.dot_general(
        left, right, (((1,), (1,)), ((), ())), preferred_element_type=jnp.float32
    )


def shifted_down(values, steps):
    if steps == 0:
        return values
    filler = jnp.zeros((steps,) + values.shape[1:], values.dtype)
    return jnp.concatenate([filler, values[:-steps]], axis=0)


def shifted_up(values, steps):
    if steps == 0:
        return values
    filler = jnp.zeros((steps,) + values.shape[1:], values.dtype)
    return jnp.concatenate([values[steps:], filler], axis=0)


def same_document(doc_ids, steps):
    if steps == 0:
        return jnp.ones(doc_ids.shape, jnp.float32)
    filler = jnp.full((steps,), -1, jnp.int32)
    earlier = jnp.concatenate([filler, doc_ids[:-steps]])
    return (earlier == doc_ids).astype(jnp.float32)


def silu_slope(values):
    logistic = jax.nn.sigmoid(values)
    return logistic * (1.0 + values * (1.0 - logistic))


def rms_back(grad_unit, unit, scale):
    return scale * (grad_unit - unit * jnp.mean(grad_unit * unit, axis=1, keepdims=True))


LOG2E = 1.4426950408889634
LANES = 128
F32, BF16 = jnp.float32, jnp.bfloat16
MESH = pl.DeviceIdType.MESH


def fold_rows(parts, masks):
    m4, m2, m1 = masks

    def join(a, b, m, shift):
        return jnp.where(m, a, b) + pltpu.roll(jnp.where(m, b, a), shift, 0)

    c = [join(parts[i], parts[i + 4], m4[i], 4) for i in range(4)]
    d = [join(c[i], c[i + 2], m2[i], 6) for i in range(2)]
    return join(d[0], d[1], m1, 7)


def fold_masks(width):
    sub = lax.broadcasted_iota(jnp.int32, (8, width), 0)
    m4 = [((sub - i) & 7) < 4 for i in range(4)]
    m2 = [((sub - i) & 2) == 0 for i in range(2)]
    m1 = (sub & 1) == 0
    return m4, m2, m1


def softplus(v):
    return jnp.maximum(v, 0.0) + jnp.log1p(jnp.exp(-jnp.abs(v)))


def row(ref, c, t, ns):
    one = ref[c, pl.ds(t, 8, stride=0), :]
    return jnp.concatenate([one] * (ns // 8), axis=0)


def spread(ref, value):
    for c in range(ref.shape[0]):
        ref[c] = value[:, c * LANES:(c + 1) * LANES]


def own_column(ns, rank):
    lane = lax.broadcasted_iota(jnp.int32, (ns, LANES), 1)
    n = lax.broadcasted_iota(jnp.int32, (ns, LANES), 0)
    return (lane == rank + n) | (lane == rank + ns + n)


def coefficient_rows(ns, rank, proj_ref, first):
    own = own_column(ns, rank)
    lane = lax.broadcasted_iota(jnp.int32, (LANES, 2 * LANES), 1)
    k = lax.broadcasted_iota(jnp.int32, (LANES, 2 * LANES), 0)
    pick = ((lane < LANES) & (k >= rank) & (k < rank + ns)) | ((lane >= LANES) & (k >= rank + ns) & (k < rank + 2 * ns))
    pick = jnp.where(pick, 1.0, 0.0).astype(BF16)
    rows = []
    for j in range(8):
        one = proj_ref[pl.ds(first + j, 8, stride=0), :]
        rows.append(jnp.where(own, jnp.concatenate([one] * (ns // 8), axis=0), 0.0).astype(BF16))
    return jnp.dot(jnp.concatenate(rows, axis=0), pick, preferred_element_type=F32)


def forward_tokens(ns, rank, proj_ref, stepd_s, drive_s, r2_s, states_ref, scan_ref, state, wide_a, wide_b):
    tb = proj_ref.shape[0]
    groups = len(state)
    masks = fold_masks(LANES)

    def eight(first, wide, state):
        parts = [[] for _ in range(groups)]
        for j in range(8):
            t = first + j
            in_b = wide[j * ns:(j + 1) * ns, :LANES]
            out_b = wide[j * ns:(j + 1) * ns, LANES:]
            for c in range(groups):
                dec = jnp.exp2(row(stepd_s, c, t, ns) * r2_s[c])
                s = dec * state[c] + row(drive_s, c, t, ns) * in_b
                state[c] = s
                states_ref[pl.ds(pl.multiple_of(t * ns, ns), ns), pl.ds(c * LANES, LANES)] = s.astype(BF16)
                z = out_b * s
                parts[c].append(sum(z[8 * k:8 * k + 8] for k in range(ns // 8)))
        for c in range(groups):
            scan_ref[pl.ds(pl.multiple_of(first, 8), 8), pl.ds(c * LANES, LANES)] = fold_rows(parts[c], masks)
        return state

    def body(g, state):
        state = list(state)
        first = g * 16
        wide_b[...] = coefficient_rows(ns, rank, proj_ref, first + 8)
        state = eight(first, wide_a, state)
        wide_a[...] = coefficient_rows(ns, rank, proj_ref, jnp.minimum(first + 16, tb - 8))
        return tuple(eight(first + 8, wide_b, state))

    wide_a[...] = coefficient_rows(ns, rank, proj_ref, 0)
    return lax.fori_loop(0, tb // 16, body, state)


def backward_tokens(ns, rank, proj_ref, states_ref, starts_ref, stepd_s, drive_s, dscan_s, step_s, r2_s, coeff_s, exps_s, dproj_ref,
                    later, acc, wide_a, wide_b, sums_a, sums_b):
    tb = proj_ref.shape[0]
    groups = len(later)
    masks = fold_masks(LANES)
    own = own_column(ns, rank)
    k = lax.broadcasted_iota(jnp.int32, (2 * LANES, LANES), 0)
    lane = lax.broadcasted_iota(jnp.int32, (2 * LANES, LANES), 1)
    into = ((k < LANES) & (lane >= rank) & (lane < rank + ns)) | ((k >= LANES) & (lane >= rank + ns) & (lane < rank + 2 * ns))
    into = jnp.where(into, 1.0, 0.0).astype(BF16)

    def gather(sums, first):
        got = jnp.dot(sums[...], into, preferred_element_type=F32)
        parts = []
        for j in range(8):
            one = jnp.where(own, got[j * ns:(j + 1) * ns], 0.0)
            parts.append(sum(one[8 * q:8 * q + 8] for q in range(ns // 8)))
        dproj_ref[pl.ds(pl.multiple_of(first, 8), 8), :] = fold_rows(parts, masks)

    def eight(first, wide, sums, later, acc):
        cparts = [[None] * 8 for _ in range(groups)]
        eparts = [[None] * 8 for _ in range(groups)]
        last = pl.ds(pl.multiple_of((first + 7) * ns, ns), ns)
        now = [states_ref[last, pl.ds(c * LANES, LANES)].astype(F32) for c in range(groups)]
        for j in range(7, -1, -1):
            t = first + j
            prior = pl.ds(pl.multiple_of((t - 1 if j else jnp.maximum(t - 1, 0)) * ns, ns), ns)
            here = slice(j * ns, (j + 1) * ns)
            in_b = wide[here, :LANES]
            out_b = wide[here, LANES:]
            din = dout = None
            for c in range(groups):
                cols = pl.ds(c * LANES, LANES)
                before = states_ref[prior, cols].astype(F32)
                if j == 0:
                    before = jnp.where(jnp.full((ns, LANES), t, jnp.int32) == 0, starts_ref[0, :, cols], before)
                r2 = r2_s[c]
                dec = jnp.exp2(row(stepd_s, c, t, ns) * r2)
                ds = row(dscan_s, c, t, ns)
                d = later[c] + out_b * ds
                later[c] = dec * d
                dexp = later[c] * before
                e = dexp * r2
                cf = d * in_b
                cparts[c][j] = sum(cf[8 * q:8 * q + 8] for q in range(ns // 8))
                eparts[c][j] = sum(e[8 * q:8 * q + 8] for q in range(ns // 8))
                acc[c] = acc[c] + dexp * row(step_s, c, t, ns)
                a = d * row(drive_s, c, t, ns)
                b = now[c] * ds
                din = a if din is None else din + a
                dout = b if dout is None else dout + b
                now[c] = before
            sums[here, :LANES] = din.astype(BF16)
            sums[here, LANES:] = dout.astype(BF16)
        rows = pl.ds(pl.multiple_of(first, 8), 8)
        for c in range(groups):
            cols = pl.ds(c * LANES, LANES)
            coeff_s[rows, cols] = fold_rows(cparts[c], masks)
            exps_s[rows, cols] = fold_rows(eparts[c], masks)
        return later, acc

    def body(k, carry):
        later, acc = [list(v) for v in carry]
        first = tb - 16 - k * 16
        gather(sums_a, jnp.minimum(first + 16, tb - 8))
        wide_a[...] = coefficient_rows(ns, rank, proj_ref, first)
        later, acc = eight(first + 8, wide_b, sums_b, later, acc)
        gather(sums_b, first + 8)
        wide_b[...] = coefficient_rows(ns, rank, proj_ref, jnp.maximum(first - 8, 0))
        later, acc = eight(first, wide_a, sums_a, later, acc)
        return tuple(later), tuple(acc)

    wide_b[...] = coefficient_rows(ns, rank, proj_ref, tb - 8)
    sums_a[...] = jnp.zeros_like(sums_a)
    later, acc = lax.fori_loop(0, tb // 16, body, (later, acc))
    gather(sums_a, 0)
    return later, acc


def scan_fwd_kernel(ns, rank, proj_ref, inner_ref, keep_ref, sproj_ref, sbias_ref, lr_ref, skip_ref,
                    scan_ref, step_ref, states_ref, starts_ref, state_s, stepd_s, drive_s, r2_s, wide_a, wide_b):
    tb, ch = inner_ref.shape
    groups = ch // LANES
    i = pl.program_id(0)

    @pl.when(i == 0)
    def _():
        state_s[...] = jnp.zeros_like(state_s)
        spread(r2_s, jnp.exp(lr_ref[...]) * (-LOG2E))

    step_in = proj_ref[...].astype(BF16)
    pre = jnp.dot(step_in, sproj_ref[...], preferred_element_type=F32) + sbias_ref[...]
    step = softplus(pre)
    step_ref[...] = step
    spread(stepd_s, jnp.where(keep_ref[...] > 0.0, step, 1e30))
    inner = inner_ref[...].astype(F32)
    spread(drive_s, step * inner)
    starts_ref[0] = state_s[...]
    start = tuple(state_s[:, c * LANES:(c + 1) * LANES] for c in range(groups))
    state = forward_tokens(ns, rank, proj_ref, stepd_s, drive_s, r2_s, states_ref, scan_ref, start, wide_a, wide_b)
    for c in range(groups):
        state_s[:, c * LANES:(c + 1) * LANES] = state[c]
    scan_ref[...] += skip_ref[...] * inner


def scan_fwd(proj, inner, keep, sproj, sbias, log_rates, skip, rank):
    seq, ch = inner.shape
    ns = log_rates.shape[0]
    tb = LANES
    nb = seq // tb
    full = lambda a: pl.BlockSpec(a.shape, lambda i: (0,) * a.ndim)
    rows = pl.BlockSpec((tb, ch), lambda i: (i, 0))
    return pl.pallas_call(
        functools.partial(scan_fwd_kernel, ns, rank),
        grid=(nb,),
        in_specs=[pl.BlockSpec((tb, LANES), lambda i: (i, 0)), rows, pl.BlockSpec((tb, 1), lambda i: (i, 0)),
                  full(sproj), full(sbias), full(log_rates), full(skip)],
        out_specs=[rows, rows, pl.BlockSpec((tb * ns, ch), lambda i: (i, 0)), pl.BlockSpec((1, ns, ch), lambda i: (i, 0, 0))],
        out_shape=[jax.ShapeDtypeStruct((seq, ch), F32), jax.ShapeDtypeStruct((seq, ch), F32),
                   jax.ShapeDtypeStruct((seq * ns, ch), BF16), jax.ShapeDtypeStruct((nb, ns, ch), F32)],
        scratch_shapes=[pltpu.VMEM((ns, ch), F32)] + [pltpu.VMEM((ch // LANES, tb, LANES), F32)] * 2 + [pltpu.VMEM((ch // LANES, ns, LANES), F32),
                        *[pltpu.VMEM((8 * ns, 2 * LANES), F32)] * 2],
        compiler_params=pltpu.CompilerParams(vmem_limit_bytes=48 << 20),
        name="scan_fwd",
    )(proj, inner, keep, sproj, sbias, log_rates, skip)


def scan_bwd_kernel(ns, rank, proj_ref, inner_ref, keep_ref, step_ref, states_ref, starts_ref, dscan_ref, sproj_ref, lr_ref, skip_ref,
                    dpre_ref, dinner_ref, dproj_ref, gstep_ref, gsbias_ref, grates_ref, gskip_ref,
                    carry_s, stepd_s, drive_s, dscan_s, step_s, r2_s, coeff_s, exps_s, acc_s, wide_a, wide_b, sums_a, sums_b):
    tb, ch = inner_ref.shape
    groups = ch // LANES
    i = pl.program_id(0)

    @pl.when(i == 0)
    def _():
        carry_s[...] = jnp.zeros_like(carry_s)
        acc_s[...] = jnp.zeros_like(acc_s)
        spread(r2_s, jnp.exp(lr_ref[...]) * (-LOG2E))
        gstep_ref[...] = jnp.zeros_like(gstep_ref)
        gsbias_ref[...] = jnp.zeros_like(gsbias_ref)
        gskip_ref[...] = jnp.zeros_like(gskip_ref)

    step = step_ref[...]
    inner = inner_ref[...].astype(F32)
    dscan = dscan_ref[...]
    spread(stepd_s, jnp.where(keep_ref[...] > 0.0, step, 1e30))
    spread(drive_s, step * inner)
    spread(dscan_s, dscan)
    spread(step_s, step)
    pick = lambda ref: tuple(ref[:, c * LANES:(c + 1) * LANES] for c in range(groups))
    later, acc = backward_tokens(ns, rank, proj_ref, states_ref, starts_ref, stepd_s, drive_s, dscan_s, step_s, r2_s, coeff_s, exps_s,
                                 dproj_ref, pick(carry_s), pick(acc_s), wide_a, wide_b, sums_a, sums_b)
    for c in range(groups):
        carry_s[:, c * LANES:(c + 1) * LANES] = later[c]
        acc_s[:, c * LANES:(c + 1) * LANES] = acc[c]
    coeff = coeff_s[...]
    d_step = coeff * inner + exps_s[...] * (1.0 / LOG2E)
    d_pre = (d_step * (1.0 - jnp.exp(-step))).astype(BF16)
    dpre_ref[...] = d_pre
    dinner_ref[...] = dscan * skip_ref[...] + step * coeff
    step_in = proj_ref[...].astype(BF16)
    gstep_ref[...] += lax.dot_general(step_in, d_pre, (((0,), (0,)), ((), ())), preferred_element_type=F32)
    gsbias_ref[...] += jnp.sum(d_pre.astype(F32), axis=0, keepdims=True)
    gskip_ref[...] += jnp.sum(dscan * inner, axis=0, keepdims=True)
    dproj_ref[...] += lax.dot_general(d_pre, sproj_ref[...], (((1,), (1,)), ((), ())), preferred_element_type=F32)

    @pl.when(i == pl.num_programs(0) - 1)
    def _():
        grates_ref[...] = -jnp.exp(lr_ref[...]) * acc_s[...]


def scan_bwd(proj, inner, keep, step, states, starts, dscan, sproj, log_rates, skip, rank):
    seq, ch = inner.shape
    ns = log_rates.shape[0]
    tb = LANES
    nb = seq // tb
    full = lambda a: pl.BlockSpec(a.shape, lambda i: (0,) * a.ndim)
    rows = pl.BlockSpec((tb, ch), lambda i: (nb - 1 - i, 0))
    prow = pl.BlockSpec((tb, LANES), lambda i: (nb - 1 - i, 0))
    whole = lambda *s: pl.BlockSpec(s, lambda i: (0,) * len(s))
    shape = jax.ShapeDtypeStruct
    return pl.pallas_call(
        functools.partial(scan_bwd_kernel, ns, rank),
        grid=(nb,),
        in_specs=[prow, rows, pl.BlockSpec((tb, 1), lambda i: (nb - 1 - i, 0)), rows,
                  pl.BlockSpec((tb * ns, ch), lambda i: (nb - 1 - i, 0)), pl.BlockSpec((1, ns, ch), lambda i: (nb - 1 - i, 0, 0)),
                  rows, full(sproj), full(log_rates), full(skip)],
        out_specs=[rows, rows, prow, whole(LANES, ch), whole(1, ch), whole(ns, ch), whole(1, ch)],
        out_shape=[shape((seq, ch), BF16), shape((seq, ch), F32), shape((seq, LANES), F32), shape((LANES, ch), F32), shape((1, ch), F32),
                   shape((ns, ch), F32), shape((1, ch), F32)],
        scratch_shapes=[pltpu.VMEM((ns, ch), F32)] + [pltpu.VMEM((ch // LANES, tb, LANES), F32)] * 4 + [pltpu.VMEM((ch // LANES, ns, LANES), F32),
                        pltpu.VMEM((tb, ch), F32), pltpu.VMEM((tb, ch), F32), pltpu.VMEM((ns, ch), F32),
                        *[pltpu.VMEM((8 * ns, 2 * LANES), F32)] * 2, *[pltpu.VMEM((8 * ns, 2 * LANES), BF16)] * 2],
        compiler_params=pltpu.CompilerParams(vmem_limit_bytes=48 << 20),
        name="scan_bwd",
    )(proj, inner, keep, step, states, starts, dscan, sproj, log_rates, skip)


def tall(ref):
    value = ref[...]
    return jnp.concatenate([value, jnp.zeros((LANES - value.shape[0], value.shape[1]), value.dtype)], axis=0)


def as_row(ref):
    return ref[...].reshape(1, ref.shape[0])


def line_roles():
    me = lax.axis_index("tp")
    end = (me == 0) | (me == 3)
    mate = jnp.where(me < 2, 1 - me, 5 - me)
    return end, jnp.logical_not(end), mate, 3 - me


LINE = 4
PIECES, SLOT_PIECES = 2, 2
MIX_BEHIND, SLOT_BEHIND, DN_BEHIND = 2, 2, 2
OUT_STEPS = (0, 1, 2, 3, 4, 5, 6, 7)


def greet(wide):
    barrier = pltpu.get_barrier_semaphore()
    for axis, size in (("tp", LINE), ("wide", wide)):
        me = lax.axis_index(axis)
        for k in range(1, size):
            pl.semaphore_signal(barrier, inc=1, device_id={axis: lax.rem(me + k, size)}, device_id_type=MESH)
    pl.semaphore_wait(barrier, LINE + wide - 2)


class LineSum:
    def __init__(self, roles, rows, pieces, own, near, half, far, sends, arrivals, behind=None, last=None):
        self.end, self.mid, self.mate, self.other = roles
        self.rows, self.pieces = rows // pieces, pieces
        self.behind = pieces if behind is None else behind
        self.last = last
        self.own, self.near, self.half, self.far = own, near, half, far
        self.sends, self.arrivals = sends, arrivals

    def part(self, ref, n):
        return ref.at[pl.ds(pl.multiple_of(n * self.rows, self.rows), self.rows)]

    def copy(self, source, target, hop, n, to):
        return pltpu.make_async_remote_copy(
            self.part(source, n), self.part(target, n), self.sends.at[hop, n], self.arrivals.at[hop, n],
            device_id={"tp": to}, device_id_type=MESH)

    def up(self, n):
        return self.copy(self.own, self.near, 0, n, self.mate)

    def across(self, n):
        return self.copy(self.half, self.far, 1, n, self.other)

    def down(self, n):
        return self.copy(self.far, self.far, 2, n, self.mate)

    def add(self, a, b, c, n):
        self.part(c, n)[...] = (self.part(a, n)[...].astype(F32) + self.part(b, n)[...].astype(F32)).astype(BF16)

    def each(self, k):
        return [k * self.pieces + j for j in range(self.pieces)]

    def start(self, k):
        for n in self.each(k):
            self.up(n).start()

    def first(self, n):
        self.up(n).wait_recv()
        self.add(self.own, self.near, self.half, n)
        self.across(n).start()

    def second(self, n):
        self.across(n).wait_recv()
        self.add(self.half, self.far, self.far, n)
        self.down(n).start()

    def place(self, m):
        if self.last is None:
            return m
        return (self.last - m // self.pieces) * self.pieces + m % self.pieces

    def flow(self, k, done=None):
        for j in range(self.pieces):
            m = k * self.pieces + j
            self.first(self.place(m))

            @pl.when(m >= self.behind)
            def _():
                self.second(self.place(m - self.behind))
                if done and (j - self.behind) % self.pieces == self.pieces - 1:
                    done(self.place(m - self.behind) // self.pieces)

    def flush(self, count, done=None):
        for m in range(count * self.pieces - self.behind, count * self.pieces):
            self.second(self.place(m))
            if done and m % self.pieces == self.pieces - 1:
                done(jnp.int32(self.place(m) // self.pieces))

    def arrived(self, k):
        for n in self.each(k):
            self.down(n).wait_recv()

    def sent(self, count):
        def block(n, _):
            @pl.when(self.end)
            def _():
                self.up(n).wait_send()

            @pl.when(self.mid)
            def _():
                self.across(n).wait_send()
                self.down(n).wait_send()
            return 0

        lax.fori_loop(0, count * self.pieces, block, 0)


def pack_rows(rank, states, experts, width, ch, wide):
    rows = 8 + states + rank + (rank + 2 * states) + 8 + (width // ch) * experts
    return -(-rows // (8 * wide)) * (8 * wide)


def finish_kernel(rank, states, tokens_ref, mixed_ref, scol_ref, got_ref, dhidden_ref, dn_ref, scale_ref, gain_ref, small_ref,
                  gx_ref, gz_ref, go_ref, gup_ref, gdown_ref, gub_ref, gdb_ref,
                  result_ref, tgrad_ref, first_ref, gx_out, gz_out, cw_ref, cb_ref, state_ref, step_ref, sb_ref, rates_ref, skip_ref, go_out,
                  second_ref, router_ref, gup_out, gub_out, gdown_out, gdb_out):
    i = pl.program_id(0)
    ch = small_ref.shape[1]
    experts, width = router_ref.shape
    gup_out[0] = gup_ref[...]
    gdown_out[0] = gdown_ref[...]

    @pl.when(i == 0)
    def _():
        for ref, out in ((gx_ref, gx_out), (gz_ref, gz_out), (go_ref, go_out), (gub_ref, gub_out), (gdb_ref, gdb_out)):
            out[...] = ref[...]
        flat = lambda r: small_ref[r:r + 1, :].reshape(ch)
        cb_ref[...] = flat(0)
        sb_ref[...] = flat(1)
        skip_ref[...] = flat(2)
        cw_ref[...] = small_ref[4:8, :]
        at = 8
        rates_ref[...] = small_ref[at:at + states, :]
        at += states
        step_ref[...] = small_ref[at:at + rank, :]
        at += rank
        held = rank + 2 * states
        state_ref[...] = small_ref[at:at + held, :]
        at += held
        halves = width // ch
        for h in range(halves):
            cols = slice(h * ch, (h + 1) * ch)
            first_ref[cols] = flat(at + h)
            second_ref[cols] = flat(at + halves + h)
            router_ref[:, cols] = small_ref[at + 8 + h * experts:at + 8 + (h + 1) * experts, :]

    ids = lax.broadcasted_iota(jnp.int32, (scol_ref.shape[0], got_ref.shape[0]), 1)
    chosen = jnp.where(ids == scol_ref[...], 1.0, 0.0).astype(BF16)
    tokens = tokens_ref[...]
    result_ref[...] = tokens + mixed_ref[...].astype(F32) + jnp.dot(chosen, got_ref[...], preferred_element_type=F32)
    scale = scale_ref[...]
    unit = tokens * scale
    through = dn_ref[...].astype(F32) * as_row(gain_ref)
    mean = jnp.mean(through * unit, axis=1, keepdims=True)
    tgrad_ref[...] = dhidden_ref[...] + scale * (through - unit * mean)


def finish(rank, states, experts, *operands):
    tokens, mixed, scol, got, dhidden, dn, scale, gain, small, gx, gz, go, gup, gdown, gub, gdb = operands
    seq, width = tokens.shape
    ch = small.shape[1]
    tb = 2 * LANES
    row = lambda n: pl.BlockSpec((tb, n), lambda i: (i, 0))
    full = lambda a: pl.BlockSpec(a.shape, lambda i: (0,) * a.ndim)
    whole = lambda *s: pl.BlockSpec(s, lambda i: (0,) * len(s))
    sizes = [(width,), gx.shape, gz.shape, (4, ch), (ch,), (rank + 2 * states, ch), (rank, ch), (ch,), (states, ch), (ch,), go.shape,
             (width,), (experts, width), (1, *gup.shape), gub.shape, (1, *gdown.shape), gdb.shape]
    nb = seq // tb
    piece = lambda a: pl.BlockSpec((a.shape[0] // nb, a.shape[1]), lambda i: (i, 0))
    placed = lambda size: pl.BlockSpec((1, size[1] // nb, size[2]), lambda i: (0, i, 0)) if len(size) == 3 else whole(*size)
    return pl.pallas_call(
        functools.partial(finish_kernel, rank, states),
        grid=(seq // tb,),
        in_specs=[row(width), row(width), row(1), full(got), row(width), row(width), row(1), full(gain), full(small), full(gx), full(gz), full(go), piece(gup), piece(gdown), full(gub), full(gdb)],
        out_specs=[row(width), row(width), *[placed(size) for size in sizes]],
        out_shape=[jax.ShapeDtypeStruct(size, F32) for size in [(seq, width), (seq, width), *sizes]],
        compiler_params=pltpu.CompilerParams(vmem_limit_bytes=62 << 20),
        name="finish",
    )(*operands)


def mixer_back_kernel(ns, rank, wide, taps, proj_ref, keep_ref, step_ref, states_ref, starts_ref, tokens_ref, mixed_ref, ograd_ref, scol_ref, z_ref, scan_ref,
                      inner_ref, sproj_ref, lr_ref, skip_ref, ret_ref, gain_ref, wo_ref, term_ref,
                      x_ref, csum_ref, masks_ref, wproj_ref, cw_ref, normed_ref, gated_ref, wx_ref, wz_ref, first_gain_ref, grow_ref,
                      dhidden_ref, dn_ref, gx_ref, gz_ref, go_ref, small_ref, got_ref,
                      carry_s, stepd_s, drive_s, dscan_s, step_s, r2_s, coeff_s, exps_s, acc_s, dproj_s, wide_a, wide_b, sums_a, sums_b,
                      near_s, half_s, far_s, sends, arrivals, got_sends, got_arrivals,
                      dp_own, dp_near, dp_far, dp_sends, dp_arrivals, dn_own, dn_near, dn_far, dn_sends, dn_arrivals,
                      prod_s, inbox_s, prod_sends, prod_arrivals, pack_s, pack_in, small_s, pack_sends, pack_arrivals,
                      dinner_s, dmixed_s, dz_s, dconv_s, dx_s, gstep_s, state_s, first_s, second_s, dscan_all, gains_s):
    seq, ch = inner_ref.shape
    width = normed_ref.shape[1]
    tb = LANES
    nb = seq // tb
    groups = ch // LANES
    i = pl.program_id(0)
    me = lax.axis_index("wide")
    roles = line_roles()
    end, mid, mate, other = roles
    cap = term_ref.shape[0] // wide
    line = LineSum(roles, cap, SLOT_PIECES, term_ref, near_s, half_s, far_s, sends, arrivals)
    dp = LineSum(roles, tb, 1, dp_own, dp_near, dp_own, dp_far, dp_sends, dp_arrivals, last=nb - 1)
    dn = LineSum(roles, tb, PIECES, dn_own, dn_near, dn_own, dn_far, dn_sends, dn_arrivals, behind=DN_BEHIND, last=nb - 1)
    block = width // wide
    turned = (((1,), (1,)), ((), ()))
    across_rows = (((0,), (0,)), ((), ()))

    def slot_rows(c):
        return pl.ds(pl.multiple_of(c * cap, cap), cap)

    def rows_of(b):
        return pl.ds(pl.multiple_of(b * tb, tb), tb)

    def give_back(c):
        return pltpu.make_async_remote_copy(
            far_s.at[slot_rows(c)], got_ref.at[slot_rows(me)], got_sends.at[c], got_arrivals.at[c],
            device_id={"wide": lax.rem(me + wide - c, wide)}, device_id_type=MESH)

    def return_chunk(c):
        @pl.when(c == 0)
        def _():
            here = pltpu.make_async_copy(far_s.at[slot_rows(0)], got_ref.at[slot_rows(me)], got_sends.at[0])
            here.start()
            here.wait()

        @pl.when(c != 0)
        def _():
            give_back(c).start()

    def deliver(which, k):
        to = lax.rem(me + k, wide)
        return pltpu.make_async_remote_copy(
            prod_s.at[which, pl.ds(pl.multiple_of(to * block, block), block)], inbox_s.at[which, k],
            prod_sends.at[which, k], prod_arrivals.at[which, k], device_id={"wide": to}, device_id_type=MESH)

    def product(which, left, right):
        def tile(j, _):
            cols = pl.ds(pl.multiple_of(j * LANES, LANES), LANES)
            got = lax.dot_general(left[:, cols], right[...], across_rows, preferred_element_type=F32)
            prod_s[which, cols, :] = got.astype(BF16)
            return 0

        lax.fori_loop(0, width // LANES, tile, 0)
        for k in range(1, wide):
            deliver(which, k).start()

    @pl.when(i == 0)
    def _():
        greet(wide)
        for ref in (carry_s, acc_s, gstep_s, state_s, first_s, second_s, pack_s):
            ref[...] = jnp.zeros_like(ref)
        dconv_s[pl.ds(seq, 8), :] = jnp.zeros((8, ch), F32)
        spread(r2_s, jnp.exp(lr_ref[...]) * (-LOG2E))

    def at_out_steps(role, lag, work):
        for c, step in enumerate(OUT_STEPS):
            @pl.when(role & (i == step + lag))
            def _():
                work(jnp.int32(c))

    at_out_steps(end, 0, line.start)

    def glue(g):
        part = tokens_ref.shape[0]
        rows = pl.ds(pl.multiple_of((seq // part - 1 - g) * part, part), part)
        hidden = tokens_ref[...] + mixed_ref[...].astype(F32)
        scale = lax.rsqrt(jnp.mean(hidden * hidden, axis=1, keepdims=True) + EPS)
        unit = hidden * scale
        ids = lax.broadcasted_iota(jnp.int32, (part, wide * cap), 1)
        chosen = jnp.where(ids == scol_ref[...], 1.0, 0.0).astype(BF16)
        d_norm_two = jnp.dot(chosen, ret_ref[...], preferred_element_type=F32)
        second_s[...] += jnp.sum(d_norm_two * unit, axis=0, keepdims=True)
        through = d_norm_two * as_row(gain_ref)
        d_hidden = ograd_ref[...] + scale * (through - unit * jnp.mean(through * unit, axis=1, keepdims=True))
        dhidden_ref[...] = d_hidden
        d_mixed = d_hidden.astype(BF16)
        dmixed_s[rows, :] = d_mixed
        d_gated = jnp.dot(d_mixed, wo_ref[...], preferred_element_type=F32)
        z = z_ref[...]
        logistic = 1.0 / (1.0 + jnp.exp(-z))
        dz_s[rows, :] = (d_gated * scan_ref[...] * (logistic * (1.0 + z * (1.0 - logistic)))).astype(BF16)
        dscan_all[rows, :] = d_gated * (z * logistic)

    def scan_block():
        b = nb - 1 - i
        rows = rows_of(b)
        step = step_ref[...]
        inner = inner_ref[rows, :].astype(F32)
        dscan = dscan_all[rows, :]
        spread(stepd_s, jnp.where(keep_ref[...] > 0.0, step, 1e30))
        spread(drive_s, step * inner)
        spread(dscan_s, dscan)
        spread(step_s, step)
        pick = lambda ref: tuple(ref[:, c * LANES:(c + 1) * LANES] for c in range(groups))
        later, acc = backward_tokens(ns, rank, proj_ref, states_ref, starts_ref, stepd_s, drive_s, dscan_s, step_s, r2_s, coeff_s, exps_s,
                                     dproj_s, pick(carry_s), pick(acc_s), wide_a, wide_b, sums_a, sums_b)
        for c in range(groups):
            carry_s[:, c * LANES:(c + 1) * LANES] = later[c]
            acc_s[:, c * LANES:(c + 1) * LANES] = acc[c]
        coeff = coeff_s[...]
        d_step = coeff * inner + exps_s[...] * (1.0 / LOG2E)
        d_pre = (d_step * (1.0 - jnp.exp(-step))).astype(BF16)
        dinner_s[rows, :] = dscan * as_row(skip_ref) + step * coeff
        step_in = proj_ref[...].astype(BF16)
        gstep_s[...] += lax.dot_general(step_in, d_pre, across_rows, preferred_element_type=F32)
        pack_s[1:2, :] += jnp.sum(d_pre.astype(F32), axis=0, keepdims=True)
        pack_s[2:3, :] += jnp.sum(dscan * inner, axis=0, keepdims=True)
        both = dproj_s[...] + lax.dot_general(d_pre, tall(sproj_ref), turned, preferred_element_type=F32)
        dp_own[rows, :] = both.astype(BF16)

        @pl.when(end)
        def _():
            dp.start(b)

    def conv_block(k):
        b = nb - 1 - k
        rows = rows_of(b)
        base = pl.multiple_of(b * tb, tb)

        @pl.when(end)
        def _():
            dp.arrived(b)

        d_proj = dp_far[rows, :]
        state_s[...] += lax.dot_general(d_proj, inner_ref[rows, :], across_rows, preferred_element_type=F32)
        d_inner = dinner_s[rows, :] + jnp.dot(d_proj[:, :wproj_ref.shape[0]], wproj_ref[...], preferred_element_type=F32)
        csum = csum_ref[rows, :]
        logistic = 1.0 / (1.0 + jnp.exp(-csum))
        d_conv = d_inner * (logistic * (1.0 + csum * (1.0 - logistic)))
        prior = x_ref[pl.ds(pl.multiple_of(jnp.maximum(base - 8, 0), 8), 8), :]
        history = jnp.concatenate([prior, x_ref[rows, :]], axis=0)
        ahead = jnp.concatenate([d_conv, dconv_s[pl.ds(pl.multiple_of(base + tb, 8), 8), :]], axis=0)
        dconv_s[rows, :] = d_conv
        same = masks_ref[pl.ds(base, tb + 8), :]
        d_x = cw_ref[taps - 1:taps, :] * d_conv
        pack_s[0:1, :] += jnp.sum(d_conv, axis=0, keepdims=True)
        pack_s[8 - 1:8, :] += jnp.sum(d_conv * history[8:, :], axis=0, keepdims=True)
        for s in range(1, taps):
            linked = same[:, s:s + 1] * ahead
            d_x = d_x + cw_ref[taps - 1 - s:taps - s, :] * linked[s:s + tb, :]
            pack_s[7 - s:8 - s, :] += jnp.sum(linked[:tb, :] * history[8 - s:8 - s + tb, :], axis=0, keepdims=True)
        d_x = d_x.astype(BF16)
        dx_s[rows, :] = d_x
        both = lax.dot_general(d_x, wx_ref[...], turned, preferred_element_type=F32)
        both = both + lax.dot_general(dz_s[rows, :], wz_ref[...], turned, preferred_element_type=F32)
        dn_own[rows, :] = both.astype(BF16)

        @pl.when(end)
        def _():
            dn.start(b)

    def last_block(k):
        b = nb - 1 - k
        rows = rows_of(b)

        @pl.when(end)
        def _():
            dn.arrived(b)

        d_normed = dn_far[rows, :]
        dn_ref[...] = d_normed
        first_s[...] += jnp.sum(d_normed.astype(F32) * normed_ref[rows, :].astype(F32), axis=0, keepdims=True)

    def at_step(lag, count, work):
        @pl.when((i >= lag) & (i < lag + count))
        def _():
            work(i - lag)

    def on_mid(lag, count, work):
        @pl.when(mid & (i >= lag) & (i < lag + count))
        def _():
            work(i - lag)

    def line_down(c):
        line.arrived(c)
        return_chunk(c)

    parts = seq // tokens_ref.shape[0]
    at_step(0, parts, glue)
    at_step(parts, 1, lambda k: product(0, dmixed_s, gated_ref))
    at_step(parts + 1, 1, lambda k: product(1, normed_ref, dz_s))
    at_step(0, nb, lambda k: scan_block())
    on_mid(1, nb, dp.flow)
    on_mid(nb + 1, 1, lambda k: dp.flush(nb))
    at_step(3, nb, conv_block)
    on_mid(4, nb, dn.flow)
    on_mid(nb + 4, 1, lambda k: dn.flush(nb))
    at_out_steps(mid, 1, lambda c: line.flow(c, return_chunk))
    on_mid(OUT_STEPS[-1] + 2, 1, lambda k: line.flush(wide, return_chunk))

    at_out_steps(end, 3, line_down)
    at_step(nb + 2, 1, lambda k: product(2, normed_ref, dx_s))
    at_step(6, nb, last_block)

    share = pack_s.shape[0] // wide
    halves = width // ch
    gains_at = 8 + ns + rank + rank + 2 * ns

    def chunk(ref, n):
        return ref.at[pl.ds(pl.multiple_of(n * share, share), share)]

    def scatter(k):
        to = lax.rem(me + k, wide)
        return pltpu.make_async_remote_copy(chunk(pack_s, to), pack_in.at[k], pack_sends.at[0, k], pack_arrivals.at[0, k],
                                            device_id={"wide": to}, device_id_type=MESH)

    def spread_out(k):
        to = lax.rem(me + k, wide)
        return pltpu.make_async_remote_copy(chunk(small_s, me), chunk(small_s, me), pack_sends.at[1, k], pack_arrivals.at[1, k],
                                            device_id={"wide": to}, device_id_type=MESH)

    def gain_term(k):
        to = lax.rem(me + k, wide)
        return pltpu.make_async_remote_copy(gains_s.at[me], gains_s.at[me], pack_sends.at[2, k], pack_arrivals.at[2, k],
                                            device_id={"wide": to}, device_id_type=MESH)

    def collect(which, ref):
        total = prod_s[which, pl.ds(pl.multiple_of(me * block, block), block), :].astype(F32)
        for k in range(1, wide):
            deliver(which, k).wait_recv()
            total = total + inbox_s[which, k].astype(F32)
        ref[...] = total

    @pl.when(i == nb + 3)
    def _():
        at = 8
        pack_s[at:at + ns, :] = -jnp.exp(lr_ref[...]) * acc_s[...]
        at += ns
        pack_s[at:at + rank, :] = gstep_s[0:rank, :]
        at += rank
        held = rank + 2 * ns
        pack_s[at:at + held, :] = state_s[0:held, :]
        own_row = lax.broadcasted_iota(jnp.int32, (wide, ch), 0) == me
        for h in range(halves):
            cols = slice(h * ch, (h + 1) * ch)
            pack_s[gains_at + halves + h:gains_at + halves + h + 1, :] = second_s[:, cols]
            pack_s[gains_at + 8 + h * wide:gains_at + 8 + (h + 1) * wide, :] = jnp.where(own_row, grow_ref[:, cols], 0.0)
        for k in range(1, wide):
            scatter(k).start()
        collect(0, go_ref)

    @pl.when(i == nb + 4)
    def _():
        total = chunk(pack_s, me)[...]
        for k in range(1, wide):
            scatter(k).wait_recv()
            total = total + pack_in[k]
        chunk(small_s, me)[...] = total
        for k in range(1, wide):
            spread_out(k).start()
        collect(1, gz_ref)

    @pl.when(i == pl.num_programs(0) - 1)
    def _():
        gains_s[me] = jnp.broadcast_to(first_s[...] / as_row(first_gain_ref), (8, width))
        for k in range(1, wide):
            gain_term(k).start()
        collect(2, gx_ref)
        line.sent(wide)
        dp.sent(nb)
        dn.sent(nb)
        for k in range(1, wide):
            spread_out(k).wait_recv()
        small_ref[...] = small_s[...]
        for k in range(1, wide):
            gain_term(k).wait_recv()
        first = gains_s[0, 0:1, :]
        for n in range(1, wide):
            first = first + gains_s[n, 0:1, :]
        for h in range(halves):
            small_ref[gains_at + h:gains_at + h + 1, :] = first[:, h * ch:(h + 1) * ch]
        for k in range(1, wide):
            give_back(k).wait_recv()
            give_back(k).wait_send()
            for which in range(3):
                deliver(which, k).wait_send()
            scatter(k).wait_send()
            spread_out(k).wait_send()
            gain_term(k).wait_send()


def mixer_back(wide, taps, rank, by_rows, whole_ones):
    proj, keep, step, states, starts, tokens, mixed, ograd, scol, z, scan = by_rows
    inner, log_rates, ret = whole_ones[0], whole_ones[2], whole_ones[4]
    seq, ch = inner.shape
    width = tokens.shape[1]
    ns = log_rates.shape[0]
    tb = LANES
    nb = seq // tb
    packed = pack_rows(rank, ns, wide, width, ch, wide)
    back = lambda i: jnp.maximum(nb - 1 - i, 0)
    early = lambda i: jnp.maximum(nb // 2 - 1 - i, 0)
    final = lambda i: nb - 1 - jnp.maximum(i - 6, 0)
    row = lambda n, size=tb: pl.BlockSpec((size, n), lambda i: (back(i), 0))
    full = lambda a: pl.BlockSpec(a.shape, lambda i: (0,) * a.ndim, pipeline_mode=pl.Buffered(1))
    whole = lambda *s: pl.BlockSpec(s, lambda i: (0,) * len(s))
    shape = jax.ShapeDtypeStruct
    dma = pltpu.SemaphoreType.DMA
    vm = pltpu.VMEM
    return pl.pallas_call(
        functools.partial(mixer_back_kernel, ns, rank, wide, taps),
        grid=(nb + 6,),
        in_specs=[row(LANES), row(1), row(ch), row(ch, tb * ns), pl.BlockSpec((1, ns, ch), lambda i: (back(i), 0, 0)),
                  *[pl.BlockSpec((2 * tb, n), lambda i: (early(i), 0)) for n in (width, width, width, 1, ch, ch)], *[full(a) for a in whole_ones]],
        out_specs=[pl.BlockSpec((2 * tb, width), lambda i: (early(i), 0)), pl.BlockSpec((tb, width), lambda i: (final(i), 0)), *[whole(width // wide, ch)] * 3, whole(packed, ch),
                   pl.BlockSpec(memory_space=pl.ANY)],
        out_shape=[shape((seq, width), F32), shape((seq, width), BF16), *[shape((width // wide, ch), F32)] * 3, shape((packed, ch), F32),
                   shape(ret.shape, BF16)],
        scratch_shapes=[
            vm((ns, ch), F32), *[vm((ch // LANES, tb, LANES), F32)] * 4, vm((ch // LANES, ns, LANES), F32), vm((tb, ch), F32), vm((tb, ch), F32),
            vm((ns, ch), F32), vm((tb, LANES), F32), *[vm((8 * ns, 2 * LANES), F32)] * 2, *[vm((8 * ns, 2 * LANES), BF16)] * 2,
            *[vm(ret.shape, BF16)] * 3, *[dma((3, wide * SLOT_PIECES))] * 2, dma((wide,)), dma((wide,)),
            *[vm((seq, LANES), BF16)] * 3, dma((3, nb)), dma((3, nb)), *[vm((seq, width), BF16)] * 3, *[dma((3, nb * PIECES))] * 2,
            vm((3, width, ch), BF16), vm((3, wide, width // wide, ch), BF16), dma((3, wide)), dma((3, wide)),
            vm((packed, ch), F32), vm((wide, packed // wide, ch), F32), vm((packed, ch), F32), dma((3, wide)), dma((3, wide)),
            vm((seq, ch), F32), vm((seq, width), BF16), vm((seq, ch), BF16), vm((seq + 8, ch), F32), vm((seq, ch), BF16),
            vm((LANES, ch), F32), vm((LANES, ch), F32), vm((1, width), F32), vm((1, width), F32),
            vm((seq, ch), F32), vm((wide, 8, width), F32)],
        compiler_params=pltpu.CompilerParams(collective_id=1, has_side_effects=True, vmem_limit_bytes=62 << 20),
        name="mixer_back",
    )(*by_rows, *whole_ones)


def gelu_pair(v):
    root = 0.7978845608028654
    square = v * v
    t = jnp.tanh(root * v * (1.0 + 0.044715 * square))
    half = 0.5 * (1.0 + t)
    slope = half + (0.5 * root) * v * (1.0 - t * t) * (1.0 + (3.0 * 0.044715) * square)
    return v * half, slope


def scan_mix_kernel(ns, rank, wide, proj_ref, inner_ref, keep_ref, sproj_ref, sbias_ref, lr_ref, skip_ref, z_ref, wo_ref, ograd_ref, srow_ref,
                    scan_ref, step_ref, states_ref, starts_ref, gated_ref, mixed_ref, gin_ref,
                    state_s, stepd_s, drive_s, r2_s, wide_a, wide_b, own_s, near_s, far_s, sends, arrivals, grad_s, send_s, g_sends, g_arrivals):
    tb, ch = inner_ref.shape
    groups = ch // LANES
    i = pl.program_id(0)
    roles = line_roles()
    end, mid, mate, other = roles
    line = LineSum(roles, tb, PIECES, own_s, near_s, own_s, far_s, sends, arrivals, behind=MIX_BEHIND)
    steps = pl.num_programs(0)
    seq_blocks = own_s.shape[0] // tb

    me = lax.axis_index("wide")
    cap = send_s.shape[0] // wide

    def slot_rows(k):
        return pl.ds(pl.multiple_of(k * cap, cap), cap)

    def dispatch(k):
        return pltpu.make_async_remote_copy(
            send_s.at[slot_rows(k)], gin_ref.at[slot_rows(k)], g_sends.at[k], g_arrivals.at[k],
            device_id={"wide": lax.rem(me + k, wide)}, device_id_type=MESH)

    own_rows = pltpu.make_async_copy(send_s.at[slot_rows(0)], gin_ref.at[slot_rows(0)], g_sends.at[0])

    @pl.when(i == 0)
    def _():
        greet(wide)
        state_s[...] = jnp.zeros_like(state_s)
        spread(r2_s, jnp.exp(lr_ref[...]) * (-LOG2E))

    step_in = proj_ref[...].astype(BF16)
    pre = jnp.dot(step_in, tall(sproj_ref), preferred_element_type=F32) + as_row(sbias_ref)
    step = softplus(pre)
    step_ref[...] = step
    spread(stepd_s, jnp.where(keep_ref[...] > 0.0, step, 1e30))
    inner = inner_ref[...].astype(F32)
    spread(drive_s, step * inner)
    starts_ref[0] = state_s[...]
    start = tuple(state_s[:, c * LANES:(c + 1) * LANES] for c in range(groups))
    state = forward_tokens(ns, rank, proj_ref, stepd_s, drive_s, r2_s, states_ref, scan_ref, start, wide_a, wide_b)
    for c in range(groups):
        state_s[:, c * LANES:(c + 1) * LANES] = state[c]
    scan = scan_ref[...] + as_row(skip_ref) * inner
    scan_ref[...] = scan
    z = z_ref[...]
    gated = (scan * (z / (1.0 + jnp.exp(-z)))).astype(BF16)
    gated_ref[...] = gated
    here = pl.ds(pl.multiple_of(i * tb, tb), tb)
    own_s[here, :] = lax.dot_general(gated, wo_ref[...], (((1,), (1,)), ((), ())), preferred_element_type=F32).astype(BF16)

    @pl.when(end)
    def _():
        line.start(i)

    @pl.when(i < wide)
    def _():
        @pl.when(i == 0)
        def _():
            grad_s[...] = ograd_ref[...].astype(BF16)

        ids = lax.broadcasted_iota(jnp.int32, (cap, grad_s.shape[0]), 0) + lax.rem(me + i, wide) * cap
        chosen = jnp.where(ids == srow_ref[...], 1.0, 0.0).astype(BF16)
        send_s[slot_rows(i), :] = jnp.dot(chosen, grad_s[...], preferred_element_type=F32).astype(BF16)

        @pl.when(i == 0)
        def _():
            own_rows.start()

        @pl.when(i > 0)
        def _():
            dispatch(i).start()

    @pl.when(mid & (i > 0))
    def _():
        line.flow(i - 1)

    @pl.when(i == steps - 1)
    def _():
        @pl.when(mid)
        def _():
            line.flow(i)
            line.flush(seq_blocks)

        @pl.when(end)
        def _():
            for k in range(steps):
                line.arrived(k)

        mixed_ref[...] = far_s[...]
        line.sent(steps)
        own_rows.wait()
        for k in range(1, wide):
            dispatch(k).wait_recv()
            dispatch(k).wait_send()


def scan_mix(proj, inner, keep, sproj, sbias, log_rates, skip, z, wo, ograd, srow, rank, wide, cap):
    seq, ch = inner.shape
    ns = log_rates.shape[0]
    tb = LANES
    nb = seq // tb
    width = wo.shape[0]
    full = lambda a: pl.BlockSpec(a.shape, lambda i: (0,) * a.ndim)
    rows = pl.BlockSpec((tb, ch), lambda i: (i, 0))
    return pl.pallas_call(
        functools.partial(scan_mix_kernel, ns, rank, wide),
        grid=(nb,),
        in_specs=[pl.BlockSpec((tb, LANES), lambda i: (i, 0)), rows, pl.BlockSpec((tb, 1), lambda i: (i, 0)),
                  full(sproj), full(sbias), full(log_rates), full(skip), rows, full(wo), full(ograd), full(srow)],
        out_specs=[rows, rows, pl.BlockSpec((tb * ns, ch), lambda i: (i, 0)), pl.BlockSpec((1, ns, ch), lambda i: (i, 0, 0)),
                   rows, pl.BlockSpec((seq, width), lambda i: (0, 0)), pl.BlockSpec(memory_space=pl.ANY)],
        out_shape=[jax.ShapeDtypeStruct((seq, ch), F32), jax.ShapeDtypeStruct((seq, ch), F32),
                   jax.ShapeDtypeStruct((seq * ns, ch), BF16), jax.ShapeDtypeStruct((nb, ns, ch), F32),
                   jax.ShapeDtypeStruct((seq, ch), BF16), jax.ShapeDtypeStruct((seq, width), BF16),
                   jax.ShapeDtypeStruct((wide * cap, width), BF16)],
        scratch_shapes=[pltpu.VMEM((ns, ch), F32)] + [pltpu.VMEM((ch // LANES, tb, LANES), F32)] * 2 + [pltpu.VMEM((ch // LANES, ns, LANES), F32),
                        *[pltpu.VMEM((8 * ns, 2 * LANES), F32)] * 2,
                        *[pltpu.VMEM((seq, width), BF16)] * 3, *[pltpu.SemaphoreType.DMA((3, nb * PIECES))] * 2,
                        pltpu.VMEM((seq, width), BF16), pltpu.VMEM((wide * cap, width), BF16),
                        pltpu.SemaphoreType.DMA((wide,)), pltpu.SemaphoreType.DMA((wide,))],
        compiler_params=pltpu.CompilerParams(collective_id=4, has_side_effects=True, vmem_limit_bytes=62 << 20),
        name="scan_mix",
    )(proj, inner, keep, sproj, sbias, log_rates, skip, z, wo, ograd, srow)


def experts_kernel(wide, tokens_ref, mixed_ref, gin_ref, srow_ref, gain_ref, router_ref, up_ref, ub_ref, down_ref, db_ref,
                   gup_out, gub_ref, gdown_out, gdb_ref, ret_ref, terms_out, grow_ref,
                   pay_s, send_s, inbox_s, rgrad_s, act_s, dpre_s, own_s, near_s, far_s, acc_s, column_s, rows_s,
                   pay_sends, pay_arrivals, sends, arrivals, ret_sends, ret_arrivals, r_sends, r_arrivals, gup_ref, gdown_ref, out_ref, leaving):
    seq, width = tokens_ref.shape
    hid = up_ref.shape[1]
    cap = inbox_s.shape[0] // wide
    tb = LANES
    me, rank = lax.axis_index("wide"), lax.axis_index("tp")
    roles = line_roles()
    end, mid, mate, other = roles
    greet(wide)
    back = LineSum(roles, cap, SLOT_PIECES, own_s, near_s, own_s, far_s, sends, arrivals, behind=SLOT_BEHIND)

    def rows_of(b, size):
        return pl.ds(pl.multiple_of(b * size, size), size)

    def prepare(b, _):
        rows = rows_of(b, tb)
        hidden = tokens_ref[rows, :] + mixed_ref[rows, :].astype(F32)
        scale = lax.rsqrt(jnp.mean(hidden * hidden, axis=1, keepdims=True) + EPS)
        pay_s[rows, :] = (hidden * scale * as_row(gain_ref)).astype(BF16)
        return 0

    lax.fori_loop(0, seq // tb, prepare, 0)

    def payload(expert):
        ids = lax.broadcasted_iota(jnp.int32, (cap, seq), 0) + expert * cap
        chosen = jnp.where(ids == srow_ref[...], 1.0, 0.0).astype(BF16)
        return jnp.dot(chosen, pay_s[...], preferred_element_type=F32).astype(BF16)

    def dispatch(k):
        return pltpu.make_async_remote_copy(
            send_s.at[rows_of(k, cap)], inbox_s.at[rows_of(k, cap)], pay_sends.at[k], pay_arrivals.at[k],
            device_id={"wide": lax.rem(me + k, wide)}, device_id_type=MESH)

    def send(k):
        send_s[rows_of(k, cap), :] = payload(lax.rem(me + k, wide))
        dispatch(k).start()

    ahead = 2

    def send_first(k, _):
        send(k)
        return 0

    lax.fori_loop(1, ahead + 1, send_first, 0)
    inbox_s[0:cap, :] = payload(me)

    def give_back(c):
        return pltpu.make_async_remote_copy(
            far_s.at[rows_of(c, cap)], ret_ref.at[rows_of(me, cap)], ret_sends.at[c], ret_arrivals.at[c],
            device_id={"wide": lax.rem(me + wide - c, wide)}, device_id_type=MESH)

    def return_chunk(c):
        @pl.when(c == 0)
        def _():
            ret_ref[rows_of(me, cap), :] = far_s[0:cap, :]

        @pl.when(c != 0)
        def _():
            give_back(c).start()

    gub_ref[...] = jnp.zeros_like(gub_ref)
    gdb_ref[...] = jnp.zeros_like(gdb_ref)
    acc_s[...] = jnp.zeros_like(acc_s)
    turned = (((1,), (1,)), ((), ()))
    mine = lax.broadcasted_iota(jnp.int32, router_ref.shape, 0) == me
    column_s[...] = jnp.sum(jnp.where(mine, router_ref[...].astype(F32), 0.0), axis=0, keepdims=True)
    lane = lax.broadcasted_iota(jnp.int32, (cap, wide), 1)

    def compute(k, _):
        @pl.when(k + ahead < wide - 1)
        def _():
            send(k + ahead + 1)

        @pl.when(k > 0)
        def _():
            dispatch(k).wait_recv()

        part = rows_of(k, cap)
        rows_in = inbox_s[part, :]
        rows_raw = gin_ref[part, :].astype(F32)
        logits = lax.dot_general(rows_in, router_ref[...], turned, preferred_element_type=F32)
        logit = jnp.sum(jnp.where(lane == me, logits, 0.0), axis=1, keepdims=True)
        gate = 1.0 / (1.0 + jnp.exp(-logit))
        rows_grad = (gate * rows_raw).astype(BF16)
        rgrad_s[part, :] = rows_grad
        pre = jnp.dot(rows_in, up_ref[...], preferred_element_type=F32) + ub_ref[...]
        act, slope = gelu_pair(pre)
        act = act.astype(BF16)
        act_s[part, :] = act
        d_pre = (lax.dot_general(rows_grad, down_ref[...], turned, preferred_element_type=F32) * slope).astype(BF16)
        dpre_s[part, :] = d_pre
        out = jnp.dot(act, down_ref[...], preferred_element_type=F32) + db_ref[...] * (1.0 / LINE)
        d_logit = jnp.sum(rows_raw * out, axis=1, keepdims=True) * (gate * (1.0 - gate))
        own_s[part, :] = (lax.dot_general(d_pre, up_ref[...], turned, preferred_element_type=F32) + d_logit * column_s[...]).astype(BF16)

        @pl.when(end)
        def _():
            back.start(k)

        out_ref[part, :] = (gate * out).astype(BF16)
        acc_s[...] += jnp.sum(d_logit * rows_in.astype(F32), axis=0, keepdims=True)
        gub_ref[...] += jnp.sum(d_pre.astype(F32), axis=0, keepdims=True)
        gdb_ref[...] += jnp.sum(rows_grad.astype(F32), axis=0, keepdims=True)

        @pl.when(mid & (k > 0))
        def _():
            back.flow(k - 1, return_chunk)
        return 0

    lax.fori_loop(0, wide, compute, 0)
    moves = [pltpu.make_async_copy(a, b, leaving.at[n])
             for n, (a, b) in enumerate(((out_ref, terms_out), (gdown_ref, gdown_out), (gup_ref, gup_out)))]
    moves[0].start()

    def term(k):
        return pltpu.make_async_remote_copy(rows_s.at[rank], rows_s.at[rank], r_sends.at[k], r_arrivals.at[k],
                                            device_id={"tp": lax.rem(rank + k, LINE)}, device_id_type=MESH)

    rows_s[rank] = jnp.broadcast_to(acc_s[...], (8, width))
    for k in range(1, LINE):
        term(k).start()

    @pl.when(mid)
    def _():
        back.flow(jnp.int32(wide - 1), return_chunk)

    tiles = hid // LANES
    across_rows = (((0,), (0,)), ((), ()))

    def tile(j, _):
        @pl.when(j < tiles)
        def _():
            cols = rows_of(j, LANES)
            gdown_ref[cols, :] = lax.dot_general(act_s[:, cols], rgrad_s[...], across_rows, preferred_element_type=F32)

        @pl.when(j >= tiles)
        def _():
            cols = rows_of(j - tiles, LANES)
            gup_ref[cols, :] = lax.dot_general(inbox_s[:, cols], dpre_s[...], across_rows, preferred_element_type=F32)

        @pl.when(end & (j < wide))
        def _():
            back.arrived(j)
            return_chunk(j)

        @pl.when(mid & (j == 1))
        def _():
            back.flush(wide, return_chunk)
        return 0

    lax.fori_loop(0, 2 * tiles, tile, 0)
    moves[1].start()
    moves[2].start()
    for k in range(1, LINE):
        term(k).wait_recv()
    grow_ref[...] = ((rows_s[0] + rows_s[1]) + rows_s[2]) + rows_s[3]
    for c in range(1, wide):
        give_back(c).wait_recv()
    back.sent(wide)
    for k in range(1, wide):
        dispatch(k).wait_send()
        give_back(k).wait_send()
    for k in range(1, LINE):
        term(k).wait_send()
    for move in moves:
        move.wait()


def experts_block(wide, cap, *operands):
    tokens, mixed, gin, srow, gain, router, up, ub, down, db = operands
    seq, width = tokens.shape
    hid = up.shape[1]
    vm = pl.BlockSpec(memory_space=pltpu.VMEM)
    hbm = pl.BlockSpec(memory_space=pl.ANY)
    shape = jax.ShapeDtypeStruct
    dma = pltpu.SemaphoreType.DMA
    slots = wide * cap
    return pl.pallas_call(
        functools.partial(experts_kernel, wide),
        in_specs=[vm] * len(operands),
        out_specs=[hbm, vm, hbm, vm, vm, hbm, vm],
        out_shape=[shape((width, hid), F32), shape((1, hid), F32), shape((hid, width), F32), shape((1, width), F32),
                   shape((slots, width), BF16), shape((slots, width), BF16), shape((8, width), F32)],
        scratch_shapes=[
            pltpu.VMEM((seq, width), BF16), *[pltpu.VMEM((slots, width), BF16)] * 3,
            pltpu.VMEM((slots, hid), BF16), pltpu.VMEM((slots, hid), BF16),
            *[pltpu.VMEM((slots, width), BF16)] * 3, pltpu.VMEM((1, width), F32), pltpu.VMEM((1, width), F32), pltpu.VMEM((LINE, 8, width), F32),
            dma((wide,)), dma((wide,)), *[dma((3, wide * SLOT_PIECES))] * 2, dma((wide,)), dma((wide,)), dma((LINE,)), dma((LINE,)),
            pltpu.VMEM((width, hid), F32), pltpu.VMEM((hid, width), F32), pltpu.VMEM((slots, width), BF16), dma((3,))],
        compiler_params=pltpu.CompilerParams(collective_id=2, has_side_effects=True, vmem_limit_bytes=62 << 20),
        name="experts",
    )(*operands)


def front_kernel(wide, taps, tokens_ref, gain_ref, inx_ref, inz_ref, outp_ref, cw_ref, cb_ref, wproj_ref, masks_ref,
                 scale_ref, normed_out, x_out, z_out, csum_out, inner_out, proj_ref, wx_out, wz_out, wo_out,
                 own_s, near_s, far_s, w_sends, w_arrivals, sends, arrivals,
                 normed_ref, x_ref, z_ref, csum_ref, inner_ref, wx_ref, wz_ref, wo_ref, leaving):
    seq, width = tokens_ref.shape
    ch = x_ref.shape[1]
    block = inx_ref.shape[0]
    tb = LANES
    nb = seq // tb
    me = lax.axis_index("wide")
    roles = line_roles()
    end, mid, mate, other = roles
    greet(wide)
    line = LineSum(roles, 2 * tb, 1, own_s, near_s, own_s, far_s, sends, arrivals)
    pairs = ((normed_ref, normed_out), (wx_ref, wx_out), (x_ref, x_out), (csum_ref, csum_out), (inner_ref, inner_out),
             (z_ref, z_out), (wz_ref, wz_out), (wo_ref, wo_out))
    moves = [pltpu.make_async_copy(a, b, leaving.at[n]) for n, (a, b) in enumerate(pairs)]
    mine = pl.ds(pl.multiple_of(me * block, block), block)
    weights = ((inx_ref, wx_ref), (inz_ref, wz_ref), (outp_ref, wo_ref))

    def share(which, k):
        source, target = weights[which]
        return pltpu.make_async_remote_copy(source, target.at[mine], w_sends.at[which, k], w_arrivals.at[which, k],
                                            device_id={"wide": lax.rem(me + k, wide)}, device_id_type=MESH)

    for which in range(3):
        for k in range(1, wide):
            share(which, k).start()
    for source, target in weights:
        target[mine, :] = source[...]

    def rows_of(b):
        return pl.ds(pl.multiple_of(b * tb, tb), tb)

    def norm(b, _):
        rows = rows_of(b)
        tokens = tokens_ref[rows, :]
        scale = lax.rsqrt(jnp.mean(tokens * tokens, axis=1, keepdims=True) + EPS)
        scale_ref[rows, :] = scale
        normed_ref[rows, :] = (tokens * scale * as_row(gain_ref)).astype(BF16)
        return 0

    own_s[...] = jnp.zeros_like(own_s)
    lax.fori_loop(0, nb, norm, 0)
    moves[0].start()
    for k in range(1, wide):
        share(0, k).wait_recv()
    moves[1].start()

    def step(b, _):
        rows = rows_of(b)
        base = pl.multiple_of(b * tb, tb)
        x = jnp.dot(normed_ref[rows, :], wx_ref[...], preferred_element_type=F32)
        x_ref[rows, :] = x
        prior = x_ref[pl.ds(pl.multiple_of(jnp.maximum(base - 8, 0), 8), 8), :]
        history = jnp.concatenate([prior, x], axis=0)
        same = masks_ref[rows, :]
        csum = as_row(cb_ref) + cw_ref[taps - 1:taps, :] * x
        for s in range(1, taps):
            csum = csum + cw_ref[taps - 1 - s:taps - s, :] * (same[:, s:s + 1] * history[8 - s:8 - s + tb, :])
        csum_ref[rows, :] = csum
        inner = (csum / (1.0 + jnp.exp(-csum))).astype(BF16)
        inner_ref[rows, :] = inner
        own_s[rows, :wproj_ref.shape[0]] = lax.dot_general(
            inner, wproj_ref[...], (((1,), (1,)), ((), ())), preferred_element_type=F32).astype(BF16)

        @pl.when(end & (lax.rem(b, 2) == 1))
        def _():
            line.start(b // 2)

        @pl.when(mid & (lax.rem(b, 2) == 1) & (b > 2))
        def _():
            line.flow(b // 2 - 1)
        return 0

    lax.fori_loop(0, nb, step, 0)
    steps = nb // 2
    for move in moves[2:5]:
        move.start()
    for k in range(1, wide):
        share(1, k).wait_recv()
    moves[6].start()

    def gate(b, _):
        rows = rows_of(b)
        z_ref[rows, :] = jnp.dot(normed_ref[rows, :], wz_ref[...], preferred_element_type=F32)
        return 0

    lax.fori_loop(0, steps, gate, 0)

    @pl.when(mid)
    def _():
        line.flow(jnp.int32(steps - 1))

    lax.fori_loop(steps, nb, gate, 0)
    moves[5].start()

    @pl.when(mid)
    def _():
        line.flush(steps)

    @pl.when(end)
    def _():
        for k in range(steps):
            line.arrived(k)

    proj_ref[...] = far_s[...].astype(F32)
    line.sent(steps)
    for k in range(1, wide):
        share(2, k).wait_recv()
    moves[7].start()
    for k in range(1, wide):
        for which in range(3):
            share(which, k).wait_send()
    for move in moves:
        move.wait()


def front(wide, taps, *operands):
    tokens, gain, inx, inz, outp, cw, cb, wproj, masks = operands
    seq, width = tokens.shape
    ch = inx.shape[1]
    vm = pl.BlockSpec(memory_space=pltpu.VMEM)
    hbm = pl.BlockSpec(memory_space=pl.ANY)
    shape = jax.ShapeDtypeStruct
    dma = pltpu.SemaphoreType.DMA
    return pl.pallas_call(
        functools.partial(front_kernel, wide, taps),
        in_specs=[vm] * len(operands),
        out_specs=[vm, *[hbm] * 5, vm, *[hbm] * 3],
        out_shape=[shape((seq, 1), F32), shape((seq, width), BF16), shape((seq, ch), F32), shape((seq, ch), F32), shape((seq, ch), F32),
                   shape((seq, ch), BF16), shape((seq, LANES), F32), *[shape((width, ch), BF16)] * 3],
        scratch_shapes=[*[pltpu.VMEM((seq, LANES), BF16)] * 3, dma((3, wide)), dma((3, wide)), dma((3, seq // LANES // 2)), dma((3, seq // LANES // 2)),
                        pltpu.VMEM((seq, width), BF16), *[pltpu.VMEM((seq, ch), F32)] * 3, pltpu.VMEM((seq, ch), BF16),
                        *[pltpu.VMEM((width, ch), BF16)] * 3, dma((8,))],
        compiler_params=pltpu.CompilerParams(collective_id=3, has_side_effects=True, vmem_limit_bytes=62 << 20),
        name="mixer_front",
    )(*operands)


def plain_device(
    tokens,
    segment_ids,
    routes,
    out_grad,
    mixer_gain,
    in_proj_x,
    in_proj_z,
    conv_weight,
    conv_bias,
    state_proj,
    step_proj,
    step_bias,
    log_rates,
    skip_gain,
    out_proj,
    expert_gain,
    router_weight,
    expert_up,
    up_bias,
    expert_down,
    down_bias,
):
    seq_len, model_width = tokens.shape
    conv_taps = conv_weight.shape[0]
    step_rank = step_proj.shape[0]
    experts = router_weight.shape[1]
    capacity = 5 * seq_len // (4 * experts)
    doc_ids = segment_ids[0]
    conv_masks = [same_document(doc_ids, offset)[:, None] for offset in range(conv_taps)]
    first_scale = lax.rsqrt(jnp.mean(tokens * tokens, axis=1, keepdims=True) + EPS)
    first_unit = tokens * first_scale
    normed = (first_unit * mixer_gain).astype(jnp.bfloat16)
    gathered_x, gathered_z, gathered_out = (
        lax.all_gather(in_proj_x, "wide", axis=0, tiled=True),
        lax.all_gather(in_proj_z, "wide", axis=0, tiled=True),
        lax.all_gather(out_proj, "wide", axis=0, tiled=True),
    )
    x_branch = multiply(normed, gathered_x)
    z_branch = multiply(normed, gathered_z)
    conv_sum = conv_bias + jnp.zeros_like(x_branch)
    for offset in range(conv_taps):
        conv_sum = conv_sum + conv_weight[conv_taps - 1 - offset] * conv_masks[
            offset
        ] * shifted_down(x_branch, offset)
    inner_act = jax.nn.silu(conv_sum).astype(jnp.bfloat16)
    wide_proj = jnp.pad(state_proj, ((0, 0), (0, LANES - state_proj.shape[1])))
    projected = lax.psum(multiply(inner_act, wide_proj), "tp")
    tall_proj = jnp.pad(step_proj, ((0, LANES - step_rank), (0, 0)))
    carry_mask = same_document(doc_ids, 1)[:, None]
    scan_out, step_size, states, starts = scan_fwd(
        projected, inner_act, carry_mask, tall_proj, step_bias[None], log_rates, skip_gain[None], step_rank
    )
    z_gate = jax.nn.silu(z_branch)
    gated = (scan_out * z_gate).astype(jnp.bfloat16)
    mixed = lax.psum(contract_cols(gated, gathered_out).astype(jnp.bfloat16), "tp").astype(
        jnp.float32
    )
    hidden = tokens + mixed
    second_scale = lax.rsqrt(jnp.mean(hidden * hidden, axis=1, keepdims=True) + EPS)
    second_unit = hidden * second_scale
    expert_in = (second_unit * expert_gain).astype(jnp.bfloat16)
    route_ids = routes[:, 0]
    chosen_int = (routes == jnp.arange(experts, dtype=jnp.int32)[None, :]).astype(jnp.int32)
    chosen = chosen_int.astype(jnp.float32)
    logits = multiply(expert_in, router_weight)
    gate = jax.nn.sigmoid(jnp.sum(logits * chosen, axis=1))
    rank_of = jnp.arange(seq_len, dtype=jnp.int32)
    earlier = (rank_of[:, None] > rank_of[None, :]).astype(jnp.bfloat16)
    position = jnp.sum(multiply(earlier, chosen.astype(jnp.bfloat16)) * chosen, axis=1).astype(jnp.int32)
    kept = position < capacity
    slots = jnp.where(kept, route_ids * capacity + position, experts * capacity)
    scaled_grad = (gate[:, None] * out_grad).astype(jnp.bfloat16)
    sent_width = expert_in.shape[1]
    send_in = (
        jnp.zeros((experts * capacity + 1, sent_width), jnp.bfloat16).at[slots].set(expert_in)[:-1]
    )
    send_grad = (
        jnp.zeros((experts * capacity + 1, sent_width), jnp.bfloat16)
        .at[slots]
        .set(scaled_grad)[:-1]
    )
    recv_in, recv_grad = (
        lax.all_to_all(
            send_in.reshape(experts, capacity, sent_width),
            "wide",
            split_axis=0,
            concat_axis=0,
            tiled=True,
        ),
        lax.all_to_all(
            send_grad.reshape(experts, capacity, sent_width),
            "wide",
            split_axis=0,
            concat_axis=0,
            tiled=True,
        ),
    )
    rows_in = recv_in.reshape(-1, model_width)
    rows_grad = recv_grad.reshape(-1, model_width)
    pre_act = multiply(rows_in, expert_up[0]) + up_bias[0]
    hidden_act = jax.nn.gelu(pre_act).astype(jnp.bfloat16)
    partial_out = multiply(hidden_act, expert_down[0])
    up_grad = contract_cols(rows_grad, expert_down[0])
    d_pre = jax.vjp(jax.nn.gelu, pre_act)[1](up_grad)[0].astype(jnp.bfloat16)
    partial_back = contract_cols(d_pre, expert_up[0])
    grad_down = contract_rows(hidden_act, rows_grad)
    grad_dbias = jnp.sum(rows_grad.astype(jnp.float32), axis=0)
    grad_up = contract_rows(rows_in, d_pre)
    grad_ubias = jnp.sum(d_pre.astype(jnp.float32), axis=0)
    out_sum, back_sum = (
        lax.psum(partial_out.astype(jnp.bfloat16), "tp").astype(jnp.float32),
        lax.psum(partial_back.astype(jnp.bfloat16), "tp").astype(jnp.float32),
    )
    bias_part = down_bias[0]
    outgoing = (out_sum + bias_part).astype(jnp.bfloat16).reshape(experts, capacity, -1)
    back_rows = back_sum.astype(jnp.bfloat16).reshape(experts, capacity, -1)
    incoming, arriving = (
        lax.all_to_all(outgoing, "wide", split_axis=0, concat_axis=0, tiled=True),
        lax.all_to_all(back_rows, "wide", split_axis=0, concat_axis=0, tiled=True),
    )
    safe_slots = jnp.minimum(slots, experts * capacity - 1)
    returned = jnp.where(
        kept[:, None], incoming.reshape(-1, model_width)[safe_slots].astype(jnp.float32), 0.0
    )
    result = hidden + gate[:, None] * returned
    d_gate = jnp.sum(out_grad * returned, axis=1)
    d_logit = (d_gate * gate * (1.0 - gate))[:, None] * chosen
    grad_router = jnp.dot(expert_in.astype(jnp.float32).T, d_logit, precision=HIGH)
    d_norm_two = jnp.dot(d_logit, router_weight.astype(jnp.float32).T, precision=HIGH)
    d_norm_two = d_norm_two + jnp.where(
        kept[:, None], arriving.reshape(-1, model_width)[safe_slots].astype(jnp.float32), 0.0
    )
    grad_second_gain = jnp.sum(d_norm_two * second_unit, axis=0)
    d_hidden = out_grad + rms_back(d_norm_two * expert_gain, second_unit, second_scale)
    d_mixed = d_hidden.astype(jnp.bfloat16)
    d_gated = multiply(d_mixed, gathered_out)
    grad_out = contract_rows(d_mixed, gated)
    d_scan = d_gated * z_gate
    d_z = (d_gated * scan_out * silu_slope(z_branch)).astype(jnp.bfloat16)
    d_step_pre, d_inner, d_proj, grad_step, grad_sbias, grad_rates, grad_skip = scan_bwd(
        projected, inner_act, carry_mask, step_size, states, starts, d_scan, tall_proj, log_rates, skip_gain[None], step_rank
    )
    grad_step, grad_sbias, grad_skip = grad_step[:step_rank], grad_sbias[0], grad_skip[0]
    d_projected = lax.psum(d_proj.astype(jnp.bfloat16), "tp")
    grad_state = contract_rows(inner_act, d_projected)[:, : state_proj.shape[1]]
    d_inner = d_inner + contract_cols(d_projected, wide_proj)
    d_conv = d_inner * silu_slope(conv_sum)
    grad_cbias = jnp.sum(d_conv, axis=0)
    conv_rows = []
    d_input = jnp.zeros_like(d_conv)
    for offset in range(conv_taps):
        conv_rows.append(
            jnp.sum(d_conv * conv_masks[offset] * shifted_down(x_branch, offset), axis=0)
        )
        d_input = d_input + conv_weight[conv_taps - 1 - offset] * shifted_up(
            conv_masks[offset] * d_conv, offset
        )
    grad_conv = jnp.stack(conv_rows[::-1])
    d_x_branch = d_input.astype(jnp.bfloat16)
    grad_in_x = contract_rows(normed, d_x_branch)
    grad_in_z = contract_rows(normed, d_z)
    d_normed = lax.psum(
        (contract_cols(d_x_branch, gathered_x) + contract_cols(d_z, gathered_z)).astype(
            jnp.bfloat16
        ),
        "tp",
    ).astype(jnp.float32)
    grad_first_gain = jnp.sum(d_normed * first_unit, axis=0)
    tokens_grad = d_hidden + rms_back(d_normed * mixer_gain, first_unit, first_scale)
    grad_in_x, grad_in_z, grad_out = (
        summed_on_arrival(grad_in_x.astype(jnp.bfloat16), "wide", 0),
        summed_on_arrival(grad_in_z.astype(jnp.bfloat16), "wide", 0),
        summed_on_arrival(grad_out.astype(jnp.bfloat16), "wide", 0),
    )
    (
        grad_first_gain,
        grad_conv,
        grad_cbias,
        grad_state,
        grad_step,
        grad_sbias,
        grad_rates,
        grad_skip,
        grad_second_gain,
        grad_router,
    ) = lax.psum(
        (
            grad_first_gain,
            grad_conv,
            grad_cbias,
            grad_state,
            grad_step,
            grad_sbias,
            grad_rates,
            grad_skip,
            grad_second_gain,
            grad_router,
        ),
        "wide",
    )
    return (
        result,
        tokens_grad,
        grad_first_gain,
        grad_in_x,
        grad_in_z,
        grad_conv,
        grad_cbias,
        grad_state,
        grad_step,
        grad_sbias,
        grad_rates,
        grad_skip,
        grad_out,
        grad_second_gain,
        grad_router,
        grad_up[None],
        grad_ubias[None],
        grad_down[None],
        grad_dbias[None],
    )


def fast_device(
    tokens,
    segment_ids,
    routes,
    out_grad,
    mixer_gain,
    in_proj_x,
    in_proj_z,
    conv_weight,
    conv_bias,
    state_proj,
    step_proj,
    step_bias,
    log_rates,
    skip_gain,
    out_proj,
    expert_gain,
    router_weight,
    expert_up,
    up_bias,
    expert_down,
    down_bias,
):
    seq_len, model_width = tokens.shape
    conv_taps = conv_weight.shape[0]
    step_rank = step_proj.shape[0]
    experts = router_weight.shape[1]
    capacity = 5 * seq_len // (4 * experts)
    doc_ids = segment_ids[0]
    conv_masks = [same_document(doc_ids, offset)[:, None] for offset in range(conv_taps)]
    masks = jnp.pad(jnp.concatenate(conv_masks, axis=1), ((0, 8), (0, 8 - conv_taps)))
    wide = lax.axis_size("wide")
    states = log_rates.shape[0]
    chosen = (routes == jnp.arange(experts, dtype=jnp.int32)[None, :]).astype(jnp.float32)
    rank_of = jnp.arange(seq_len, dtype=jnp.int32)
    earlier = (rank_of[:, None] > rank_of[None, :]).astype(jnp.bfloat16)
    position = jnp.sum(multiply(earlier, chosen.astype(jnp.bfloat16)) * chosen, axis=1).astype(jnp.int32)
    slots = jnp.where(position < capacity, routes[:, 0] * capacity + position, experts * capacity)
    slot_row, slot_col = slots[None], slots[:, None]
    carry_mask = same_document(doc_ids, 1)[:, None]

    first_scale, normed, x_branch, z_branch, conv_sum, inner_act, projected, gathered_x, gathered_z, gathered_out = front(
        wide, conv_taps, tokens, mixer_gain, in_proj_x, in_proj_z, out_proj, conv_weight, conv_bias, state_proj.T, masks
    )
    scan_out, step_size, held, starts, gated, mixed, grads_in = scan_mix(
        projected, inner_act, carry_mask, step_proj, step_bias, log_rates, skip_gain, z_branch, gathered_out, out_grad, slot_row,
        step_rank, wide, capacity,
    )
    grad_up, grad_ubias, grad_down, grad_dbias, returned, terms, router_grad = experts_block(
        wide, capacity, tokens, mixed, grads_in, slot_row, expert_gain, router_weight.T,
        expert_up[0], up_bias, expert_down[0], down_bias,
    )
    d_hidden, d_normed, grad_in_x, grad_in_z, grad_out, small, gated_out = mixer_back(
        wide, conv_taps, step_rank,
        (projected, carry_mask, step_size, held, starts, tokens, mixed, out_grad, slot_col, z_branch, scan_out),
        (inner_act, step_proj, log_rates, skip_gain, returned, expert_gain, gathered_out, terms, x_branch, conv_sum, masks, state_proj.T,
         conv_weight, normed, gated, gathered_x, gathered_z, mixer_gain, router_grad),
    )
    outs = finish(
        step_rank, states, experts, tokens, mixed, slot_col, gated_out, d_hidden, d_normed, first_scale, mixer_gain, small,
        grad_in_x, grad_in_z, grad_out, grad_up, grad_down, grad_ubias, grad_dbias,
    )
    return tuple(out.T if n in (7, 14) else out for n, out in enumerate(outs))


def solution(mesh):
    in_specs = (
        P("wide", None),
        P("wide", None),
        P("wide", None),
        P("wide", None),
        P(),
        P("wide", "tp"),
        P("wide", "tp"),
        P(None, "tp"),
        P("tp"),
        P("tp", None),
        P(None, "tp"),
        P("tp"),
        P(None, "tp"),
        P("tp"),
        P("wide", "tp"),
        P(),
        P(),
        P("wide", None, "tp"),
        P("wide", "tp"),
        P("wide", "tp", None),
        P("wide", None),
    )
    out_specs = (
        P("wide", None),
        P("wide", None),
        P(),
        P("wide", "tp"),
        P("wide", "tp"),
        P(None, "tp"),
        P("tp"),
        P("tp", None),
        P(None, "tp"),
        P("tp"),
        P(None, "tp"),
        P("tp"),
        P("wide", "tp"),
        P(),
        P(),
        P("wide", None, "tp"),
        P("wide", "tp"),
        P("wide", "tp", None),
        P("wide", None),
    )
    wide, line = mesh.shape["wide"], mesh.shape["tp"]
    per_device = fast_device if line == 4 and wide == 8 else plain_device
    return jax.shard_map(
        per_device, mesh=mesh, in_specs=in_specs, out_specs=out_specs, check_vma=False
    )
```

```python
import functools

import jax
import jax.numpy as jnp
from jax import lax
from jax.experimental import pallas as pl
from jax.experimental.pallas import tpu as pltpu
from jax.sharding import PartitionSpec as P

EPS = 1e-05
HIGH = lax.Precision.HIGHEST


def in_blocks(shard, dim, size):
    before, after = (shard.shape[:dim], shard.shape[dim + 1 :])
    return jnp.moveaxis(shard.reshape(*before, size, -1, *after), dim, 0)


def summed_on_arrival(shard, axis, dim):
    size = lax.axis_size(axis)
    parts = lax.all_to_all(in_blocks(shard, dim, size), axis, 0, 0, tiled=True)
    return jnp.sum(parts.astype(jnp.float32), axis=0)


def multiply(left, right):
    return jnp.dot(left, right, preferred_element_type=jnp.float32)


def contract_rows(left, right):
    return lax.dot_general(
        left, right, (((0,), (0,)), ((), ())), preferred_element_type=jnp.float32
    )


def contract_cols(left, right):
    return lax.dot_general(
        left, right, (((1,), (1,)), ((), ())), preferred_element_type=jnp.float32
    )


def shifted_down(values, steps):
    if steps == 0:
        return values
    filler = jnp.zeros((steps,) + values.shape[1:], values.dtype)
    return jnp.concatenate([filler, values[:-steps]], axis=0)


def shifted_up(values, steps):
    if steps == 0:
        return values
    filler = jnp.zeros((steps,) + values.shape[1:], values.dtype)
    return jnp.concatenate([values[steps:], filler], axis=0)


def same_document(doc_ids, steps):
    if steps == 0:
        return jnp.ones(doc_ids.shape, jnp.float32)
    filler = jnp.full((steps,), -1, jnp.int32)
    earlier = jnp.concatenate([filler, doc_ids[:-steps]])
    return (earlier == doc_ids).astype(jnp.float32)


def silu_slope(values):
    logistic = jax.nn.sigmoid(values)
    return logistic * (1.0 + values * (1.0 - logistic))


def rms_back(grad_unit, unit, scale):
    return scale * (grad_unit - unit * jnp.mean(grad_unit * unit, axis=1, keepdims=True))


LOG2E = 1.4426950408889634
LANES = 128
F32, BF16 = jnp.float32, jnp.bfloat16
MESH = pl.DeviceIdType.MESH


def fold_rows(parts, masks):
    m4, m2, m1 = masks

    def join(a, b, m, shift):
        return jnp.where(m, a, b) + pltpu.roll(jnp.where(m, b, a), shift, 0)

    c = [join(parts[i], parts[i + 4], m4[i], 4) for i in range(4)]
    d = [join(c[i], c[i + 2], m2[i], 6) for i in range(2)]
    return join(d[0], d[1], m1, 7)


def fold_masks(width):
    sub = lax.broadcasted_iota(jnp.int32, (8, width), 0)
    m4 = [((sub - i) & 7) < 4 for i in range(4)]
    m2 = [((sub - i) & 2) == 0 for i in range(2)]
    m1 = (sub & 1) == 0
    return m4, m2, m1


def softplus(v):
    return jnp.maximum(v, 0.0) + jnp.log1p(jnp.exp(-jnp.abs(v)))


def row(ref, c, t, ns):
    one = ref[c, pl.ds(t, 8, stride=0), :]
    return jnp.concatenate([one] * (ns // 8), axis=0)


def spread(ref, value):
    for c in range(ref.shape[0]):
        ref[c] = value[:, c * LANES:(c + 1) * LANES]


def own_column(ns, rank):
    lane = lax.broadcasted_iota(jnp.int32, (ns, LANES), 1)
    n = lax.broadcasted_iota(jnp.int32, (ns, LANES), 0)
    return (lane == rank + n) | (lane == rank + ns + n)


def coefficient_rows(ns, rank, proj_ref, first):
    own = own_column(ns, rank)
    lane = lax.broadcasted_iota(jnp.int32, (LANES, 2 * LANES), 1)
    k = lax.broadcasted_iota(jnp.int32, (LANES, 2 * LANES), 0)
    pick = ((lane < LANES) & (k >= rank) & (k < rank + ns)) | ((lane >= LANES) & (k >= rank + ns) & (k < rank + 2 * ns))
    pick = jnp.where(pick, 1.0, 0.0).astype(BF16)
    rows = []
    for j in range(8):
        one = proj_ref[pl.ds(first + j, 8, stride=0), :]
        rows.append(jnp.where(own, jnp.concatenate([one] * (ns // 8), axis=0), 0.0).astype(BF16))
    return jnp.dot(jnp.concatenate(rows, axis=0), pick, preferred_element_type=F32)


def forward_tokens(ns, rank, proj_ref, stepd_s, drive_s, r2_s, states_ref, scan_ref, state, wide_a, wide_b):
    tb = proj_ref.shape[0]
    groups = len(state)
    masks = fold_masks(LANES)

    def eight(first, wide, state):
        parts = [[] for _ in range(groups)]
        for j in range(8):
            t = first + j
            in_b = wide[j * ns:(j + 1) * ns, :LANES]
            out_b = wide[j * ns:(j + 1) * ns, LANES:]
            for c in range(groups):
                dec = jnp.exp2(row(stepd_s, c, t, ns) * r2_s[c])
                s = dec * state[c] + row(drive_s, c, t, ns) * in_b
                state[c] = s
                states_ref[pl.ds(pl.multiple_of(t * ns, ns), ns), pl.ds(c * LANES, LANES)] = s.astype(BF16)
                z = out_b * s
                parts[c].append(sum(z[8 * k:8 * k + 8] for k in range(ns // 8)))
        for c in range(groups):
            scan_ref[pl.ds(pl.multiple_of(first, 8), 8), pl.ds(c * LANES, LANES)] = fold_rows(parts[c], masks)
        return state

    def body(g, state):
        state = list(state)
        first = g * 16
        wide_b[...] = coefficient_rows(ns, rank, proj_ref, first + 8)
        state = eight(first, wide_a, state)
        wide_a[...] = coefficient_rows(ns, rank, proj_ref, jnp.minimum(first + 16, tb - 8))
        return tuple(eight(first + 8, wide_b, state))

    wide_a[...] = coefficient_rows(ns, rank, proj_ref, 0)
    return lax.fori_loop(0, tb // 16, body, state)


def backward_tokens(ns, rank, proj_ref, states_ref, starts_ref, stepd_s, drive_s, dscan_s, step_s, r2_s, coeff_s, exps_s, dproj_ref,
                    later, acc, wide_a, wide_b, sums_a, sums_b):
    tb = proj_ref.shape[0]
    groups = len(later)
    masks = fold_masks(LANES)
    own = own_column(ns, rank)
    k = lax.broadcasted_iota(jnp.int32, (2 * LANES, LANES), 0)
    lane = lax.broadcasted_iota(jnp.int32, (2 * LANES, LANES), 1)
    into = ((k < LANES) & (lane >= rank) & (lane < rank + ns)) | ((k >= LANES) & (lane >= rank + ns) & (lane < rank + 2 * ns))
    into = jnp.where(into, 1.0, 0.0).astype(BF16)

    def gather(sums, first):
        got = jnp.dot(sums[...], into, preferred_element_type=F32)
        parts = []
        for j in range(8):
            one = jnp.where(own, got[j * ns:(j + 1) * ns], 0.0)
            parts.append(sum(one[8 * q:8 * q + 8] for q in range(ns // 8)))
        dproj_ref[pl.ds(pl.multiple_of(first, 8), 8), :] = fold_rows(parts, masks)

    def eight(first, wide, sums, later, acc):
        cparts = [[None] * 8 for _ in range(groups)]
        eparts = [[None] * 8 for _ in range(groups)]
        last = pl.ds(pl.multiple_of((first + 7) * ns, ns), ns)
        now = [states_ref[last, pl.ds(c * LANES, LANES)].astype(F32) for c in range(groups)]
        for j in range(7, -1, -1):
            t = first + j
            prior = pl.ds(pl.multiple_of((t - 1 if j else jnp.maximum(t - 1, 0)) * ns, ns), ns)
            here = slice(j * ns, (j + 1) * ns)
            in_b = wide[here, :LANES]
            out_b = wide[here, LANES:]
            din = dout = None
            for c in range(groups):
                cols = pl.ds(c * LANES, LANES)
                before = states_ref[prior, cols].astype(F32)
                if j == 0:
                    before = jnp.where(jnp.full((ns, LANES), t, jnp.int32) == 0, starts_ref[0, :, cols], before)
                r2 = r2_s[c]
                dec = jnp.exp2(row(stepd_s, c, t, ns) * r2)
                ds = row(dscan_s, c, t, ns)
                d = later[c] + out_b * ds
                later[c] = dec * d
                dexp = later[c] * before
                e = dexp * r2
                cf = d * in_b
                cparts[c][j] = sum(cf[8 * q:8 * q + 8] for q in range(ns // 8))
                eparts[c][j] = sum(e[8 * q:8 * q + 8] for q in range(ns // 8))
                acc[c] = acc[c] + dexp * row(step_s, c, t, ns)
                a = d * row(drive_s, c, t, ns)
                b = now[c] * ds
                din = a if din is None else din + a
                dout = b if dout is None else dout + b
                now[c] = before
            sums[here, :LANES] = din.astype(BF16)
            sums[here, LANES:] = dout.astype(BF16)
        rows = pl.ds(pl.multiple_of(first, 8), 8)
        for c in range(groups):
            cols = pl.ds(c * LANES, LANES)
            coeff_s[rows, cols] = fold_rows(cparts[c], masks)
            exps_s[rows, cols] = fold_rows(eparts[c], masks)
        return later, acc

    def body(k, carry):
        later, acc = [list(v) for v in carry]
        first = tb - 16 - k * 16
        gather(sums_a, jnp.minimum(first + 16, tb - 8))
        wide_a[...] = coefficient_rows(ns, rank, proj_ref, first)
        later, acc = eight(first + 8, wide_b, sums_b, later, acc)
        gather(sums_b, first + 8)
        wide_b[...] = coefficient_rows(ns, rank, proj_ref, jnp.maximum(first - 8, 0))
        later, acc = eight(first, wide_a, sums_a, later, acc)
        return tuple(later), tuple(acc)

    wide_b[...] = coefficient_rows(ns, rank, proj_ref, tb - 8)
    sums_a[...] = jnp.zeros_like(sums_a)
    later, acc = lax.fori_loop(0, tb // 16, body, (later, acc))
    gather(sums_a, 0)
    return later, acc


def scan_fwd_kernel(ns, rank, proj_ref, inner_ref, keep_ref, sproj_ref, sbias_ref, lr_ref, skip_ref,
                    scan_ref, step_ref, states_ref, starts_ref, state_s, stepd_s, drive_s, r2_s, wide_a, wide_b):
    tb, ch = inner_ref.shape
    groups = ch // LANES
    i = pl.program_id(0)

    @pl.when(i == 0)
    def _():
        state_s[...] = jnp.zeros_like(state_s)
        spread(r2_s, jnp.exp(lr_ref[...]) * (-LOG2E))

    step_in = proj_ref[...].astype(BF16)
    pre = jnp.dot(step_in, sproj_ref[...], preferred_element_type=F32) + sbias_ref[...]
    step = softplus(pre)
    step_ref[...] = step
    spread(stepd_s, jnp.where(keep_ref[...] > 0.0, step, 1e30))
    inner = inner_ref[...].astype(F32)
    spread(drive_s, step * inner)
    starts_ref[0] = state_s[...]
    start = tuple(state_s[:, c * LANES:(c + 1) * LANES] for c in range(groups))
    state = forward_tokens(ns, rank, proj_ref, stepd_s, drive_s, r2_s, states_ref, scan_ref, start, wide_a, wide_b)
    for c in range(groups):
        state_s[:, c * LANES:(c + 1) * LANES] = state[c]
    scan_ref[...] += skip_ref[...] * inner


def scan_fwd(proj, inner, keep, sproj, sbias, log_rates, skip, rank):
    seq, ch = inner.shape
    ns = log_rates.shape[0]
    tb = LANES
    nb = seq // tb
    full = lambda a: pl.BlockSpec(a.shape, lambda i: (0,) * a.ndim)
    rows = pl.BlockSpec((tb, ch), lambda i: (i, 0))
    return pl.pallas_call(
        functools.partial(scan_fwd_kernel, ns, rank),
        grid=(nb,),
        in_specs=[pl.BlockSpec((tb, LANES), lambda i: (i, 0)), rows, pl.BlockSpec((tb, 1), lambda i: (i, 0)),
                  full(sproj), full(sbias), full(log_rates), full(skip)],
        out_specs=[rows, rows, pl.BlockSpec((tb * ns, ch), lambda i: (i, 0)), pl.BlockSpec((1, ns, ch), lambda i: (i, 0, 0))],
        out_shape=[jax.ShapeDtypeStruct((seq, ch), F32), jax.ShapeDtypeStruct((seq, ch), F32),
                   jax.ShapeDtypeStruct((seq * ns, ch), BF16), jax.ShapeDtypeStruct((nb, ns, ch), F32)],
        scratch_shapes=[pltpu.VMEM((ns, ch), F32)] + [pltpu.VMEM((ch // LANES, tb, LANES), F32)] * 2 + [pltpu.VMEM((ch // LANES, ns, LANES), F32),
                        *[pltpu.VMEM((8 * ns, 2 * LANES), F32)] * 2],
        compiler_params=pltpu.CompilerParams(vmem_limit_bytes=48 << 20),
        name="scan_fwd",
    )(proj, inner, keep, sproj, sbias, log_rates, skip)


def scan_bwd_kernel(ns, rank, proj_ref, inner_ref, keep_ref, step_ref, states_ref, starts_ref, dscan_ref, sproj_ref, lr_ref, skip_ref,
                    dpre_ref, dinner_ref, dproj_ref, gstep_ref, gsbias_ref, grates_ref, gskip_ref,
                    carry_s, stepd_s, drive_s, dscan_s, step_s, r2_s, coeff_s, exps_s, acc_s, wide_a, wide_b, sums_a, sums_b):
    tb, ch = inner_ref.shape
    groups = ch // LANES
    i = pl.program_id(0)

    @pl.when(i == 0)
    def _():
        carry_s[...] = jnp.zeros_like(carry_s)
        acc_s[...] = jnp.zeros_like(acc_s)
        spread(r2_s, jnp.exp(lr_ref[...]) * (-LOG2E))
        gstep_ref[...] = jnp.zeros_like(gstep_ref)
        gsbias_ref[...] = jnp.zeros_like(gsbias_ref)
        gskip_ref[...] = jnp.zeros_like(gskip_ref)

    step = step_ref[...]
    inner = inner_ref[...].astype(F32)
    dscan = dscan_ref[...]
    spread(stepd_s, jnp.where(keep_ref[...] > 0.0, step, 1e30))
    spread(drive_s, step * inner)
    spread(dscan_s, dscan)
    spread(step_s, step)
    pick = lambda ref: tuple(ref[:, c * LANES:(c + 1) * LANES] for c in range(groups))
    later, acc = backward_tokens(ns, rank, proj_ref, states_ref, starts_ref, stepd_s, drive_s, dscan_s, step_s, r2_s, coeff_s, exps_s,
                                 dproj_ref, pick(carry_s), pick(acc_s), wide_a, wide_b, sums_a, sums_b)
    for c in range(groups):
        carry_s[:, c * LANES:(c + 1) * LANES] = later[c]
        acc_s[:, c * LANES:(c + 1) * LANES] = acc[c]
    coeff = coeff_s[...]
    d_step = coeff * inner + exps_s[...] * (1.0 / LOG2E)
    d_pre = (d_step * (1.0 - jnp.exp(-step))).astype(BF16)
    dpre_ref[...] = d_pre
    dinner_ref[...] = dscan * skip_ref[...] + step * coeff
    step_in = proj_ref[...].astype(BF16)
    gstep_ref[...] += lax.dot_general(step_in, d_pre, (((0,), (0,)), ((), ())), preferred_element_type=F32)
    gsbias_ref[...] += jnp.sum(d_pre.astype(F32), axis=0, keepdims=True)
    gskip_ref[...] += jnp.sum(dscan * inner, axis=0, keepdims=True)
    dproj_ref[...] += lax.dot_general(d_pre, sproj_ref[...], (((1,), (1,)), ((), ())), preferred_element_type=F32)

    @pl.when(i == pl.num_programs(0) - 1)
    def _():
        grates_ref[...] = -jnp.exp(lr_ref[...]) * acc_s[...]


def scan_bwd(proj, inner, keep, step, states, starts, dscan, sproj, log_rates, skip, rank):
    seq, ch = inner.shape
    ns = log_rates.shape[0]
    tb = LANES
    nb = seq // tb
    full = lambda a: pl.BlockSpec(a.shape, lambda i: (0,) * a.ndim)
    rows = pl.BlockSpec((tb, ch), lambda i: (nb - 1 - i, 0))
    prow = pl.BlockSpec((tb, LANES), lambda i: (nb - 1 - i, 0))
    whole = lambda *s: pl.BlockSpec(s, lambda i: (0,) * len(s))
    shape = jax.ShapeDtypeStruct
    return pl.pallas_call(
        functools.partial(scan_bwd_kernel, ns, rank),
        grid=(nb,),
        in_specs=[prow, rows, pl.BlockSpec((tb, 1), lambda i: (nb - 1 - i, 0)), rows,
                  pl.BlockSpec((tb * ns, ch), lambda i: (nb - 1 - i, 0)), pl.BlockSpec((1, ns, ch), lambda i: (nb - 1 - i, 0, 0)),
                  rows, full(sproj), full(log_rates), full(skip)],
        out_specs=[rows, rows, prow, whole(LANES, ch), whole(1, ch), whole(ns, ch), whole(1, ch)],
        out_shape=[shape((seq, ch), BF16), shape((seq, ch), F32), shape((seq, LANES), F32), shape((LANES, ch), F32), shape((1, ch), F32),
                   shape((ns, ch), F32), shape((1, ch), F32)],
        scratch_shapes=[pltpu.VMEM((ns, ch), F32)] + [pltpu.VMEM((ch // LANES, tb, LANES), F32)] * 4 + [pltpu.VMEM((ch // LANES, ns, LANES), F32),
                        pltpu.VMEM((tb, ch), F32), pltpu.VMEM((tb, ch), F32), pltpu.VMEM((ns, ch), F32),
                        *[pltpu.VMEM((8 * ns, 2 * LANES), F32)] * 2, *[pltpu.VMEM((8 * ns, 2 * LANES), BF16)] * 2],
        compiler_params=pltpu.CompilerParams(vmem_limit_bytes=48 << 20),
        name="scan_bwd",
    )(proj, inner, keep, step, states, starts, dscan, sproj, log_rates, skip)


def tall(ref):
    value = ref[...]
    return jnp.concatenate([value, jnp.zeros((LANES - value.shape[0], value.shape[1]), value.dtype)], axis=0)


def as_row(ref):
    return ref[...].reshape(1, ref.shape[0])


def line_roles():
    me = lax.axis_index("tp")
    end = (me == 0) | (me == 3)
    mate = jnp.where(me < 2, 1 - me, 5 - me)
    return end, jnp.logical_not(end), mate, 3 - me


LINE = 4
PIECES, SLOT_PIECES = 2, 2
MIX_BEHIND, SLOT_BEHIND, DN_BEHIND = 2, 2, 2
OUT_STEPS = (0, 1, 2, 3, 4, 5, 6, 7)


def greet(wide):
    barrier = pltpu.get_barrier_semaphore()
    for axis, size in (("tp", LINE), ("wide", wide)):
        me = lax.axis_index(axis)
        for k in range(1, size):
            pl.semaphore_signal(barrier, inc=1, device_id={axis: lax.rem(me + k, size)}, device_id_type=MESH)
    pl.semaphore_wait(barrier, LINE + wide - 2)


class LineSum:
    def __init__(self, roles, rows, pieces, own, near, half, far, sends, arrivals, behind=None, last=None):
        self.end, self.mid, self.mate, self.other = roles
        self.rows, self.pieces = rows // pieces, pieces
        self.behind = pieces if behind is None else behind
        self.last = last
        self.own, self.near, self.half, self.far = own, near, half, far
        self.sends, self.arrivals = sends, arrivals

    def part(self, ref, n):
        return ref.at[pl.ds(pl.multiple_of(n * self.rows, self.rows), self.rows)]

    def copy(self, source, target, hop, n, to):
        return pltpu.make_async_remote_copy(
            self.part(source, n), self.part(target, n), self.sends.at[hop, n], self.arrivals.at[hop, n],
            device_id={"tp": to}, device_id_type=MESH)

    def up(self, n):
        return self.copy(self.own, self.near, 0, n, self.mate)

    def across(self, n):
        return self.copy(self.half, self.far, 1, n, self.other)

    def down(self, n):
        return self.copy(self.far, self.far, 2, n, self.mate)

    def add(self, a, b, c, n):
        self.part(c, n)[...] = (self.part(a, n)[...].astype(F32) + self.part(b, n)[...].astype(F32)).astype(BF16)

    def each(self, k):
        return [k * self.pieces + j for j in range(self.pieces)]

    def start(self, k):
        for n in self.each(k):
            self.up(n).start()

    def first(self, n):
        self.up(n).wait_recv()
        self.add(self.own, self.near, self.half, n)
        self.across(n).start()

    def second(self, n):
        self.across(n).wait_recv()
        self.add(self.half, self.far, self.far, n)
        self.down(n).start()

    def place(self, m):
        if self.last is None:
            return m
        return (self.last - m // self.pieces) * self.pieces + m % self.pieces

    def flow(self, k, done=None):
        for j in range(self.pieces):
            m = k * self.pieces + j
            self.first(self.place(m))

            @pl.when(m >= self.behind)
            def _():
                self.second(self.place(m - self.behind))
                if done and (j - self.behind) % self.pieces == self.pieces - 1:
                    done(self.place(m - self.behind) // self.pieces)

    def flush(self, count, done=None):
        for m in range(count * self.pieces - self.behind, count * self.pieces):
            self.second(self.place(m))
            if done and m % self.pieces == self.pieces - 1:
                done(jnp.int32(self.place(m) // self.pieces))

    def arrived(self, k):
        for n in self.each(k):
            self.down(n).wait_recv()

    def sent(self, count):
        def block(n, _):
            @pl.when(self.end)
            def _():
                self.up(n).wait_send()

            @pl.when(self.mid)
            def _():
                self.across(n).wait_send()
                self.down(n).wait_send()
            return 0

        lax.fori_loop(0, count * self.pieces, block, 0)


def pack_rows(rank, states, experts, width, ch, wide):
    rows = 8 + states + rank + (rank + 2 * states) + 8 + (width // ch) * experts
    return -(-rows // (8 * wide)) * (8 * wide)


def finish_kernel(rank, states, tokens_ref, mixed_ref, scol_ref, got_ref, dhidden_ref, dn_ref, scale_ref, gain_ref, small_ref,
                  gx_ref, gz_ref, go_ref, gup_ref, gdown_ref, gub_ref, gdb_ref,
                  result_ref, tgrad_ref, first_ref, gx_out, gz_out, cw_ref, cb_ref, state_ref, step_ref, sb_ref, rates_ref, skip_ref, go_out,
                  second_ref, router_ref, gup_out, gub_out, gdown_out, gdb_out):
    i = pl.program_id(0)
    ch = small_ref.shape[1]
    experts, width = router_ref.shape
    gup_out[0] = gup_ref[...]
    gdown_out[0] = gdown_ref[...]

    @pl.when(i == 0)
    def _():
        for ref, out in ((gx_ref, gx_out), (gz_ref, gz_out), (go_ref, go_out), (gub_ref, gub_out), (gdb_ref, gdb_out)):
            out[...] = ref[...]
        flat = lambda r: small_ref[r:r + 1, :].reshape(ch)
        cb_ref[...] = flat(0)
        sb_ref[...] = flat(1)
        skip_ref[...] = flat(2)
        cw_ref[...] = small_ref[4:8, :]
        at = 8
        rates_ref[...] = small_ref[at:at + states, :]
        at += states
        step_ref[...] = small_ref[at:at + rank, :]
        at += rank
        held = rank + 2 * states
        state_ref[...] = small_ref[at:at + held, :]
        at += held
        halves = width // ch
        for h in range(halves):
            cols = slice(h * ch, (h + 1) * ch)
            first_ref[cols] = flat(at + h)
            second_ref[cols] = flat(at + halves + h)
            router_ref[:, cols] = small_ref[at + 8 + h * experts:at + 8 + (h + 1) * experts, :]

    ids = lax.broadcasted_iota(jnp.int32, (scol_ref.shape[0], got_ref.shape[0]), 1)
    chosen = jnp.where(ids == scol_ref[...], 1.0, 0.0).astype(BF16)
    tokens = tokens_ref[...]
    result_ref[...] = tokens + mixed_ref[...].astype(F32) + jnp.dot(chosen, got_ref[...], preferred_element_type=F32)
    scale = scale_ref[...]
    unit = tokens * scale
    through = dn_ref[...].astype(F32) * as_row(gain_ref)
    mean = jnp.mean(through * unit, axis=1, keepdims=True)
    tgrad_ref[...] = dhidden_ref[...] + scale * (through - unit * mean)


def finish(rank, states, experts, *operands):
    tokens, mixed, scol, got, dhidden, dn, scale, gain, small, gx, gz, go, gup, gdown, gub, gdb = operands
    seq, width = tokens.shape
    ch = small.shape[1]
    tb = 2 * LANES
    row = lambda n: pl.BlockSpec((tb, n), lambda i: (i, 0))
    full = lambda a: pl.BlockSpec(a.shape, lambda i: (0,) * a.ndim)
    whole = lambda *s: pl.BlockSpec(s, lambda i: (0,) * len(s))
    sizes = [(width,), gx.shape, gz.shape, (4, ch), (ch,), (rank + 2 * states, ch), (rank, ch), (ch,), (states, ch), (ch,), go.shape,
             (width,), (experts, width), (1, *gup.shape), gub.shape, (1, *gdown.shape), gdb.shape]
    nb = seq // tb
    piece = lambda a: pl.BlockSpec((a.shape[0] // nb, a.shape[1]), lambda i: (i, 0))
    placed = lambda size: pl.BlockSpec((1, size[1] // nb, size[2]), lambda i: (0, i, 0)) if len(size) == 3 else whole(*size)
    return pl.pallas_call(
        functools.partial(finish_kernel, rank, states),
        grid=(seq // tb,),
        in_specs=[row(width), row(width), row(1), full(got), row(width), row(width), row(1), full(gain), full(small), full(gx), full(gz), full(go), piece(gup), piece(gdown), full(gub), full(gdb)],
        out_specs=[row(width), row(width), *[placed(size) for size in sizes]],
        out_shape=[jax.ShapeDtypeStruct(size, F32) for size in [(seq, width), (seq, width), *sizes]],
        compiler_params=pltpu.CompilerParams(vmem_limit_bytes=62 << 20),
        name="finish",
    )(*operands)


def mixer_back_kernel(ns, rank, wide, taps, proj_ref, keep_ref, step_ref, states_ref, starts_ref, tokens_ref, mixed_ref, ograd_ref, scol_ref, z_ref, scan_ref,
                      inner_ref, sproj_ref, lr_ref, skip_ref, ret_ref, gain_ref, wo_ref, term_ref,
                      x_ref, csum_ref, masks_ref, wproj_ref, cw_ref, normed_ref, gated_ref, wx_ref, wz_ref, first_gain_ref, grow_ref,
                      dhidden_ref, dn_ref, gx_ref, gz_ref, go_ref, small_ref, got_ref,
                      carry_s, stepd_s, drive_s, dscan_s, step_s, r2_s, coeff_s, exps_s, acc_s, dproj_s, wide_a, wide_b, sums_a, sums_b,
                      near_s, half_s, far_s, sends, arrivals, got_sends, got_arrivals,
                      dp_own, dp_near, dp_far, dp_sends, dp_arrivals, dn_own, dn_near, dn_far, dn_sends, dn_arrivals,
                      prod_s, inbox_s, prod_sends, prod_arrivals, pack_s, pack_in, small_s, pack_sends, pack_arrivals,
                      dinner_s, dmixed_s, dz_s, dconv_s, dx_s, gstep_s, state_s, first_s, second_s, dscan_all, gains_s):
    seq, ch = inner_ref.shape
    width = normed_ref.shape[1]
    tb = LANES
    nb = seq // tb
    groups = ch // LANES
    i = pl.program_id(0)
    me = lax.axis_index("wide")
    roles = line_roles()
    end, mid, mate, other = roles
    cap = term_ref.shape[0] // wide
    line = LineSum(roles, cap, SLOT_PIECES, term_ref, near_s, half_s, far_s, sends, arrivals)
    dp = LineSum(roles, tb, 1, dp_own, dp_near, dp_own, dp_far, dp_sends, dp_arrivals, last=nb - 1)
    dn = LineSum(roles, tb, PIECES, dn_own, dn_near, dn_own, dn_far, dn_sends, dn_arrivals, behind=DN_BEHIND, last=nb - 1)
    block = width // wide
    turned = (((1,), (1,)), ((), ()))
    across_rows = (((0,), (0,)), ((), ()))

    def slot_rows(c):
        return pl.ds(pl.multiple_of(c * cap, cap), cap)

    def rows_of(b):
        return pl.ds(pl.multiple_of(b * tb, tb), tb)

    def give_back(c):
        return pltpu.make_async_remote_copy(
            far_s.at[slot_rows(c)], got_ref.at[slot_rows(me)], got_sends.at[c], got_arrivals.at[c],
            device_id={"wide": lax.rem(me + wide - c, wide)}, device_id_type=MESH)

    def return_chunk(c):
        @pl.when(c == 0)
        def _():
            here = pltpu.make_async_copy(far_s.at[slot_rows(0)], got_ref.at[slot_rows(me)], got_sends.at[0])
            here.start()
            here.wait()

        @pl.when(c != 0)
        def _():
            give_back(c).start()

    def deliver(which, k):
        to = lax.rem(me + k, wide)
        return pltpu.make_async_remote_copy(
            prod_s.at[which, pl.ds(pl.multiple_of(to * block, block), block)], inbox_s.at[which, k],
            prod_sends.at[which, k], prod_arrivals.at[which, k], device_id={"wide": to}, device_id_type=MESH)

    def product(which, left, right):
        def tile(j, _):
            cols = pl.ds(pl.multiple_of(j * LANES, LANES), LANES)
            got = lax.dot_general(left[:, cols], right[...], across_rows, preferred_element_type=F32)
            prod_s[which, cols, :] = got.astype(BF16)
            return 0

        lax.fori_loop(0, width // LANES, tile, 0)
        for k in range(1, wide):
            deliver(which, k).start()

    @pl.when(i == 0)
    def _():
        greet(wide)
        for ref in (carry_s, acc_s, gstep_s, state_s, first_s, second_s, pack_s):
            ref[...] = jnp.zeros_like(ref)
        dconv_s[pl.ds(seq, 8), :] = jnp.zeros((8, ch), F32)
        spread(r2_s, jnp.exp(lr_ref[...]) * (-LOG2E))

    def at_out_steps(role, lag, work):
        for c, step in enumerate(OUT_STEPS):
            @pl.when(role & (i == step + lag))
            def _():
                work(jnp.int32(c))

    at_out_steps(end, 0, line.start)

    def glue(g):
        part = tokens_ref.shape[0]
        rows = pl.ds(pl.multiple_of((seq // part - 1 - g) * part, part), part)
        hidden = tokens_ref[...] + mixed_ref[...].astype(F32)
        scale = lax.rsqrt(jnp.mean(hidden * hidden, axis=1, keepdims=True) + EPS)
        unit = hidden * scale
        ids = lax.broadcasted_iota(jnp.int32, (part, wide * cap), 1)
        chosen = jnp.where(ids == scol_ref[...], 1.0, 0.0).astype(BF16)
        d_norm_two = jnp.dot(chosen, ret_ref[...], preferred_element_type=F32)
        second_s[...] += jnp.sum(d_norm_two * unit, axis=0, keepdims=True)
        through = d_norm_two * as_row(gain_ref)
        d_hidden = ograd_ref[...] + scale * (through - unit * jnp.mean(through * unit, axis=1, keepdims=True))
        dhidden_ref[...] = d_hidden
        d_mixed = d_hidden.astype(BF16)
        dmixed_s[rows, :] = d_mixed
        d_gated = jnp.dot(d_mixed, wo_ref[...], preferred_element_type=F32)
        z = z_ref[...]
        logistic = 1.0 / (1.0 + jnp.exp(-z))
        dz_s[rows, :] = (d_gated * scan_ref[...] * (logistic * (1.0 + z * (1.0 - logistic)))).astype(BF16)
        dscan_all[rows, :] = d_gated * (z * logistic)

    def scan_block():
        b = nb - 1 - i
        rows = rows_of(b)
        step = step_ref[...]
        inner = inner_ref[rows, :].astype(F32)
        dscan = dscan_all[rows, :]
        spread(stepd_s, jnp.where(keep_ref[...] > 0.0, step, 1e30))
        spread(drive_s, step * inner)
        spread(dscan_s, dscan)
        spread(step_s, step)
        pick = lambda ref: tuple(ref[:, c * LANES:(c + 1) * LANES] for c in range(groups))
        later, acc = backward_tokens(ns, rank, proj_ref, states_ref, starts_ref, stepd_s, drive_s, dscan_s, step_s, r2_s, coeff_s, exps_s,
                                     dproj_s, pick(carry_s), pick(acc_s), wide_a, wide_b, sums_a, sums_b)
        for c in range(groups):
            carry_s[:, c * LANES:(c + 1) * LANES] = later[c]
            acc_s[:, c * LANES:(c + 1) * LANES] = acc[c]
        coeff = coeff_s[...]
        d_step = coeff * inner + exps_s[...] * (1.0 / LOG2E)
        d_pre = (d_step * (1.0 - jnp.exp(-step))).astype(BF16)
        dinner_s[rows, :] = dscan * as_row(skip_ref) + step * coeff
        step_in = proj_ref[...].astype(BF16)
        gstep_s[...] += lax.dot_general(step_in, d_pre, across_rows, preferred_element_type=F32)
        pack_s[1:2, :] += jnp.sum(d_pre.astype(F32), axis=0, keepdims=True)
        pack_s[2:3, :] += jnp.sum(dscan * inner, axis=0, keepdims=True)
        both = dproj_s[...] + lax.dot_general(d_pre, tall(sproj_ref), turned, preferred_element_type=F32)
        dp_own[rows, :] = both.astype(BF16)

        @pl.when(end)
        def _():
            dp.start(b)

    def conv_block(k):
        b = nb - 1 - k
        rows = rows_of(b)
        base = pl.multiple_of(b * tb, tb)

        @pl.when(end)
        def _():
            dp.arrived(b)

        d_proj = dp_far[rows, :]
        state_s[...] += lax.dot_general(d_proj, inner_ref[rows, :], across_rows, preferred_element_type=F32)
        d_inner = dinner_s[rows, :] + jnp.dot(d_proj[:, :wproj_ref.shape[0]], wproj_ref[...], preferred_element_type=F32)
        csum = csum_ref[rows, :]
        logistic = 1.0 / (1.0 + jnp.exp(-csum))
        d_conv = d_inner * (logistic * (1.0 + csum * (1.0 - logistic)))
        prior = x_ref[pl.ds(pl.multiple_of(jnp.maximum(base - 8, 0), 8), 8), :]
        history = jnp.concatenate([prior, x_ref[rows, :]], axis=0)
        ahead = jnp.concatenate([d_conv, dconv_s[pl.ds(pl.multiple_of(base + tb, 8), 8), :]], axis=0)
        dconv_s[rows, :] = d_conv
        same = masks_ref[pl.ds(base, tb + 8), :]
        d_x = cw_ref[taps - 1:taps, :] * d_conv
        pack_s[0:1, :] += jnp.sum(d_conv, axis=0, keepdims=True)
        pack_s[8 - 1:8, :] += jnp.sum(d_conv * history[8:, :], axis=0, keepdims=True)
        for s in range(1, taps):
            linked = same[:, s:s + 1] * ahead
            d_x = d_x + cw_ref[taps - 1 - s:taps - s, :] * linked[s:s + tb, :]
            pack_s[7 - s:8 - s, :] += jnp.sum(linked[:tb, :] * history[8 - s:8 - s + tb, :], axis=0, keepdims=True)
        d_x = d_x.astype(BF16)
        dx_s[rows, :] = d_x
        both = lax.dot_general(d_x, wx_ref[...], turned, preferred_element_type=F32)
        both = both + lax.dot_general(dz_s[rows, :], wz_ref[...], turned, preferred_element_type=F32)
        dn_own[rows, :] = both.astype(BF16)

        @pl.when(end)
        def _():
            dn.start(b)

    def last_block(k):
        b = nb - 1 - k
        rows = rows_of(b)

        @pl.when(end)
        def _():
            dn.arrived(b)

        d_normed = dn_far[rows, :]
        dn_ref[...] = d_normed
        first_s[...] += jnp.sum(d_normed.astype(F32) * normed_ref[rows, :].astype(F32), axis=0, keepdims=True)

    def at_step(lag, count, work):
        @pl.when((i >= lag) & (i < lag + count))
        def _():
            work(i - lag)

    def on_mid(lag, count, work):
        @pl.when(mid & (i >= lag) & (i < lag + count))
        def _():
            work(i - lag)

    def line_down(c):
        line.arrived(c)
        return_chunk(c)

    parts = seq // tokens_ref.shape[0]
    at_step(0, parts, glue)
    at_step(parts, 1, lambda k: product(0, dmixed_s, gated_ref))
    at_step(parts + 1, 1, lambda k: product(1, normed_ref, dz_s))
    at_step(0, nb, lambda k: scan_block())
    on_mid(1, nb, dp.flow)
    on_mid(nb + 1, 1, lambda k: dp.flush(nb))
    at_step(3, nb, conv_block)
    on_mid(4, nb, dn.flow)
    on_mid(nb + 4, 1, lambda k: dn.flush(nb))
    at_out_steps(mid, 1, lambda c: line.flow(c, return_chunk))
    on_mid(OUT_STEPS[-1] + 2, 1, lambda k: line.flush(wide, return_chunk))

    at_out_steps(end, 3, line_down)
    at_step(nb + 2, 1, lambda k: product(2, normed_ref, dx_s))
    at_step(6, nb, last_block)

    share = pack_s.shape[0] // wide
    halves = width // ch
    gains_at = 8 + ns + rank + rank + 2 * ns

    def chunk(ref, n):
        return ref.at[pl.ds(pl.multiple_of(n * share, share), share)]

    def scatter(k):
        to = lax.rem(me + k, wide)
        return pltpu.make_async_remote_copy(chunk(pack_s, to), pack_in.at[k], pack_sends.at[0, k], pack_arrivals.at[0, k],
                                            device_id={"wide": to}, device_id_type=MESH)

    def spread_out(k):
        to = lax.rem(me + k, wide)
        return pltpu.make_async_remote_copy(chunk(small_s, me), chunk(small_s, me), pack_sends.at[1, k], pack_arrivals.at[1, k],
                                            device_id={"wide": to}, device_id_type=MESH)

    def gain_term(k):
        to = lax.rem(me + k, wide)
        return pltpu.make_async_remote_copy(gains_s.at[me], gains_s.at[me], pack_sends.at[2, k], pack_arrivals.at[2, k],
                                            device_id={"wide": to}, device_id_type=MESH)

    def collect(which, ref):
        total = prod_s[which, pl.ds(pl.multiple_of(me * block, block), block), :].astype(F32)
        for k in range(1, wide):
            deliver(which, k).wait_recv()
            total = total + inbox_s[which, k].astype(F32)
        ref[...] = total

    @pl.when(i == nb + 3)
    def _():
        at = 8
        pack_s[at:at + ns, :] = -jnp.exp(lr_ref[...]) * acc_s[...]
        at += ns
        pack_s[at:at + rank, :] = gstep_s[0:rank, :]
        at += rank
        held = rank + 2 * ns
        pack_s[at:at + held, :] = state_s[0:held, :]
        own_row = lax.broadcasted_iota(jnp.int32, (wide, ch), 0) == me
        for h in range(halves):
            cols = slice(h * ch, (h + 1) * ch)
            pack_s[gains_at + halves + h:gains_at + halves + h + 1, :] = second_s[:, cols]
            pack_s[gains_at + 8 + h * wide:gains_at + 8 + (h + 1) * wide, :] = jnp.where(own_row, grow_ref[:, cols], 0.0)
        for k in range(1, wide):
            scatter(k).start()
        collect(0, go_ref)

    @pl.when(i == nb + 4)
    def _():
        total = chunk(pack_s, me)[...]
        for k in range(1, wide):
            scatter(k).wait_recv()
            total = total + pack_in[k]
        chunk(small_s, me)[...] = total
        for k in range(1, wide):
            spread_out(k).start()
        collect(1, gz_ref)

    @pl.when(i == pl.num_programs(0) - 1)
    def _():
        gains_s[me] = jnp.broadcast_to(first_s[...] / as_row(first_gain_ref), (8, width))
        for k in range(1, wide):
            gain_term(k).start()
        collect(2, gx_ref)
        line.sent(wide)
        dp.sent(nb)
        dn.sent(nb)
        for k in range(1, wide):
            spread_out(k).wait_recv()
        small_ref[...] = small_s[...]
        for k in range(1, wide):
            gain_term(k).wait_recv()
        first = gains_s[0, 0:1, :]
        for n in range(1, wide):
            first = first + gains_s[n, 0:1, :]
        for h in range(halves):
            small_ref[gains_at + h:gains_at + h + 1, :] = first[:, h * ch:(h + 1) * ch]
        for k in range(1, wide):
            give_back(k).wait_recv()
            give_back(k).wait_send()
            for which in range(3):
                deliver(which, k).wait_send()
            scatter(k).wait_send()
            spread_out(k).wait_send()
            gain_term(k).wait_send()


def mixer_back(wide, taps, rank, by_rows, whole_ones):
    proj, keep, step, states, starts, tokens, mixed, ograd, scol, z, scan = by_rows
    inner, log_rates, ret = whole_ones[0], whole_ones[2], whole_ones[4]
    seq, ch = inner.shape
    width = tokens.shape[1]
    ns = log_rates.shape[0]
    tb = LANES
    nb = seq // tb
    packed = pack_rows(rank, ns, wide, width, ch, wide)
    back = lambda i: jnp.maximum(nb - 1 - i, 0)
    early = lambda i: jnp.maximum(nb // 2 - 1 - i, 0)
    final = lambda i: nb - 1 - jnp.maximum(i - 6, 0)
    row = lambda n, size=tb: pl.BlockSpec((size, n), lambda i: (back(i), 0))
    full = lambda a: pl.BlockSpec(a.shape, lambda i: (0,) * a.ndim, pipeline_mode=pl.Buffered(1))
    whole = lambda *s: pl.BlockSpec(s, lambda i: (0,) * len(s))
    shape = jax.ShapeDtypeStruct
    dma = pltpu.SemaphoreType.DMA
    vm = pltpu.VMEM
    return pl.pallas_call(
        functools.partial(mixer_back_kernel, ns, rank, wide, taps),
        grid=(nb + 6,),
        in_specs=[row(LANES), row(1), row(ch), row(ch, tb * ns), pl.BlockSpec((1, ns, ch), lambda i: (back(i), 0, 0)),
                  *[pl.BlockSpec((2 * tb, n), lambda i: (early(i), 0)) for n in (width, width, width, 1, ch, ch)], *[full(a) for a in whole_ones]],
        out_specs=[pl.BlockSpec((2 * tb, width), lambda i: (early(i), 0)), pl.BlockSpec((tb, width), lambda i: (final(i), 0)), *[whole(width // wide, ch)] * 3, whole(packed, ch),
                   pl.BlockSpec(memory_space=pl.ANY)],
        out_shape=[shape((seq, width), F32), shape((seq, width), BF16), *[shape((width // wide, ch), F32)] * 3, shape((packed, ch), F32),
                   shape(ret.shape, BF16)],
        scratch_shapes=[
            vm((ns, ch), F32), *[vm((ch // LANES, tb, LANES), F32)] * 4, vm((ch // LANES, ns, LANES), F32), vm((tb, ch), F32), vm((tb, ch), F32),
            vm((ns, ch), F32), vm((tb, LANES), F32), *[vm((8 * ns, 2 * LANES), F32)] * 2, *[vm((8 * ns, 2 * LANES), BF16)] * 2,
            *[vm(ret.shape, BF16)] * 3, *[dma((3, wide * SLOT_PIECES))] * 2, dma((wide,)), dma((wide,)),
            *[vm((seq, LANES), BF16)] * 3, dma((3, nb)), dma((3, nb)), *[vm((seq, width), BF16)] * 3, *[dma((3, nb * PIECES))] * 2,
            vm((3, width, ch), BF16), vm((3, wide, width // wide, ch), BF16), dma((3, wide)), dma((3, wide)),
            vm((packed, ch), F32), vm((wide, packed // wide, ch), F32), vm((packed, ch), F32), dma((3, wide)), dma((3, wide)),
            vm((seq, ch), F32), vm((seq, width), BF16), vm((seq, ch), BF16), vm((seq + 8, ch), F32), vm((seq, ch), BF16),
            vm((LANES, ch), F32), vm((LANES, ch), F32), vm((1, width), F32), vm((1, width), F32),
            vm((seq, ch), F32), vm((wide, 8, width), F32)],
        compiler_params=pltpu.CompilerParams(collective_id=1, has_side_effects=True, vmem_limit_bytes=62 << 20),
        name="mixer_back",
    )(*by_rows, *whole_ones)


def gelu_pair(v):
    root = 0.7978845608028654
    square = v * v
    t = jnp.tanh(root * v * (1.0 + 0.044715 * square))
    half = 0.5 * (1.0 + t)
    slope = half + (0.5 * root) * v * (1.0 - t * t) * (1.0 + (3.0 * 0.044715) * square)
    return v * half, slope


def scan_mix_kernel(ns, rank, wide, proj_ref, inner_ref, keep_ref, sproj_ref, sbias_ref, lr_ref, skip_ref, z_ref, wo_ref, ograd_ref, srow_ref,
                    scan_ref, step_ref, states_ref, starts_ref, gated_ref, mixed_ref, gin_ref,
                    state_s, stepd_s, drive_s, r2_s, wide_a, wide_b, own_s, near_s, far_s, sends, arrivals, grad_s, send_s, g_sends, g_arrivals):
    tb, ch = inner_ref.shape
    groups = ch // LANES
    i = pl.program_id(0)
    roles = line_roles()
    end, mid, mate, other = roles
    line = LineSum(roles, tb, PIECES, own_s, near_s, own_s, far_s, sends, arrivals, behind=MIX_BEHIND)
    steps = pl.num_programs(0)
    seq_blocks = own_s.shape[0] // tb

    me = lax.axis_index("wide")
    cap = send_s.shape[0] // wide

    def slot_rows(k):
        return pl.ds(pl.multiple_of(k * cap, cap), cap)

    def dispatch(k):
        return pltpu.make_async_remote_copy(
            send_s.at[slot_rows(k)], gin_ref.at[slot_rows(k)], g_sends.at[k], g_arrivals.at[k],
            device_id={"wide": lax.rem(me + k, wide)}, device_id_type=MESH)

    own_rows = pltpu.make_async_copy(send_s.at[slot_rows(0)], gin_ref.at[slot_rows(0)], g_sends.at[0])

    @pl.when(i == 0)
    def _():
        greet(wide)
        state_s[...] = jnp.zeros_like(state_s)
        spread(r2_s, jnp.exp(lr_ref[...]) * (-LOG2E))

    step_in = proj_ref[...].astype(BF16)
    pre = jnp.dot(step_in, tall(sproj_ref), preferred_element_type=F32) + as_row(sbias_ref)
    step = softplus(pre)
    step_ref[...] = step
    spread(stepd_s, jnp.where(keep_ref[...] > 0.0, step, 1e30))
    inner = inner_ref[...].astype(F32)
    spread(drive_s, step * inner)
    starts_ref[0] = state_s[...]
    start = tuple(state_s[:, c * LANES:(c + 1) * LANES] for c in range(groups))
    state = forward_tokens(ns, rank, proj_ref, stepd_s, drive_s, r2_s, states_ref, scan_ref, start, wide_a, wide_b)
    for c in range(groups):
        state_s[:, c * LANES:(c + 1) * LANES] = state[c]
    scan = scan_ref[...] + as_row(skip_ref) * inner
    scan_ref[...] = scan
    z = z_ref[...]
    gated = (scan * (z / (1.0 + jnp.exp(-z)))).astype(BF16)
    gated_ref[...] = gated
    here = pl.ds(pl.multiple_of(i * tb, tb), tb)
    own_s[here, :] = lax.dot_general(gated, wo_ref[...], (((1,), (1,)), ((), ())), preferred_element_type=F32).astype(BF16)

    @pl.when(end)
    def _():
        line.start(i)

    @pl.when(i < wide)
    def _():
        @pl.when(i == 0)
        def _():
            grad_s[...] = ograd_ref[...].astype(BF16)

        ids = lax.broadcasted_iota(jnp.int32, (cap, grad_s.shape[0]), 0) + lax.rem(me + i, wide) * cap
        chosen = jnp.where(ids == srow_ref[...], 1.0, 0.0).astype(BF16)
        send_s[slot_rows(i), :] = jnp.dot(chosen, grad_s[...], preferred_element_type=F32).astype(BF16)

        @pl.when(i == 0)
        def _():
            own_rows.start()

        @pl.when(i > 0)
        def _():
            dispatch(i).start()

    @pl.when(mid & (i > 0))
    def _():
        line.flow(i - 1)

    @pl.when(i == steps - 1)
    def _():
        @pl.when(mid)
        def _():
            line.flow(i)
            line.flush(seq_blocks)

        @pl.when(end)
        def _():
            for k in range(steps):
                line.arrived(k)

        mixed_ref[...] = far_s[...]
        line.sent(steps)
        own_rows.wait()
        for k in range(1, wide):
            dispatch(k).wait_recv()
            dispatch(k).wait_send()


def scan_mix(proj, inner, keep, sproj, sbias, log_rates, skip, z, wo, ograd, srow, rank, wide, cap):
    seq, ch = inner.shape
    ns = log_rates.shape[0]
    tb = LANES
    nb = seq // tb
    width = wo.shape[0]
    full = lambda a: pl.BlockSpec(a.shape, lambda i: (0,) * a.ndim)
    rows = pl.BlockSpec((tb, ch), lambda i: (i, 0))
    return pl.pallas_call(
        functools.partial(scan_mix_kernel, ns, rank, wide),
        grid=(nb,),
        in_specs=[pl.BlockSpec((tb, LANES), lambda i: (i, 0)), rows, pl.BlockSpec((tb, 1), lambda i: (i, 0)),
                  full(sproj), full(sbias), full(log_rates), full(skip), rows, full(wo), full(ograd), full(srow)],
        out_specs=[rows, rows, pl.BlockSpec((tb * ns, ch), lambda i: (i, 0)), pl.BlockSpec((1, ns, ch), lambda i: (i, 0, 0)),
                   rows, pl.BlockSpec((seq, width), lambda i: (0, 0)), pl.BlockSpec(memory_space=pl.ANY)],
        out_shape=[jax.ShapeDtypeStruct((seq, ch), F32), jax.ShapeDtypeStruct((seq, ch), F32),
                   jax.ShapeDtypeStruct((seq * ns, ch), BF16), jax.ShapeDtypeStruct((nb, ns, ch), F32),
                   jax.ShapeDtypeStruct((seq, ch), BF16), jax.ShapeDtypeStruct((seq, width), BF16),
                   jax.ShapeDtypeStruct((wide * cap, width), BF16)],
        scratch_shapes=[pltpu.VMEM((ns, ch), F32)] + [pltpu.VMEM((ch // LANES, tb, LANES), F32)] * 2 + [pltpu.VMEM((ch // LANES, ns, LANES), F32),
                        *[pltpu.VMEM((8 * ns, 2 * LANES), F32)] * 2,
                        *[pltpu.VMEM((seq, width), BF16)] * 3, *[pltpu.SemaphoreType.DMA((3, nb * PIECES))] * 2,
                        pltpu.VMEM((seq, width), BF16), pltpu.VMEM((wide * cap, width), BF16),
                        pltpu.SemaphoreType.DMA((wide,)), pltpu.SemaphoreType.DMA((wide,))],
        compiler_params=pltpu.CompilerParams(collective_id=4, has_side_effects=True, vmem_limit_bytes=62 << 20),
        name="scan_mix",
    )(proj, inner, keep, sproj, sbias, log_rates, skip, z, wo, ograd, srow)


def experts_kernel(wide, tokens_ref, mixed_ref, gin_in, srow_ref, gain_ref, router_ref, up_in, ub_ref, down_in, db_ref,
                   gup_out, gub_ref, gdown_out, gdb_ref, ret_ref, terms_out, grow_ref,
                   pay_s, send_s, inbox_s, rgrad_s, act_s, dpre_s, own_s, near_s, far_s, acc_s, column_s, rows_s,
                   pay_sends, pay_arrivals, sends, arrivals, ret_sends, ret_arrivals, r_sends, r_arrivals, gup_ref, gdown_ref, out_ref, leaving,
                   gin_ref, up_ref, down_ref, coming):
    seq, width = tokens_ref.shape
    hid = up_ref.shape[1]
    cap = inbox_s.shape[0] // wide
    tb = LANES
    me, rank = lax.axis_index("wide"), lax.axis_index("tp")
    roles = line_roles()
    end, mid, mate, other = roles
    reads = [pltpu.make_async_copy(a, b, coming.at[n]) for n, (a, b) in enumerate(((gin_in, gin_ref), (up_in, up_ref), (down_in, down_ref)))]
    for read in reads:
        read.start()
    greet(wide)
    back = LineSum(roles, cap, SLOT_PIECES, own_s, near_s, own_s, far_s, sends, arrivals, behind=SLOT_BEHIND)

    def rows_of(b, size):
        return pl.ds(pl.multiple_of(b * size, size), size)

    def prepare(b, _):
        rows = rows_of(b, tb)
        hidden = tokens_ref[rows, :] + mixed_ref[rows, :].astype(F32)
        scale = lax.rsqrt(jnp.mean(hidden * hidden, axis=1, keepdims=True) + EPS)
        pay_s[rows, :] = (hidden * scale * as_row(gain_ref)).astype(BF16)
        return 0

    lax.fori_loop(0, seq // tb, prepare, 0)

    def payload(expert):
        ids = lax.broadcasted_iota(jnp.int32, (cap, seq), 0) + expert * cap
        chosen = jnp.where(ids == srow_ref[...], 1.0, 0.0).astype(BF16)
        return jnp.dot(chosen, pay_s[...], preferred_element_type=F32).astype(BF16)

    def dispatch(k):
        return pltpu.make_async_remote_copy(
            send_s.at[rows_of(k, cap)], inbox_s.at[rows_of(k, cap)], pay_sends.at[k], pay_arrivals.at[k],
            device_id={"wide": lax.rem(me + k, wide)}, device_id_type=MESH)

    def send(k):
        send_s[rows_of(k, cap), :] = payload(lax.rem(me + k, wide))
        dispatch(k).start()

    ahead = 2

    def send_first(k, _):
        send(k)
        return 0

    lax.fori_loop(1, ahead + 1, send_first, 0)
    inbox_s[0:cap, :] = payload(me)

    def give_back(c):
        return pltpu.make_async_remote_copy(
            far_s.at[rows_of(c, cap)], ret_ref.at[rows_of(me, cap)], ret_sends.at[c], ret_arrivals.at[c],
            device_id={"wide": lax.rem(me + wide - c, wide)}, device_id_type=MESH)

    def return_chunk(c):
        @pl.when(c == 0)
        def _():
            ret_ref[rows_of(me, cap), :] = far_s[0:cap, :]

        @pl.when(c != 0)
        def _():
            give_back(c).start()

    gub_ref[...] = jnp.zeros_like(gub_ref)
    gdb_ref[...] = jnp.zeros_like(gdb_ref)
    acc_s[...] = jnp.zeros_like(acc_s)
    turned = (((1,), (1,)), ((), ()))
    mine = lax.broadcasted_iota(jnp.int32, router_ref.shape, 0) == me
    column_s[...] = jnp.sum(jnp.where(mine, router_ref[...].astype(F32), 0.0), axis=0, keepdims=True)
    lane = lax.broadcasted_iota(jnp.int32, (cap, wide), 1)

    def compute(k, _):
        @pl.when(k + ahead < wide - 1)
        def _():
            send(k + ahead + 1)

        @pl.when(k > 0)
        def _():
            dispatch(k).wait_recv()

        part = rows_of(k, cap)
        rows_in = inbox_s[part, :]
        rows_raw = gin_ref[part, :].astype(F32)
        logits = lax.dot_general(rows_in, router_ref[...], turned, preferred_element_type=F32)
        logit = jnp.sum(jnp.where(lane == me, logits, 0.0), axis=1, keepdims=True)
        gate = 1.0 / (1.0 + jnp.exp(-logit))
        rows_grad = (gate * rows_raw).astype(BF16)
        rgrad_s[part, :] = rows_grad
        pre = jnp.dot(rows_in, up_ref[...], preferred_element_type=F32) + ub_ref[...]
        act, slope = gelu_pair(pre)
        act = act.astype(BF16)
        act_s[part, :] = act
        d_pre = (lax.dot_general(rows_grad, down_ref[...], turned, preferred_element_type=F32) * slope).astype(BF16)
        dpre_s[part, :] = d_pre
        out = jnp.dot(act, down_ref[...], preferred_element_type=F32) + db_ref[...] * (1.0 / LINE)
        d_logit = jnp.sum(rows_raw * out, axis=1, keepdims=True) * (gate * (1.0 - gate))
        own_s[part, :] = (lax.dot_general(d_pre, up_ref[...], turned, preferred_element_type=F32) + d_logit * column_s[...]).astype(BF16)

        @pl.when(end)
        def _():
            back.start(k)

        out_ref[part, :] = (gate * out).astype(BF16)
        acc_s[...] += jnp.sum(d_logit * rows_in.astype(F32), axis=0, keepdims=True)
        gub_ref[...] += jnp.sum(d_pre.astype(F32), axis=0, keepdims=True)
        gdb_ref[...] += jnp.sum(rows_grad.astype(F32), axis=0, keepdims=True)

        @pl.when(mid & (k > 0))
        def _():
            back.flow(k - 1, return_chunk)
        return 0

    for read in reads:
        read.wait()
    lax.fori_loop(0, wide, compute, 0)
    moves = [pltpu.make_async_copy(a, b, leaving.at[n])
             for n, (a, b) in enumerate(((out_ref, terms_out), (gdown_ref, gdown_out), (gup_ref, gup_out)))]
    moves[0].start()

    def term(k):
        return pltpu.make_async_remote_copy(rows_s.at[rank], rows_s.at[rank], r_sends.at[k], r_arrivals.at[k],
                                            device_id={"tp": lax.rem(rank + k, LINE)}, device_id_type=MESH)

    rows_s[rank] = jnp.broadcast_to(acc_s[...], (8, width))
    for k in range(1, LINE):
        term(k).start()

    @pl.when(mid)
    def _():
        back.flow(jnp.int32(wide - 1), return_chunk)

    tiles = hid // LANES
    across_rows = (((0,), (0,)), ((), ()))

    def tile(j, _):
        @pl.when(j < tiles)
        def _():
            cols = rows_of(j, LANES)
            gdown_ref[cols, :] = lax.dot_general(act_s[:, cols], rgrad_s[...], across_rows, preferred_element_type=F32)

        @pl.when(j >= tiles)
        def _():
            cols = rows_of(j - tiles, LANES)
            gup_ref[cols, :] = lax.dot_general(inbox_s[:, cols], dpre_s[...], across_rows, preferred_element_type=F32)

        @pl.when(end & (j < wide))
        def _():
            back.arrived(j)
            return_chunk(j)

        @pl.when(mid & (j == 1))
        def _():
            back.flush(wide, return_chunk)
        return 0

    lax.fori_loop(0, 2 * tiles, tile, 0)
    moves[1].start()
    moves[2].start()
    for k in range(1, LINE):
        term(k).wait_recv()
    grow_ref[...] = ((rows_s[0] + rows_s[1]) + rows_s[2]) + rows_s[3]
    for c in range(1, wide):
        give_back(c).wait_recv()
    back.sent(wide)
    for k in range(1, wide):
        dispatch(k).wait_send()
        give_back(k).wait_send()
    for k in range(1, LINE):
        term(k).wait_send()
    for move in moves:
        move.wait()


def experts_block(wide, cap, *operands):
    tokens, mixed, gin, srow, gain, router, up, ub, down, db = operands
    seq, width = tokens.shape
    hid = up.shape[1]
    vm = pl.BlockSpec(memory_space=pltpu.VMEM)
    hbm = pl.BlockSpec(memory_space=pl.ANY)
    shape = jax.ShapeDtypeStruct
    dma = pltpu.SemaphoreType.DMA
    slots = wide * cap
    return pl.pallas_call(
        functools.partial(experts_kernel, wide),
        in_specs=[vm, vm, hbm, vm, vm, vm, hbm, vm, hbm, vm],
        out_specs=[hbm, vm, hbm, vm, vm, hbm, vm],
        out_shape=[shape((width, hid), F32), shape((1, hid), F32), shape((hid, width), F32), shape((1, width), F32),
                   shape((slots, width), BF16), shape((slots, width), BF16), shape((8, width), F32)],
        scratch_shapes=[
            pltpu.VMEM((seq, width), BF16), *[pltpu.VMEM((slots, width), BF16)] * 3,
            pltpu.VMEM((slots, hid), BF16), pltpu.VMEM((slots, hid), BF16),
            *[pltpu.VMEM((slots, width), BF16)] * 3, pltpu.VMEM((1, width), F32), pltpu.VMEM((1, width), F32), pltpu.VMEM((LINE, 8, width), F32),
            dma((wide,)), dma((wide,)), *[dma((3, wide * SLOT_PIECES))] * 2, dma((wide,)), dma((wide,)), dma((LINE,)), dma((LINE,)),
            pltpu.VMEM((width, hid), F32), pltpu.VMEM((hid, width), F32), pltpu.VMEM((slots, width), BF16), dma((3,)),
            pltpu.VMEM((slots, width), BF16), pltpu.VMEM((width, hid), BF16), pltpu.VMEM((hid, width), BF16), dma((3,))],
        compiler_params=pltpu.CompilerParams(collective_id=2, has_side_effects=True, vmem_limit_bytes=62 << 20),
        name="experts",
    )(*operands)


def front_kernel(wide, taps, tokens_ref, gain_ref, inx_ref, inz_ref, outp_ref, cw_ref, cb_ref, wproj_ref, masks_ref,
                 scale_ref, normed_out, x_out, z_out, csum_out, inner_out, proj_ref, wx_out, wz_out, wo_out,
                 own_s, near_s, far_s, w_sends, w_arrivals, sends, arrivals,
                 normed_ref, x_ref, z_ref, csum_ref, inner_ref, wx_ref, wz_ref, wo_ref, leaving):
    seq, width = tokens_ref.shape
    ch = x_ref.shape[1]
    block = inx_ref.shape[0]
    tb = LANES
    nb = seq // tb
    me = lax.axis_index("wide")
    roles = line_roles()
    end, mid, mate, other = roles
    greet(wide)
    line = LineSum(roles, 2 * tb, 1, own_s, near_s, own_s, far_s, sends, arrivals)
    pairs = ((normed_ref, normed_out), (wx_ref, wx_out), (x_ref, x_out), (csum_ref, csum_out), (inner_ref, inner_out),
             (z_ref, z_out), (wz_ref, wz_out), (wo_ref, wo_out))
    moves = [pltpu.make_async_copy(a, b, leaving.at[n]) for n, (a, b) in enumerate(pairs)]
    mine = pl.ds(pl.multiple_of(me * block, block), block)
    weights = ((inx_ref, wx_ref), (inz_ref, wz_ref), (outp_ref, wo_ref))

    def share(which, k):
        source, target = weights[which]
        return pltpu.make_async_remote_copy(source, target.at[mine], w_sends.at[which, k], w_arrivals.at[which, k],
                                            device_id={"wide": lax.rem(me + k, wide)}, device_id_type=MESH)

    for which in range(3):
        for k in range(1, wide):
            share(which, k).start()
    for source, target in weights:
        target[mine, :] = source[...]

    def rows_of(b):
        return pl.ds(pl.multiple_of(b * tb, tb), tb)

    def norm(b, _):
        rows = rows_of(b)
        tokens = tokens_ref[rows, :]
        scale = lax.rsqrt(jnp.mean(tokens * tokens, axis=1, keepdims=True) + EPS)
        scale_ref[rows, :] = scale
        normed_ref[rows, :] = (tokens * scale * as_row(gain_ref)).astype(BF16)
        return 0

    own_s[...] = jnp.zeros_like(own_s)
    lax.fori_loop(0, nb, norm, 0)
    moves[0].start()
    for k in range(1, wide):
        share(0, k).wait_recv()
    moves[1].start()

    def step(b, _):
        rows = rows_of(b)
        base = pl.multiple_of(b * tb, tb)
        x = jnp.dot(normed_ref[rows, :], wx_ref[...], preferred_element_type=F32)
        x_ref[rows, :] = x
        prior = x_ref[pl.ds(pl.multiple_of(jnp.maximum(base - 8, 0), 8), 8), :]
        history = jnp.concatenate([prior, x], axis=0)
        same = masks_ref[rows, :]
        csum = as_row(cb_ref) + cw_ref[taps - 1:taps, :] * x
        for s in range(1, taps):
            csum = csum + cw_ref[taps - 1 - s:taps - s, :] * (same[:, s:s + 1] * history[8 - s:8 - s + tb, :])
        csum_ref[rows, :] = csum
        inner = (csum / (1.0 + jnp.exp(-csum))).astype(BF16)
        inner_ref[rows, :] = inner
        own_s[rows, :wproj_ref.shape[0]] = lax.dot_general(
            inner, wproj_ref[...], (((1,), (1,)), ((), ())), preferred_element_type=F32).astype(BF16)

        @pl.when(end & (lax.rem(b, 2) == 1))
        def _():
            line.start(b // 2)

        @pl.when(mid & (lax.rem(b, 2) == 1) & (b > 2))
        def _():
            line.flow(b // 2 - 1)
        return 0

    lax.fori_loop(0, nb, step, 0)
    steps = nb // 2
    for move in moves[2:5]:
        move.start()
    for k in range(1, wide):
        share(1, k).wait_recv()
    moves[6].start()

    def gate(b, _):
        rows = rows_of(b)
        z_ref[rows, :] = jnp.dot(normed_ref[rows, :], wz_ref[...], preferred_element_type=F32)
        return 0

    lax.fori_loop(0, steps, gate, 0)

    @pl.when(mid)
    def _():
        line.flow(jnp.int32(steps - 1))

    lax.fori_loop(steps, nb, gate, 0)
    moves[5].start()

    @pl.when(mid)
    def _():
        line.flush(steps)

    @pl.when(end)
    def _():
        for k in range(steps):
            line.arrived(k)

    proj_ref[...] = far_s[...].astype(F32)
    line.sent(steps)
    for k in range(1, wide):
        share(2, k).wait_recv()
    moves[7].start()
    for k in range(1, wide):
        for which in range(3):
            share(which, k).wait_send()
    for move in moves:
        move.wait()


def front(wide, taps, *operands):
    tokens, gain, inx, inz, outp, cw, cb, wproj, masks = operands
    seq, width = tokens.shape
    ch = inx.shape[1]
    vm = pl.BlockSpec(memory_space=pltpu.VMEM)
    hbm = pl.BlockSpec(memory_space=pl.ANY)
    shape = jax.ShapeDtypeStruct
    dma = pltpu.SemaphoreType.DMA
    return pl.pallas_call(
        functools.partial(front_kernel, wide, taps),
        in_specs=[vm] * len(operands),
        out_specs=[vm, *[hbm] * 5, vm, *[hbm] * 3],
        out_shape=[shape((seq, 1), F32), shape((seq, width), BF16), shape((seq, ch), F32), shape((seq, ch), F32), shape((seq, ch), F32),
                   shape((seq, ch), BF16), shape((seq, LANES), F32), *[shape((width, ch), BF16)] * 3],
        scratch_shapes=[*[pltpu.VMEM((seq, LANES), BF16)] * 3, dma((3, wide)), dma((3, wide)), dma((3, seq // LANES // 2)), dma((3, seq // LANES // 2)),
                        pltpu.VMEM((seq, width), BF16), *[pltpu.VMEM((seq, ch), F32)] * 3, pltpu.VMEM((seq, ch), BF16),
                        *[pltpu.VMEM((width, ch), BF16)] * 3, dma((8,))],
        compiler_params=pltpu.CompilerParams(collective_id=3, has_side_effects=True, vmem_limit_bytes=62 << 20),
        name="mixer_front",
    )(*operands)


def plain_device(
    tokens,
    segment_ids,
    routes,
    out_grad,
    mixer_gain,
    in_proj_x,
    in_proj_z,
    conv_weight,
    conv_bias,
    state_proj,
    step_proj,
    step_bias,
    log_rates,
    skip_gain,
    out_proj,
    expert_gain,
    router_weight,
    expert_up,
    up_bias,
    expert_down,
    down_bias,
):
    seq_len, model_width = tokens.shape
    conv_taps = conv_weight.shape[0]
    step_rank = step_proj.shape[0]
    experts = router_weight.shape[1]
    capacity = 5 * seq_len // (4 * experts)
    doc_ids = segment_ids[0]
    conv_masks = [same_document(doc_ids, offset)[:, None] for offset in range(conv_taps)]
    first_scale = lax.rsqrt(jnp.mean(tokens * tokens, axis=1, keepdims=True) + EPS)
    first_unit = tokens * first_scale
    normed = (first_unit * mixer_gain).astype(jnp.bfloat16)
    gathered_x, gathered_z, gathered_out = (
        lax.all_gather(in_proj_x, "wide", axis=0, tiled=True),
        lax.all_gather(in_proj_z, "wide", axis=0, tiled=True),
        lax.all_gather(out_proj, "wide", axis=0, tiled=True),
    )
    x_branch = multiply(normed, gathered_x)
    z_branch = multiply(normed, gathered_z)
    conv_sum = conv_bias + jnp.zeros_like(x_branch)
    for offset in range(conv_taps):
        conv_sum = conv_sum + conv_weight[conv_taps - 1 - offset] * conv_masks[
            offset
        ] * shifted_down(x_branch, offset)
    inner_act = jax.nn.silu(conv_sum).astype(jnp.bfloat16)
    wide_proj = jnp.pad(state_proj, ((0, 0), (0, LANES - state_proj.shape[1])))
    projected = lax.psum(multiply(inner_act, wide_proj), "tp")
    tall_proj = jnp.pad(step_proj, ((0, LANES - step_rank), (0, 0)))
    carry_mask = same_document(doc_ids, 1)[:, None]
    scan_out, step_size, states, starts = scan_fwd(
        projected, inner_act, carry_mask, tall_proj, step_bias[None], log_rates, skip_gain[None], step_rank
    )
    z_gate = jax.nn.silu(z_branch)
    gated = (scan_out * z_gate).astype(jnp.bfloat16)
    mixed = lax.psum(contract_cols(gated, gathered_out).astype(jnp.bfloat16), "tp").astype(
        jnp.float32
    )
    hidden = tokens + mixed
    second_scale = lax.rsqrt(jnp.mean(hidden * hidden, axis=1, keepdims=True) + EPS)
    second_unit = hidden * second_scale
    expert_in = (second_unit * expert_gain).astype(jnp.bfloat16)
    route_ids = routes[:, 0]
    chosen_int = (routes == jnp.arange(experts, dtype=jnp.int32)[None, :]).astype(jnp.int32)
    chosen = chosen_int.astype(jnp.float32)
    logits = multiply(expert_in, router_weight)
    gate = jax.nn.sigmoid(jnp.sum(logits * chosen, axis=1))
    rank_of = jnp.arange(seq_len, dtype=jnp.int32)
    earlier = (rank_of[:, None] > rank_of[None, :]).astype(jnp.bfloat16)
    position = jnp.sum(multiply(earlier, chosen.astype(jnp.bfloat16)) * chosen, axis=1).astype(jnp.int32)
    kept = position < capacity
    slots = jnp.where(kept, route_ids * capacity + position, experts * capacity)
    scaled_grad = (gate[:, None] * out_grad).astype(jnp.bfloat16)
    sent_width = expert_in.shape[1]
    send_in = (
        jnp.zeros((experts * capacity + 1, sent_width), jnp.bfloat16).at[slots].set(expert_in)[:-1]
    )
    send_grad = (
        jnp.zeros((experts * capacity + 1, sent_width), jnp.bfloat16)
        .at[slots]
        .set(scaled_grad)[:-1]
    )
    recv_in, recv_grad = (
        lax.all_to_all(
            send_in.reshape(experts, capacity, sent_width),
            "wide",
            split_axis=0,
            concat_axis=0,
            tiled=True,
        ),
        lax.all_to_all(
            send_grad.reshape(experts, capacity, sent_width),
            "wide",
            split_axis=0,
            concat_axis=0,
            tiled=True,
        ),
    )
    rows_in = recv_in.reshape(-1, model_width)
    rows_grad = recv_grad.reshape(-1, model_width)
    pre_act = multiply(rows_in, expert_up[0]) + up_bias[0]
    hidden_act = jax.nn.gelu(pre_act).astype(jnp.bfloat16)
    partial_out = multiply(hidden_act, expert_down[0])
    up_grad = contract_cols(rows_grad, expert_down[0])
    d_pre = jax.vjp(jax.nn.gelu, pre_act)[1](up_grad)[0].astype(jnp.bfloat16)
    partial_back = contract_cols(d_pre, expert_up[0])
    grad_down = contract_rows(hidden_act, rows_grad)
    grad_dbias = jnp.sum(rows_grad.astype(jnp.float32), axis=0)
    grad_up = contract_rows(rows_in, d_pre)
    grad_ubias = jnp.sum(d_pre.astype(jnp.float32), axis=0)
    out_sum, back_sum = (
        lax.psum(partial_out.astype(jnp.bfloat16), "tp").astype(jnp.float32),
        lax.psum(partial_back.astype(jnp.bfloat16), "tp").astype(jnp.float32),
    )
    bias_part = down_bias[0]
    outgoing = (out_sum + bias_part).astype(jnp.bfloat16).reshape(experts, capacity, -1)
    back_rows = back_sum.astype(jnp.bfloat16).reshape(experts, capacity, -1)
    incoming, arriving = (
        lax.all_to_all(outgoing, "wide", split_axis=0, concat_axis=0, tiled=True),
        lax.all_to_all(back_rows, "wide", split_axis=0, concat_axis=0, tiled=True),
    )
    safe_slots = jnp.minimum(slots, experts * capacity - 1)
    returned = jnp.where(
        kept[:, None], incoming.reshape(-1, model_width)[safe_slots].astype(jnp.float32), 0.0
    )
    result = hidden + gate[:, None] * returned
    d_gate = jnp.sum(out_grad * returned, axis=1)
    d_logit = (d_gate * gate * (1.0 - gate))[:, None] * chosen
    grad_router = jnp.dot(expert_in.astype(jnp.float32).T, d_logit, precision=HIGH)
    d_norm_two = jnp.dot(d_logit, router_weight.astype(jnp.float32).T, precision=HIGH)
    d_norm_two = d_norm_two + jnp.where(
        kept[:, None], arriving.reshape(-1, model_width)[safe_slots].astype(jnp.float32), 0.0
    )
    grad_second_gain = jnp.sum(d_norm_two * second_unit, axis=0)
    d_hidden = out_grad + rms_back(d_norm_two * expert_gain, second_unit, second_scale)
    d_mixed = d_hidden.astype(jnp.bfloat16)
    d_gated = multiply(d_mixed, gathered_out)
    grad_out = contract_rows(d_mixed, gated)
    d_scan = d_gated * z_gate
    d_z = (d_gated * scan_out * silu_slope(z_branch)).astype(jnp.bfloat16)
    d_step_pre, d_inner, d_proj, grad_step, grad_sbias, grad_rates, grad_skip = scan_bwd(
        projected, inner_act, carry_mask, step_size, states, starts, d_scan, tall_proj, log_rates, skip_gain[None], step_rank
    )
    grad_step, grad_sbias, grad_skip = grad_step[:step_rank], grad_sbias[0], grad_skip[0]
    d_projected = lax.psum(d_proj.astype(jnp.bfloat16), "tp")
    grad_state = contract_rows(inner_act, d_projected)[:, : state_proj.shape[1]]
    d_inner = d_inner + contract_cols(d_projected, wide_proj)
    d_conv = d_inner * silu_slope(conv_sum)
    grad_cbias = jnp.sum(d_conv, axis=0)
    conv_rows = []
    d_input = jnp.zeros_like(d_conv)
    for offset in range(conv_taps):
        conv_rows.append(
            jnp.sum(d_conv * conv_masks[offset] * shifted_down(x_branch, offset), axis=0)
        )
        d_input = d_input + conv_weight[conv_taps - 1 - offset] * shifted_up(
            conv_masks[offset] * d_conv, offset
        )
    grad_conv = jnp.stack(conv_rows[::-1])
    d_x_branch = d_input.astype(jnp.bfloat16)
    grad_in_x = contract_rows(normed, d_x_branch)
    grad_in_z = contract_rows(normed, d_z)
    d_normed = lax.psum(
        (contract_cols(d_x_branch, gathered_x) + contract_cols(d_z, gathered_z)).astype(
            jnp.bfloat16
        ),
        "tp",
    ).astype(jnp.float32)
    grad_first_gain = jnp.sum(d_normed * first_unit, axis=0)
    tokens_grad = d_hidden + rms_back(d_normed * mixer_gain, first_unit, first_scale)
    grad_in_x, grad_in_z, grad_out = (
        summed_on_arrival(grad_in_x.astype(jnp.bfloat16), "wide", 0),
        summed_on_arrival(grad_in_z.astype(jnp.bfloat16), "wide", 0),
        summed_on_arrival(grad_out.astype(jnp.bfloat16), "wide", 0),
    )
    (
        grad_first_gain,
        grad_conv,
        grad_cbias,
        grad_state,
        grad_step,
        grad_sbias,
        grad_rates,
        grad_skip,
        grad_second_gain,
        grad_router,
    ) = lax.psum(
        (
            grad_first_gain,
            grad_conv,
            grad_cbias,
            grad_state,
            grad_step,
            grad_sbias,
            grad_rates,
            grad_skip,
            grad_second_gain,
            grad_router,
        ),
        "wide",
    )
    return (
        result,
        tokens_grad,
        grad_first_gain,
        grad_in_x,
        grad_in_z,
        grad_conv,
        grad_cbias,
        grad_state,
        grad_step,
        grad_sbias,
        grad_rates,
        grad_skip,
        grad_out,
        grad_second_gain,
        grad_router,
        grad_up[None],
        grad_ubias[None],
        grad_down[None],
        grad_dbias[None],
    )


def fast_device(
    tokens,
    segment_ids,
    routes,
    out_grad,
    mixer_gain,
    in_proj_x,
    in_proj_z,
    conv_weight,
    conv_bias,
    state_proj,
    step_proj,
    step_bias,
    log_rates,
    skip_gain,
    out_proj,
    expert_gain,
    router_weight,
    expert_up,
    up_bias,
    expert_down,
    down_bias,
):
    seq_len, model_width = tokens.shape
    conv_taps = conv_weight.shape[0]
    step_rank = step_proj.shape[0]
    experts = router_weight.shape[1]
    capacity = 5 * seq_len // (4 * experts)
    doc_ids = segment_ids[0]
    conv_masks = [same_document(doc_ids, offset)[:, None] for offset in range(conv_taps)]
    masks = jnp.pad(jnp.concatenate(conv_masks, axis=1), ((0, 8), (0, 8 - conv_taps)))
    wide = lax.axis_size("wide")
    states = log_rates.shape[0]
    chosen = (routes == jnp.arange(experts, dtype=jnp.int32)[None, :]).astype(jnp.float32)
    rank_of = jnp.arange(seq_len, dtype=jnp.int32)
    earlier = (rank_of[:, None] > rank_of[None, :]).astype(jnp.bfloat16)
    position = jnp.sum(multiply(earlier, chosen.astype(jnp.bfloat16)) * chosen, axis=1).astype(jnp.int32)
    slots = jnp.where(position < capacity, routes[:, 0] * capacity + position, experts * capacity)
    slot_row, slot_col = slots[None], slots[:, None]
    carry_mask = same_document(doc_ids, 1)[:, None]

    first_scale, normed, x_branch, z_branch, conv_sum, inner_act, projected, gathered_x, gathered_z, gathered_out = front(
        wide, conv_taps, tokens, mixer_gain, in_proj_x, in_proj_z, out_proj, conv_weight, conv_bias, state_proj.T, masks
    )
    scan_out, step_size, held, starts, gated, mixed, grads_in = scan_mix(
        projected, inner_act, carry_mask, step_proj, step_bias, log_rates, skip_gain, z_branch, gathered_out, out_grad, slot_row,
        step_rank, wide, capacity,
    )
    grad_up, grad_ubias, grad_down, grad_dbias, returned, terms, router_grad = experts_block(
        wide, capacity, tokens, mixed, grads_in, slot_row, expert_gain, router_weight.T,
        expert_up[0], up_bias, expert_down[0], down_bias,
    )
    d_hidden, d_normed, grad_in_x, grad_in_z, grad_out, small, gated_out = mixer_back(
        wide, conv_taps, step_rank,
        (projected, carry_mask, step_size, held, starts, tokens, mixed, out_grad, slot_col, z_branch, scan_out),
        (inner_act, step_proj, log_rates, skip_gain, returned, expert_gain, gathered_out, terms, x_branch, conv_sum, masks, state_proj.T,
         conv_weight, normed, gated, gathered_x, gathered_z, mixer_gain, router_grad),
    )
    outs = finish(
        step_rank, states, experts, tokens, mixed, slot_col, gated_out, d_hidden, d_normed, first_scale, mixer_gain, small,
        grad_in_x, grad_in_z, grad_out, grad_up, grad_down, grad_ubias, grad_dbias,
    )
    return tuple(out.T if n in (7, 14) else out for n, out in enumerate(outs))


def solution(mesh):
    in_specs = (
        P("wide", None),
        P("wide", None),
        P("wide", None),
        P("wide", None),
        P(),
        P("wide", "tp"),
        P("wide", "tp"),
        P(None, "tp"),
        P("tp"),
        P("tp", None),
        P(None, "tp"),
        P("tp"),
        P(None, "tp"),
        P("tp"),
        P("wide", "tp"),
        P(),
        P(),
        P("wide", None, "tp"),
        P("wide", "tp"),
        P("wide", "tp", None),
        P("wide", None),
    )
    out_specs = (
        P("wide", None),
        P("wide", None),
        P(),
        P("wide", "tp"),
        P("wide", "tp"),
        P(None, "tp"),
        P("tp"),
        P("tp", None),
        P(None, "tp"),
        P("tp"),
        P(None, "tp"),
        P("tp"),
        P("wide", "tp"),
        P(),
        P(),
        P("wide", None, "tp"),
        P("wide", "tp"),
        P("wide", "tp", None),
        P("wide", None),
    )
    wide, line = mesh.shape["wide"], mesh.shape["tp"]
    per_device = fast_device if line == 4 and wide == 8 else plain_device
    return jax.shard_map(
        per_device, mesh=mesh, in_specs=in_specs, out_specs=out_specs, check_vma=False
    )
```
